32 devices in a mesh: dp: 16 (over z, y, x), seq: 2 (over core).
Axes of the slice: x: 2, y: 2, z: 4, core: 2. Of those that a mesh axis runs over, the one named last changes fastest.
Arguments:
- layer_input: bfloat16 [16, 256, 1088], P('dp', 'seq'), may hold values from -6 to 6
- segments: int32 [16, 256], P('dp'), may hold values from 0 to 3, never falling along the last dimension, each value on 1 to 128 neighbouring positions
- w_attn: bfloat16 [3551232], P(('dp', 'seq')), may hold values from -1 to 1
- w_out: bfloat16 [1183744], P(('dp', 'seq')), may hold values from -1.5 to 1.5
- w_fc: bfloat16 [4734976], P(('dp', 'seq')), may hold values from -0.1875 to 0.1875
- w_proj: bfloat16 [4734976], P(('dp', 'seq')), may hold values from -0.09375 to 0.09375
- norm_params: bfloat16 [4352], P(('dp', 'seq')), may hold values from -1 to 3
- lin_bias: bfloat16 [4352], P(('dp', 'seq')), may hold values from -3 to 3
- fc_bias: bfloat16 [4352], P(('dp', 'seq')), may hold values from -3 to 3
- out_cotangent: bfloat16 [16, 256, 1088], P('dp', 'seq'), may hold values from -6 to 6
Outputs:
- layer_output: bfloat16 [16, 256, 1088], P('dp', 'seq')
- input_grad: float32 [16, 256, 1088], P('dp', 'seq')
- w_attn_grad: float32 [3551232], P(('dp', 'seq'))
- w_out_grad: float32 [1183744], P(('dp', 'seq'))
- w_fc_grad: float32 [4734976], P(('dp', 'seq'))
- w_proj_grad: float32 [4734976], P(('dp', 'seq'))
- norm_grad: float32 [4352], P(('dp', 'seq'))
- bias_grad: float32 [4352], P(('dp', 'seq'))
- fc_bias_grad: float32 [4352], P(('dp', 'seq'))
The draws below stay inside these ranges and needn't reach their ends.
Inputs may be any that keep to these rules, and one draw needn't show every extreme that they name: `segments`: along each sequence the numbers never fall; each number marks one document.
All inputs are finite; a program needn't handle non-finite values.
Results may differ from the reference program's by a relative error of at most 0.011.
Values may be sent and summed in bfloat16 or wider, within the bound.
A program may use at most 320 MiB of HBM per device.

```python
import math
import jax
import jax.numpy as jnp
import numpy as np
from jax import lax

D = 1088
H = 17
HD = 64
FF = 4352
SEQLEN = 256
SEQS = 16


def draw_w_attn(key, part):
    base_key = jax.random.fold_in(key, 11)
    matrix = jnp.clip(jax.random.normal(base_key, (D, 3 * D), jnp.float32), -6.0, 6.0) * D ** (-0.5)
    return jnp.clip(matrix, -1.0, 1.0).reshape(-1).astype(jnp.bfloat16)


def draw_norm_params(key, part):
    gain_key = jax.random.fold_in(key, 21)
    offset_key = jax.random.fold_in(key, 22)
    gains = jax.random.uniform(gain_key, (2, 1, D), jnp.float32, 0.5, 1.5)
    offsets = jnp.clip(0.3 * jax.random.normal(offset_key, (2, 1, D), jnp.float32), -1.0, 1.0)
    return jnp.concatenate([gains, offsets], axis=1).reshape(-1).astype(jnp.bfloat16)


def shard_levels(key, extent, cuts, low, high):
    gain, own = 1.0, jax.random.fold_in(key, 6)
    for dim, shards_of in cuts:
        steps = jnp.exp(jax.random.uniform(jax.random.fold_in(own, dim), (shards_of,), jnp.float32, low / len(cuts), high / len(cuts)))
        gain = gain * jnp.repeat(steps, extent[dim] // shards_of).reshape([-1 if axis == dim else 1 for axis in range(len(extent))])
    return gain


def profile(number_of, total, reach, lean):
    weights = [(1 << 20) // math.isqrt(grade ** lean) + 1 for grade in range(2, number_of + 1)]
    surplus, holding = total - reach - (number_of - 1), [1] * (number_of - 1)
    while surplus > 0:
        candidates = [i for i in range(number_of - 1) if holding[i] < reach]
        mass, remaining = sum([weights[i] for i in candidates]), surplus
        for i in candidates:
            addition = min(reach - holding[i], max(1, remaining * weights[i] // mass), surplus)
            holding[i] = holding[i] + addition
            surplus = surplus - addition
    return np.array([reach] + holding)


def ragged(rng, number_of, total, most, lean):
    if number_of == 2:
        one = jax.random.randint(rng, (), max(1, total - most), min(most, total - 1) + 1)
        return jnp.stack([one, total - one])
    sizes = jnp.asarray(profile(number_of, total, most, lean), jnp.int32)
    pairs = (number_of - 1) // 2
    giver, sink = sizes[1:1 + 2 * pairs:2], sizes[2:2 + 2 * pairs:2]
    slack = jnp.minimum(giver - 1, most - sink)
    passed = jax.random.randint(jax.random.fold_in(rng, 1), (pairs,), 0, 1 << 20) % (slack + 1)
    sizes = sizes.at[1:1 + 2 * pairs:2].set(giver - passed).at[2:2 + 2 * pairs:2].set(sink + passed)
    return sizes[jax.random.permutation(jax.random.fold_in(rng, 2), number_of)]


def scatter_about(key, dims, spread, bound, pieces=(), dtype=jnp.bfloat16):
    entries = jax.random.normal(key, dims, jnp.float32) * spread
    if len(pieces) > 0:
        entries = shard_levels(key, dims, pieces, -0.22, 0.18) * entries
    return jnp.clip(entries, min=-bound, max=bound).astype(dtype)


def setup_inputs(seed: int = 0) -> dict:
    key_of = jax.random.split(jax.random.key(seed), 11)
    return {
        "layer_input": scatter_about(key_of[0], (SEQS, SEQLEN, D), 1.0, 6.0, ((0, 16), (1, 2))),
        "segments": jax.vmap(lambda own: jnp.searchsorted(jnp.cumsum(ragged(own, 4, SEQLEN, SEQLEN // 2, 0)), jnp.arange(SEQLEN), side="right"))(jax.random.split(key_of[1], SEQS)).reshape((SEQS, SEQLEN)).astype(jnp.int32),
        "w_attn": draw_w_attn(jax.random.fold_in(key_of[10], 71), 0),
        "w_out": scatter_about(key_of[3], (D * D,), (D // 64) ** -0.5, 1.5, ((0, 32),)),
        "w_fc": scatter_about(key_of[4], (D * FF,), D ** -0.5, 0.1875, ((0, 32),)),
        "w_proj": scatter_about(key_of[5], (FF * D,), FF ** -0.5, 0.09375, ((0, 32),)),
        "norm_params": draw_norm_params(jax.random.fold_in(key_of[10], 71), 0),
        "lin_bias": scatter_about(key_of[7], (4 * D,), 0.3, 3.0, ((0, 32),)),
        "fc_bias": scatter_about(key_of[8], (FF,), 0.3, 3.0, ((0, 32),)),
        "out_cotangent": scatter_about(key_of[9], (SEQS, SEQLEN, D), 1.0, 6.0, ((0, 16), (1, 2))),
    }


GELU_C = 0.7978845608028654
NORM_EPS = 1e-05

def gelu_parts(inputs):
    tanh_value = jnp.tanh(GELU_C * (inputs + 0.044715 * inputs * inputs * inputs))
    value = 0.5 * inputs * (1.0 + tanh_value)
    slope = 0.5 * (1.0 + tanh_value) + 0.5 * inputs * (1.0 - tanh_value * tanh_value) * GELU_C * (1.0 + 3.0 * 0.044715 * inputs * inputs)
    return (value, slope)

def layer_norm(inputs, gains, offsets):
    average = lax.optimization_barrier(jnp.mean(inputs, axis=-1, keepdims=True))
    centred = inputs - average
    inv_std = lax.rsqrt(lax.optimization_barrier(jnp.mean(centred * centred, axis=-1, keepdims=True)) + NORM_EPS)
    x_hat = centred * inv_std
    return (x_hat * gains + offsets, x_hat, inv_std)

def norm_back(grad_out, x_hat, inv_std, gains):
    grad_hat = grad_out * gains
    grad_in = inv_std * (grad_hat - lax.optimization_barrier(jnp.mean(grad_hat, axis=-1, keepdims=True)) - x_hat * lax.optimization_barrier(jnp.mean(grad_hat * x_hat, axis=-1, keepdims=True)))
    return (grad_in, lax.optimization_barrier(jnp.sum(grad_out * x_hat, axis=0)), lax.optimization_barrier(jnp.sum(grad_out, axis=0)))

def score_block(queries, key_rows, allowed):
    scores = jnp.einsum('qhd,khd->hqk', queries.astype(jnp.float32), key_rows.astype(jnp.float32)) * HD ** (-0.5)
    return jnp.where(allowed[None], scores, -1e+30)

def one_sequence(seq_input, seq_segments, seq_cotangent, mats):
    w_qkv, w_o, w_up, w_down, norms, biases, up_bias = mats
    length = seq_input.shape[0]
    inputs_f = seq_input.astype(jnp.float32)
    normed1, x_hat1, inv_std1 = layer_norm(inputs_f, norms[0], norms[1])
    act_in1 = normed1.astype(jnp.bfloat16)
    projected = jnp.dot(act_in1, w_qkv, preferred_element_type=jnp.float32)
    queries = (projected[:, :D] + biases[0]).astype(jnp.bfloat16).reshape(length, H, HD)
    key_rows = projected[:, D:2 * D].astype(jnp.bfloat16).reshape(length, H, HD)
    value_rows = (projected[:, 2 * D:] + biases[1]).astype(jnp.bfloat16).reshape(length, H, HD)
    positions = jnp.arange(length)
    allowed = (positions[None, :] <= positions[:, None]) & (seq_segments[None, :] == seq_segments[:, None])
    scores = score_block(queries, key_rows, allowed)
    top_score = lax.optimization_barrier(jnp.max(scores, axis=-1, keepdims=True))
    log_total = top_score + jnp.log(lax.optimization_barrier(jnp.sum(jnp.exp(scores - top_score), axis=-1, keepdims=True)))
    attn_probs = jnp.exp(scores - log_total).astype(jnp.bfloat16)
    attended = jnp.einsum('hqk,khd->qhd', attn_probs.astype(jnp.float32), value_rows.astype(jnp.float32))
    attended = attended.reshape(length, D).astype(jnp.bfloat16)
    resid = inputs_f + jnp.dot(attended, w_o, preferred_element_type=jnp.float32) + biases[2]
    normed2, x_hat2, inv_std2 = layer_norm(resid, norms[2], norms[3])
    act_in2 = normed2.astype(jnp.bfloat16)
    hidden_pre = jnp.dot(act_in2, w_up, preferred_element_type=jnp.float32) + up_bias
    hidden_act, hidden_slope = gelu_parts(hidden_pre)
    hidden_b = hidden_act.astype(jnp.bfloat16)
    result = (resid + jnp.dot(hidden_b, w_down, preferred_element_type=jnp.float32) + biases[3]).astype(jnp.bfloat16)
    grad_out = seq_cotangent.astype(jnp.float32)
    grad_down = jnp.dot(hidden_b.T, seq_cotangent, preferred_element_type=jnp.float32)
    grad_bp = lax.optimization_barrier(jnp.sum(grad_out, axis=0))
    grad_hidden = jnp.dot(seq_cotangent, w_down.T, preferred_element_type=jnp.float32) * hidden_slope
    grad_hidden_b = grad_hidden.astype(jnp.bfloat16)
    grad_up = jnp.dot(act_in2.T, grad_hidden_b, preferred_element_type=jnp.float32)
    grad_up_bias = lax.optimization_barrier(jnp.sum(grad_hidden, axis=0))
    grad_norm2 = jnp.dot(grad_hidden_b, w_up.T, preferred_element_type=jnp.float32)
    grad_resid_n, grad_g2, grad_b2 = norm_back(grad_norm2, x_hat2, inv_std2, norms[2])
    grad_resid = grad_out + grad_resid_n
    grad_resid_b = grad_resid.astype(jnp.bfloat16)
    grad_o = jnp.dot(attended.T, grad_resid_b, preferred_element_type=jnp.float32)
    grad_bo = lax.optimization_barrier(jnp.sum(grad_resid, axis=0))
    grad_att = jnp.dot(grad_resid_b, w_o.T, preferred_element_type=jnp.float32).astype(jnp.bfloat16).reshape(length, H, HD)
    probs_full = jnp.exp(score_block(queries, key_rows, allowed) - log_total)
    probs_b = probs_full.astype(jnp.bfloat16)
    grad_probs = jnp.einsum('qhd,khd->hqk', grad_att.astype(jnp.float32), value_rows.astype(jnp.float32))
    delta = lax.optimization_barrier(jnp.sum(probs_full * grad_probs, axis=-1, keepdims=True))
    grad_scores = (probs_full * (grad_probs - delta) * HD ** (-0.5)).astype(jnp.bfloat16).astype(jnp.float32)
    grad_q = jnp.einsum('hqk,khd->qhd', grad_scores, key_rows.astype(jnp.float32)).reshape(length, D)
    grad_k = jnp.einsum('hqk,qhd->khd', grad_scores, queries.astype(jnp.float32)).reshape(length, D)
    grad_v = jnp.einsum('hqk,qhd->khd', probs_b.astype(jnp.float32), grad_att.astype(jnp.float32)).reshape(length, D)
    grad_proj_b = jnp.concatenate([grad_q, grad_k, grad_v], axis=1).astype(jnp.bfloat16)
    grad_qkv = jnp.dot(act_in1.T, grad_proj_b, preferred_element_type=jnp.float32)
    grad_norm1 = jnp.dot(grad_proj_b, w_qkv.T, preferred_element_type=jnp.float32)
    grad_in_n, grad_g1, grad_b1 = norm_back(grad_norm1, x_hat1, inv_std1, norms[0])
    grad_input = grad_resid + grad_in_n
    norm_terms = jnp.stack([grad_g1, grad_b1, grad_g2, grad_b2])
    bias_terms = jnp.stack([lax.optimization_barrier(jnp.sum(grad_q, axis=0)), lax.optimization_barrier(jnp.sum(grad_v, axis=0)), grad_bo, grad_bp])
    grads = (grad_qkv, grad_o, grad_up, grad_down, norm_terms, bias_terms, grad_up_bias)
    return (result, grad_input, grads)

def reference(layer_input, segments, w_attn, w_out, w_fc, w_proj, norm_params, lin_bias, fc_bias, out_cotangent):
    mats = (w_attn.reshape(D, 3 * D), w_out.reshape(D, D), w_fc.reshape(D, FF), w_proj.reshape(FF, D), norm_params.astype(jnp.float32).reshape(4, D), lin_bias.astype(jnp.float32).reshape(4, D), fc_bias.astype(jnp.float32))
    zeros = (jnp.zeros((D, 3 * D), jnp.float32), jnp.zeros((D, D), jnp.float32), jnp.zeros((D, FF), jnp.float32), jnp.zeros((FF, D), jnp.float32), jnp.zeros((4, D), jnp.float32), jnp.zeros((4, D), jnp.float32), jnp.zeros((FF,), jnp.float32))

    def scan_body(running, inputs):
        result, grad_input, grads = one_sequence(inputs[0], inputs[1], inputs[2], mats)
        return (tuple((total + term for total, term in zip(running, grads))), (result, grad_input))
    totals, stacked = lax.scan(scan_body, zeros, (layer_input, segments, out_cotangent))
    return (stacked[0], stacked[1], totals[0].reshape(-1), totals[1].reshape(-1), totals[2].reshape(-1), totals[3].reshape(-1), totals[4].reshape(-1), totals[5].reshape(-1), totals[6])
```

```python
import functools

import jax
import jax.numpy as jnp
from jax import lax
from jax.experimental import pallas as pl
from jax.experimental.pallas import tpu as pltpu
from jax.sharding import PartitionSpec as P

HD = 64
FF = 4352


GELU_C = 0.7978845608028654
NORM_EPS = 1e-05


def gelu_parts(inputs):
    tanh_value = jnp.tanh(GELU_C * (inputs + 0.044715 * inputs * inputs * inputs))
    value = 0.5 * inputs * (1.0 + tanh_value)
    slope = 0.5 * (1.0 + tanh_value) + 0.5 * inputs * (1.0 - tanh_value * tanh_value) * GELU_C * (
        1.0 + 3.0 * 0.044715 * inputs * inputs
    )
    return (value, slope)


def layer_norm(inputs, gains, offsets):
    average = jnp.mean(inputs, axis=-1, keepdims=True)
    centred = inputs - average
    inv_std = lax.rsqrt(jnp.mean(centred * centred, axis=-1, keepdims=True) + NORM_EPS)
    x_hat = centred * inv_std
    return (x_hat * gains + offsets, x_hat, inv_std)


def norm_back(grad_out, x_hat, inv_std, gains):
    grad_hat = grad_out * gains
    grad_in = inv_std * (
        grad_hat
        - jnp.mean(grad_hat, axis=-1, keepdims=True)
        - x_hat * jnp.mean(grad_hat * x_hat, axis=-1, keepdims=True)
    )
    return (grad_in, jnp.sum(grad_out * x_hat, axis=0), jnp.sum(grad_out, axis=0))


def score_block(queries, key_rows, allowed):
    scores = jnp.einsum(
        "qhd,khd->hqk", queries, key_rows, preferred_element_type=jnp.float32
    ) * HD ** (-0.5)
    return jnp.where(allowed[None], scores, -1e30)


def outer_sum(left, right):
    return jnp.einsum("na,nb->ab", left, right, preferred_element_type=jnp.float32)


AXES = ("dp", "seq")


def shard_height(shard, columns):
    size = shard.shape[0]
    return size // columns if size % columns == 0 else 0


def tile_height(shard, columns):
    height = shard_height(shard, columns)
    return 0 if height % 8 else height


def padded(height):
    return -(-height // 8) * 8


def gather_rows(shard, columns, height, extra=None):
    if not height:
        return lax.all_gather(shard, AXES, axis=0, tiled=True).reshape(-1, columns)
    block = shard.reshape(height, columns)
    room = padded(height) - height
    if extra is not None:
        row = jnp.pad(extra, (0, columns - extra.shape[0]))[None]
        block = jnp.concatenate([block, row], axis=0)
        room -= 1
    if room:
        block = jnp.pad(block, ((0, room), (0, 0)))
    return lax.all_gather(block, AXES, axis=0, tiled=True)


def spread(acts, height):
    room = padded(height) - height
    if not room:
        return acts
    tokens = acts.shape[0]
    parts = acts.reshape(tokens, -1, height)
    return jnp.pad(parts, ((0, 0), (0, 0), (0, room))).reshape(tokens, -1)


def unspread(acts, height):
    if padded(height) == height:
        return acts
    tokens = acts.shape[0]
    return acts.reshape(tokens, -1, padded(height))[:, :, :height].reshape(tokens, -1)


def scatter_rows(blocks, height):
    count = lax.axis_size(AXES)
    sums = lax.psum_scatter(
        blocks.astype(jnp.bfloat16).reshape(count, -1, blocks.shape[-1]),
        AXES,
        scatter_dimension=0,
        tiled=True,
    )[0]
    return sums.astype(jnp.float32)


def scatter_flat(block, shard):
    count = lax.axis_size(AXES)
    return lax.psum_scatter(
        block.reshape(count, shard), AXES, scatter_dimension=0, tiled=True
    )[0]


def own_half_sum(terms, place, tokens):
    if lax.axis_size("seq") != 2:
        return lax.psum_scatter(
            terms.astype(jnp.bfloat16), "seq", scatter_dimension=0, tiled=True
        ).astype(jnp.float32)
    own = lax.dynamic_slice_in_dim(terms, place * tokens, tokens)
    other = lax.dynamic_slice_in_dim(terms, (1 - place) * tokens, tokens)
    came = lax.ppermute(other.astype(jnp.bfloat16), "seq", [(0, 1), (1, 0)])
    return own + came.astype(jnp.float32)


def per_device(
    layer_input,
    segments,
    w_attn,
    w_out,
    w_fc,
    w_proj,
    norm_params,
    lin_bias,
    fc_bias,
    out_cotangent,
):
    tokens = layer_input.shape[1]
    width = layer_input.shape[2]
    heads = width // HD
    place = lax.axis_index("seq")
    first = place * tokens
    small = norm_params.shape[0]
    height = shard_height(w_attn, 3 * width)
    height = height if shard_height(w_out, width) == height == shard_height(w_fc, FF) else 0
    down_height = tile_height(w_proj, width)
    own_small = jnp.concatenate([norm_params, lin_bias, fc_bias])
    packed = height and padded(height) > height and own_small.shape[0] <= width
    if height:
        lanes = -(-width // 128) * 128
        joined_shard = jnp.concatenate(
            [
                jnp.pad(w_out.reshape(height, width), ((0, 0), (0, lanes - width))),
                w_attn.reshape(height, 3 * width),
            ],
            axis=1,
        ).reshape(-1)
        joined_w = gather_rows(
            joined_shard, lanes + 3 * width, height, own_small if packed else None
        )
        w_o = joined_w[:, :width]
        w_qkv = joined_w[:, lanes:]
    else:
        w_qkv = gather_rows(w_attn, 3 * width, 0)
        w_o = gather_rows(w_out, width, 0)
    w_up = gather_rows(w_fc, FF, height)
    w_down = gather_rows(w_proj, width, down_height)
    if packed:
        smalls = w_o.reshape(-1, padded(height), width)[:, height, : 3 * small]
    else:
        smalls = lax.all_gather(own_small, AXES, axis=0)
    smalls = smalls.astype(jnp.float32).reshape(-1, 3, small)
    norms = smalls[:, 0].reshape(4, width)
    biases = smalls[:, 1].reshape(4, width)
    up_bias = smalls[:, 2].reshape(FF)
    inputs_f = layer_input[0].astype(jnp.float32)
    normed1, x_hat1, inv_std1 = layer_norm(inputs_f, norms[0], norms[1])
    act_in1 = normed1.astype(jnp.bfloat16)
    act_rows1 = spread(act_in1, height)
    projected = jnp.dot(act_rows1, w_qkv, preferred_element_type=jnp.float32)
    queries = (projected[:, :width] + biases[0]).astype(jnp.bfloat16)
    own_keys = projected[:, width : 2 * width].astype(jnp.bfloat16)
    own_values = (projected[:, 2 * width :] + biases[1]).astype(jnp.bfloat16)
    key_rows, value_rows = (
        lax.all_gather(own_keys, "seq", axis=0, tiled=True),
        lax.all_gather(own_values, "seq", axis=0, tiled=True),
    )
    key_count = key_rows.shape[0]
    key_pos = jnp.arange(key_count)
    query_pos = first + jnp.arange(tokens)
    padded_seg = jnp.concatenate([jnp.full((tokens,), -1, jnp.int32), segments[0]])
    key_seg = lax.dynamic_slice_in_dim(padded_seg, tokens, key_count)
    query_seg = lax.dynamic_slice_in_dim(segments[0], first, tokens)
    allowed = (key_pos[None, :] <= query_pos[:, None]) & (key_seg[None, :] == query_seg[:, None])
    q_heads = queries.reshape(tokens, heads, HD)
    k_heads = key_rows.reshape(key_count, heads, HD)
    v_heads = value_rows.reshape(key_count, heads, HD)
    scores = score_block(q_heads, k_heads, allowed)
    top_score = jnp.max(scores, axis=-1, keepdims=True)
    log_total = top_score + jnp.log(jnp.sum(jnp.exp(scores - top_score), axis=-1, keepdims=True))
    attn_probs = jnp.exp(scores - log_total).astype(jnp.bfloat16)
    attended = jnp.einsum("hqk,khd->qhd", attn_probs, v_heads, preferred_element_type=jnp.float32)
    attended = attended.reshape(tokens, width).astype(jnp.bfloat16)
    attended_rows = spread(attended, height)
    resid = inputs_f + jnp.dot(attended_rows, w_o, preferred_element_type=jnp.float32) + biases[2]
    normed2, x_hat2, inv_std2 = layer_norm(resid, norms[2], norms[3])
    act_in2 = normed2.astype(jnp.bfloat16)
    act_rows2 = spread(act_in2, height)
    hidden_pre = jnp.dot(act_rows2, w_up, preferred_element_type=jnp.float32) + up_bias
    hidden_act, hidden_slope = gelu_parts(hidden_pre)
    hidden_b = hidden_act.astype(jnp.bfloat16)
    hidden_rows = spread(hidden_b, down_height)
    result = (
        resid + jnp.dot(hidden_rows, w_down, preferred_element_type=jnp.float32) + biases[3]
    ).astype(jnp.bfloat16)
    cotangent = out_cotangent[0]
    grad_out = cotangent.astype(jnp.float32)
    grad_bp = jnp.sum(grad_out, axis=0)
    grad_hidden = (
        unspread(
            jnp.einsum("nd,fd->nf", cotangent, w_down, preferred_element_type=jnp.float32),
            down_height,
        )
        * hidden_slope
    )
    grad_hidden_b = grad_hidden.astype(jnp.bfloat16)
    grad_down = outer_sum(hidden_rows, cotangent)
    if down_height:
        grad_hidden_b, grad_down = lax.optimization_barrier(
            (grad_hidden_b, grad_down.astype(jnp.bfloat16))
        )
    grad_up_bias = jnp.sum(grad_hidden, axis=0)
    if down_height:
        proj_sums = scatter_rows(grad_down, down_height)[:down_height].reshape(-1)
    else:
        proj_sums = scatter_flat(grad_down, w_proj.shape[0])
    grad_up = outer_sum(act_rows2, grad_hidden_b)
    if height:
        fc_sums = scatter_rows(grad_up, height)[:height].reshape(-1)
    else:
        fc_sums = scatter_flat(grad_up, w_fc.shape[0])
    grad_norm2 = unspread(
        jnp.einsum("nf,df->nd", grad_hidden_b, w_up, preferred_element_type=jnp.float32), height
    )
    grad_resid_n, grad_g2, grad_b2 = norm_back(grad_norm2, x_hat2, inv_std2, norms[2])
    grad_resid = grad_out + grad_resid_n
    grad_resid_b = grad_resid.astype(jnp.bfloat16)
    grad_bo = jnp.sum(grad_resid, axis=0)
    grad_att = unspread(
        jnp.einsum(
            "ne,de->nd", grad_resid_b, w_o, preferred_element_type=jnp.float32
        ).astype(jnp.bfloat16),
        height,
    )
    grad_att_heads = grad_att.reshape(tokens, heads, HD)
    probs_full = jnp.exp(score_block(q_heads, k_heads, allowed) - log_total)
    probs_b = probs_full.astype(jnp.bfloat16)
    grad_probs = jnp.einsum(
        "qhd,khd->hqk", grad_att_heads, v_heads, preferred_element_type=jnp.float32
    )
    delta = jnp.sum(probs_full * grad_probs, axis=-1, keepdims=True)
    grad_scores = (probs_full * (grad_probs - delta) * HD ** (-0.5)).astype(jnp.bfloat16)
    grad_q = jnp.einsum(
        "hqk,khd->qhd", grad_scores, k_heads, preferred_element_type=jnp.float32
    ).reshape(tokens, width)
    grad_k_all = jnp.einsum(
        "hqk,qhd->khd", grad_scores, q_heads, preferred_element_type=jnp.float32
    ).reshape(key_count, width)
    grad_v_all = jnp.einsum(
        "hqk,qhd->khd", probs_b, grad_att_heads, preferred_element_type=jnp.float32
    ).reshape(key_count, width)
    grad_k = own_half_sum(grad_k_all, place, tokens)
    grad_v = own_half_sum(grad_v_all, place, tokens)
    grad_proj_b = jnp.concatenate([grad_q, grad_k, grad_v], axis=1).astype(jnp.bfloat16)
    grad_norm1 = unspread(
        jnp.einsum("ne,de->nd", grad_proj_b, w_qkv, preferred_element_type=jnp.float32), height
    )
    grad_in_n, grad_g1, grad_b1 = norm_back(grad_norm1, x_hat1, inv_std1, norms[0])
    grad_input = grad_resid + grad_in_n
    norm_terms = jnp.concatenate([grad_g1, grad_b1, grad_g2, grad_b2])
    bias_terms = jnp.concatenate(
        [jnp.sum(grad_q, axis=0), jnp.sum(grad_v, axis=0), grad_bo, grad_bp]
    )
    small_terms = jnp.concatenate(
        [term.reshape(-1, 1, small) for term in (norm_terms, bias_terms, grad_up_bias)], axis=1
    )
    grad_attn = outer_sum(act_rows1, grad_proj_b)
    grad_wo = outer_sum(attended_rows, grad_resid_b)
    if height:
        joined = jnp.concatenate(
            [grad_attn.astype(jnp.bfloat16), grad_wo.astype(jnp.bfloat16)], axis=1
        )
        if packed:
            blocks = joined.reshape(-1, padded(height), 4 * width)
            row = small_terms.astype(jnp.bfloat16).reshape(-1, 1, 3 * small)
            row = jnp.pad(row, ((0, 0), (height, padded(height) - height - 1), (0, width * 4 - 3 * small)))
            joined = (blocks + row).reshape(joined.shape)
        sums = scatter_rows(joined, height)
        qkv_sums = sums[:height, : 3 * width].reshape(-1)
        out_sums = sums[:height, 3 * width :].reshape(-1)
    else:
        qkv_sums = scatter_flat(grad_attn, w_attn.shape[0])
        out_sums = scatter_flat(grad_wo, w_out.shape[0])
    if packed:
        small_sums = sums[height, : 3 * small].reshape(3, small)
    else:
        small_sums = lax.psum_scatter(small_terms, AXES, scatter_dimension=0, tiled=True)[0]
    norm_sums, bias_sums, fcb_sums = small_sums[0], small_sums[1], small_sums[2]
    return (
        result[None],
        grad_input[None],
        qkv_sums,
        out_sums,
        fc_sums,
        proj_sums,
        norm_sums,
        bias_sums,
        fcb_sums,
    )


MESH = pl.DeviceIdType.MESH


class Place:
    def __init__(self, nz):
        self.nz = nz
        self.dp = lax.axis_index("dp")
        self.core = lax.axis_index("seq")
        self.x = lax.rem(self.dp, 2)
        self.y = lax.rem(self.dp // 2, 2)
        self.z = self.dp // 4
        fx, fy = 1 - 2 * self.x, 2 - 4 * self.y
        self.flip = (0, fx, fy, fx + fy)

    def chip(self, dz, p):
        return self.dp + 4 * dz + self.flip[p]

    def has(self, dz):
        return jnp.logical_and(self.z + dz >= 0, self.z + dz < self.nz)

    def meet(self):
        barrier = pltpu.get_barrier_semaphore()
        for dz, p in ((0, 1), (0, 2)):
            pl.semaphore_signal(
                barrier, inc=1, device_id=(self.chip(dz, p), self.core), device_id_type=MESH
            )
        for dz in (1, -1):
            @pl.when(self.has(dz))
            def _():
                pl.semaphore_signal(
                    barrier, inc=1, device_id=(self.chip(dz, 0), self.core), device_id_type=MESH
                )
        pl.semaphore_wait(barrier, 2 + self.has(1).astype(jnp.int32) + self.has(-1).astype(jnp.int32))


def slots(nz):
    return [0] + [s * k for k in range(1, nz) for s in (1, -1)]


def gather_kernel(nz, items, count, *refs):
    ins, outs = refs[:count], refs[count : 2 * count]
    send_sem, recv_sem, local_sem = refs[2 * count :]
    at = Place(nz)
    ids = {}

    def number(key):
        return ids.setdefault(key, len(ids))

    def copy(item, key, chip, to, part, src=None):
        array, lo, mid, hi, _ = item
        lanes = {"all": (lo, hi - lo), "a": (lo, mid - lo), "b": (mid, hi - mid)}[part]
        cut = pl.ds(*lanes)
        dst = outs[array].at[chip, :, cut]
        n = number((item, key))
        return pltpu.make_async_remote_copy(
            src_ref=dst if src is None else ins[array].at[:, cut],
            dst_ref=dst,
            send_sem=send_sem.at[n],
            recv_sem=recv_sem.at[n],
            device_id=(to, at.core),
            device_id_type=MESH,
        )

    locals_ = []
    for a in range(count):
        cp = pltpu.make_async_copy(ins[a], outs[a].at[at.dp], local_sem.at[a])
        cp.start()
        locals_.append(cp)
    at.meet()
    events = []
    ends = []

    def always(fn):
        fn()

    def add(when, order, pred, fn):
        events.append((when, order, pred, fn))

    def launch(pred, make):
        make().start()
        ends.append(((0, q), lambda: make().wait_send()))

    for order, item in enumerate(items):
        kind = item[4]
        if kind == "zp":
            for q in slots(nz):
                d = abs(q)
                step = 1 if q > 0 else -1
                pred = None if q == 0 else at.has(q)

                def start(item=item, q=q, step=step, pred=pred):
                    src = True if q == 0 else None
                    if q != 0:
                        copy(item, ("z", q), at.chip(q, 0), at.dp, "all").wait_recv()
                    for go in ((1, -1) if q == 0 else (-step,)):
                        pr = at.has(go)
                        key = ("z", q - go)
                        if abs(q - go) >= nz:
                            continue
                        def mk(go=go, key=key, src=src):
                            return copy(item, key, at.chip(q, 0), at.chip(go, 0), "all", src)
                        @pl.when(pr)
                        def _():
                            mk().start()
                        ends.append(((go, q), lambda mk=mk: mk().wait_send()))
                    for p in (1, 2):
                        def mk2(p=p, src=src):
                            return copy(item, ("p", p, q), at.chip(q, 0), at.chip(0, p), "all", src)
                        mk2().start()
                        ends.append(((0, q), lambda mk2=mk2: mk2().wait_send()))

                def relay(item=item, q=q, pred=pred):
                    for p, part in ((1, "a"), (2, "b")):
                        copy(item, ("p", p, q), at.chip(q, p), at.dp, "all").wait_recv()
                        def mk(p=p, part=part):
                            return copy(item, ("d", p, q), at.chip(q, p), at.chip(0, 3 - p), part)
                        mk().start()
                        ends.append(((0, q), lambda mk=mk: mk().wait_send()))

                def last(item=item, q=q):
                    for p, part in ((1, "a"), (2, "b")):
                        copy(item, ("d", p, q), at.chip(q, 3), at.dp, part).wait_recv()

                add(d, order, pred, start)
                add(d + 1.5, order, pred, relay)
                add(90, order, pred, last)
        else:
            def to_z(item, q, p, pred, src=None):
                for go in (1, -1) if q == 0 else ((-1,) if q > 0 else (1,)):
                    if abs(q - go) >= nz:
                        continue
                    pr = at.has(go)
                    def mk(go=go):
                        return copy(item, ("z", p, q - go), at.chip(q, p), at.chip(go, 0), "all", src)
                    @pl.when(pr)
                    def _():
                        mk().start()
                    ends.append(((go, q), lambda mk=mk: mk().wait_send()))

            def start(item=item):
                for p in (1, 2):
                    def mk2(p=p):
                        return copy(item, ("p", p), at.dp, at.chip(0, p), "all", True)
                    mk2().start()
                    ends.append(((0, 0), lambda mk2=mk2: mk2().wait_send()))
                to_z(item, 0, 0, None, True)

            def relay(item=item):
                for p, part in ((1, "a"), (2, "b")):
                    copy(item, ("p", p), at.chip(0, p), at.dp, "all").wait_recv()
                    def mk(p=p, part=part):
                        return copy(item, ("d", p), at.chip(0, p), at.chip(0, 3 - p), part)
                    mk().start()
                    ends.append(((0, 0), lambda mk=mk: mk().wait_send()))
                    to_z(item, 0, p, None)

            def diagonal(item=item):
                for p, part in ((1, "a"), (2, "b")):
                    copy(item, ("d", p), at.chip(0, 3), at.dp, part).wait_recv()
                to_z(item, 0, 3, None)

            add(0, order, None, start)
            add(1.2, order, None, relay)
            add(2.2, order, None, diagonal)
            for q in slots(nz)[1:]:
                for p in range(4):
                    pred = at.has(q)
                    def onward(item=item, q=q, p=p, pred=pred):
                        copy(item, ("z", p, q), at.chip(q, p), at.dp, "all").wait_recv()
                        to_z(item, q, p, pred)
                    add(abs(q) + 0.8 * (0, 1, 1, 2)[p], order, pred, onward)
    for _, _, pred, fn in sorted(events, key=lambda e: e[:2]):
        if pred is None:
            fn()
        else:
            pl.when(pred)(fn)
    for needs, fn in ends:
        pl.when(functools.reduce(jnp.logical_and, [at.has(dz) for dz in needs]))(fn)
    for cp in locals_:
        cp.wait()


def gather_call(nz, arrays, items, collective_id):
    count = len(arrays)
    sems = 40 * len(items)
    return pl.pallas_call(
        functools.partial(gather_kernel, nz, items, count),
        out_shape=[jax.ShapeDtypeStruct((4 * nz, *a.shape), a.dtype) for a in arrays],
        in_specs=[pl.BlockSpec(memory_space=pl.ANY)] * count,
        out_specs=[pl.BlockSpec(memory_space=pl.ANY)] * count,
        scratch_shapes=[
            pltpu.SemaphoreType.DMA((sems,)),
            pltpu.SemaphoreType.DMA((sems,)),
            pltpu.SemaphoreType.DMA((count,)),
        ],
        compiler_params=pltpu.CompilerParams(
            collective_id=collective_id, has_side_effects=True, vmem_limit_bytes=56 * 2**20
        ),
    )(*arrays)


def strips(lo, hi, fn):
    def body(i, carry):
        fn(pl.multiple_of(i * 128, 128))
        return carry

    lax.fori_loop(0, (hi - lo) // 128, body, 0)


def far_first(nz):
    return [sorted(range(nz), key=lambda t: -abs(t - z)) for z in range(nz)]


def choose(scalar, values):
    picked = jnp.int32(values[0])
    for i, v in enumerate(values[1:], 1):
        picked = jnp.where(scalar == i, jnp.int32(v), picked)
    return picked


def scatter_kernel(nz, items, count, *refs):
    ins, outs = refs[:count], refs[count : 2 * count]
    bufs = refs[2 * count : 2 * count + 4 * len(items)]
    send_sem, recv_sem = refs[2 * count + 4 * len(items) :]
    at = Place(nz)
    table = far_first(nz)
    dest = [choose(at.z, [table[z][k] for z in range(nz)]) for k in range(nz)]
    at.meet()
    used = [0]

    def numbers(size):
        used[0] += size
        return used[0] - size

    events, ends = [], []

    def add(when, order, fn):
        events.append((when, order, fn))

    def send(src, dst, n, chip, needs=None):
        def make():
            return pltpu.make_async_remote_copy(
                src_ref=src,
                dst_ref=dst,
                send_sem=send_sem.at[n],
                recv_sem=recv_sem.at[n],
                device_id=(chip, at.core),
                device_id_type=MESH,
            )
        return make

    def go(make, needs=None):
        make().start()
        ends.append((needs, make))

    def came(dst, n):
        pltpu.make_async_remote_copy(
            src_ref=dst, dst_ref=dst, send_sem=send_sem.at[n], recv_sem=recv_sem.at[n],
            device_id=(at.dp, at.core), device_id_type=MESH,
        ).wait_recv()

    f32 = jnp.float32

    for order, item in enumerate(items):
        array, lo, mid, hi, kind = item
        width, na = hi - lo, mid - lo
        src, out = ins[array], outs[array]
        part_d, part_x, part_y, line = bufs[4 * order : 4 * order + 4]
        cut = {"a": (pl.ds(0, na), pl.ds(lo, na)), "b": (pl.ds(na, width - na), pl.ds(mid, width - na))}
        whole = pl.ds(lo, width)

        def plane(k, value, t0, finish, order=order, part_d=part_d, part_x=part_x, part_y=part_y,
                  cut=cut, na=na, width=width, lo=lo):
            base = numbers(6)
            landing = {1: part_x, 2: part_y}

            def lanes(p, half):
                ref, first = value(p)
                start, size = (0, na) if half == "a" else (na, width - na)
                return ref.at[:, pl.ds(first + start, size)]

            def first():
                for p, half, n in ((2, "a", 0), (1, "b", 1)):
                    go(send(lanes(3, half), part_d.at[k, :, cut[half][0]], base + n, at.chip(0, p)))
                for p, half, n in ((1, "b", 2), (2, "a", 3)):
                    go(send(lanes(p, half), landing[p].at[k, :, cut[half][0]], base + n, at.chip(0, p)))

            def second():
                for p, half, n, m in ((1, "a", 0, 4), (2, "b", 1, 5)):
                    here = part_d.at[k, :, cut[half][0]]
                    came(here, base + n)
                    ref, start = value(p)
                    l, h = (0, na) if half == "a" else (na, width)

                    def one(i, ref=ref, start=start, l=l):
                        at_d = pl.ds(pl.multiple_of(l + i, 128), 128)
                        at_v = pl.ds(pl.multiple_of(start + l + i, 128), 128)
                        part_d[k, :, at_d] = (
                            part_d[k, :, at_d].astype(f32) + ref[:, at_v].astype(f32)
                        ).astype(part_d.dtype)

                    strips(l, h, one)
                    go(send(here, landing[p].at[k, :, cut[half][0]], base + m, at.chip(0, p)))

            def third():
                for p, half, n in ((1, "b", 2), (2, "a", 3), (1, "a", 4), (2, "b", 5)):
                    came(landing[p].at[k, :, cut[half][0]], base + n)
                finish()

            add(t0, order, first)
            add(t0 + 1, order, second)
            add(t0 + 2, order, third)

        if kind == "zp":
            line_n = numbers(nz + 1)
            for k in range(nz):
                dst = dest[k]

                def value(p, dst=dst, src=src, lo=lo):
                    return src.at[dst * 4 + lax.rem(at.chip(0, p), 4)], lo

                def total(i, k=k, dst=dst, src=src, lo=lo, part_x=part_x, part_y=part_y):
                    at_v = pl.ds(pl.multiple_of(lo + i, 128), 128)
                    at_i = pl.ds(i, 128)
                    return (
                        src[dst * 4 + lax.rem(at.dp, 4), :, at_v].astype(f32)
                        + part_x[k, :, at_i].astype(f32)
                        + part_y[k, :, at_i].astype(f32)
                    )

                if k < nz - 1:

                    def finish(k=k, dst=dst, total=total, width=width, part_x=part_x, line=line, line_n=line_n):
                        for step in (1, -1):
                            ahead = dst > at.z if step > 0 else dst < at.z
                            first = at.z == (0 if step > 0 else nz - 1)
                            slot = dst if step > 0 else jnp.where(dst == at.z - 1, nz, dst)

                            @pl.when(jnp.logical_and(ahead, first))
                            def _():
                                def one(i):
                                    part_x[k, :, pl.ds(i, 128)] = total(i).astype(part_x.dtype)
                                strips(0, width, one)
                                make = send(part_x.at[k], line.at[slot], line_n + slot, at.chip(step, 0))
                                make().start()

                            @pl.when(jnp.logical_and(ahead, jnp.logical_not(first)))
                            def _():
                                came(line.at[dst], line_n + dst)
                                def one(i):
                                    line[dst, :, pl.ds(i, 128)] = (
                                        total(i) + line[dst, :, pl.ds(i, 128)].astype(f32)
                                    ).astype(line.dtype)
                                strips(0, width, one)
                                make = send(line.at[dst], line.at[slot], line_n + slot, at.chip(step, 0))
                                make().start()

                        def done():
                            for step in (1, -1):
                                ahead = dst > at.z if step > 0 else dst < at.z
                                slot = dst if step > 0 else jnp.where(dst == at.z - 1, nz, dst)
                                @pl.when(ahead)
                                def _():
                                    send(line.at[dst], line.at[slot], line_n + slot, at.chip(step, 0))().wait_send()
                        ends.append((None, done))

                else:

                    def finish(dst=dst, total=total, width=width, lo=lo, out=out, line=line, line_n=line_n):
                        def one(i):
                            out[:, pl.ds(pl.multiple_of(lo + i, 128), 128)] = total(i)
                        strips(0, width, one)
                        for step, slot in ((-1, at.z), (1, nz)):
                            @pl.when(at.has(step))
                            def _():
                                came(line.at[slot], line_n + slot)
                                def two(i):
                                    at_v = pl.ds(pl.multiple_of(lo + i, 128), 128)
                                    out[:, at_v] += line[slot, :, pl.ds(i, 128)].astype(f32)
                                strips(0, width, two)

                plane(k, value, float(k) if k < nz - 1 else k + 0.0, finish)
        else:
            line_n = numbers(4 * (nz + 1))
            mine = (nz + 1) * 4
            for k in range(nz - 1):
                dst = dest[k]
                for p in (3, 1, 2, 0):

                    def chain(p=p, dst=dst, src=src, line=line, line_n=line_n, lo=lo, width=width, whole=whole):
                        piece = dst * 4 + lax.rem(at.chip(0, p), 4)
                        for step in (1, -1):
                            ahead = dst > at.z if step > 0 else dst < at.z
                            first = at.z == (0 if step > 0 else nz - 1)
                            slot = (dst if step > 0 else jnp.where(dst == at.z - 1, nz, dst)) * 4 + p
                            here = dst * 4 + p

                            @pl.when(jnp.logical_and(ahead, first))
                            def _():
                                send(src.at[piece, :, whole], line.at[slot], line_n + slot, at.chip(step, 0))().start()

                            @pl.when(jnp.logical_and(ahead, jnp.logical_not(first)))
                            def _():
                                came(line.at[here], line_n + here)
                                def one(i):
                                    line[here, :, pl.ds(i, 128)] = (
                                        src[piece, :, pl.ds(pl.multiple_of(lo + i, 128), 128)].astype(f32)
                                        + line[here, :, pl.ds(i, 128)].astype(f32)
                                    ).astype(line.dtype)
                                strips(0, width, one)
                                send(line.at[here], line.at[slot], line_n + slot, at.chip(step, 0))().start()

                        def done():
                            for step in (1, -1):
                                ahead = dst > at.z if step > 0 else dst < at.z
                                slot = (dst if step > 0 else jnp.where(dst == at.z - 1, nz, dst)) * 4 + p
                                @pl.when(ahead)
                                def _():
                                    send(line.at[slot], line.at[slot], line_n + slot, at.chip(step, 0))().wait_send()
                        ends.append((None, done))

                    add(k + (0.0, 0.0, 0.0, 0.5)[p], order, chain)

            def gathered(src=src, line=line, line_n=line_n, lo=lo, width=width):
                for p in (3, 1, 2, 0):
                    piece = at.z * 4 + lax.rem(at.chip(0, p), 4)
                    low, high = at.z * 4 + p, nz * 4 + p
                    for step, slot in ((-1, low), (1, high)):
                        @pl.when(at.has(step))
                        def _():
                            came(line.at[slot], line_n + slot)

                    def one(i):
                        cut_i = pl.ds(i, 128)
                        own = src[piece, :, pl.ds(pl.multiple_of(lo + i, 128), 128)].astype(f32)
                        below = jnp.where(at.has(-1), line[low, :, cut_i].astype(f32), 0.0)
                        above = jnp.where(at.has(1), line[high, :, cut_i].astype(f32), 0.0)
                        line[mine + p, :, cut_i] = (own + below + above).astype(line.dtype)
                    strips(0, width, one)

            def value(p, line=line):
                return line.at[mine + p], 0

            def finish(line=line, out=out, lo=lo, width=width, part_x=part_x, part_y=part_y):
                def one(i):
                    cut_i = pl.ds(i, 128)
                    out[:, pl.ds(pl.multiple_of(lo + i, 128), 128)] = (
                        line[mine, :, cut_i].astype(f32)
                        + part_x[0, :, cut_i].astype(f32)
                        + part_y[0, :, cut_i].astype(f32)
                    )
                strips(0, width, one)

            add(nz - 1 + 0.2, order, gathered)
            plane(0, value, nz - 1 + 0.3, finish)
    for _, _, fn in sorted(events, key=lambda e: e[:2]):
        fn()
    for needs, fn in ends:
        if needs is None and not hasattr(fn, "__wrapped_send__"):
            r = fn()
            if r is not None:
                r.wait_send()


def scatter_call(nz, arrays, items, collective_id):
    count = len(arrays)
    scratch = []
    for array, lo, mid, hi, kind in items:
        rows, width, dtype = arrays[array].shape[1], hi - lo, arrays[array].dtype
        planes = nz if kind == "zp" else 1
        lines = nz + 1 if kind == "zp" else 4 * (nz + 1) + 4
        scratch += [pltpu.VMEM((n, rows, width), dtype) for n in (planes, planes, planes, lines)]
    sems = sum(7 * nz + 1 if i[4] == "zp" else 4 * (nz + 1) + 6 for i in items)
    return pl.pallas_call(
        functools.partial(scatter_kernel, nz, items, count),
        out_shape=[jax.ShapeDtypeStruct(a.shape[1:], jnp.float32) for a in arrays],
        in_specs=[pl.BlockSpec(memory_space=pltpu.VMEM)] * count,
        out_specs=[pl.BlockSpec(memory_space=pltpu.VMEM)] * count,
        scratch_shapes=scratch
        + [pltpu.SemaphoreType.DMA((sems,)), pltpu.SemaphoreType.DMA((sems,))],
        compiler_params=pltpu.CompilerParams(
            collective_id=collective_id, has_side_effects=True, vmem_limit_bytes=60 * 2**20
        ),
    )(*arrays)


def attend(scores_of, heads, lse_ref, q_ref, k_ref, v_ref, o_ref, allowed):
    for h in range(heads):
        at = slice(h * HD, (h + 1) * HD)
        scores = scores_of(q_ref[:, at], k_ref[:, at], allowed)
        top = jnp.max(scores, axis=-1, keepdims=True)
        total = top + jnp.log(jnp.sum(jnp.exp(scores - top), axis=-1, keepdims=True))
        probs = jnp.exp(scores - total).astype(jnp.bfloat16)
        lse_ref[:, h : h + 1] = total
        o_ref[:, at] = jnp.dot(
            probs, v_ref[:, at], preferred_element_type=jnp.float32
        ).astype(o_ref.dtype)


def head_scores(queries, key_rows, allowed):
    scores = lax.dot_general(
        queries, key_rows, (((1,), (1,)), ((), ())), preferred_element_type=jnp.float32
    ) * HD ** (-0.5)
    return jnp.where(allowed, scores, -1e30)


def may_see(seg_rows, seg_cols):
    length = seg_cols.shape[1]
    i = lax.broadcasted_iota(jnp.int32, (length, length), 0)
    j = lax.broadcasted_iota(jnp.int32, (length, length), 1)
    return (j <= i) & (seg_rows == seg_cols)


def attention_kernel(heads, q_ref, k_ref, v_ref, rows_ref, cols_ref, o_ref, lse_ref):
    allowed = may_see(rows_ref[...], cols_ref[...])
    attend(head_scores, heads, lse_ref, q_ref, k_ref, v_ref, o_ref, allowed)


def attention_back_kernel(
    heads, q_ref, k_ref, v_ref, rows_ref, cols_ref, lse_ref, do_ref, dq_ref, dk_ref, dv_ref, sums_ref
):
    allowed = may_see(rows_ref[...], cols_ref[...])
    f32 = jnp.float32
    lanes = (((1,), (1,)), ((), ()))
    rows = (((0,), (0,)), ((), ()))
    for h in range(heads):
        at = slice(h * HD, (h + 1) * HD)
        q, k, v, do = q_ref[:, at], k_ref[:, at], v_ref[:, at], do_ref[:, at]
        probs = jnp.exp(head_scores(q, k, allowed) - lse_ref[:, h : h + 1])
        grad_probs = lax.dot_general(do, v, lanes, preferred_element_type=f32)
        delta = jnp.sum(probs * grad_probs, axis=-1, keepdims=True)
        grad_scores = (probs * (grad_probs - delta) * HD ** (-0.5)).astype(jnp.bfloat16)
        dq = jnp.dot(grad_scores, k, preferred_element_type=f32)
        dk = lax.dot_general(grad_scores, q, rows, preferred_element_type=f32)
        dv = lax.dot_general(probs.astype(jnp.bfloat16), do, rows, preferred_element_type=f32)
        sums_ref[0:1, at] = jnp.sum(dq, axis=0, keepdims=True)
        sums_ref[1:2, at] = jnp.sum(dv, axis=0, keepdims=True)
        dq_ref[:, at] = dq.astype(dq_ref.dtype)
        dk_ref[:, at] = dk.astype(dk_ref.dtype)
        dv_ref[:, at] = dv.astype(dv_ref.dtype)


VMEM_LIMIT = 60 * 2**20


def local_call(kernel, outs, *args):
    spec = pl.BlockSpec(memory_space=pltpu.VMEM)
    return pl.pallas_call(
        kernel,
        out_shape=outs,
        in_specs=[spec] * len(args),
        out_specs=[spec] * len(outs),
        compiler_params=pltpu.CompilerParams(vmem_limit_bytes=VMEM_LIMIT),
    )(*args)


def up_to(value, step):
    return -(-value // step) * step


def split_items(shapes, dtype_rows=None):
    (_, wa), (_, wf), (_, wp) = shapes
    first = up_to(2 * wa // 3, 128)

    def cut(array, lo, hi, kind):
        return (array, lo, lo + up_to((hi - lo) // 2, 128), hi, kind)

    return (
        cut(0, 0, first, "pz"),
        cut(0, first, wa, "zp"),
        cut(1, 0, wf, "zp"),
        cut(2, 0, wp, "zp"),
    )


def per_device_grid(
    nz,
    layer_input,
    segments,
    w_attn,
    w_out,
    w_fc,
    w_proj,
    norm_params,
    lin_bias,
    fc_bias,
    out_cotangent,
):
    f32, bf16 = jnp.float32, jnp.bfloat16
    core = lax.axis_index("seq")
    low = core == 0
    chips = lax.axis_size("dp")
    tokens, width = layer_input.shape[1:]
    heads = width // HD
    own_heads = -(-heads // 2)
    hw = own_heads * HD
    over = 2 * hw - width
    half = width // 2
    small = norm_params.shape[0]
    h = w_out.shape[0] // width
    rows, rp = 2 * h, up_to(2 * h, 8)
    fh = w_proj.shape[0] // width
    fp = up_to(fh + 2, 16)
    hidden = chips * fp
    wide = up_to(width, 128)
    owide = up_to(3 * hw + half, 128) - 3 * hw

    def swap(value):
        return lax.ppermute(value, "seq", [(0, 1), (1, 0)])

    def pair(own, came):
        return jnp.where(low, own, came), jnp.where(low, came, own)

    def lanes_of(value, size):
        first, second = value[..., :size], value[..., value.shape[-1] - size :]
        return jnp.where(low, first, second), jnp.where(low, second, first)

    def tokens_of(value):
        first, second = value[:tokens], value[tokens:]
        return jnp.where(low, first, second), jnp.where(low, second, first)

    def spread(acts):
        parts = acts.reshape(acts.shape[0], chips, rows)
        return jnp.pad(parts, ((0, 0), (0, 0), (0, rp - rows))).reshape(acts.shape[0], -1)

    def unspread(acts):
        return acts.reshape(acts.shape[0], chips, rp)[:, :, :rows].reshape(acts.shape[0], width)

    def dot(a, b):
        return jnp.dot(a, b, preferred_element_type=f32)

    def dot_t(a, b):
        return lax.dot_general(a, b, (((1,), (1,)), ((), ())), preferred_element_type=f32)

    def outer(a, b):
        return lax.dot_general(a, b, (((0,), (0,)), ((), ())), preferred_element_type=bf16)

    own_small = jnp.concatenate([norm_params, lin_bias, fc_bias])
    wa = w_attn.reshape(h, 3 * width)
    wo = w_out.reshape(h, width)
    wf = w_fc.reshape(h, chips, 2, fh)
    parts = [lanes_of(wa[:, i * width : (i + 1) * width], hw) for i in range(3)]
    parts.append(lanes_of(wo, half))
    gap = jnp.zeros((h, owide - half), bf16)
    attn_own, attn_other = (
        jnp.concatenate([p[i] for p in parts] + [gap], axis=1) for i in range(2)
    )
    fc_pads = ((0, 0), (0, 0), (0, fp - fh))
    fc_own, fc_other = (
        jnp.pad(jnp.where(low == first, wf[:, :, 0], wf[:, :, 1]), fc_pads).reshape(h, hidden)
        for first in (True, False)
    )
    attn_came, fc_came = swap(attn_other), swap(fc_other)
    acts_came = swap(jnp.stack([layer_input[0], out_cotangent[0]]))
    small_came = swap(own_small)
    row_pads = ((0, rp - rows), (0, 0))
    attn_piece = jnp.pad(jnp.concatenate(pair(attn_own, attn_came)), row_pads)
    fc_piece = jnp.pad(jnp.concatenate(pair(fc_own, fc_came)), row_pads)
    small_rows = jnp.pad(jnp.stack(pair(own_small, small_came)), ((0, 0), (0, wide - 3 * small)))
    proj_piece = jnp.concatenate(
        [
            jnp.pad(w_proj.reshape(fh, width), ((0, 0), (0, wide - width))),
            jnp.pad(small_rows, ((0, fp - fh - 2), (0, 0))),
        ]
    )
    shapes = (attn_piece.shape, fc_piece.shape, proj_piece.shape)
    items = split_items(shapes)
    attn_all, fc_all, proj_all = gather_call(nz, (attn_piece, fc_piece, proj_piece), items, 0)
    w_joined = attn_all.reshape(-1, attn_piece.shape[1])
    w_qkv, w_o = w_joined[:, : 3 * hw], w_joined[:, 3 * hw : 3 * hw + half]
    w_up = fc_all.reshape(-1, hidden)
    w_down = proj_all.reshape(hidden, wide)
    smalls = proj_all[:, fh : fh + 2, : 3 * small].astype(f32)
    by_kind = smalls.reshape(-1, 3, small)
    norms = by_kind[:, 0].reshape(4, width)
    biases = by_kind[:, 1].reshape(4, width)
    fc_own_bias = jnp.where(low, smalls[:, 0, 2 * small :], smalls[:, 1, 2 * small :])
    up_bias = jnp.pad(fc_own_bias, ((0, 0), (0, fp - fh))).reshape(hidden)
    real = jnp.pad(jnp.ones((chips, fh), f32), ((0, 0), (0, fp - fh))).reshape(hidden)

    acts = jnp.concatenate(pair(layer_input[0], acts_came[0]))
    cotangent = jnp.concatenate(pair(out_cotangent[0], acts_came[1]))
    inputs_f = acts.astype(f32)
    grad_out = cotangent.astype(f32)
    normed1, x_hat1, inv_std1 = layer_norm(inputs_f, norms[0], norms[1])
    act_rows1 = spread(normed1.astype(bf16))
    projected = dot(act_rows1, w_qkv)
    queries = (projected[:, :hw] + lanes_of(biases[0], hw)[0]).astype(bf16)
    key_rows = projected[:, hw : 2 * hw].astype(bf16)
    value_rows = (projected[:, 2 * hw :] + lanes_of(biases[1], hw)[0]).astype(bf16)
    seg_rows, seg_cols = segments.reshape(-1, 1), segments.reshape(1, -1)
    length = 2 * tokens
    shape = jax.ShapeDtypeStruct
    attended, log_total = local_call(
        functools.partial(attention_kernel, own_heads),
        [shape((length, hw), bf16), shape((length, 128), f32)],
        queries, key_rows, value_rows, seg_rows, seg_cols,
    )
    att_low, att_high = pair(attended, swap(attended))
    attended_rows = spread(jnp.concatenate([att_low, att_high[:, over:]], axis=1))
    mixed = dot(attended_rows, w_o)
    resid = inputs_f + jnp.concatenate(pair(mixed, swap(mixed)), axis=1) + biases[2]
    normed2, x_hat2, inv_std2 = layer_norm(resid, norms[2], norms[3])
    act_rows2 = spread(normed2.astype(bf16))
    hidden_pre = dot(act_rows2, w_up) + up_bias
    hidden_act, hidden_slope = gelu_parts(hidden_pre)
    hidden_b = hidden_act.astype(bf16)
    down, down_other = tokens_of(dot(hidden_b, w_down)[:, :width])
    result = tokens_of(resid)[0] + (down + swap(down_other)) + biases[3]

    cot_wide = jnp.pad(cotangent, ((0, 0), (0, wide - width)))
    grad_down = outer(hidden_b, cot_wide)
    grad_hidden = dot_t(cot_wide, w_down) * (hidden_slope * real)
    grad_hidden_b = grad_hidden.astype(bf16)
    grad_up = outer(act_rows2, grad_hidden_b)
    grad_norm2 = unspread(dot_t(grad_hidden_b, w_up))
    grad_norm2 = grad_norm2 + swap(grad_norm2)
    grad_resid_n, grad_g2, grad_b2 = norm_back(grad_norm2, x_hat2, inv_std2, norms[2])
    grad_resid = grad_out + grad_resid_n
    grad_resid_b = grad_resid.astype(bf16)
    grad_mixed = lanes_of(grad_resid_b, half)[0]
    grad_att, grad_att_other = lanes_of(unspread(dot_t(grad_mixed, w_o)), hw)
    grad_att = (grad_att + swap(grad_att_other)).astype(bf16)
    if over:
        twice = jnp.logical_and(core == 1, jnp.arange(hw) < over)
        grad_att = jnp.where(twice[None], jnp.zeros((), bf16), grad_att)
    grad_q, grad_k, grad_v, head_sums = local_call(
        functools.partial(attention_back_kernel, own_heads),
        [shape((length, hw), bf16)] * 3 + [shape((2, hw), f32)],
        queries, key_rows, value_rows, seg_rows, seg_cols, log_total, grad_att,
    )
    grad_proj_b = jnp.concatenate([grad_q, grad_k, grad_v], axis=1)
    grad_norm1 = unspread(dot_t(grad_proj_b, w_qkv))
    grad_norm1 = grad_norm1 + swap(grad_norm1)
    sums_low, sums_high = pair(head_sums, swap(head_sums))
    if over:
        grad_qv = jnp.concatenate([sums_low, sums_high[:, over:]], axis=1)
    else:
        grad_qv = jnp.concatenate([sums_low, sums_high], axis=1)
    grad_in_n, grad_g1, grad_b1 = norm_back(grad_norm1, x_hat1, inv_std1, norms[0])
    grad_input = tokens_of(grad_resid + grad_in_n)[0]
    norm_terms = jnp.concatenate([grad_g1, grad_b1, grad_g2, grad_b2]).reshape(chips, 2, small)
    bias_terms = jnp.concatenate(
        [grad_qv[0], grad_qv[1], jnp.sum(grad_resid, axis=0), jnp.sum(grad_out, axis=0)]
    ).reshape(chips, 2, small)
    fc_terms = jnp.sum(grad_hidden, axis=0).reshape(chips, fp)[:, :fh]
    small_terms = jnp.concatenate(
        [
            jnp.where(low, norm_terms[:, 0], norm_terms[:, 1]),
            jnp.where(low, bias_terms[:, 0], bias_terms[:, 1]),
            fc_terms,
        ],
        axis=1,
    )
    grad_joined = jnp.concatenate(
        [
            outer(act_rows1, grad_proj_b),
            outer(attended_rows, jnp.pad(grad_mixed, ((0, 0), (0, owide - half)))),
        ],
        axis=1,
    ).reshape(attn_all.shape)
    grad_down = grad_down.reshape(proj_all.shape)
    grad_down = lax.dynamic_update_slice(
        grad_down, small_terms.astype(bf16)[:, None], (0, fh, 0)
    )
    attn_sums, fc_sums, proj_sums = scatter_call(
        nz, (grad_joined, grad_up.reshape(fc_all.shape), grad_down), items[::-1], 1
    )

    def rows_of(value):
        first, second = value[:h], value[h:rows]
        own, other = jnp.where(low, first, second), jnp.where(low, second, first)
        return pair(own, swap(other))

    fc_pair = rows_of(fc_sums)
    fc_grad = jnp.stack([v.reshape(h, chips, fp)[:, :, :fh] for v in fc_pair], axis=2)
    at_low, at_high = rows_of(attn_sums)
    blocks = []
    for i in range(3):
        blocks += [at_low[:, i * hw : (i + 1) * hw], at_high[:, i * hw + over : (i + 1) * hw]]
    attn_grad = jnp.concatenate(blocks, axis=1)
    out_grad = jnp.concatenate(
        [at_low[:, 3 * hw : 3 * hw + half], at_high[:, 3 * hw : 3 * hw + half]], axis=1
    )
    small_sums = proj_sums[fh]
    return (
        result.astype(bf16)[None],
        grad_input[None],
        attn_grad.reshape(-1),
        out_grad.reshape(-1),
        fc_grad.reshape(-1),
        proj_sums[:fh, :width].reshape(-1),
        small_sums[:small],
        small_sums[small : 2 * small],
        small_sums[2 * small : 3 * small],
    )


def grid_height(mesh):
    shape = dict(mesh.shape)
    devices = mesh.devices.reshape(-1)
    if tuple(mesh.axis_names) != AXES or shape["seq"] != 2 or shape["dp"] % 4:
        return 0
    nz = shape["dp"] // 4
    base = getattr(devices[0], "coords", None)
    if base is None:
        return 0
    for n, device in enumerate(devices):
        chip = n // 2
        place = (chip % 2, chip // 2 % 2, chip // 4)
        if tuple(a - b for a, b in zip(device.coords, base)) != place:
            return 0
    return nz if 1 < nz <= 4 else 0


def solution(mesh):
    nz = grid_height(mesh)
    return jax.shard_map(
        functools.partial(per_device_grid, nz) if nz else per_device,
        mesh=mesh,
        in_specs=(
            P("dp", "seq", None),
            P("dp", None),
            P(("dp", "seq")),
            P(("dp", "seq")),
            P(("dp", "seq")),
            P(("dp", "seq")),
            P(("dp", "seq")),
            P(("dp", "seq")),
            P(("dp", "seq")),
            P("dp", "seq", None),
        ),
        out_specs=(
            P("dp", "seq", None),
            P("dp", "seq", None),
            P(("dp", "seq")),
            P(("dp", "seq")),
            P(("dp", "seq")),
            P(("dp", "seq")),
            P(("dp", "seq")),
            P(("dp", "seq")),
            P(("dp", "seq")),
        ),
        check_vma=False,
    )
```

```python
import functools

import jax
import jax.numpy as jnp
from jax import lax
from jax.experimental import pallas as pl
from jax.experimental.pallas import tpu as pltpu
from jax.sharding import PartitionSpec as P

HD = 64
FF = 4352


GELU_C = 0.7978845608028654
NORM_EPS = 1e-05


def gelu_parts(inputs):
    tanh_value = jnp.tanh(GELU_C * (inputs + 0.044715 * inputs * inputs * inputs))
    value = 0.5 * inputs * (1.0 + tanh_value)
    slope = 0.5 * (1.0 + tanh_value) + 0.5 * inputs * (1.0 - tanh_value * tanh_value) * GELU_C * (
        1.0 + 3.0 * 0.044715 * inputs * inputs
    )
    return (value, slope)


def layer_norm(inputs, gains, offsets):
    average = jnp.mean(inputs, axis=-1, keepdims=True)
    centred = inputs - average
    inv_std = lax.rsqrt(jnp.mean(centred * centred, axis=-1, keepdims=True) + NORM_EPS)
    x_hat = centred * inv_std
    return (x_hat * gains + offsets, x_hat, inv_std)


def norm_back(grad_out, x_hat, inv_std, gains):
    grad_hat = grad_out * gains
    grad_in = inv_std * (
        grad_hat
        - jnp.mean(grad_hat, axis=-1, keepdims=True)
        - x_hat * jnp.mean(grad_hat * x_hat, axis=-1, keepdims=True)
    )
    return (grad_in, jnp.sum(grad_out * x_hat, axis=0), jnp.sum(grad_out, axis=0))


def score_block(queries, key_rows, allowed):
    scores = jnp.einsum(
        "qhd,khd->hqk", queries, key_rows, preferred_element_type=jnp.float32
    ) * HD ** (-0.5)
    return jnp.where(allowed[None], scores, -1e30)


def outer_sum(left, right):
    return jnp.einsum("na,nb->ab", left, right, preferred_element_type=jnp.float32)


AXES = ("dp", "seq")


def shard_height(shard, columns):
    size = shard.shape[0]
    return size // columns if size % columns == 0 else 0


def tile_height(shard, columns):
    height = shard_height(shard, columns)
    return 0 if height % 8 else height


def padded(height):
    return -(-height // 8) * 8


def gather_rows(shard, columns, height, extra=None):
    if not height:
        return lax.all_gather(shard, AXES, axis=0, tiled=True).reshape(-1, columns)
    block = shard.reshape(height, columns)
    room = padded(height) - height
    if extra is not None:
        row = jnp.pad(extra, (0, columns - extra.shape[0]))[None]
        block = jnp.concatenate([block, row], axis=0)
        room -= 1
    if room:
        block = jnp.pad(block, ((0, room), (0, 0)))
    return lax.all_gather(block, AXES, axis=0, tiled=True)


def spread(acts, height):
    room = padded(height) - height
    if not room:
        return acts
    tokens = acts.shape[0]
    parts = acts.reshape(tokens, -1, height)
    return jnp.pad(parts, ((0, 0), (0, 0), (0, room))).reshape(tokens, -1)


def unspread(acts, height):
    if padded(height) == height:
        return acts
    tokens = acts.shape[0]
    return acts.reshape(tokens, -1, padded(height))[:, :, :height].reshape(tokens, -1)


def scatter_rows(blocks, height):
    count = lax.axis_size(AXES)
    sums = lax.psum_scatter(
        blocks.astype(jnp.bfloat16).reshape(count, -1, blocks.shape[-1]),
        AXES,
        scatter_dimension=0,
        tiled=True,
    )[0]
    return sums.astype(jnp.float32)


def scatter_flat(block, shard):
    count = lax.axis_size(AXES)
    return lax.psum_scatter(
        block.reshape(count, shard), AXES, scatter_dimension=0, tiled=True
    )[0]


def own_half_sum(terms, place, tokens):
    if lax.axis_size("seq") != 2:
        return lax.psum_scatter(
            terms.astype(jnp.bfloat16), "seq", scatter_dimension=0, tiled=True
        ).astype(jnp.float32)
    own = lax.dynamic_slice_in_dim(terms, place * tokens, tokens)
    other = lax.dynamic_slice_in_dim(terms, (1 - place) * tokens, tokens)
    came = lax.ppermute(other.astype(jnp.bfloat16), "seq", [(0, 1), (1, 0)])
    return own + came.astype(jnp.float32)


def per_device(
    layer_input,
    segments,
    w_attn,
    w_out,
    w_fc,
    w_proj,
    norm_params,
    lin_bias,
    fc_bias,
    out_cotangent,
):
    tokens = layer_input.shape[1]
    width = layer_input.shape[2]
    heads = width // HD
    place = lax.axis_index("seq")
    first = place * tokens
    small = norm_params.shape[0]
    height = shard_height(w_attn, 3 * width)
    height = height if shard_height(w_out, width) == height == shard_height(w_fc, FF) else 0
    down_height = tile_height(w_proj, width)
    own_small = jnp.concatenate([norm_params, lin_bias, fc_bias])
    packed = height and padded(height) > height and own_small.shape[0] <= width
    if height:
        lanes = -(-width // 128) * 128
        joined_shard = jnp.concatenate(
            [
                jnp.pad(w_out.reshape(height, width), ((0, 0), (0, lanes - width))),
                w_attn.reshape(height, 3 * width),
            ],
            axis=1,
        ).reshape(-1)
        joined_w = gather_rows(
            joined_shard, lanes + 3 * width, height, own_small if packed else None
        )
        w_o = joined_w[:, :width]
        w_qkv = joined_w[:, lanes:]
    else:
        w_qkv = gather_rows(w_attn, 3 * width, 0)
        w_o = gather_rows(w_out, width, 0)
    w_up = gather_rows(w_fc, FF, height)
    w_down = gather_rows(w_proj, width, down_height)
    if packed:
        smalls = w_o.reshape(-1, padded(height), width)[:, height, : 3 * small]
    else:
        smalls = lax.all_gather(own_small, AXES, axis=0)
    smalls = smalls.astype(jnp.float32).reshape(-1, 3, small)
    norms = smalls[:, 0].reshape(4, width)
    biases = smalls[:, 1].reshape(4, width)
    up_bias = smalls[:, 2].reshape(FF)
    inputs_f = layer_input[0].astype(jnp.float32)
    normed1, x_hat1, inv_std1 = layer_norm(inputs_f, norms[0], norms[1])
    act_in1 = normed1.astype(jnp.bfloat16)
    act_rows1 = spread(act_in1, height)
    projected = jnp.dot(act_rows1, w_qkv, preferred_element_type=jnp.float32)
    queries = (projected[:, :width] + biases[0]).astype(jnp.bfloat16)
    own_keys = projected[:, width : 2 * width].astype(jnp.bfloat16)
    own_values = (projected[:, 2 * width :] + biases[1]).astype(jnp.bfloat16)
    key_rows, value_rows = (
        lax.all_gather(own_keys, "seq", axis=0, tiled=True),
        lax.all_gather(own_values, "seq", axis=0, tiled=True),
    )
    key_count = key_rows.shape[0]
    key_pos = jnp.arange(key_count)
    query_pos = first + jnp.arange(tokens)
    padded_seg = jnp.concatenate([jnp.full((tokens,), -1, jnp.int32), segments[0]])
    key_seg = lax.dynamic_slice_in_dim(padded_seg, tokens, key_count)
    query_seg = lax.dynamic_slice_in_dim(segments[0], first, tokens)
    allowed = (key_pos[None, :] <= query_pos[:, None]) & (key_seg[None, :] == query_seg[:, None])
    q_heads = queries.reshape(tokens, heads, HD)
    k_heads = key_rows.reshape(key_count, heads, HD)
    v_heads = value_rows.reshape(key_count, heads, HD)
    scores = score_block(q_heads, k_heads, allowed)
    top_score = jnp.max(scores, axis=-1, keepdims=True)
    log_total = top_score + jnp.log(jnp.sum(jnp.exp(scores - top_score), axis=-1, keepdims=True))
    attn_probs = jnp.exp(scores - log_total).astype(jnp.bfloat16)
    attended = jnp.einsum("hqk,khd->qhd", attn_probs, v_heads, preferred_element_type=jnp.float32)
    attended = attended.reshape(tokens, width).astype(jnp.bfloat16)
    attended_rows = spread(attended, height)
    resid = inputs_f + jnp.dot(attended_rows, w_o, preferred_element_type=jnp.float32) + biases[2]
    normed2, x_hat2, inv_std2 = layer_norm(resid, norms[2], norms[3])
    act_in2 = normed2.astype(jnp.bfloat16)
    act_rows2 = spread(act_in2, height)
    hidden_pre = jnp.dot(act_rows2, w_up, preferred_element_type=jnp.float32) + up_bias
    hidden_act, hidden_slope = gelu_parts(hidden_pre)
    hidden_b = hidden_act.astype(jnp.bfloat16)
    hidden_rows = spread(hidden_b, down_height)
    result = (
        resid + jnp.dot(hidden_rows, w_down, preferred_element_type=jnp.float32) + biases[3]
    ).astype(jnp.bfloat16)
    cotangent = out_cotangent[0]
    grad_out = cotangent.astype(jnp.float32)
    grad_bp = jnp.sum(grad_out, axis=0)
    grad_hidden = (
        unspread(
            jnp.einsum("nd,fd->nf", cotangent, w_down, preferred_element_type=jnp.float32),
            down_height,
        )
        * hidden_slope
    )
    grad_hidden_b = grad_hidden.astype(jnp.bfloat16)
    grad_down = outer_sum(hidden_rows, cotangent)
    if down_height:
        grad_hidden_b, grad_down = lax.optimization_barrier(
            (grad_hidden_b, grad_down.astype(jnp.bfloat16))
        )
    grad_up_bias = jnp.sum(grad_hidden, axis=0)
    if down_height:
        proj_sums = scatter_rows(grad_down, down_height)[:down_height].reshape(-1)
    else:
        proj_sums = scatter_flat(grad_down, w_proj.shape[0])
    grad_up = outer_sum(act_rows2, grad_hidden_b)
    if height:
        fc_sums = scatter_rows(grad_up, height)[:height].reshape(-1)
    else:
        fc_sums = scatter_flat(grad_up, w_fc.shape[0])
    grad_norm2 = unspread(
        jnp.einsum("nf,df->nd", grad_hidden_b, w_up, preferred_element_type=jnp.float32), height
    )
    grad_resid_n, grad_g2, grad_b2 = norm_back(grad_norm2, x_hat2, inv_std2, norms[2])
    grad_resid = grad_out + grad_resid_n
    grad_resid_b = grad_resid.astype(jnp.bfloat16)
    grad_bo = jnp.sum(grad_resid, axis=0)
    grad_att = unspread(
        jnp.einsum(
            "ne,de->nd", grad_resid_b, w_o, preferred_element_type=jnp.float32
        ).astype(jnp.bfloat16),
        height,
    )
    grad_att_heads = grad_att.reshape(tokens, heads, HD)
    probs_full = jnp.exp(score_block(q_heads, k_heads, allowed) - log_total)
    probs_b = probs_full.astype(jnp.bfloat16)
    grad_probs = jnp.einsum(
        "qhd,khd->hqk", grad_att_heads, v_heads, preferred_element_type=jnp.float32
    )
    delta = jnp.sum(probs_full * grad_probs, axis=-1, keepdims=True)
    grad_scores = (probs_full * (grad_probs - delta) * HD ** (-0.5)).astype(jnp.bfloat16)
    grad_q = jnp.einsum(
        "hqk,khd->qhd", grad_scores, k_heads, preferred_element_type=jnp.float32
    ).reshape(tokens, width)
    grad_k_all = jnp.einsum(
        "hqk,qhd->khd", grad_scores, q_heads, preferred_element_type=jnp.float32
    ).reshape(key_count, width)
    grad_v_all = jnp.einsum(
        "hqk,qhd->khd", probs_b, grad_att_heads, preferred_element_type=jnp.float32
    ).reshape(key_count, width)
    grad_k = own_half_sum(grad_k_all, place, tokens)
    grad_v = own_half_sum(grad_v_all, place, tokens)
    grad_proj_b = jnp.concatenate([grad_q, grad_k, grad_v], axis=1).astype(jnp.bfloat16)
    grad_norm1 = unspread(
        jnp.einsum("ne,de->nd", grad_proj_b, w_qkv, preferred_element_type=jnp.float32), height
    )
    grad_in_n, grad_g1, grad_b1 = norm_back(grad_norm1, x_hat1, inv_std1, norms[0])
    grad_input = grad_resid + grad_in_n
    norm_terms = jnp.concatenate([grad_g1, grad_b1, grad_g2, grad_b2])
    bias_terms = jnp.concatenate(
        [jnp.sum(grad_q, axis=0), jnp.sum(grad_v, axis=0), grad_bo, grad_bp]
    )
    small_terms = jnp.concatenate(
        [term.reshape(-1, 1, small) for term in (norm_terms, bias_terms, grad_up_bias)], axis=1
    )
    grad_attn = outer_sum(act_rows1, grad_proj_b)
    grad_wo = outer_sum(attended_rows, grad_resid_b)
    if height:
        joined = jnp.concatenate(
            [grad_attn.astype(jnp.bfloat16), grad_wo.astype(jnp.bfloat16)], axis=1
        )
        if packed:
            blocks = joined.reshape(-1, padded(height), 4 * width)
            row = small_terms.astype(jnp.bfloat16).reshape(-1, 1, 3 * small)
            row = jnp.pad(row, ((0, 0), (height, padded(height) - height - 1), (0, width * 4 - 3 * small)))
            joined = (blocks + row).reshape(joined.shape)
        sums = scatter_rows(joined, height)
        qkv_sums = sums[:height, : 3 * width].reshape(-1)
        out_sums = sums[:height, 3 * width :].reshape(-1)
    else:
        qkv_sums = scatter_flat(grad_attn, w_attn.shape[0])
        out_sums = scatter_flat(grad_wo, w_out.shape[0])
    if packed:
        small_sums = sums[height, : 3 * small].reshape(3, small)
    else:
        small_sums = lax.psum_scatter(small_terms, AXES, scatter_dimension=0, tiled=True)[0]
    norm_sums, bias_sums, fcb_sums = small_sums[0], small_sums[1], small_sums[2]
    return (
        result[None],
        grad_input[None],
        qkv_sums,
        out_sums,
        fc_sums,
        proj_sums,
        norm_sums,
        bias_sums,
        fcb_sums,
    )


MESH = pl.DeviceIdType.MESH


class Place:
    def __init__(self, nz):
        self.nz = nz
        self.dp = lax.axis_index("dp")
        self.core = lax.axis_index("seq")
        self.x = lax.rem(self.dp, 2)
        self.y = lax.rem(self.dp // 2, 2)
        self.z = self.dp // 4
        fx, fy = 1 - 2 * self.x, 2 - 4 * self.y
        self.flip = (0, fx, fy, fx + fy)

    def chip(self, dz, p):
        return self.dp + 4 * dz + self.flip[p]

    def has(self, dz):
        return jnp.logical_and(self.z + dz >= 0, self.z + dz < self.nz)

    def meet(self, other=False):
        barrier = pltpu.get_barrier_semaphore()
        for dz, p in ((0, 1), (0, 2)):
            pl.semaphore_signal(
                barrier, inc=1, device_id=(self.chip(dz, p), self.core), device_id_type=MESH
            )
        for dz in (1, -1):
            @pl.when(self.has(dz))
            def _():
                pl.semaphore_signal(
                    barrier, inc=1, device_id=(self.chip(dz, 0), self.core), device_id_type=MESH
                )
        if other:
            pl.semaphore_signal(
                barrier, inc=1, device_id=(self.dp, 1 - self.core), device_id_type=MESH
            )
        near = 3 if other else 2
        pl.semaphore_wait(barrier, near + self.has(1).astype(jnp.int32) + self.has(-1).astype(jnp.int32))


def slots(nz):
    return [0] + [s * k for k in range(1, nz) for s in (1, -1)]


def gather_kernel(nz, items, count, *refs):
    ins, outs = refs[:count], refs[count : 2 * count]
    send_sem, recv_sem, local_sem = refs[2 * count :]
    at = Place(nz)
    ids = {}

    def number(key):
        return ids.setdefault(key, len(ids))

    def copy(item, key, chip, to, part, src=None):
        array, lo, mid, hi, _ = item
        lanes = {"all": (lo, hi - lo), "a": (lo, mid - lo), "b": (mid, hi - mid)}[part]
        cut = pl.ds(*lanes)
        dst = outs[array].at[chip, :, cut]
        n = number((item, key))
        return pltpu.make_async_remote_copy(
            src_ref=dst if src is None else ins[array].at[:, cut],
            dst_ref=dst,
            send_sem=send_sem.at[n],
            recv_sem=recv_sem.at[n],
            device_id=(to, at.core),
            device_id_type=MESH,
        )

    locals_ = []
    for a in range(count):
        cp = pltpu.make_async_copy(ins[a], outs[a].at[at.dp], local_sem.at[a])
        cp.start()
        locals_.append(cp)
    at.meet()
    events = []
    ends = []

    def always(fn):
        fn()

    def add(when, order, pred, fn):
        events.append((when, order, pred, fn))

    def launch(pred, make):
        make().start()
        ends.append(((0, q), lambda: make().wait_send()))

    for order, item in enumerate(items):
        kind = item[4]
        if kind == "zp":
            for q in slots(nz):
                d = abs(q)
                step = 1 if q > 0 else -1
                pred = None if q == 0 else at.has(q)

                def start(item=item, q=q, step=step, pred=pred):
                    src = True if q == 0 else None
                    if q != 0:
                        copy(item, ("z", q), at.chip(q, 0), at.dp, "all").wait_recv()
                    for go in ((1, -1) if q == 0 else (-step,)):
                        pr = at.has(go)
                        key = ("z", q - go)
                        if abs(q - go) >= nz:
                            continue
                        def mk(go=go, key=key, src=src):
                            return copy(item, key, at.chip(q, 0), at.chip(go, 0), "all", src)
                        @pl.when(pr)
                        def _():
                            mk().start()
                        ends.append(((go, q), lambda mk=mk: mk().wait_send()))
                    for p in (1, 2):
                        def mk2(p=p, src=src):
                            return copy(item, ("p", p, q), at.chip(q, 0), at.chip(0, p), "all", src)
                        mk2().start()
                        ends.append(((0, q), lambda mk2=mk2: mk2().wait_send()))

                def relay(item=item, q=q, pred=pred):
                    for p, part in ((1, "a"), (2, "b")):
                        copy(item, ("p", p, q), at.chip(q, p), at.dp, "all").wait_recv()
                        def mk(p=p, part=part):
                            return copy(item, ("d", p, q), at.chip(q, p), at.chip(0, 3 - p), part)
                        mk().start()
                        ends.append(((0, q), lambda mk=mk: mk().wait_send()))

                def last(item=item, q=q):
                    for p, part in ((1, "a"), (2, "b")):
                        copy(item, ("d", p, q), at.chip(q, 3), at.dp, part).wait_recv()

                add(d, order, pred, start)
                add(d + 1.5, order, pred, relay)
                add(90, order, pred, last)
        else:
            def to_z(item, q, p, pred, src=None):
                for go in (1, -1) if q == 0 else ((-1,) if q > 0 else (1,)):
                    if abs(q - go) >= nz:
                        continue
                    pr = at.has(go)
                    def mk(go=go):
                        return copy(item, ("z", p, q - go), at.chip(q, p), at.chip(go, 0), "all", src)
                    @pl.when(pr)
                    def _():
                        mk().start()
                    ends.append(((go, q), lambda mk=mk: mk().wait_send()))

            def start(item=item):
                for p in (1, 2):
                    def mk2(p=p):
                        return copy(item, ("p", p), at.dp, at.chip(0, p), "all", True)
                    mk2().start()
                    ends.append(((0, 0), lambda mk2=mk2: mk2().wait_send()))
                to_z(item, 0, 0, None, True)

            def relay(item=item):
                for p, part in ((1, "a"), (2, "b")):
                    copy(item, ("p", p), at.chip(0, p), at.dp, "all").wait_recv()
                    def mk(p=p, part=part):
                        return copy(item, ("d", p), at.chip(0, p), at.chip(0, 3 - p), part)
                    mk().start()
                    ends.append(((0, 0), lambda mk=mk: mk().wait_send()))
                    to_z(item, 0, p, None)

            def diagonal(item=item):
                for p, part in ((1, "a"), (2, "b")):
                    copy(item, ("d", p), at.chip(0, 3), at.dp, part).wait_recv()
                to_z(item, 0, 3, None)

            add(0, order, None, start)
            add(1.2, order, None, relay)
            add(2.2, order, None, diagonal)
            for q in slots(nz)[1:]:
                for p in range(4):
                    pred = at.has(q)
                    def onward(item=item, q=q, p=p, pred=pred):
                        copy(item, ("z", p, q), at.chip(q, p), at.dp, "all").wait_recv()
                        to_z(item, q, p, pred)
                    add(abs(q) + 0.8 * (0, 1, 1, 2)[p], order, pred, onward)
    for _, _, pred, fn in sorted(events, key=lambda e: e[:2]):
        if pred is None:
            fn()
        else:
            pl.when(pred)(fn)
    for needs, fn in ends:
        pl.when(functools.reduce(jnp.logical_and, [at.has(dz) for dz in needs]))(fn)
    for cp in locals_:
        cp.wait()


def gather_call(nz, arrays, items, collective_id):
    count = len(arrays)
    sems = 40 * len(items)
    return pl.pallas_call(
        functools.partial(gather_kernel, nz, items, count),
        out_shape=[jax.ShapeDtypeStruct((4 * nz, *a.shape), a.dtype) for a in arrays],
        in_specs=[pl.BlockSpec(memory_space=pl.ANY)] * count,
        out_specs=[pl.BlockSpec(memory_space=pl.ANY)] * count,
        scratch_shapes=[
            pltpu.SemaphoreType.DMA((sems,)),
            pltpu.SemaphoreType.DMA((sems,)),
            pltpu.SemaphoreType.DMA((count,)),
        ],
        compiler_params=pltpu.CompilerParams(
            collective_id=collective_id, has_side_effects=True, vmem_limit_bytes=56 * 2**20
        ),
    )(*arrays)


def strips(lo, hi, fn):
    def body(i, carry):
        fn(pl.multiple_of(i * 128, 128))
        return carry

    lax.fori_loop(0, (hi - lo) // 128, body, 0)


def far_first(nz):
    return [sorted(range(nz), key=lambda t: -abs(t - z)) for z in range(nz)]


def choose(scalar, values):
    picked = jnp.int32(values[0])
    for i, v in enumerate(values[1:], 1):
        picked = jnp.where(scalar == i, jnp.int32(v), picked)
    return picked


class Links:
    def __init__(self, at, send_sem, recv_sem):
        self.at, self.send_sem, self.recv_sem = at, send_sem, recv_sem
        self.used, self.events, self.ends = 0, [], []

    def numbers(self, size):
        self.used += size
        return self.used - size

    def add(self, when, fn):
        self.events.append((when, len(self.events), fn))

    def make(self, src, dst, n, chip, other=False):
        core = 1 - self.at.core if other else self.at.core
        return pltpu.make_async_remote_copy(
            src_ref=src,
            dst_ref=dst,
            send_sem=self.send_sem.at[n],
            recv_sem=self.recv_sem.at[n],
            device_id=(chip, core),
            device_id_type=MESH,
        )

    def go(self, src, dst, n, chip, other=False):
        self.make(src, dst, n, chip, other).start()
        self.ends.append(lambda: self.make(src, dst, n, chip, other).wait_send())

    def came(self, dst, n):
        self.make(dst, dst, n, self.at.dp).wait_recv()

    def run(self):
        for _, _, fn in sorted(self.events, key=lambda e: e[:2]):
            fn()
        for fn in self.ends:
            fn()


def line_cases(at, nz, dst):
    for step in (1, -1):
        ahead = dst > at.z if step > 0 else dst < at.z
        first = at.z == (0 if step > 0 else nz - 1)
        slot = dst if step > 0 else jnp.where(dst == at.z - 1, nz, dst)
        yield step, ahead, first, slot


def scatter_item(links, nz, dest, item, src, out, bufs, times):
    f32 = jnp.float32
    at = links.at
    _, lo, mid, hi, kind = item
    width, na = hi - lo, mid - lo
    part_d, part_x, part_y, line = bufs
    landing = {1: part_x, 2: part_y}
    halves = {"a": (0, na), "b": (na, width - na)}

    def mod4(chip):
        return lax.rem(chip, 4)

    def lanes(start, i):
        return pl.ds(pl.multiple_of(start + i, 128), 128)

    def plane(k, value, finish):
        base = links.numbers(6)

        def cut(ref, half, first=0):
            start, size = halves[half]
            return ref.at[:, pl.ds(first + start, size)]

        def first():
            for p, half, n in ((2, "a", 0), (1, "b", 1)):
                ref, start = value(3)
                links.go(cut(ref, half, start), cut(part_d.at[k], half), base + n, at.chip(0, p))
            for p, half, n in ((1, "b", 2), (2, "a", 3)):
                ref, start = value(p)
                links.go(cut(ref, half, start), cut(landing[p].at[k], half), base + n, at.chip(0, p))

        def second():
            for p, half, n, m in ((1, "a", 0, 4), (2, "b", 1, 5)):
                here = cut(part_d.at[k], half)
                links.came(here, base + n)
                ref, start = value(p)
                l, size = halves[half]

                def one(i, ref=ref, start=start, l=l):
                    part_d[k, :, lanes(l, i)] = (
                        part_d[k, :, lanes(l, i)].astype(f32) + ref[:, lanes(start + l, i)].astype(f32)
                    ).astype(part_d.dtype)

                strips(0, size, one)
                links.go(here, cut(landing[p].at[k], half), base + m, at.chip(0, p))

        def third():
            for p, half, n in ((1, "b", 2), (2, "a", 3), (1, "a", 4), (2, "b", 5)):
                links.came(cut(landing[p].at[k], half), base + n)
            finish()

        links.add(times("first", k), first)
        links.add(times("second", k), second)
        links.add(times("third", k), third)

    if kind == "zp":
        line_n = links.numbers(nz + 1)
        for k in range(nz):
            dst = dest[k]

            def value(p, dst=dst):
                return src.at[dst * 4 + mod4(at.chip(0, p))], lo

            def total(i, k=k, dst=dst):
                return (
                    src[dst * 4 + mod4(at.dp), :, lanes(lo, i)].astype(f32)
                    + part_x[k, :, pl.ds(i, 128)].astype(f32)
                    + part_y[k, :, pl.ds(i, 128)].astype(f32)
                )

            if k < nz - 1:

                def finish(k=k, dst=dst, total=total):
                    for step, ahead, first, slot in line_cases(at, nz, dst):
                        def send(ref, step=step, slot=slot):
                            links.make(ref, line.at[slot], line_n + slot, at.chip(step, 0)).start()

                        @pl.when(jnp.logical_and(ahead, first))
                        def _():
                            def one(i):
                                part_x[k, :, pl.ds(i, 128)] = total(i).astype(part_x.dtype)
                            strips(0, width, one)
                            send(part_x.at[k])

                        @pl.when(jnp.logical_and(ahead, jnp.logical_not(first)))
                        def _():
                            links.came(line.at[dst], line_n + dst)
                            def one(i):
                                line[dst, :, pl.ds(i, 128)] = (
                                    total(i) + line[dst, :, pl.ds(i, 128)].astype(f32)
                                ).astype(line.dtype)
                            strips(0, width, one)
                            send(line.at[dst])

                    def done():
                        for step, ahead, _, slot in line_cases(at, nz, dst):
                            @pl.when(ahead)
                            def _():
                                links.make(line.at[slot], line.at[slot], line_n + slot, at.chip(step, 0)).wait_send()
                    links.ends.append(done)

            else:

                def finish(total=total):
                    def one(i):
                        out[:, lanes(lo, i)] = total(i)
                    strips(0, width, one)
                    for step, slot in ((-1, at.z), (1, nz)):
                        @pl.when(at.has(step))
                        def _():
                            links.came(line.at[slot], line_n + slot)
                            def two(i):
                                out[:, lanes(lo, i)] += line[slot, :, pl.ds(i, 128)].astype(f32)
                            strips(0, width, two)

            plane(k, value, finish)
        return
    line_n = links.numbers(4 * (nz + 1))
    mine = (nz + 1) * 4
    for k in range(nz - 1):
        dst = dest[k]
        for p in (3, 1, 2, 0):

            def chain(starts, p=p, dst=dst):
                piece = dst * 4 + mod4(at.chip(0, p))
                here = dst * 4 + p
                for step, ahead, first, plane_slot in line_cases(at, nz, dst):
                    slot = plane_slot * 4 + p

                    def send(ref, step=step, slot=slot):
                        links.make(ref, line.at[slot], line_n + slot, at.chip(step, 0)).start()

                    if starts:
                        @pl.when(jnp.logical_and(ahead, first))
                        def _():
                            send(src.at[piece, :, pl.ds(lo, width)])
                        continue

                    @pl.when(jnp.logical_and(ahead, jnp.logical_not(first)))
                    def _():
                        links.came(line.at[here], line_n + here)
                        def one(i):
                            line[here, :, pl.ds(i, 128)] = (
                                src[piece, :, lanes(lo, i)].astype(f32)
                                + line[here, :, pl.ds(i, 128)].astype(f32)
                            ).astype(line.dtype)
                        strips(0, width, one)
                        send(line.at[here])

                if starts:
                    return

                def done():
                    for step, ahead, _, plane_slot in line_cases(at, nz, dst):
                        slot = plane_slot * 4 + p
                        @pl.when(ahead)
                        def _():
                            links.make(line.at[slot], line.at[slot], line_n + slot, at.chip(step, 0)).wait_send()
                links.ends.append(done)

            links.add(times("start", k), functools.partial(chain, True))
            links.add(times("chain", k), functools.partial(chain, False))

    def gathered():
        for p in (3, 1, 2, 0):
            piece = at.z * 4 + mod4(at.chip(0, p))
            low, high = at.z * 4 + p, nz * 4 + p
            for step, slot in ((-1, low), (1, high)):
                @pl.when(at.has(step))
                def _():
                    links.came(line.at[slot], line_n + slot)

            def one(i):
                own = src[piece, :, lanes(lo, i)].astype(f32)
                below = jnp.where(at.has(-1), line[low, :, pl.ds(i, 128)].astype(f32), 0.0)
                above = jnp.where(at.has(1), line[high, :, pl.ds(i, 128)].astype(f32), 0.0)
                line[mine + p, :, pl.ds(i, 128)] = (own + below + above).astype(line.dtype)
            strips(0, width, one)

    def value(p):
        return line.at[mine + p], 0

    def finish():
        def one(i):
            out[:, lanes(lo, i)] = (
                line[mine, :, pl.ds(i, 128)].astype(f32)
                + part_x[0, :, pl.ds(i, 128)].astype(f32)
                + part_y[0, :, pl.ds(i, 128)].astype(f32)
            )
        strips(0, width, one)

    links.add(times("gathered", 0), gathered)
    plane(0, value, finish)


def item_bufs(nz, arrays, items):
    scratch, sems = [], 0
    for array, lo, mid, hi, kind in items:
        rows, width = arrays[array][1], hi - lo
        planes = nz if kind == "zp" else 1
        lines = nz + 1 if kind == "zp" else 4 * (nz + 1) + 4
        scratch += [pltpu.VMEM((n, rows, width), jnp.bfloat16) for n in (planes, planes, planes, lines)]
        sems += 7 * nz + 1 if kind == "zp" else 4 * (nz + 1) + 6
    return scratch, sems


NT = (((1,), (1,)), ((), ()))


def dot_nt(a, b):
    return lax.dot_general(a, b, NT, preferred_element_type=jnp.float32)


def dot_nn(a, b):
    return jnp.dot(a, b, preferred_element_type=jnp.float32)


def fill_spread(st_ref, rows, rp):
    wide, width = st_ref.shape
    step = 128

    def body(t, carry):
        at = pl.multiple_of(t * step, step)
        i = at + lax.broadcasted_iota(jnp.int32, (step, 1), 0)
        block = i // rp
        inner = i - block * rp
        column = jnp.where(inner < rows, block * rows + inner, -1)
        n = lax.broadcasted_iota(jnp.int32, (step, width), 1)
        st_ref[pl.ds(at, step), :] = jnp.where(n == column, 1.0, 0.0).astype(st_ref.dtype)
        return carry

    lax.fori_loop(0, wide // step, body, 0)


def stream(hbm, buf, sem, fn):
    size = buf.shape[1]
    count = hbm.shape[0] // size

    def copy(i, slot):
        rows = pl.ds(pl.multiple_of(i * size, 16), size)
        return pltpu.make_async_copy(hbm.at[rows, :], buf.at[slot], sem.at[slot])

    copy(0, 0).start()

    def body(i, carry):
        slot = lax.rem(i, 2)

        @pl.when(i + 1 < count)
        def _():
            copy(i + 1, 1 - slot).start()

        copy(i, slot).wait()
        fn(i, buf.at[slot])
        return carry

    lax.fori_loop(0, count, body, 0)


def back_kernel(nz, items, sizes, names, *refs):
    f32, bf16 = jnp.float32, jnp.bfloat16
    r = dict(zip(names, refs))
    bufs = refs[len(names) :]
    own_heads, rows, rp, fh, fp, half, over = sizes
    hw = own_heads * HD
    at = Place(nz)
    links = Links(at, r["send_sem"], r["recv_sem"])
    table = far_first(nz)
    dest = [choose(at.z, [table[z][k] for z in range(nz)]) for k in range(nz)]
    at.meet(True)
    cot, st, small, small_d = r["cot"], r["st"], r["small"], r["small_d"]
    dub, dp, drc = r["dub"], r["dp"], r["drc"]
    length, wide = cot.shape
    hidden = dub.shape[1]
    width = st.shape[1]
    joined = dp.shape[1]
    shift = joined - drc.shape[1]

    def tall(name):
        rows_in = r[name].shape[0]
        return pltpu.make_async_copy(r[name], r["tall"].at[pl.ds(0, rows_in), :], r["sem_tall"].at[0])

    def setup():
        tall("gt").start()
        small[...] = jnp.zeros_like(small)
        small_d[...] = jnp.zeros_like(small_d)
        small_d[0:1, :] = jnp.sum(cot[...].astype(f32), axis=0, keepdims=True)
        tall("gt").wait()

    def grad_down(k):
        top = pl.multiple_of(dest[k] * 4 * fp, 16)
        step = wide // 3

        def body(i, carry):
            n = pl.ds(pl.multiple_of(i * step, 128), step)
            val = dot_nn(r["tall"][pl.ds(top, 4 * fp), :], cot[:, n]).reshape(4, fp, step)
            val = jnp.concatenate([val[:, : fp - 8], val[:, fp - 8 :] + small_d[:, n][None]], axis=1)
            r["g2"][pl.ds(dest[k] * 4, 4), :, n] = val.astype(bf16)
            return carry

        lax.fori_loop(0, 3, body, 0)

    def grad_hidden():
        def fn(i, w):
            n = pl.ds(pl.multiple_of(i * w.shape[0], 128), w.shape[0])
            val = dot_nt(cot[...], w[...]) * r["slope"][:, n].astype(f32)
            dub[:, n] = val.astype(bf16)
            small[6:7, n] = jnp.sum(val, axis=0, keepdims=True)

        stream(r["w_down"], r["buf_down"], r["sem_down"], fn)

    def grad_up(k):
        top = pl.multiple_of(dest[k] * 4 * rp, 16)
        step = 256

        def body(i, carry):
            n = pl.ds(pl.multiple_of(i * step, 128), step)
            val = dot_nn(r["a2t"][pl.ds(top, 4 * rp), :], dub[:, n])
            r["g1"][pl.ds(dest[k] * 4, 4), :, n] = val.reshape(4, rp, step).astype(bf16)
            return carry

        lax.fori_loop(0, hidden // step, body, 0)

    def swap(n, fn, weights):
        step = r["buf_up"].shape[1]
        slot = n % 2

        def part(i):
            cut = pl.ds(pl.multiple_of(i * step, 128), step)
            return links.make(
                r["send"].at[:, cut], r["came"].at[slot, :, cut], swap_n[n] + i, at.dp, True
            )

        def body(i, w):
            r["send"][:, pl.ds(pl.multiple_of(i * step, 128), step)] = fn(w)
            part(i).start()

        stream(weights, r["buf_up"], r["sem_up"], body)

        def finish(i, carry):
            part(i).wait()
            return carry

        lax.fori_loop(0, weights.shape[0] // step, finish, 0)

    swap_n = [links.numbers(wide // r["buf_up"].shape[1]) for _ in range(3)]

    def norm_grad(n, xh, rstd, gain, base, row, out_rows, store):
        step = out_rows

        def body(i, carry):
            at_i = pl.ds(pl.multiple_of(i * step, step), step)
            val = r["send"][at_i, :] + r["came"][n % 2, at_i, :]
            high = val.astype(bf16)
            low = (val - high.astype(f32)).astype(bf16)
            dh = dot_nn(high, st[...]) + dot_nn(low, st[...])
            x = xh[at_i, :]
            small[row : row + 1, 0:width] += jnp.sum(dh * x, axis=0, keepdims=True)
            small[row : row + 1, wide : wide + width] += jnp.sum(dh, axis=0, keepdims=True)
            dxh = dh * gain[...]
            inner = (
                dxh
                - jnp.mean(dxh, axis=-1, keepdims=True)
                - x * jnp.mean(dxh * x, axis=-1, keepdims=True)
            )
            store(i, at_i, base[at_i, :].astype(f32)[:, :width] + r["rstd"][at_i, rstd : rstd + 1] * inner)
            return carry

        lax.fori_loop(0, length // step, body, 0)

    def mid():
        fill_spread(st, rows, rp)
        swap(0, lambda w: dot_nt(dub[...], w[...]), r["w_up"])
        drc[...] = jnp.zeros_like(drc)

        def store(i, at_i, val):
            r["dres"][at_i, :] = val
            small[7:8, wide : wide + width] += jnp.sum(val, axis=0, keepdims=True)
            own = jnp.where(at.core == 0, val[:, :half], val[:, half:])
            drc[at_i, 3 * hw - shift : 3 * hw - shift + half] = own.astype(bf16)

        norm_grad(0, r["xh2"], 1, r["gain2"], cot, 5, 128, store)
        swap(1, lambda w: dot_nt(drc[...], w[:, shift:]), r["w_joined"])
        summed = (r["send"][...] + r["came"][1]).astype(bf16)

        for c in range(2):
            @pl.when(at.core == c)
            def _():
                first = 0 if c == 0 else width - hw
                val = dot_nn(summed, st[:, first : first + hw])
                if c == 1 and over:
                    lane = lax.broadcasted_iota(jnp.int32, val.shape, 1)
                    val = jnp.where(lane < over, 0.0, val)
                r["do"][...] = val.astype(bf16)

    def attention():
        allowed = may_see(r["seg_rows"][...], r["seg_cols"][...])
        dp[:, shift:] = jnp.zeros((length, joined - shift), bf16)
        rows_dim = (((0,), (0,)), ((), ()))
        for h in range(own_heads):
            here = [slice(i * hw + h * HD, i * hw + (h + 1) * HD) for i in range(3)]
            q, k, v, do = (r[n][:, here[0]] for n in ("q", "k", "v", "do"))
            probs = jnp.exp(head_scores(q, k, allowed) - r["lse"][:, h : h + 1])
            grad_probs = dot_nt(do, v)
            delta = jnp.sum(probs * grad_probs, axis=-1, keepdims=True)
            grad_scores = (probs * (grad_probs - delta) * HD ** (-0.5)).astype(bf16)
            dq = dot_nn(grad_scores, k)
            dk = lax.dot_general(grad_scores, q, rows_dim, preferred_element_type=f32)
            dv = lax.dot_general(probs.astype(bf16), do, rows_dim, preferred_element_type=f32)
            small[7:8, here[0]] = jnp.sum(dq, axis=0, keepdims=True)
            small[7:8, here[1]] = jnp.sum(dv, axis=0, keepdims=True)
            for at_h, val in zip(here, (dq, dk, dv)):
                dp[:, at_h] = val.astype(bf16)

    def last_norm():
        cut = up_to(3 * hw, 128)
        swap(2, lambda w: dot_nt(dp[:, :cut], w[:, :cut]), r["w_joined"])

        def store(i, at_i, val):
            @pl.when(i == at.core)
            def _():
                r["grad_input"][...] = val

        norm_grad(2, r["xh1"], 0, r["gain1"], r["dres"], 4, length // 2, store)

    def grad_joined(k):
        top = pl.multiple_of(dest[k] * 4 * rp, 16)

        def put(n, val):
            val = val.reshape(4, rp, val.shape[-1])
            val = jnp.concatenate([val[:, : rp - 8], val[:, rp - 8 :] + small[:, n][None]], axis=1)
            r["g0"][pl.ds(dest[k] * 4, 4), :, n] = val.astype(bf16)

        step = 256

        def body(i, carry):
            n = pl.ds(pl.multiple_of(i * step, 128), step)
            put(n, dot_nn(r["tall"][pl.ds(top, 4 * rp), :], dp[:, n]))
            return carry

        lax.fori_loop(0, shift // step, body, 0)

        def both(i, carry):
            n = pl.ds(pl.multiple_of(shift + i * step, 128), step)
            m = pl.ds(pl.multiple_of(i * step, 128), step)
            put(
                n,
                dot_nn(r["tall"][pl.ds(top, 4 * rp), :], dp[:, n])
                + dot_nn(r["tall"][pl.ds(wide + top, 4 * rp), :], drc[:, m]),
            )
            return carry

        lax.fori_loop(0, (joined - shift) // step, both, 0)

    h = rows // 2
    part_n = links.numbers(4)

    def trade(sums, base, n):
        high = up_to(h, 8)
        for c in range(2):
            @pl.when(at.core == c)
            def _():
                for e in range(2):
                    r["send"][base + e * high : base + e * high + h, :] = sums[
                        (1 - c) * h : (2 - c) * h, e * wide : (e + 1) * wide
                    ]
        cut = pl.ds(base, 2 * high)
        return links.make(r["send"].at[cut, :], r["came"].at[1, cut, :], part_n + n, at.dp, True)

    def halves(sums, base):
        high = up_to(h, 8)
        for c in range(2):
            def rows_by(s, lo, hi, c=c):
                if s == c:
                    return sums[c * h : (c + 1) * h, lo:hi]
                if hi <= wide or lo >= wide:
                    e = 0 if hi <= wide else 1
                    top = base + e * high
                    return r["came"][1, top : top + h, lo - e * wide : hi - e * wide]
                return jnp.concatenate([rows_by(s, lo, wide), rows_by(s, wide, hi)], axis=1)
            yield c, rows_by

    def fc_out():
        sums = r["sums1"]
        copy = trade(sums, 0, 0)
        copy.start()
        copy.wait()
        for c, rows_by in halves(sums, 0):
            @pl.when(at.core == c)
            def _():
                for j in range(hidden // fp):
                    for s in range(2):
                        lo, to = j * fp, (2 * j + s) * fh
                        cuts = [lo, lo + fh] if not lo < wide < lo + fh else [lo, wide, lo + fh]
                        for u, v in zip(cuts, cuts[1:]):
                            r["fc_grad"][:, to + u - lo : to + v - lo] = rows_by(s, u, v)

    def attn_out():
        sums = r["sums0"]
        base = 2 * up_to(h, 8)
        copy = trade(sums, base, 1)
        copy.start()
        r["row"][...] = sums[rp - 8 :, :]
        row_copy = links.make(r["row"], r["row_came"], part_n + 2, at.dp, True)
        row_copy.start()
        copy.wait()
        row_copy.wait()
        for c, rows_by in halves(sums, base):
            @pl.when(at.core == c)
            def _():
                for i in range(4):
                    size, skip = (hw, over) if i < 3 else (half, 0)
                    to, out = (i * width, r["attn_grad"]) if i < 3 else (0, r["out_grad"])
                    for s, lo in ((0, i * hw), (1, i * hw + skip)):
                        hi = i * hw + size
                        cuts = [lo, hi] if not lo < wide < hi else [lo, wide, hi]
                        for u, v in zip(cuts, cuts[1:]):
                            out[:, to + u - lo : to + v - lo] = rows_by(s, u, v)
                        to += hi - lo
                kinds = r["kinds"]
                kinds[...] = jnp.zeros_like(kinds)
                own = r["row"]
                low, high = (r["row"], r["row_came"]) if c == 0 else (r["row_came"], r["row"])
                for i, (line, first) in enumerate(((4, 0), (4, wide), (5, 0), (5, wide))):
                    kinds[i : i + 1, 0:width] = own[line : line + 1, first : first + width]
                for i in range(2):
                    kinds[4 + i : 5 + i, 0:hw] = low[7:8, i * hw : (i + 1) * hw]
                    kinds[4 + i : 5 + i, hw:width] = high[7:8, i * hw + over : (i + 1) * hw]
                kinds[6:7, 0:width] = own[7:8, wide : wide + width]
                kinds[7:8, 0:width] = r["sums2"][fp - 8 : fp - 7, 0:width]
        size = width // (2 * nz)
        device = at.dp * 2 + at.core
        kind, block = device // (2 * nz), lax.rem(device, 2 * nz)
        for i, place in enumerate((kind, 4 + kind)):
            line = jnp.broadcast_to(r["kinds"][pl.ds(place, 1), :], (8, wide))
            r["small_out"][8 * i : 8 * i + 8, :] = pltpu.roll(line, lax.rem(wide - block * size, wide), 1)
        line = jnp.broadcast_to(r["row"][6:7, :], (8, hidden))
        line = pltpu.roll(line, lax.rem(hidden - at.dp * fp, hidden), 1)
        r["small_out"][16:24, :] = line[:, :wide]

    links.add(-1.0, setup)
    for k in range(nz):
        links.add(1.0 * k, functools.partial(grad_down, k))
    links.add(4.9, lambda: tall("a1t_ot").start())
    links.add(49.9, lambda: tall("a1t_ot").wait())
    links.add(5.0, grad_hidden)
    for k in range(nz):
        links.add(10.0 + k, functools.partial(grad_up, k))
    links.add(20.0, mid)
    links.add(31.0, attention)
    links.add(33.0, last_norm)
    for k in range(nz):
        links.add(50.0 + k, functools.partial(grad_joined, k))
    grads, sums = ("g0", "g1", "g2"), ("sums0", "sums1", "sums2")
    for n, item in enumerate(items):
        scatter_item(
            links, nz, dest, item, r[grads[item[0]]], r[sums[item[0]]],
            bufs[4 * n : 4 * n + 4], functools.partial(step_time, nz, item),
        )
    links.add(65.0, fc_out)
    links.add(99.0, attn_out)
    links.run()


def step_time(nz, item, stage, k):
    array, _, _, _, kind = item
    spread = k / nz
    if kind == "pz":
        return {
            "start": (0.6, 18.6, 30.2),
            "chain": (30.3, 55.0, 56.0),
            "gathered": (61.0,),
            "first": (61.1,),
            "second": (72.0,),
            "third": (79.5,),
        }[stage][min(k, 2)]
    if array == 2:
        return {
            "first": (0.5, 1.5, 2.5, 3.5),
            "second": (9.0, 9.1, 9.2, 9.3),
            "third": (18.0, 30.1, 32.0, 41.0),
        }[stage][min(k, 3)]
    if array == 1:
        return {"first": 18.5, "second": 40.0, "third": 60.0}[stage] + (spread if stage != "third" else k / 8)
    return {"first": 50.5, "second": 70.0, "third": 80.0}[stage] + (k if stage == "first" else spread)


def back_call(nz, items, pieces, sizes, inputs, hbm, outs, collective_id):
    bf16, f32 = jnp.bfloat16, jnp.float32
    own_heads, rows, rp, fh, fp, half, over = sizes
    length, wide = inputs["cot"].shape
    width = inputs["xh1"].shape[1]
    hidden = inputs["slope"].shape[1]
    joined = hbm["w_joined"].shape[1]
    shift = 3 * own_heads * HD // 256 * 256
    bufs, sems = item_bufs(nz, pieces, items)
    sems += 3 * (wide // 384) + 4
    scratch = {
        "g0": pltpu.VMEM(pieces[0], bf16),
        "g1": pltpu.VMEM(pieces[1], bf16),
        "g2": pltpu.VMEM(pieces[2], bf16),
        "st": pltpu.VMEM((wide, width), bf16),
        "small": pltpu.VMEM((8, joined), f32),
        "small_d": pltpu.VMEM((8, wide), f32),
        "dub": pltpu.VMEM((length, hidden), bf16),
        "dp": pltpu.VMEM((length, joined), bf16),
        "drc": pltpu.VMEM((length, joined - shift), bf16),
        "do": pltpu.VMEM((length, own_heads * HD), bf16),
        "dres": pltpu.VMEM((length, width), f32),
        "send": pltpu.VMEM((length, wide), f32),
        "came": pltpu.VMEM((2, length, wide), f32),
        "sums0": pltpu.VMEM(pieces[0][1:], f32),
        "sums1": pltpu.VMEM(pieces[1][1:], f32),
        "tall": pltpu.VMEM((max(hidden, 2 * wide), length), bf16),
        "sem_tall": pltpu.SemaphoreType.DMA((1,)),
        "row": pltpu.VMEM((8, joined), f32),
        "row_came": pltpu.VMEM((8, joined), f32),
        "kinds": pltpu.VMEM((8, wide), f32),
        "buf_down": pltpu.VMEM((2, 256, wide), bf16),
        "buf_up": pltpu.VMEM((2, 384, joined), bf16),
        "sem_down": pltpu.SemaphoreType.DMA((2,)),
        "sem_up": pltpu.SemaphoreType.DMA((2,)),
        "send_sem": pltpu.SemaphoreType.DMA((sems,)),
        "recv_sem": pltpu.SemaphoreType.DMA((sems,)),
    }
    names = (*inputs, *hbm, *outs, *scratch)
    vmem, far = pl.BlockSpec(memory_space=pltpu.VMEM), pl.BlockSpec(memory_space=pl.ANY)
    return pl.pallas_call(
        functools.partial(back_kernel, nz, items, sizes, names),
        out_shape=list(outs.values()),
        in_specs=[vmem] * len(inputs) + [far] * len(hbm),
        out_specs=[vmem] * len(outs),
        scratch_shapes=[*scratch.values(), *bufs],
        compiler_params=pltpu.CompilerParams(
            collective_id=collective_id, has_side_effects=True, vmem_limit_bytes=63 * 2**20
        ),
    )(*inputs.values(), *hbm.values())


def attend(scores_of, heads, lse_ref, q_ref, k_ref, v_ref, o_ref, allowed):
    for h in range(heads):
        at = slice(h * HD, (h + 1) * HD)
        scores = scores_of(q_ref[:, at], k_ref[:, at], allowed)
        top = jnp.max(scores, axis=-1, keepdims=True)
        total = top + jnp.log(jnp.sum(jnp.exp(scores - top), axis=-1, keepdims=True))
        probs = jnp.exp(scores - total).astype(jnp.bfloat16)
        lse_ref[:, h : h + 1] = total
        o_ref[:, at] = jnp.dot(
            probs, v_ref[:, at], preferred_element_type=jnp.float32
        ).astype(o_ref.dtype)


def head_scores(queries, key_rows, allowed):
    scores = lax.dot_general(
        queries, key_rows, (((1,), (1,)), ((), ())), preferred_element_type=jnp.float32
    ) * HD ** (-0.5)
    return jnp.where(allowed, scores, -1e30)


def may_see(seg_rows, seg_cols):
    length = seg_cols.shape[1]
    i = lax.broadcasted_iota(jnp.int32, (length, length), 0)
    j = lax.broadcasted_iota(jnp.int32, (length, length), 1)
    return (j <= i) & (seg_rows == seg_cols)


def attention_kernel(heads, q_ref, k_ref, v_ref, rows_ref, cols_ref, o_ref, lse_ref):
    allowed = may_see(rows_ref[...], cols_ref[...])
    attend(head_scores, heads, lse_ref, q_ref, k_ref, v_ref, o_ref, allowed)


VMEM_LIMIT = 60 * 2**20


def local_call(kernel, outs, *args):
    spec = pl.BlockSpec(memory_space=pltpu.VMEM)
    return pl.pallas_call(
        kernel,
        out_shape=outs,
        in_specs=[spec] * len(args),
        out_specs=[spec] * len(outs),
        compiler_params=pltpu.CompilerParams(vmem_limit_bytes=VMEM_LIMIT),
    )(*args)


def up_to(value, step):
    return -(-value // step) * step


def split_items(shapes, dtype_rows=None):
    (_, wa), (_, wf), (_, wp) = shapes
    first = up_to(2 * wa // 3, 128)

    def cut(array, lo, hi, kind):
        return (array, lo, lo + up_to((hi - lo) // 2, 128), hi, kind)

    return (
        cut(0, 0, first, "pz"),
        cut(0, first, wa, "zp"),
        cut(1, 0, wf, "zp"),
        cut(2, 0, wp, "zp"),
    )


def per_device_grid(
    nz,
    layer_input,
    segments,
    w_attn,
    w_out,
    w_fc,
    w_proj,
    norm_params,
    lin_bias,
    fc_bias,
    out_cotangent,
):
    f32, bf16 = jnp.float32, jnp.bfloat16
    core = lax.axis_index("seq")
    low = core == 0
    chips = lax.axis_size("dp")
    tokens, width = layer_input.shape[1:]
    heads = width // HD
    own_heads = -(-heads // 2)
    hw = own_heads * HD
    over = 2 * hw - width
    half = width // 2
    small = norm_params.shape[0]
    h = w_out.shape[0] // width
    rows, rp = 2 * h, up_to(2 * h, 8)
    fh = w_proj.shape[0] // width
    fp = up_to(fh + 2, 16)
    hidden = chips * fp
    wide = up_to(width, 128)
    owide = up_to(3 * hw + half, 128) - 3 * hw

    def swap(value):
        return lax.ppermute(value, "seq", [(0, 1), (1, 0)])

    def pair(own, came):
        return jnp.where(low, own, came), jnp.where(low, came, own)

    def lanes_of(value, size):
        first, second = value[..., :size], value[..., value.shape[-1] - size :]
        return jnp.where(low, first, second), jnp.where(low, second, first)

    def tokens_of(value):
        first, second = value[:tokens], value[tokens:]
        return jnp.where(low, first, second), jnp.where(low, second, first)

    def spread(acts):
        parts = acts.reshape(acts.shape[0], chips, rows)
        return jnp.pad(parts, ((0, 0), (0, 0), (0, rp - rows))).reshape(acts.shape[0], -1)

    def unspread(acts):
        return acts.reshape(acts.shape[0], chips, rp)[:, :, :rows].reshape(acts.shape[0], width)

    def dot(a, b):
        return jnp.dot(a, b, preferred_element_type=f32)

    def dot_t(a, b):
        return lax.dot_general(a, b, (((1,), (1,)), ((), ())), preferred_element_type=f32)

    def outer(a, b):
        return lax.dot_general(a, b, (((0,), (0,)), ((), ())), preferred_element_type=bf16)

    own_small = jnp.concatenate([norm_params, lin_bias, fc_bias])
    wa = w_attn.reshape(h, 3 * width)
    wo = w_out.reshape(h, width)
    wf = w_fc.reshape(h, chips, 2, fh)
    parts = [lanes_of(wa[:, i * width : (i + 1) * width], hw) for i in range(3)]
    parts.append(lanes_of(wo, half))
    gap = jnp.zeros((h, owide - half), bf16)
    attn_own, attn_other = (
        jnp.concatenate([p[i] for p in parts] + [gap], axis=1) for i in range(2)
    )
    fc_pads = ((0, 0), (0, 0), (0, fp - fh))
    fc_own, fc_other = (
        jnp.pad(jnp.where(low == first, wf[:, :, 0], wf[:, :, 1]), fc_pads).reshape(h, hidden)
        for first in (True, False)
    )
    attn_came, fc_came = swap(attn_other), swap(fc_other)
    acts_came = swap(jnp.stack([layer_input[0], out_cotangent[0]]))
    small_came = swap(own_small)
    row_pads = ((0, rp - rows), (0, 0))
    attn_piece = jnp.pad(jnp.concatenate(pair(attn_own, attn_came)), row_pads)
    fc_piece = jnp.pad(jnp.concatenate(pair(fc_own, fc_came)), row_pads)
    small_rows = jnp.pad(jnp.stack(pair(own_small, small_came)), ((0, 0), (0, wide - 3 * small)))
    proj_piece = jnp.concatenate(
        [
            jnp.pad(w_proj.reshape(fh, width), ((0, 0), (0, wide - width))),
            jnp.pad(small_rows, ((0, fp - fh - 2), (0, 0))),
        ]
    )
    shapes = (attn_piece.shape, fc_piece.shape, proj_piece.shape)
    items = split_items(shapes)
    attn_all, fc_all, proj_all = gather_call(nz, (attn_piece, fc_piece, proj_piece), items, 0)
    w_joined = attn_all.reshape(-1, attn_piece.shape[1])
    w_qkv, w_o = w_joined[:, : 3 * hw], w_joined[:, 3 * hw : 3 * hw + half]
    w_up = fc_all.reshape(-1, hidden)
    w_down = proj_all.reshape(hidden, wide)
    smalls = proj_all[:, fh : fh + 2, : 3 * small].astype(f32)
    by_kind = smalls.reshape(-1, 3, small)
    norms = by_kind[:, 0].reshape(4, width)
    biases = by_kind[:, 1].reshape(4, width)
    fc_own_bias = jnp.where(low, smalls[:, 0, 2 * small :], smalls[:, 1, 2 * small :])
    up_bias = jnp.pad(fc_own_bias, ((0, 0), (0, fp - fh))).reshape(hidden)
    real = jnp.pad(jnp.ones((chips, fh), f32), ((0, 0), (0, fp - fh))).reshape(hidden)

    acts = jnp.concatenate(pair(layer_input[0], acts_came[0]))
    cotangent = jnp.concatenate(pair(out_cotangent[0], acts_came[1]))
    inputs_f = acts.astype(f32)
    grad_out = cotangent.astype(f32)
    normed1, x_hat1, inv_std1 = layer_norm(inputs_f, norms[0], norms[1])
    act_rows1 = spread(normed1.astype(bf16))
    projected = dot(act_rows1, w_qkv)
    queries = (projected[:, :hw] + lanes_of(biases[0], hw)[0]).astype(bf16)
    key_rows = projected[:, hw : 2 * hw].astype(bf16)
    value_rows = (projected[:, 2 * hw :] + lanes_of(biases[1], hw)[0]).astype(bf16)
    seg_rows, seg_cols = segments.reshape(-1, 1), segments.reshape(1, -1)
    length = 2 * tokens
    shape = jax.ShapeDtypeStruct
    attended, log_total = local_call(
        functools.partial(attention_kernel, own_heads),
        [shape((length, hw), bf16), shape((length, 128), f32)],
        queries, key_rows, value_rows, seg_rows, seg_cols,
    )
    att_low, att_high = pair(attended, swap(attended))
    attended_rows = spread(jnp.concatenate([att_low, att_high[:, over:]], axis=1))
    mixed = dot(attended_rows, w_o)
    resid = inputs_f + jnp.concatenate(pair(mixed, swap(mixed)), axis=1) + biases[2]
    normed2, x_hat2, inv_std2 = layer_norm(resid, norms[2], norms[3])
    act_rows2 = spread(normed2.astype(bf16))
    hidden_pre = dot(act_rows2, w_up) + up_bias
    hidden_act, hidden_slope = gelu_parts(hidden_pre)
    hidden_b = hidden_act.astype(bf16)
    down, down_other = tokens_of(dot(hidden_b, w_down)[:, :width])
    result = tokens_of(resid)[0] + (down + swap(down_other)) + biases[3]

    cot_wide = jnp.pad(cotangent, ((0, 0), (0, wide - width)))
    back = (
        (2, 0, up_to(wide // 3, 128), 2 * up_to(wide // 3, 128), "pz"),
        (2, 2 * up_to(wide // 3, 128), 2 * up_to(wide // 3, 128) + up_to(wide // 6, 128), wide, "zp"),
        (1, 0, up_to(hidden // 2, 128), hidden, "zp"),
        (0, 0, up_to(hidden // 2, 128), attn_piece.shape[1], "zp"),
    )
    attn_grad, out_grad, fc_grad, proj_grad, grad_input, small_out = back_call(
        nz,
        back,
        (attn_all.shape, fc_all.shape, proj_all.shape),
        (own_heads, rows, rp, fh, fp, half, over),
        {
            "slope": (hidden_slope * real).astype(bf16),
            "cot": cot_wide,
            "a2t": act_rows2.T,
            "q": queries,
            "k": key_rows,
            "v": value_rows,
            "seg_rows": seg_rows,
            "seg_cols": seg_cols,
            "lse": log_total,
            "xh1": x_hat1,
            "xh2": x_hat2,
            "rstd": jnp.concatenate([inv_std1, inv_std2], axis=1),
            "gain1": norms[0:1],
            "gain2": norms[2:3],
        },
        {"gt": hidden_b.T, "a1t_ot": jnp.concatenate([act_rows1, attended_rows], axis=1).T, "w_down": w_down, "w_up": w_up, "w_joined": w_joined},
        {
            "attn_grad": shape((h, 3 * width), f32),
            "out_grad": shape((h, width), f32),
            "fc_grad": shape((h, 2 * chips * fh), f32),
            "sums2": shape(proj_piece.shape, f32),
            "grad_input": shape((tokens, width), f32),
            "small_out": shape((24, wide), f32),
        },
        1,
    )

    return (
        result.astype(bf16)[None],
        grad_input[None],
        attn_grad.reshape(-1),
        out_grad.reshape(-1),
        fc_grad.reshape(-1),
        proj_grad[:fh, :width].reshape(-1),
        small_out[0, :small],
        small_out[8, :small],
        small_out[16, :small],
    )


def grid_height(mesh):
    shape = dict(mesh.shape)
    devices = mesh.devices.reshape(-1)
    if tuple(mesh.axis_names) != AXES or shape["seq"] != 2 or shape["dp"] % 4:
        return 0
    nz = shape["dp"] // 4
    base = getattr(devices[0], "coords", None)
    if base is None:
        return 0
    for n, device in enumerate(devices):
        chip = n // 2
        place = (chip % 2, chip // 2 % 2, chip // 4)
        if tuple(a - b for a, b in zip(device.coords, base)) != place:
            return 0
    return nz if 1 < nz <= 4 else 0


def solution(mesh):
    nz = grid_height(mesh)
    return jax.shard_map(
        functools.partial(per_device_grid, nz) if nz else per_device,
        mesh=mesh,
        in_specs=(
            P("dp", "seq", None),
            P("dp", None),
            P(("dp", "seq")),
            P(("dp", "seq")),
            P(("dp", "seq")),
            P(("dp", "seq")),
            P(("dp", "seq")),
            P(("dp", "seq")),
            P(("dp", "seq")),
            P("dp", "seq", None),
        ),
        out_specs=(
            P("dp", "seq", None),
            P("dp", "seq", None),
            P(("dp", "seq")),
            P(("dp", "seq")),
            P(("dp", "seq")),
            P(("dp", "seq")),
            P(("dp", "seq")),
            P(("dp", "seq")),
            P(("dp", "seq")),
        ),
        check_vma=False,
    )
```

```python
import functools

import jax
import jax.numpy as jnp
from jax import lax
from jax.experimental import pallas as pl
from jax.experimental.pallas import tpu as pltpu
from jax.sharding import PartitionSpec as P

HD = 64
FF = 4352


GELU_C = 0.7978845608028654
NORM_EPS = 1e-05


def gelu_parts(inputs):
    tanh_value = jnp.tanh(GELU_C * (inputs + 0.044715 * inputs * inputs * inputs))
    value = 0.5 * inputs * (1.0 + tanh_value)
    slope = 0.5 * (1.0 + tanh_value) + 0.5 * inputs * (1.0 - tanh_value * tanh_value) * GELU_C * (
        1.0 + 3.0 * 0.044715 * inputs * inputs
    )
    return (value, slope)


def layer_norm(inputs, gains, offsets):
    average = jnp.mean(inputs, axis=-1, keepdims=True)
    centred = inputs - average
    inv_std = lax.rsqrt(jnp.mean(centred * centred, axis=-1, keepdims=True) + NORM_EPS)
    x_hat = centred * inv_std
    return (x_hat * gains + offsets, x_hat, inv_std)


def norm_back(grad_out, x_hat, inv_std, gains):
    grad_hat = grad_out * gains
    grad_in = inv_std * (
        grad_hat
        - jnp.mean(grad_hat, axis=-1, keepdims=True)
        - x_hat * jnp.mean(grad_hat * x_hat, axis=-1, keepdims=True)
    )
    return (grad_in, jnp.sum(grad_out * x_hat, axis=0), jnp.sum(grad_out, axis=0))


def score_block(queries, key_rows, allowed):
    scores = jnp.einsum(
        "qhd,khd->hqk", queries, key_rows, preferred_element_type=jnp.float32
    ) * HD ** (-0.5)
    return jnp.where(allowed[None], scores, -1e30)


def outer_sum(left, right):
    return jnp.einsum("na,nb->ab", left, right, preferred_element_type=jnp.float32)


AXES = ("dp", "seq")


def shard_height(shard, columns):
    size = shard.shape[0]
    return size // columns if size % columns == 0 else 0


def tile_height(shard, columns):
    height = shard_height(shard, columns)
    return 0 if height % 8 else height


def padded(height):
    return -(-height // 8) * 8


def gather_rows(shard, columns, height, extra=None):
    if not height:
        return lax.all_gather(shard, AXES, axis=0, tiled=True).reshape(-1, columns)
    block = shard.reshape(height, columns)
    room = padded(height) - height
    if extra is not None:
        row = jnp.pad(extra, (0, columns - extra.shape[0]))[None]
        block = jnp.concatenate([block, row], axis=0)
        room -= 1
    if room:
        block = jnp.pad(block, ((0, room), (0, 0)))
    return lax.all_gather(block, AXES, axis=0, tiled=True)


def spread(acts, height):
    room = padded(height) - height
    if not room:
        return acts
    tokens = acts.shape[0]
    parts = acts.reshape(tokens, -1, height)
    return jnp.pad(parts, ((0, 0), (0, 0), (0, room))).reshape(tokens, -1)


def unspread(acts, height):
    if padded(height) == height:
        return acts
    tokens = acts.shape[0]
    return acts.reshape(tokens, -1, padded(height))[:, :, :height].reshape(tokens, -1)


def scatter_rows(blocks, height):
    count = lax.axis_size(AXES)
    sums = lax.psum_scatter(
        blocks.astype(jnp.bfloat16).reshape(count, -1, blocks.shape[-1]),
        AXES,
        scatter_dimension=0,
        tiled=True,
    )[0]
    return sums.astype(jnp.float32)


def scatter_flat(block, shard):
    count = lax.axis_size(AXES)
    return lax.psum_scatter(
        block.reshape(count, shard), AXES, scatter_dimension=0, tiled=True
    )[0]


def own_half_sum(terms, place, tokens):
    if lax.axis_size("seq") != 2:
        return lax.psum_scatter(
            terms.astype(jnp.bfloat16), "seq", scatter_dimension=0, tiled=True
        ).astype(jnp.float32)
    own = lax.dynamic_slice_in_dim(terms, place * tokens, tokens)
    other = lax.dynamic_slice_in_dim(terms, (1 - place) * tokens, tokens)
    came = lax.ppermute(other.astype(jnp.bfloat16), "seq", [(0, 1), (1, 0)])
    return own + came.astype(jnp.float32)


def per_device(
    layer_input,
    segments,
    w_attn,
    w_out,
    w_fc,
    w_proj,
    norm_params,
    lin_bias,
    fc_bias,
    out_cotangent,
):
    tokens = layer_input.shape[1]
    width = layer_input.shape[2]
    heads = width // HD
    place = lax.axis_index("seq")
    first = place * tokens
    small = norm_params.shape[0]
    height = shard_height(w_attn, 3 * width)
    height = height if shard_height(w_out, width) == height == shard_height(w_fc, FF) else 0
    down_height = tile_height(w_proj, width)
    own_small = jnp.concatenate([norm_params, lin_bias, fc_bias])
    packed = height and padded(height) > height and own_small.shape[0] <= width
    if height:
        lanes = -(-width // 128) * 128
        joined_shard = jnp.concatenate(
            [
                jnp.pad(w_out.reshape(height, width), ((0, 0), (0, lanes - width))),
                w_attn.reshape(height, 3 * width),
            ],
            axis=1,
        ).reshape(-1)
        joined_w = gather_rows(
            joined_shard, lanes + 3 * width, height, own_small if packed else None
        )
        w_o = joined_w[:, :width]
        w_qkv = joined_w[:, lanes:]
    else:
        w_qkv = gather_rows(w_attn, 3 * width, 0)
        w_o = gather_rows(w_out, width, 0)
    w_up = gather_rows(w_fc, FF, height)
    w_down = gather_rows(w_proj, width, down_height)
    if packed:
        smalls = w_o.reshape(-1, padded(height), width)[:, height, : 3 * small]
    else:
        smalls = lax.all_gather(own_small, AXES, axis=0)
    smalls = smalls.astype(jnp.float32).reshape(-1, 3, small)
    norms = smalls[:, 0].reshape(4, width)
    biases = smalls[:, 1].reshape(4, width)
    up_bias = smalls[:, 2].reshape(FF)
    inputs_f = layer_input[0].astype(jnp.float32)
    normed1, x_hat1, inv_std1 = layer_norm(inputs_f, norms[0], norms[1])
    act_in1 = normed1.astype(jnp.bfloat16)
    act_rows1 = spread(act_in1, height)
    projected = jnp.dot(act_rows1, w_qkv, preferred_element_type=jnp.float32)
    queries = (projected[:, :width] + biases[0]).astype(jnp.bfloat16)
    own_keys = projected[:, width : 2 * width].astype(jnp.bfloat16)
    own_values = (projected[:, 2 * width :] + biases[1]).astype(jnp.bfloat16)
    key_rows, value_rows = (
        lax.all_gather(own_keys, "seq", axis=0, tiled=True),
        lax.all_gather(own_values, "seq", axis=0, tiled=True),
    )
    key_count = key_rows.shape[0]
    key_pos = jnp.arange(key_count)
    query_pos = first + jnp.arange(tokens)
    padded_seg = jnp.concatenate([jnp.full((tokens,), -1, jnp.int32), segments[0]])
    key_seg = lax.dynamic_slice_in_dim(padded_seg, tokens, key_count)
    query_seg = lax.dynamic_slice_in_dim(segments[0], first, tokens)
    allowed = (key_pos[None, :] <= query_pos[:, None]) & (key_seg[None, :] == query_seg[:, None])
    q_heads = queries.reshape(tokens, heads, HD)
    k_heads = key_rows.reshape(key_count, heads, HD)
    v_heads = value_rows.reshape(key_count, heads, HD)
    scores = score_block(q_heads, k_heads, allowed)
    top_score = jnp.max(scores, axis=-1, keepdims=True)
    log_total = top_score + jnp.log(jnp.sum(jnp.exp(scores - top_score), axis=-1, keepdims=True))
    attn_probs = jnp.exp(scores - log_total).astype(jnp.bfloat16)
    attended = jnp.einsum("hqk,khd->qhd", attn_probs, v_heads, preferred_element_type=jnp.float32)
    attended = attended.reshape(tokens, width).astype(jnp.bfloat16)
    attended_rows = spread(attended, height)
    resid = inputs_f + jnp.dot(attended_rows, w_o, preferred_element_type=jnp.float32) + biases[2]
    normed2, x_hat2, inv_std2 = layer_norm(resid, norms[2], norms[3])
    act_in2 = normed2.astype(jnp.bfloat16)
    act_rows2 = spread(act_in2, height)
    hidden_pre = jnp.dot(act_rows2, w_up, preferred_element_type=jnp.float32) + up_bias
    hidden_act, hidden_slope = gelu_parts(hidden_pre)
    hidden_b = hidden_act.astype(jnp.bfloat16)
    hidden_rows = spread(hidden_b, down_height)
    result = (
        resid + jnp.dot(hidden_rows, w_down, preferred_element_type=jnp.float32) + biases[3]
    ).astype(jnp.bfloat16)
    cotangent = out_cotangent[0]
    grad_out = cotangent.astype(jnp.float32)
    grad_bp = jnp.sum(grad_out, axis=0)
    grad_hidden = (
        unspread(
            jnp.einsum("nd,fd->nf", cotangent, w_down, preferred_element_type=jnp.float32),
            down_height,
        )
        * hidden_slope
    )
    grad_hidden_b = grad_hidden.astype(jnp.bfloat16)
    grad_down = outer_sum(hidden_rows, cotangent)
    if down_height:
        grad_hidden_b, grad_down = lax.optimization_barrier(
            (grad_hidden_b, grad_down.astype(jnp.bfloat16))
        )
    grad_up_bias = jnp.sum(grad_hidden, axis=0)
    if down_height:
        proj_sums = scatter_rows(grad_down, down_height)[:down_height].reshape(-1)
    else:
        proj_sums = scatter_flat(grad_down, w_proj.shape[0])
    grad_up = outer_sum(act_rows2, grad_hidden_b)
    if height:
        fc_sums = scatter_rows(grad_up, height)[:height].reshape(-1)
    else:
        fc_sums = scatter_flat(grad_up, w_fc.shape[0])
    grad_norm2 = unspread(
        jnp.einsum("nf,df->nd", grad_hidden_b, w_up, preferred_element_type=jnp.float32), height
    )
    grad_resid_n, grad_g2, grad_b2 = norm_back(grad_norm2, x_hat2, inv_std2, norms[2])
    grad_resid = grad_out + grad_resid_n
    grad_resid_b = grad_resid.astype(jnp.bfloat16)
    grad_bo = jnp.sum(grad_resid, axis=0)
    grad_att = unspread(
        jnp.einsum(
            "ne,de->nd", grad_resid_b, w_o, preferred_element_type=jnp.float32
        ).astype(jnp.bfloat16),
        height,
    )
    grad_att_heads = grad_att.reshape(tokens, heads, HD)
    probs_full = jnp.exp(score_block(q_heads, k_heads, allowed) - log_total)
    probs_b = probs_full.astype(jnp.bfloat16)
    grad_probs = jnp.einsum(
        "qhd,khd->hqk", grad_att_heads, v_heads, preferred_element_type=jnp.float32
    )
    delta = jnp.sum(probs_full * grad_probs, axis=-1, keepdims=True)
    grad_scores = (probs_full * (grad_probs - delta) * HD ** (-0.5)).astype(jnp.bfloat16)
    grad_q = jnp.einsum(
        "hqk,khd->qhd", grad_scores, k_heads, preferred_element_type=jnp.float32
    ).reshape(tokens, width)
    grad_k_all = jnp.einsum(
        "hqk,qhd->khd", grad_scores, q_heads, preferred_element_type=jnp.float32
    ).reshape(key_count, width)
    grad_v_all = jnp.einsum(
        "hqk,qhd->khd", probs_b, grad_att_heads, preferred_element_type=jnp.float32
    ).reshape(key_count, width)
    grad_k = own_half_sum(grad_k_all, place, tokens)
    grad_v = own_half_sum(grad_v_all, place, tokens)
    grad_proj_b = jnp.concatenate([grad_q, grad_k, grad_v], axis=1).astype(jnp.bfloat16)
    grad_norm1 = unspread(
        jnp.einsum("ne,de->nd", grad_proj_b, w_qkv, preferred_element_type=jnp.float32), height
    )
    grad_in_n, grad_g1, grad_b1 = norm_back(grad_norm1, x_hat1, inv_std1, norms[0])
    grad_input = grad_resid + grad_in_n
    norm_terms = jnp.concatenate([grad_g1, grad_b1, grad_g2, grad_b2])
    bias_terms = jnp.concatenate(
        [jnp.sum(grad_q, axis=0), jnp.sum(grad_v, axis=0), grad_bo, grad_bp]
    )
    small_terms = jnp.concatenate(
        [term.reshape(-1, 1, small) for term in (norm_terms, bias_terms, grad_up_bias)], axis=1
    )
    grad_attn = outer_sum(act_rows1, grad_proj_b)
    grad_wo = outer_sum(attended_rows, grad_resid_b)
    if height:
        joined = jnp.concatenate(
            [grad_attn.astype(jnp.bfloat16), grad_wo.astype(jnp.bfloat16)], axis=1
        )
        if packed:
            blocks = joined.reshape(-1, padded(height), 4 * width)
            row = small_terms.astype(jnp.bfloat16).reshape(-1, 1, 3 * small)
            row = jnp.pad(row, ((0, 0), (height, padded(height) - height - 1), (0, width * 4 - 3 * small)))
            joined = (blocks + row).reshape(joined.shape)
        sums = scatter_rows(joined, height)
        qkv_sums = sums[:height, : 3 * width].reshape(-1)
        out_sums = sums[:height, 3 * width :].reshape(-1)
    else:
        qkv_sums = scatter_flat(grad_attn, w_attn.shape[0])
        out_sums = scatter_flat(grad_wo, w_out.shape[0])
    if packed:
        small_sums = sums[height, : 3 * small].reshape(3, small)
    else:
        small_sums = lax.psum_scatter(small_terms, AXES, scatter_dimension=0, tiled=True)[0]
    norm_sums, bias_sums, fcb_sums = small_sums[0], small_sums[1], small_sums[2]
    return (
        result[None],
        grad_input[None],
        qkv_sums,
        out_sums,
        fc_sums,
        proj_sums,
        norm_sums,
        bias_sums,
        fcb_sums,
    )


MESH = pl.DeviceIdType.MESH


class Place:
    def __init__(self, nz):
        self.nz = nz
        self.dp = lax.axis_index("dp")
        self.core = lax.axis_index("seq")
        self.x = lax.rem(self.dp, 2)
        self.y = lax.rem(self.dp // 2, 2)
        self.z = self.dp // 4
        fx, fy = 1 - 2 * self.x, 2 - 4 * self.y
        self.flip = (0, fx, fy, fx + fy)

    def chip(self, dz, p):
        return self.dp + 4 * dz + self.flip[p]

    def has(self, dz):
        return jnp.logical_and(self.z + dz >= 0, self.z + dz < self.nz)

    def meet(self, other=False):
        barrier = pltpu.get_barrier_semaphore()
        for dz, p in ((0, 1), (0, 2)):
            pl.semaphore_signal(
                barrier, inc=1, device_id=(self.chip(dz, p), self.core), device_id_type=MESH
            )
        for dz in (1, -1):
            @pl.when(self.has(dz))
            def _():
                pl.semaphore_signal(
                    barrier, inc=1, device_id=(self.chip(dz, 0), self.core), device_id_type=MESH
                )
        if other:
            pl.semaphore_signal(
                barrier, inc=1, device_id=(self.dp, 1 - self.core), device_id_type=MESH
            )
        near = 3 if other else 2
        pl.semaphore_wait(barrier, near + self.has(1).astype(jnp.int32) + self.has(-1).astype(jnp.int32))


def slots(nz):
    return [0] + [s * k for k in range(1, nz) for s in (1, -1)]


def strips(lo, hi, fn):
    def body(i, carry):
        fn(pl.multiple_of(i * 128, 128))
        return carry

    lax.fori_loop(0, (hi - lo) // 128, body, 0)


def far_first(nz):
    return [sorted(range(nz), key=lambda t: -abs(t - z)) for z in range(nz)]


def choose(scalar, values):
    picked = jnp.int32(values[0])
    for i, v in enumerate(values[1:], 1):
        picked = jnp.where(scalar == i, jnp.int32(v), picked)
    return picked


class Links:
    def __init__(self, at, send_sem, recv_sem):
        self.at, self.send_sem, self.recv_sem = at, send_sem, recv_sem
        self.used, self.events, self.ends = 0, [], []

    def numbers(self, size):
        self.used += size
        return self.used - size

    def add(self, when, fn):
        self.events.append((when, len(self.events), fn))

    def make(self, src, dst, n, chip, other=False):
        core = 1 - self.at.core if other else self.at.core
        return pltpu.make_async_remote_copy(
            src_ref=src,
            dst_ref=dst,
            send_sem=self.send_sem.at[n],
            recv_sem=self.recv_sem.at[n],
            device_id=(chip, core),
            device_id_type=MESH,
        )

    def go(self, src, dst, n, chip, other=False):
        self.make(src, dst, n, chip, other).start()
        self.ends.append(lambda: self.make(src, dst, n, chip, other).wait_send())

    def came(self, dst, n):
        self.make(dst, dst, n, self.at.dp).wait_recv()

    def run(self):
        for _, _, fn in sorted(self.events, key=lambda e: e[:2]):
            fn()
        for fn in self.ends:
            fn()


def line_cases(at, nz, dst):
    for step in (1, -1):
        ahead = dst > at.z if step > 0 else dst < at.z
        first = at.z == (0 if step > 0 else nz - 1)
        slot = dst if step > 0 else jnp.where(dst == at.z - 1, nz, dst)
        yield step, ahead, first, slot


def scatter_item(links, nz, dest, item, src, out, bufs, times):
    f32 = jnp.float32
    at = links.at
    _, lo, mid, hi, kind = item
    width, na = hi - lo, mid - lo
    part_d, part_x, part_y, line = bufs
    landing = {1: part_x, 2: part_y}
    halves = {"a": (0, na), "b": (na, width - na)}

    def mod4(chip):
        return lax.rem(chip, 4)

    def lanes(start, i):
        return pl.ds(pl.multiple_of(start + i, 128), 128)

    def plane(k, value, finish):
        base = links.numbers(6)

        def cut(ref, half, first=0):
            start, size = halves[half]
            return ref.at[:, pl.ds(first + start, size)]

        def first():
            for p, half, n in ((2, "a", 0), (1, "b", 1)):
                ref, start = value(3)
                links.go(cut(ref, half, start), cut(part_d.at[k], half), base + n, at.chip(0, p))
            for p, half, n in ((1, "b", 2), (2, "a", 3)):
                ref, start = value(p)
                links.go(cut(ref, half, start), cut(landing[p].at[k], half), base + n, at.chip(0, p))

        def second():
            for p, half, n, m in ((1, "a", 0, 4), (2, "b", 1, 5)):
                here = cut(part_d.at[k], half)
                links.came(here, base + n)
                ref, start = value(p)
                l, size = halves[half]

                def one(i, ref=ref, start=start, l=l):
                    part_d[k, :, lanes(l, i)] = (
                        part_d[k, :, lanes(l, i)].astype(f32) + ref[:, lanes(start + l, i)].astype(f32)
                    ).astype(part_d.dtype)

                strips(0, size, one)
                links.go(here, cut(landing[p].at[k], half), base + m, at.chip(0, p))

        def third():
            for p, half, n in ((1, "b", 2), (2, "a", 3), (1, "a", 4), (2, "b", 5)):
                links.came(cut(landing[p].at[k], half), base + n)
            finish()

        links.add(times("first", k), first)
        links.add(times("second", k), second)
        links.add(times("third", k), third)

    if kind == "zp":
        line_n = links.numbers(nz + 1)
        for k in range(nz):
            dst = dest[k]

            def value(p, dst=dst):
                return src.at[dst * 4 + mod4(at.chip(0, p))], lo

            def total(i, k=k, dst=dst):
                return (
                    src[dst * 4 + mod4(at.dp), :, lanes(lo, i)].astype(f32)
                    + part_x[k, :, pl.ds(i, 128)].astype(f32)
                    + part_y[k, :, pl.ds(i, 128)].astype(f32)
                )

            if k < nz - 1:

                def finish(k=k, dst=dst, total=total):
                    for step, ahead, first, slot in line_cases(at, nz, dst):
                        def send(ref, step=step, slot=slot):
                            links.make(ref, line.at[slot], line_n + slot, at.chip(step, 0)).start()

                        @pl.when(jnp.logical_and(ahead, first))
                        def _():
                            def one(i):
                                part_x[k, :, pl.ds(i, 128)] = total(i).astype(part_x.dtype)
                            strips(0, width, one)
                            send(part_x.at[k])

                        @pl.when(jnp.logical_and(ahead, jnp.logical_not(first)))
                        def _():
                            links.came(line.at[dst], line_n + dst)
                            def one(i):
                                line[dst, :, pl.ds(i, 128)] = (
                                    total(i) + line[dst, :, pl.ds(i, 128)].astype(f32)
                                ).astype(line.dtype)
                            strips(0, width, one)
                            send(line.at[dst])

                    def done():
                        for step, ahead, _, slot in line_cases(at, nz, dst):
                            @pl.when(ahead)
                            def _():
                                links.make(line.at[slot], line.at[slot], line_n + slot, at.chip(step, 0)).wait_send()
                    links.ends.append(done)

            else:

                def finish(total=total):
                    def one(i):
                        out[:, lanes(lo, i)] = total(i)
                    strips(0, width, one)
                    for step, slot in ((-1, at.z), (1, nz)):
                        @pl.when(at.has(step))
                        def _():
                            links.came(line.at[slot], line_n + slot)
                            def two(i):
                                out[:, lanes(lo, i)] += line[slot, :, pl.ds(i, 128)].astype(f32)
                            strips(0, width, two)

            plane(k, value, finish)
        return
    line_n = links.numbers(4 * (nz + 1))
    mine = (nz + 1) * 4
    for k in range(nz - 1):
        dst = dest[k]
        for p in (3, 1, 2, 0):

            def chain(starts, p=p, dst=dst):
                piece = dst * 4 + mod4(at.chip(0, p))
                here = dst * 4 + p
                for step, ahead, first, plane_slot in line_cases(at, nz, dst):
                    slot = plane_slot * 4 + p

                    def send(ref, step=step, slot=slot):
                        links.make(ref, line.at[slot], line_n + slot, at.chip(step, 0)).start()

                    if starts:
                        @pl.when(jnp.logical_and(ahead, first))
                        def _():
                            send(src.at[piece, :, pl.ds(lo, width)])
                        continue

                    @pl.when(jnp.logical_and(ahead, jnp.logical_not(first)))
                    def _():
                        links.came(line.at[here], line_n + here)
                        def one(i):
                            line[here, :, pl.ds(i, 128)] = (
                                src[piece, :, lanes(lo, i)].astype(f32)
                                + line[here, :, pl.ds(i, 128)].astype(f32)
                            ).astype(line.dtype)
                        strips(0, width, one)
                        send(line.at[here])

                if starts:
                    return

                def done():
                    for step, ahead, _, plane_slot in line_cases(at, nz, dst):
                        slot = plane_slot * 4 + p
                        @pl.when(ahead)
                        def _():
                            links.make(line.at[slot], line.at[slot], line_n + slot, at.chip(step, 0)).wait_send()
                links.ends.append(done)

            links.add(times("start", k), functools.partial(chain, True))
            links.add(times("chain", k), functools.partial(chain, False))

    def gathered():
        for p in (3, 1, 2, 0):
            piece = at.z * 4 + mod4(at.chip(0, p))
            low, high = at.z * 4 + p, nz * 4 + p
            for step, slot in ((-1, low), (1, high)):
                @pl.when(at.has(step))
                def _():
                    links.came(line.at[slot], line_n + slot)

            def one(i):
                own = src[piece, :, lanes(lo, i)].astype(f32)
                below = jnp.where(at.has(-1), line[low, :, pl.ds(i, 128)].astype(f32), 0.0)
                above = jnp.where(at.has(1), line[high, :, pl.ds(i, 128)].astype(f32), 0.0)
                line[mine + p, :, pl.ds(i, 128)] = (own + below + above).astype(line.dtype)
            strips(0, width, one)

    def value(p):
        return line.at[mine + p], 0

    def finish():
        def one(i):
            out[:, lanes(lo, i)] = (
                line[mine, :, pl.ds(i, 128)].astype(f32)
                + part_x[0, :, pl.ds(i, 128)].astype(f32)
                + part_y[0, :, pl.ds(i, 128)].astype(f32)
            )
        strips(0, width, one)

    links.add(times("gathered", 0), gathered)
    plane(0, value, finish)


def item_bufs(nz, arrays, items):
    scratch, sems = [], 0
    for array, lo, mid, hi, kind in items:
        rows, width = arrays[array][1], hi - lo
        planes = nz if kind == "zp" else 1
        lines = nz + 1 if kind == "zp" else 4 * (nz + 1) + 4
        scratch += [pltpu.VMEM((n, rows, width), jnp.bfloat16) for n in (planes, planes, planes, lines)]
        sems += 7 * nz + 1 if kind == "zp" else 4 * (nz + 1) + 6
    return scratch, sems


NT = (((1,), (1,)), ((), ()))


def dot_nt(a, b):
    return lax.dot_general(a, b, NT, preferred_element_type=jnp.float32)


def dot_nn(a, b):
    return jnp.dot(a, b, preferred_element_type=jnp.float32)


def fill_spread(st_ref, rows, rp):
    wide, width = st_ref.shape
    step = 128

    def body(t, carry):
        at = pl.multiple_of(t * step, step)
        i = at + lax.broadcasted_iota(jnp.int32, (step, 1), 0)
        block = i // rp
        inner = i - block * rp
        column = jnp.where(inner < rows, block * rows + inner, -1)
        n = lax.broadcasted_iota(jnp.int32, (step, width), 1)
        st_ref[pl.ds(at, step), :] = jnp.where(n == column, 1.0, 0.0).astype(st_ref.dtype)
        return carry

    lax.fori_loop(0, wide // step, body, 0)


def stream(hbm, buf, sem, fn):
    size = buf.shape[1]
    count = hbm.shape[0] // size

    def copy(i, slot):
        rows = pl.ds(pl.multiple_of(i * size, 16), size)
        return pltpu.make_async_copy(hbm.at[rows, :], buf.at[slot], sem.at[slot])

    copy(0, 0).start()

    def body(i, carry):
        slot = lax.rem(i, 2)

        @pl.when(i + 1 < count)
        def _():
            copy(i + 1, 1 - slot).start()

        copy(i, slot).wait()
        fn(i, buf.at[slot])
        return carry

    lax.fori_loop(0, count, body, 0)


def back_kernel(nz, items, sizes, names, *refs):
    f32, bf16 = jnp.float32, jnp.bfloat16
    r = dict(zip(names, refs))
    bufs = refs[len(names) :]
    own_heads, rows, rp, fh, fp, half, over = sizes
    hw = own_heads * HD
    at = Place(nz)
    links = Links(at, r["send_sem"], r["recv_sem"])
    table = far_first(nz)
    dest = [choose(at.z, [table[z][k] for z in range(nz)]) for k in range(nz)]
    at.meet(True)
    cot, st, small, small_d = r["cot"], r["st"], r["small"], r["small_d"]
    dub, dp, drc = r["dub"], r["dp"], r["drc"]
    length, wide = cot.shape
    hidden = dub.shape[1]
    width = st.shape[1]
    joined = dp.shape[1]
    shift = joined - drc.shape[1]

    def tall(name):
        rows_in = r[name].shape[0]
        return pltpu.make_async_copy(r[name], r["tall"].at[pl.ds(0, rows_in), :], r["sem_tall"].at[0])

    def setup():
        tall("gt").start()
        small[...] = jnp.zeros_like(small)
        small_d[...] = jnp.zeros_like(small_d)
        small_d[0:1, :] = jnp.sum(cot[...].astype(f32), axis=0, keepdims=True)
        tall("gt").wait()

    def grad_down(k):
        top = pl.multiple_of(dest[k] * 4 * fp, 16)
        step = wide // 3

        def body(i, carry):
            n = pl.ds(pl.multiple_of(i * step, 128), step)
            val = dot_nn(r["tall"][pl.ds(top, 4 * fp), :], cot[:, n]).reshape(4, fp, step)
            val = jnp.concatenate([val[:, : fp - 8], val[:, fp - 8 :] + small_d[:, n][None]], axis=1)
            r["g2"][pl.ds(dest[k] * 4, 4), :, n] = val.astype(bf16)
            return carry

        lax.fori_loop(0, 3, body, 0)

    def grad_hidden():
        def fn(i, w):
            n = pl.ds(pl.multiple_of(i * w.shape[0], 128), w.shape[0])
            val = dot_nt(cot[...], w[...]) * r["slope"][:, n].astype(f32)
            dub[:, n] = val.astype(bf16)
            small[6:7, n] = jnp.sum(val, axis=0, keepdims=True)

        stream(r["w_down"], r["buf_down"], r["sem_down"], fn)

    def grad_up(k):
        top = pl.multiple_of(dest[k] * 4 * rp, 16)
        step = 256

        def body(i, carry):
            n = pl.ds(pl.multiple_of(i * step, 128), step)
            val = dot_nn(r["a2t"][pl.ds(top, 4 * rp), :], dub[:, n])
            r["g1"][pl.ds(dest[k] * 4, 4), :, n] = val.reshape(4, rp, step).astype(bf16)
            return carry

        lax.fori_loop(0, hidden // step, body, 0)

    def swap(n, fn, weights):
        step = r["buf_up"].shape[1]
        slot = n % 2

        def part(i):
            cut = pl.ds(pl.multiple_of(i * step, 128), step)
            return links.make(
                r["send"].at[:, cut], r["came"].at[slot, :, cut], swap_n[n] + i, at.dp, True
            )

        def body(i, w):
            r["send"][:, pl.ds(pl.multiple_of(i * step, 128), step)] = fn(w)
            part(i).start()

        stream(weights, r["buf_up"], r["sem_up"], body)

        def finish(i, carry):
            part(i).wait()
            return carry

        lax.fori_loop(0, weights.shape[0] // step, finish, 0)

    swap_n = [links.numbers(wide // r["buf_up"].shape[1]) for _ in range(3)]

    def norm_grad(n, xh, rstd, gain, base, row, out_rows, store):
        step = out_rows

        def body(i, carry):
            at_i = pl.ds(pl.multiple_of(i * step, step), step)
            val = r["send"][at_i, :] + r["came"][n % 2, at_i, :]
            high = val.astype(bf16)
            low = (val - high.astype(f32)).astype(bf16)
            dh = dot_nn(high, st[...]) + dot_nn(low, st[...])
            x = xh[at_i, :]
            small[row : row + 1, 0:width] += jnp.sum(dh * x, axis=0, keepdims=True)
            small[row : row + 1, wide : wide + width] += jnp.sum(dh, axis=0, keepdims=True)
            dxh = dh * gain[...]
            inner = (
                dxh
                - jnp.mean(dxh, axis=-1, keepdims=True)
                - x * jnp.mean(dxh * x, axis=-1, keepdims=True)
            )
            store(i, at_i, base[at_i, :].astype(f32)[:, :width] + r["rstd"][at_i, rstd : rstd + 1] * inner)
            return carry

        lax.fori_loop(0, length // step, body, 0)

    def mid():
        fill_spread(st, rows, rp)
        swap(0, lambda w: dot_nt(dub[...], w[...]), r["w_up"])
        drc[...] = jnp.zeros_like(drc)

        def store(i, at_i, val):
            r["dres"][at_i, :] = val
            small[7:8, wide : wide + width] += jnp.sum(val, axis=0, keepdims=True)
            own = jnp.where(at.core == 0, val[:, :half], val[:, half:])
            drc[at_i, 3 * hw - shift : 3 * hw - shift + half] = own.astype(bf16)

        norm_grad(0, r["xh2"], 1, r["gain2"], cot, 5, 128, store)
        swap(1, lambda w: dot_nt(drc[...], w[:, shift:]), r["w_joined"])
        summed = (r["send"][...] + r["came"][1]).astype(bf16)

        for c in range(2):
            @pl.when(at.core == c)
            def _():
                first = 0 if c == 0 else width - hw
                val = dot_nn(summed, st[:, first : first + hw])
                if c == 1 and over:
                    lane = lax.broadcasted_iota(jnp.int32, val.shape, 1)
                    val = jnp.where(lane < over, 0.0, val)
                r["do"][...] = val.astype(bf16)

    def attention():
        allowed = may_see(r["seg_rows"][...], r["seg_cols"][...])
        dp[:, shift:] = jnp.zeros((length, joined - shift), bf16)
        rows_dim = (((0,), (0,)), ((), ()))
        for h in range(own_heads):
            here = [slice(i * hw + h * HD, i * hw + (h + 1) * HD) for i in range(3)]
            q, k, v, do = (r[n][:, here[0]] for n in ("q", "k", "v", "do"))
            probs = jnp.exp(head_scores(q, k, allowed) - r["lse"][:, h : h + 1])
            grad_probs = dot_nt(do, v)
            delta = jnp.sum(probs * grad_probs, axis=-1, keepdims=True)
            grad_scores = (probs * (grad_probs - delta) * HD ** (-0.5)).astype(bf16)
            dq = dot_nn(grad_scores, k)
            dk = lax.dot_general(grad_scores, q, rows_dim, preferred_element_type=f32)
            dv = lax.dot_general(probs.astype(bf16), do, rows_dim, preferred_element_type=f32)
            small[7:8, here[0]] = jnp.sum(dq, axis=0, keepdims=True)
            small[7:8, here[1]] = jnp.sum(dv, axis=0, keepdims=True)
            for at_h, val in zip(here, (dq, dk, dv)):
                dp[:, at_h] = val.astype(bf16)

    def last_norm():
        cut = up_to(3 * hw, 128)
        swap(2, lambda w: dot_nt(dp[:, :cut], w[:, :cut]), r["w_joined"])

        def store(i, at_i, val):
            @pl.when(i == at.core)
            def _():
                r["grad_input"][...] = val

        norm_grad(2, r["xh1"], 0, r["gain1"], r["dres"], 4, length // 2, store)

    def grad_joined(k):
        top = pl.multiple_of(dest[k] * 4 * rp, 16)

        def put(n, val):
            val = val.reshape(4, rp, val.shape[-1])
            val = jnp.concatenate([val[:, : rp - 8], val[:, rp - 8 :] + small[:, n][None]], axis=1)
            r["g0"][pl.ds(dest[k] * 4, 4), :, n] = val.astype(bf16)

        step = 256

        def body(i, carry):
            n = pl.ds(pl.multiple_of(i * step, 128), step)
            put(n, dot_nn(r["tall"][pl.ds(top, 4 * rp), :], dp[:, n]))
            return carry

        lax.fori_loop(0, shift // step, body, 0)

        def both(i, carry):
            n = pl.ds(pl.multiple_of(shift + i * step, 128), step)
            m = pl.ds(pl.multiple_of(i * step, 128), step)
            put(
                n,
                dot_nn(r["tall"][pl.ds(top, 4 * rp), :], dp[:, n])
                + dot_nn(r["tall"][pl.ds(wide + top, 4 * rp), :], drc[:, m]),
            )
            return carry

        lax.fori_loop(0, (joined - shift) // step, both, 0)

    h = rows // 2
    part_n = links.numbers(4)

    def trade(sums, base, n):
        high = up_to(h, 8)
        for c in range(2):
            @pl.when(at.core == c)
            def _():
                for e in range(2):
                    r["send"][base + e * high : base + e * high + h, :] = sums[
                        (1 - c) * h : (2 - c) * h, e * wide : (e + 1) * wide
                    ]
        cut = pl.ds(base, 2 * high)
        return links.make(r["send"].at[cut, :], r["came"].at[1, cut, :], part_n + n, at.dp, True)

    def halves(sums, base):
        high = up_to(h, 8)
        for c in range(2):
            def rows_by(s, lo, hi, c=c):
                if s == c:
                    return sums[c * h : (c + 1) * h, lo:hi]
                if hi <= wide or lo >= wide:
                    e = 0 if hi <= wide else 1
                    top = base + e * high
                    return r["came"][1, top : top + h, lo - e * wide : hi - e * wide]
                return jnp.concatenate([rows_by(s, lo, wide), rows_by(s, wide, hi)], axis=1)
            yield c, rows_by

    def fc_out():
        sums = r["sums1"]
        copy = trade(sums, 0, 0)
        copy.start()
        copy.wait()
        for c, rows_by in halves(sums, 0):
            @pl.when(at.core == c)
            def _():
                for j in range(hidden // fp):
                    for s in range(2):
                        lo, to = j * fp, (2 * j + s) * fh
                        cuts = [lo, lo + fh] if not lo < wide < lo + fh else [lo, wide, lo + fh]
                        for u, v in zip(cuts, cuts[1:]):
                            r["fc_grad"][:, to + u - lo : to + v - lo] = rows_by(s, u, v)

    def attn_out():
        sums = r["sums0"]
        base = 2 * up_to(h, 8)
        copy = trade(sums, base, 1)
        copy.start()
        r["row"][...] = sums[rp - 8 :, :]
        row_copy = links.make(r["row"], r["row_came"], part_n + 2, at.dp, True)
        row_copy.start()
        copy.wait()
        row_copy.wait()
        for c, rows_by in halves(sums, base):
            @pl.when(at.core == c)
            def _():
                for i in range(4):
                    size, skip = (hw, over) if i < 3 else (half, 0)
                    to, out = (i * width, r["attn_grad"]) if i < 3 else (0, r["out_grad"])
                    for s, lo in ((0, i * hw), (1, i * hw + skip)):
                        hi = i * hw + size
                        cuts = [lo, hi] if not lo < wide < hi else [lo, wide, hi]
                        for u, v in zip(cuts, cuts[1:]):
                            out[:, to + u - lo : to + v - lo] = rows_by(s, u, v)
                        to += hi - lo
                kinds = r["kinds"]
                kinds[...] = jnp.zeros_like(kinds)
                own = r["row"]
                low, high = (r["row"], r["row_came"]) if c == 0 else (r["row_came"], r["row"])
                for i, (line, first) in enumerate(((4, 0), (4, wide), (5, 0), (5, wide))):
                    kinds[i : i + 1, 0:width] = own[line : line + 1, first : first + width]
                for i in range(2):
                    kinds[4 + i : 5 + i, 0:hw] = low[7:8, i * hw : (i + 1) * hw]
                    kinds[4 + i : 5 + i, hw:width] = high[7:8, i * hw + over : (i + 1) * hw]
                kinds[6:7, 0:width] = own[7:8, wide : wide + width]
                kinds[7:8, 0:width] = r["sums2"][fp - 8 : fp - 7, 0:width]
        size = width // (2 * nz)
        device = at.dp * 2 + at.core
        kind, block = device // (2 * nz), lax.rem(device, 2 * nz)
        for i, place in enumerate((kind, 4 + kind)):
            line = jnp.broadcast_to(r["kinds"][pl.ds(place, 1), :], (8, wide))
            r["small_out"][8 * i : 8 * i + 8, :] = pltpu.roll(line, lax.rem(wide - block * size, wide), 1)
        line = jnp.broadcast_to(r["row"][6:7, :], (8, hidden))
        line = pltpu.roll(line, lax.rem(hidden - at.dp * fp, hidden), 1)
        r["small_out"][16:24, :] = line[:, :wide]

    links.add(-1.0, setup)
    for k in range(nz):
        links.add(1.0 * k, functools.partial(grad_down, k))
    links.add(4.9, lambda: tall("a1t_ot").start())
    links.add(49.9, lambda: tall("a1t_ot").wait())
    links.add(5.0, grad_hidden)
    for k in range(nz):
        links.add(10.0 + k, functools.partial(grad_up, k))
    links.add(20.0, mid)
    links.add(31.0, attention)
    links.add(33.0, last_norm)
    for k in range(nz):
        links.add(50.0 + k, functools.partial(grad_joined, k))
    grads, sums = ("g0", "g1", "g2"), ("sums0", "sums1", "sums2")
    for n, item in enumerate(items):
        scatter_item(
            links, nz, dest, item, r[grads[item[0]]], r[sums[item[0]]],
            bufs[4 * n : 4 * n + 4], functools.partial(step_time, nz, item),
        )
    links.add(65.0, fc_out)
    links.add(99.0, attn_out)
    links.run()


def step_time(nz, item, stage, k):
    array, _, _, _, kind = item
    spread = k / nz
    if kind == "pz":
        return {
            "start": (0.6, 18.6, 30.2),
            "chain": (30.3, 55.0, 56.0),
            "gathered": (61.0,),
            "first": (61.1,),
            "second": (72.0,),
            "third": (79.5,),
        }[stage][min(k, 2)]
    if array == 2:
        return {
            "first": (0.5, 1.5, 2.5, 3.5),
            "second": (9.0, 9.1, 9.2, 9.3),
            "third": (18.0, 30.1, 32.0, 41.0),
        }[stage][min(k, 3)]
    if array == 1:
        return {"first": 18.5, "second": 40.0, "third": 60.0}[stage] + (spread if stage != "third" else k / 8)
    return {"first": 50.5, "second": 70.0, "third": 80.0}[stage] + (k if stage == "first" else spread)


def back_call(nz, items, pieces, sizes, inputs, hbm, outs, collective_id):
    bf16, f32 = jnp.bfloat16, jnp.float32
    own_heads, rows, rp, fh, fp, half, over = sizes
    length, wide = inputs["cot"].shape
    width = inputs["xh1"].shape[1]
    hidden = inputs["slope"].shape[1]
    joined = hbm["w_joined"].shape[1]
    shift = 3 * own_heads * HD // 256 * 256
    bufs, sems = item_bufs(nz, pieces, items)
    sems += 3 * (wide // 384) + 4
    scratch = {
        "g0": pltpu.VMEM(pieces[0], bf16),
        "g1": pltpu.VMEM(pieces[1], bf16),
        "g2": pltpu.VMEM(pieces[2], bf16),
        "st": pltpu.VMEM((wide, width), bf16),
        "small": pltpu.VMEM((8, joined), f32),
        "small_d": pltpu.VMEM((8, wide), f32),
        "dub": pltpu.VMEM((length, hidden), bf16),
        "dp": pltpu.VMEM((length, joined), bf16),
        "drc": pltpu.VMEM((length, joined - shift), bf16),
        "do": pltpu.VMEM((length, own_heads * HD), bf16),
        "dres": pltpu.VMEM((length, width), f32),
        "send": pltpu.VMEM((length, wide), f32),
        "came": pltpu.VMEM((2, length, wide), f32),
        "sums0": pltpu.VMEM(pieces[0][1:], f32),
        "sums1": pltpu.VMEM(pieces[1][1:], f32),
        "tall": pltpu.VMEM((max(hidden, 2 * wide), length), bf16),
        "sem_tall": pltpu.SemaphoreType.DMA((1,)),
        "row": pltpu.VMEM((8, joined), f32),
        "row_came": pltpu.VMEM((8, joined), f32),
        "kinds": pltpu.VMEM((8, wide), f32),
        "buf_down": pltpu.VMEM((2, 256, wide), bf16),
        "buf_up": pltpu.VMEM((2, 384, joined), bf16),
        "sem_down": pltpu.SemaphoreType.DMA((2,)),
        "sem_up": pltpu.SemaphoreType.DMA((2,)),
        "send_sem": pltpu.SemaphoreType.DMA((sems,)),
        "recv_sem": pltpu.SemaphoreType.DMA((sems,)),
    }
    names = (*inputs, *hbm, *outs, *scratch)
    vmem, far = pl.BlockSpec(memory_space=pltpu.VMEM), pl.BlockSpec(memory_space=pl.ANY)
    return pl.pallas_call(
        functools.partial(back_kernel, nz, items, sizes, names),
        out_shape=list(outs.values()),
        in_specs=[vmem] * len(inputs) + [far] * len(hbm),
        out_specs=[vmem] * len(outs),
        scratch_shapes=[*scratch.values(), *bufs],
        compiler_params=pltpu.CompilerParams(
            collective_id=collective_id, has_side_effects=True, vmem_limit_bytes=63 * 2**20
        ),
    )(*inputs.values(), *hbm.values())


def gather_item(links, nz, item, src, out, times):
    at = links.at
    _, lo, mid, hi, kind = item
    part = {"all": pl.ds(lo, hi - lo), "a": pl.ds(lo, mid - lo), "b": pl.ds(mid, hi - mid)}
    base = links.numbers((2 * nz - 1) * 8)

    def number(stage, q, p):
        return base + (q + nz - 1) * 8 + stage * 4 + p

    def send(n, piece, to, cut="all", own=False):
        q, p = piece

        def make(ref=None):
            dst = out.at[at.chip(q, p), :, part[cut]]
            return links.make(dst if ref is None else ref, dst, n, at.chip(*to))

        make(src.at[:, part[cut]] if own else None).start()

        def done():
            flag = jnp.logical_and(at.has(q), at.has(to[0]))
            pl.when(flag)(lambda: make().wait_send())

        links.ends.append(done)

    def came(n, chip, cut="all"):
        links.came(out.at[chip, :, part[cut]], n)

    def along(q, p, own=False):
        for go in (1, -1) if q == 0 else ((-1,) if q > 0 else (1,)):
            if abs(q - go) < nz:
                @pl.when(at.has(go))
                def _():
                    send(number(0, q - go, p), (q, p), (go, 0), "all", own)

    def across(q, own=False):
        for p in (1, 2):
            send(number(1, q, p - 1), (q, 0), (0, p), "all", own)

    def relay(q, p):
        came(number(1, q, p - 1), at.chip(q, p))
        send(number(1, q, p + 1), (q, p), (0, 3 - p), "ab"[p - 1])

    def corner(q):
        for p in (1, 2):
            came(number(1, q, p + 1), at.chip(q, 3), "ab"[p - 1])

    def put(when, q, fn):
        links.add(when, fn if q == 0 else lambda: pl.when(at.has(q))(fn))

    def arrive(q, p=0):
        came(number(0, q, p), at.chip(q, p))
        along(q, p)

    if kind == "zp":
        for q in slots(nz):
            if q == 0:
                put(times("z", 0), 0, lambda: along(0, 0, True))
                put(times("plane", 0), 0, lambda: across(0, True))
            else:
                put(times("z", q), q, lambda q=q: arrive(q))
                put(times("plane", q), q, lambda q=q: across(q))
            put(times("relay", q), q, lambda q=q: [relay(q, p) for p in (1, 2)] and None)
            put(times("last", q), q, lambda q=q: corner(q))
        return
    put(times("plane", 0), 0, lambda: across(0, True))
    put(times("own", 0), 0, lambda: along(0, 0, True))
    for p in (1, 2):
        put(times("relay", 0), 0, lambda p=p: relay(0, p))
        put(times("own", 0), 0, lambda p=p: along(0, p))

    def diagonal():
        corner(0)
        along(0, 3)

    put(times("own", 0) + 0.01, 0, diagonal)
    for q in slots(nz)[1:]:
        for p in range(4):
            put(times("z", q) + 0.01 * p, q, lambda q=q, p=p: arrive(q, p))


def gather_time(item, stage, q):
    array, _, _, _, kind = item
    d = abs(q)
    if kind == "pz":
        return {"plane": 3.2, "relay": 4.8, "own": 5.6, "z": (0, 9.9, 11.9, 13.9)[d]}[stage]
    if array == 0:
        return {"z": 1.0 * d, "plane": 1.0 * d + 0.01, "relay": 1.6 + 1.4 * d, "last": 6.2}[stage]
    if array == 1:
        return {
            "z": (3.0, 4.2, 5.4, 6.6)[d], "plane": (5.0, 5.5, 6.7, 7.4)[d],
            "relay": (7.4, 8.4, 10.0, 11.0)[d], "last": 12.0,
        }[stage]
    return {
        "z": (6.8, 7.45, 8.45, 9.95)[d], "plane": (10.1, 10.2, 10.3, 10.4)[d],
        "relay": (12.3, 12.4, 12.5, 12.6)[d], "last": 14.5,
    }[stage]


def forward_kernel(nz, items, sizes, names, *refs):
    f32, bf16 = jnp.float32, jnp.bfloat16
    r = dict(zip(names, refs))
    own_heads, rows, rp, fh, fp, half, over, small = sizes
    hw = own_heads * HD
    at = Place(nz)
    links = Links(at, r["send_sem"], r["recv_sem"])
    acts, st, par = r["acts"], r["st"], r["par"]
    length, width = acts.shape
    wide = st.shape[0]
    hidden = r["gt"].shape[0]
    joined = r["w2d"].shape[1]
    shift = 3 * hw // 128 * 128
    skip = 3 * hw - shift
    chips = 4 * nz
    outs = ("attn_all", "fc_all", "proj_all")
    ins = ("attn_piece", "fc_piece", "proj_piece")
    own = [
        pltpu.make_async_copy(r[i], r[o].at[at.dp], r["sem"].at[n])
        for n, (i, o) in enumerate(zip(ins, outs))
    ]
    for copy in own:
        copy.start()
    at.meet(True)
    trade_n = links.numbers(3)

    def trade(n, mine, theirs):
        copy = links.make(mine, theirs, trade_n + n, at.dp, True)
        copy.start()
        copy.wait()

    def normalise(value, xh_ref, column):
        mu = jnp.mean(value, axis=-1, keepdims=True)
        centred = value - mu
        inv = lax.rsqrt(jnp.mean(centred * centred, axis=-1, keepdims=True) + NORM_EPS)
        return centred * inv, inv

    step = 64

    def by_rows(fn):
        def body(i, carry):
            fn(pl.ds(pl.multiple_of(i * step, step), step))
            return carry
        lax.fori_loop(0, length // step, body, 0)

    def prepare():
        fill_spread(st, rows, rp)

        def one(cut):
            xh, inv = normalise(acts[cut, :].astype(f32), None, 0)
            r["xh1"][cut, :] = xh
            r["rstd"][cut, 0:1] = inv

        by_rows(one)

    def load(name, n):
        own[n].wait()
        copy = pltpu.make_async_copy(r[name], r["w3d"], r["sem"].at[3])
        copy.start()
        copy.wait()

    def flatten():
        def body(i, carry):
            r["w2d"][pl.ds(pl.multiple_of(i * 2 * rp, 16), 2 * rp), :] = jnp.concatenate(
                [r["w3d"][2 * i], r["w3d"][2 * i + 1]], axis=0
            )
            return carry
        lax.fori_loop(0, chips // 2, body, 0)

    def parameters():
        par[...] = jnp.zeros_like(par)
        r["up_bias"][...] = jnp.zeros_like(r["up_bias"])
        for j in range(chips):
            block = r["w3d"][j, rp - 8 :, 0 : 3 * small].astype(f32)
            for c in range(2):
                line = block[rows - rp + 8 + c : rows - rp + 9 + c, :]
                device = 2 * j + c
                kind, lane = device // (2 * nz), device % (2 * nz) * small
                par[kind : kind + 1, lane : lane + small] = line[:, 0:small]
                par[4 + kind : 5 + kind, lane : lane + small] = line[:, small : 2 * small]

                @pl.when(at.core == c)
                def _():
                    r["up_bias"][0:1, j * fp : j * fp + fh] = line[:, 2 * small :]

    def spread_both(value, t_ref, first_row):
        t_ref[first_row : first_row + wide, :] = dot_nt(st[...], value).astype(bf16)
        r["spread"][...] = dot_nt(value, st[...]).astype(bf16)

    def query_step():
        load("attn_all", 0)
        parameters()
        flatten()

        def one(cut):
            a = r["xh1"][cut, :] * par[0:1, 0:width] + par[1:2, 0:width]
            r["act"][cut, :] = a.astype(bf16)

        by_rows(one)
        spread_both(r["act"][...], r["a1t_ot"], 0)
        size = 256

        def body(i, carry):
            n = pl.ds(pl.multiple_of(i * size, 128), size)
            r["p"][:, n] = dot_nn(r["spread"][...], r["w2d"][:, n])
            return carry

        lax.fori_loop(0, r["p"].shape[1] // size, body, 0)
        low = at.core == 0
        for i, (name, line) in enumerate((("q", 4), ("k", None), ("v", 5))):
            val = r["p"][:, i * hw : (i + 1) * hw]
            if line is not None:
                val = val + jnp.where(
                    low, par[line : line + 1, 0:hw], par[line : line + 1, width - hw : width]
                )
            r[name][...] = val.astype(bf16)

    def attention():
        allowed = may_see(r["seg_rows"][...], r["seg_cols"][...])
        attend(head_scores, own_heads, r["lse"], r["q"], r["k"], r["v"], r["o"], allowed)

    def mix():
        low = at.core == 0
        trade(0, r["o"], r["o_came"])
        first = jnp.where(low, r["o"][...], r["o_came"][...])
        second = jnp.where(low, r["o_came"][...], r["o"][...])
        if over:
            lane = lax.broadcasted_iota(jnp.int32, second.shape, 1)
            second = jnp.where(lane < over, jnp.zeros((), bf16), second)
        st_low, st_high = st[:, 0:hw], st[:, width - hw : width]
        r["a1t_ot"][wide : 2 * wide, :] = (dot_nt(st_low, first) + dot_nt(st_high, second)).astype(bf16)
        r["spread"][...] = (dot_nt(first, st_low) + dot_nt(second, st_high)).astype(bf16)
        r["mixed"][...] = dot_nn(r["spread"][...], r["w2d"][:, shift:])
        trade(1, r["mixed"], r["mixed_came"])
        r["resid"][:, 0:half] = jnp.where(
            low, r["mixed"][:, skip : skip + half], r["mixed_came"][:, skip : skip + half]
        )
        r["resid"][:, half : 2 * half] = jnp.where(
            low, r["mixed_came"][:, skip : skip + half], r["mixed"][:, skip : skip + half]
        )

        def one(cut):
            val = acts[cut, :].astype(f32) + r["resid"][cut, :] + par[6:7, 0:width]
            r["resid"][cut, :] = val
            xh, inv = normalise(val, None, 1)
            r["xh2"][cut, :] = xh
            r["rstd"][cut, 1:2] = inv
            r["act"][cut, :] = (xh * par[2:3, 0:width] + par[3:4, 0:width]).astype(bf16)

        by_rows(one)
        spread_both(r["act"][...], r["a2t"], 0)
        r["gains"][...] = par[...]

    def hidden_step():
        load("fc_all", 1)
        flatten()
        size = 256

        def body(i, carry):
            n = pl.ds(pl.multiple_of(i * size, 128), size)
            u = dot_nn(r["spread"][...], r["w2d"][:, n]) + r["up_bias"][0:1, n]
            value, slope = gelu_parts(u)
            r["g"][:, n] = value.astype(bf16)
            r["gt"][n, :] = value.T.astype(bf16)
            r["slope"][:, n] = (slope * r["real"][0:1, n]).astype(bf16)
            return carry

        lax.fori_loop(0, hidden // size, body, 0)

    def result_step():
        own[2].wait()
        copy = pltpu.make_async_copy(r["proj_all"], r["wd3"], r["sem"].at[3])
        copy.start()
        copy.wait()
        size, some = 384, chips // 2
        tokens = length // 2

        def body(i, carry):
            n = pl.ds(pl.multiple_of(i * size, 128), size)
            total = 0.0
            for e in range(2):
                w = r["wd3"][e * some : (e + 1) * some, :, n].reshape(some * fp, size)
                total = total + dot_nn(r["g"][:, e * some * fp : (e + 1) * some * fp], w)
            r["down"][:, n] = total
            return carry

        lax.fori_loop(0, wide // size, body, 0)
        theirs = pl.ds(pl.multiple_of((1 - at.core) * tokens, tokens), tokens)
        mine = pl.ds(pl.multiple_of(at.core * tokens, tokens), tokens)
        trade(2, r["down"].at[theirs, :], r["down_came"])
        r["result"][...] = (
            r["resid"][mine, :]
            + (r["down"][mine, 0:width] + r["down_came"][:, 0:width])
            + par[7:8, 0:width]
        ).astype(bf16)

    links.add(0.5, prepare)
    links.add(6.3, query_step)
    links.add(7.42, attention)
    links.add(8.42, mix)
    links.add(12.2, hidden_step)
    links.add(15.0, result_step)
    for item in items:
        gather_item(links, nz, item, r[ins[item[0]]], r[outs[item[0]]], functools.partial(gather_time, item))
    links.run()


def forward_call(nz, items, sizes, inputs, pieces, collective_id):
    bf16, f32 = jnp.bfloat16, jnp.float32
    own_heads, rows, rp, fh, fp, half, over, small = sizes
    hw = own_heads * HD
    length, width = inputs["acts"].shape
    attn, fc, proj = pieces.values()
    chips, joined, hidden, wide = 4 * nz, attn.shape[1], fc.shape[1], proj.shape[1]
    shape = jax.ShapeDtypeStruct
    landing = {
        n: shape((chips, *p.shape), bf16)
        for n, p in zip(("attn_all", "fc_all", "proj_all"), (attn, fc, proj))
    }
    outs = {
        "a1t_ot": shape((2 * wide, length), bf16),
        "a2t": shape((wide, length), bf16),
        "gt": shape((hidden, length), bf16),
        "slope": shape((length, hidden), bf16),
        "q": shape((length, hw), bf16),
        "k": shape((length, hw), bf16),
        "v": shape((length, hw), bf16),
        "lse": shape((length, 128), f32),
        "xh1": shape((length, width), f32),
        "xh2": shape((length, width), f32),
        "rstd": shape((length, 2), f32),
        "gains": shape((8, wide), f32),
        "result": shape((length // 2, width), bf16),
    }
    mixed = joined - 3 * hw // 128 * 128
    sems = len(items) * (2 * nz - 1) * 8 + 3
    scratch = {
        "w3d": pltpu.VMEM((chips, *attn.shape), bf16),
        "w2d": pltpu.VMEM((chips * rp, joined), bf16),
        "wd3": pltpu.VMEM((chips, *proj.shape), bf16),
        "st": pltpu.VMEM((wide, width), bf16),
        "par": pltpu.VMEM((8, wide), f32),
        "up_bias": pltpu.VMEM((8, hidden), f32),
        "act": pltpu.VMEM((length, width), bf16),
        "spread": pltpu.VMEM((length, wide), bf16),
        "p": pltpu.VMEM((length, up_to(3 * hw, 256)), f32),
        "o": pltpu.VMEM((length, hw), bf16),
        "o_came": pltpu.VMEM((length, hw), bf16),
        "mixed": pltpu.VMEM((length, mixed), f32),
        "mixed_came": pltpu.VMEM((length, mixed), f32),
        "resid": pltpu.VMEM((length, width), f32),
        "g": pltpu.VMEM((length, hidden), bf16),
        "down": pltpu.VMEM((length, wide), f32),
        "down_came": pltpu.VMEM((length // 2, wide), f32),
        "sem": pltpu.SemaphoreType.DMA((4,)),
        "send_sem": pltpu.SemaphoreType.DMA((sems,)),
        "recv_sem": pltpu.SemaphoreType.DMA((sems,)),
    }
    names = (*inputs, *pieces, *landing, *outs, *scratch)
    vmem, far = pl.BlockSpec(memory_space=pltpu.VMEM), pl.BlockSpec(memory_space=pl.ANY)
    got = pl.pallas_call(
        functools.partial(forward_kernel, nz, items, sizes, names),
        out_shape=[*landing.values(), *outs.values()],
        in_specs=[vmem] * len(inputs) + [far] * len(pieces),
        out_specs=[far] * len(landing) + [vmem] * len(outs),
        scratch_shapes=list(scratch.values()),
        compiler_params=pltpu.CompilerParams(
            collective_id=collective_id, has_side_effects=True, vmem_limit_bytes=60 * 2**20
        ),
    )(*inputs.values(), *pieces.values())
    return dict(zip((*landing, *outs), got))


def attend(scores_of, heads, lse_ref, q_ref, k_ref, v_ref, o_ref, allowed):
    for h in range(heads):
        at = slice(h * HD, (h + 1) * HD)
        scores = scores_of(q_ref[:, at], k_ref[:, at], allowed)
        top = jnp.max(scores, axis=-1, keepdims=True)
        total = top + jnp.log(jnp.sum(jnp.exp(scores - top), axis=-1, keepdims=True))
        probs = jnp.exp(scores - total).astype(jnp.bfloat16)
        lse_ref[:, h : h + 1] = total
        o_ref[:, at] = jnp.dot(
            probs, v_ref[:, at], preferred_element_type=jnp.float32
        ).astype(o_ref.dtype)


def head_scores(queries, key_rows, allowed):
    scores = lax.dot_general(
        queries, key_rows, (((1,), (1,)), ((), ())), preferred_element_type=jnp.float32
    ) * HD ** (-0.5)
    return jnp.where(allowed, scores, -1e30)


def may_see(seg_rows, seg_cols):
    length = seg_cols.shape[1]
    i = lax.broadcasted_iota(jnp.int32, (length, length), 0)
    j = lax.broadcasted_iota(jnp.int32, (length, length), 1)
    return (j <= i) & (seg_rows == seg_cols)


def up_to(value, step):
    return -(-value // step) * step


def per_device_grid(
    nz,
    layer_input,
    segments,
    w_attn,
    w_out,
    w_fc,
    w_proj,
    norm_params,
    lin_bias,
    fc_bias,
    out_cotangent,
):
    f32, bf16 = jnp.float32, jnp.bfloat16
    core = lax.axis_index("seq")
    low = core == 0
    chips = lax.axis_size("dp")
    tokens, width = layer_input.shape[1:]
    heads = width // HD
    own_heads = -(-heads // 2)
    hw = own_heads * HD
    over = 2 * hw - width
    half = width // 2
    small = norm_params.shape[0]
    h = w_out.shape[0] // width
    rows, rp = 2 * h, up_to(2 * h, 8)
    fh = w_proj.shape[0] // width
    fp = up_to(fh + 2, 16)
    hidden = chips * fp
    wide = up_to(width, 128)
    owide = up_to(3 * hw + half, 128) - 3 * hw

    def swap(value):
        return lax.ppermute(value, "seq", [(0, 1), (1, 0)])

    def pair(own, came):
        return jnp.where(low, own, came), jnp.where(low, came, own)

    def lanes_of(value, size):
        first, second = value[..., :size], value[..., value.shape[-1] - size :]
        return jnp.where(low, first, second), jnp.where(low, second, first)

    own_small = jnp.concatenate([norm_params, lin_bias, fc_bias])
    wa = w_attn.reshape(h, 3 * width)
    wo = w_out.reshape(h, width)
    wf = w_fc.reshape(h, chips, 2, fh)
    parts = [lanes_of(wa[:, i * width : (i + 1) * width], hw) for i in range(3)]
    parts.append(lanes_of(wo, half))
    gap = jnp.zeros((h, owide - half), bf16)
    attn_own, attn_other = (
        jnp.concatenate([p[i] for p in parts] + [gap], axis=1) for i in range(2)
    )
    fc_pads = ((0, 0), (0, 0), (0, fp - fh))
    fc_own, fc_other = (
        jnp.pad(jnp.where(low == first, wf[:, :, 0], wf[:, :, 1]), fc_pads).reshape(h, hidden)
        for first in (True, False)
    )
    attn_came, fc_came = swap(attn_other), swap(fc_other)
    acts_came = swap(jnp.stack([layer_input[0], out_cotangent[0]]))
    small_came = swap(own_small)
    row_pads = ((0, rp - rows), (0, 0))
    small_rows = jnp.pad(
        jnp.stack(pair(own_small, small_came)), ((0, rp - rows - 2), (0, 3 * hw + owide - 3 * small))
    )
    attn_piece = jnp.concatenate([*pair(attn_own, attn_came), small_rows])
    fc_piece = jnp.pad(jnp.concatenate(pair(fc_own, fc_came)), row_pads)
    proj_piece = jnp.pad(w_proj.reshape(fh, width), ((0, fp - fh), (0, wide - width)))
    acts = jnp.concatenate(pair(layer_input[0], acts_came[0]))
    cotangent = jnp.concatenate(pair(out_cotangent[0], acts_came[1]))
    cot_wide = jnp.pad(cotangent, ((0, 0), (0, wide - width)))
    seg_rows, seg_cols = segments.reshape(-1, 1), segments.reshape(1, -1)
    real = jnp.pad(jnp.ones((1, chips, fh), f32), ((0, 0), (0, 0), (0, fp - fh))).reshape(1, hidden)
    shape = jax.ShapeDtypeStruct
    third, joined = up_to(wide // 3, 128), attn_piece.shape[1]
    cuts = (
        (0, 0, up_to(joined // 2, 128), joined, "zp"),
        (1, 0, up_to(hidden // 2, 128), hidden, "zp"),
        (2, 2 * third, 2 * third + up_to((wide - 2 * third) // 2, 128), wide, "zp"),
        (2, 0, third, 2 * third, "pz"),
    )
    back_cuts = (
        (2, 0, up_to(wide // 2, 128), wide, "zp"),
        (1, 0, up_to(hidden // 2, 128), hidden, "zp"),
        (0, 0, up_to(joined // 2, 128), joined, "zp"),
    )
    sizes = (own_heads, rows, rp, fh, fp, half, over)
    done = forward_call(
        nz,
        cuts,
        (*sizes, small),
        {"acts": acts, "seg_rows": seg_rows, "seg_cols": seg_cols, "real": real},
        {"attn_piece": attn_piece, "fc_piece": fc_piece, "proj_piece": proj_piece},
        0,
    )
    attn_grad, out_grad, fc_grad, sums2, grad_input, small_out = back_call(
        nz,
        back_cuts,
        tuple(done[n].shape for n in ("attn_all", "fc_all", "proj_all")),
        sizes,
        {
            "slope": done["slope"],
            "cot": cot_wide,
            "a2t": done["a2t"],
            "q": done["q"],
            "k": done["k"],
            "v": done["v"],
            "seg_rows": seg_rows,
            "seg_cols": seg_cols,
            "lse": done["lse"],
            "xh1": done["xh1"],
            "xh2": done["xh2"],
            "rstd": done["rstd"],
            "gain1": done["gains"][0:1, :width],
            "gain2": done["gains"][2:3, :width],
        },
        {
            "gt": done["gt"],
            "a1t_ot": done["a1t_ot"],
            "w_down": done["proj_all"].reshape(hidden, wide),
            "w_up": done["fc_all"].reshape(-1, hidden),
            "w_joined": done["attn_all"].reshape(-1, joined),
        },
        {
            "attn_grad": shape((h, 3 * width), f32),
            "out_grad": shape((h, width), f32),
            "fc_grad": shape((h, 2 * chips * fh), f32),
            "sums2": shape(proj_piece.shape, f32),
            "grad_input": shape((tokens, width), f32),
            "small_out": shape((24, wide), f32),
        },
        1,
    )

    return (
        done["result"][None],
        grad_input[None],
        attn_grad.reshape(-1),
        out_grad.reshape(-1),
        fc_grad.reshape(-1),
        sums2[:fh, :width].reshape(-1),
        small_out[0, :small],
        small_out[8, :small],
        small_out[16, :small],
    )


def grid_height(mesh):
    shape = dict(mesh.shape)
    devices = mesh.devices.reshape(-1)
    if tuple(mesh.axis_names) != AXES or shape["seq"] != 2 or shape["dp"] % 4:
        return 0
    nz = shape["dp"] // 4
    base = getattr(devices[0], "coords", None)
    if base is None:
        return 0
    for n, device in enumerate(devices):
        chip = n // 2
        place = (chip % 2, chip // 2 % 2, chip // 4)
        if tuple(a - b for a, b in zip(device.coords, base)) != place:
            return 0
    return nz if 1 < nz <= 4 else 0


def solution(mesh):
    nz = grid_height(mesh)
    return jax.shard_map(
        functools.partial(per_device_grid, nz) if nz else per_device,
        mesh=mesh,
        in_specs=(
            P("dp", "seq", None),
            P("dp", None),
            P(("dp", "seq")),
            P(("dp", "seq")),
            P(("dp", "seq")),
            P(("dp", "seq")),
            P(("dp", "seq")),
            P(("dp", "seq")),
            P(("dp", "seq")),
            P("dp", "seq", None),
        ),
        out_specs=(
            P("dp", "seq", None),
            P("dp", "seq", None),
            P(("dp", "seq")),
            P(("dp", "seq")),
            P(("dp", "seq")),
            P(("dp", "seq")),
            P(("dp", "seq")),
            P(("dp", "seq")),
            P(("dp", "seq")),
        ),
        check_vma=False,
    )
```

```python
import functools

import jax
import jax.numpy as jnp
from jax import lax
from jax.experimental import pallas as pl
from jax.experimental.pallas import tpu as pltpu
from jax.sharding import PartitionSpec as P

HD = 64
FF = 4352


GELU_C = 0.7978845608028654
NORM_EPS = 1e-05


def gelu_parts(inputs):
    tanh_value = jnp.tanh(GELU_C * (inputs + 0.044715 * inputs * inputs * inputs))
    value = 0.5 * inputs * (1.0 + tanh_value)
    slope = 0.5 * (1.0 + tanh_value) + 0.5 * inputs * (1.0 - tanh_value * tanh_value) * GELU_C * (
        1.0 + 3.0 * 0.044715 * inputs * inputs
    )
    return (value, slope)


def layer_norm(inputs, gains, offsets):
    average = jnp.mean(inputs, axis=-1, keepdims=True)
    centred = inputs - average
    inv_std = lax.rsqrt(jnp.mean(centred * centred, axis=-1, keepdims=True) + NORM_EPS)
    x_hat = centred * inv_std
    return (x_hat * gains + offsets, x_hat, inv_std)


def norm_back(grad_out, x_hat, inv_std, gains):
    grad_hat = grad_out * gains
    grad_in = inv_std * (
        grad_hat
        - jnp.mean(grad_hat, axis=-1, keepdims=True)
        - x_hat * jnp.mean(grad_hat * x_hat, axis=-1, keepdims=True)
    )
    return (grad_in, jnp.sum(grad_out * x_hat, axis=0), jnp.sum(grad_out, axis=0))


def score_block(queries, key_rows, allowed):
    scores = jnp.einsum(
        "qhd,khd->hqk", queries, key_rows, preferred_element_type=jnp.float32
    ) * HD ** (-0.5)
    return jnp.where(allowed[None], scores, -1e30)


def outer_sum(left, right):
    return jnp.einsum("na,nb->ab", left, right, preferred_element_type=jnp.float32)


AXES = ("dp", "seq")


def shard_height(shard, columns):
    size = shard.shape[0]
    return size // columns if size % columns == 0 else 0


def tile_height(shard, columns):
    height = shard_height(shard, columns)
    return 0 if height % 8 else height


def padded(height):
    return -(-height // 8) * 8


def gather_rows(shard, columns, height, extra=None):
    if not height:
        return lax.all_gather(shard, AXES, axis=0, tiled=True).reshape(-1, columns)
    block = shard.reshape(height, columns)
    room = padded(height) - height
    if extra is not None:
        row = jnp.pad(extra, (0, columns - extra.shape[0]))[None]
        block = jnp.concatenate([block, row], axis=0)
        room -= 1
    if room:
        block = jnp.pad(block, ((0, room), (0, 0)))
    return lax.all_gather(block, AXES, axis=0, tiled=True)


def spread(acts, height):
    room = padded(height) - height
    if not room:
        return acts
    tokens = acts.shape[0]
    parts = acts.reshape(tokens, -1, height)
    return jnp.pad(parts, ((0, 0), (0, 0), (0, room))).reshape(tokens, -1)


def unspread(acts, height):
    if padded(height) == height:
        return acts
    tokens = acts.shape[0]
    return acts.reshape(tokens, -1, padded(height))[:, :, :height].reshape(tokens, -1)


def scatter_rows(blocks, height):
    count = lax.axis_size(AXES)
    sums = lax.psum_scatter(
        blocks.astype(jnp.bfloat16).reshape(count, -1, blocks.shape[-1]),
        AXES,
        scatter_dimension=0,
        tiled=True,
    )[0]
    return sums.astype(jnp.float32)


def scatter_flat(block, shard):
    count = lax.axis_size(AXES)
    return lax.psum_scatter(
        block.reshape(count, shard), AXES, scatter_dimension=0, tiled=True
    )[0]


def own_half_sum(terms, place, tokens):
    if lax.axis_size("seq") != 2:
        return lax.psum_scatter(
            terms.astype(jnp.bfloat16), "seq", scatter_dimension=0, tiled=True
        ).astype(jnp.float32)
    own = lax.dynamic_slice_in_dim(terms, place * tokens, tokens)
    other = lax.dynamic_slice_in_dim(terms, (1 - place) * tokens, tokens)
    came = lax.ppermute(other.astype(jnp.bfloat16), "seq", [(0, 1), (1, 0)])
    return own + came.astype(jnp.float32)


def per_device(
    layer_input,
    segments,
    w_attn,
    w_out,
    w_fc,
    w_proj,
    norm_params,
    lin_bias,
    fc_bias,
    out_cotangent,
):
    tokens = layer_input.shape[1]
    width = layer_input.shape[2]
    heads = width // HD
    place = lax.axis_index("seq")
    first = place * tokens
    small = norm_params.shape[0]
    height = shard_height(w_attn, 3 * width)
    height = height if shard_height(w_out, width) == height == shard_height(w_fc, FF) else 0
    down_height = tile_height(w_proj, width)
    own_small = jnp.concatenate([norm_params, lin_bias, fc_bias])
    packed = height and padded(height) > height and own_small.shape[0] <= width
    if height:
        lanes = -(-width // 128) * 128
        joined_shard = jnp.concatenate(
            [
                jnp.pad(w_out.reshape(height, width), ((0, 0), (0, lanes - width))),
                w_attn.reshape(height, 3 * width),
            ],
            axis=1,
        ).reshape(-1)
        joined_w = gather_rows(
            joined_shard, lanes + 3 * width, height, own_small if packed else None
        )
        w_o = joined_w[:, :width]
        w_qkv = joined_w[:, lanes:]
    else:
        w_qkv = gather_rows(w_attn, 3 * width, 0)
        w_o = gather_rows(w_out, width, 0)
    w_up = gather_rows(w_fc, FF, height)
    w_down = gather_rows(w_proj, width, down_height)
    if packed:
        smalls = w_o.reshape(-1, padded(height), width)[:, height, : 3 * small]
    else:
        smalls = lax.all_gather(own_small, AXES, axis=0)
    smalls = smalls.astype(jnp.float32).reshape(-1, 3, small)
    norms = smalls[:, 0].reshape(4, width)
    biases = smalls[:, 1].reshape(4, width)
    up_bias = smalls[:, 2].reshape(FF)
    inputs_f = layer_input[0].astype(jnp.float32)
    normed1, x_hat1, inv_std1 = layer_norm(inputs_f, norms[0], norms[1])
    act_in1 = normed1.astype(jnp.bfloat16)
    act_rows1 = spread(act_in1, height)
    projected = jnp.dot(act_rows1, w_qkv, preferred_element_type=jnp.float32)
    queries = (projected[:, :width] + biases[0]).astype(jnp.bfloat16)
    own_keys = projected[:, width : 2 * width].astype(jnp.bfloat16)
    own_values = (projected[:, 2 * width :] + biases[1]).astype(jnp.bfloat16)
    key_rows, value_rows = (
        lax.all_gather(own_keys, "seq", axis=0, tiled=True),
        lax.all_gather(own_values, "seq", axis=0, tiled=True),
    )
    key_count = key_rows.shape[0]
    key_pos = jnp.arange(key_count)
    query_pos = first + jnp.arange(tokens)
    padded_seg = jnp.concatenate([jnp.full((tokens,), -1, jnp.int32), segments[0]])
    key_seg = lax.dynamic_slice_in_dim(padded_seg, tokens, key_count)
    query_seg = lax.dynamic_slice_in_dim(segments[0], first, tokens)
    allowed = (key_pos[None, :] <= query_pos[:, None]) & (key_seg[None, :] == query_seg[:, None])
    q_heads = queries.reshape(tokens, heads, HD)
    k_heads = key_rows.reshape(key_count, heads, HD)
    v_heads = value_rows.reshape(key_count, heads, HD)
    scores = score_block(q_heads, k_heads, allowed)
    top_score = jnp.max(scores, axis=-1, keepdims=True)
    log_total = top_score + jnp.log(jnp.sum(jnp.exp(scores - top_score), axis=-1, keepdims=True))
    attn_probs = jnp.exp(scores - log_total).astype(jnp.bfloat16)
    attended = jnp.einsum("hqk,khd->qhd", attn_probs, v_heads, preferred_element_type=jnp.float32)
    attended = attended.reshape(tokens, width).astype(jnp.bfloat16)
    attended_rows = spread(attended, height)
    resid = inputs_f + jnp.dot(attended_rows, w_o, preferred_element_type=jnp.float32) + biases[2]
    normed2, x_hat2, inv_std2 = layer_norm(resid, norms[2], norms[3])
    act_in2 = normed2.astype(jnp.bfloat16)
    act_rows2 = spread(act_in2, height)
    hidden_pre = jnp.dot(act_rows2, w_up, preferred_element_type=jnp.float32) + up_bias
    hidden_act, hidden_slope = gelu_parts(hidden_pre)
    hidden_b = hidden_act.astype(jnp.bfloat16)
    hidden_rows = spread(hidden_b, down_height)
    result = (
        resid + jnp.dot(hidden_rows, w_down, preferred_element_type=jnp.float32) + biases[3]
    ).astype(jnp.bfloat16)
    cotangent = out_cotangent[0]
    grad_out = cotangent.astype(jnp.float32)
    grad_bp = jnp.sum(grad_out, axis=0)
    grad_hidden = (
        unspread(
            jnp.einsum("nd,fd->nf", cotangent, w_down, preferred_element_type=jnp.float32),
            down_height,
        )
        * hidden_slope
    )
    grad_hidden_b = grad_hidden.astype(jnp.bfloat16)
    grad_down = outer_sum(hidden_rows, cotangent)
    if down_height:
        grad_hidden_b, grad_down = lax.optimization_barrier(
            (grad_hidden_b, grad_down.astype(jnp.bfloat16))
        )
    grad_up_bias = jnp.sum(grad_hidden, axis=0)
    if down_height:
        proj_sums = scatter_rows(grad_down, down_height)[:down_height].reshape(-1)
    else:
        proj_sums = scatter_flat(grad_down, w_proj.shape[0])
    grad_up = outer_sum(act_rows2, grad_hidden_b)
    if height:
        fc_sums = scatter_rows(grad_up, height)[:height].reshape(-1)
    else:
        fc_sums = scatter_flat(grad_up, w_fc.shape[0])
    grad_norm2 = unspread(
        jnp.einsum("nf,df->nd", grad_hidden_b, w_up, preferred_element_type=jnp.float32), height
    )
    grad_resid_n, grad_g2, grad_b2 = norm_back(grad_norm2, x_hat2, inv_std2, norms[2])
    grad_resid = grad_out + grad_resid_n
    grad_resid_b = grad_resid.astype(jnp.bfloat16)
    grad_bo = jnp.sum(grad_resid, axis=0)
    grad_att = unspread(
        jnp.einsum(
            "ne,de->nd", grad_resid_b, w_o, preferred_element_type=jnp.float32
        ).astype(jnp.bfloat16),
        height,
    )
    grad_att_heads = grad_att.reshape(tokens, heads, HD)
    probs_full = jnp.exp(score_block(q_heads, k_heads, allowed) - log_total)
    probs_b = probs_full.astype(jnp.bfloat16)
    grad_probs = jnp.einsum(
        "qhd,khd->hqk", grad_att_heads, v_heads, preferred_element_type=jnp.float32
    )
    delta = jnp.sum(probs_full * grad_probs, axis=-1, keepdims=True)
    grad_scores = (probs_full * (grad_probs - delta) * HD ** (-0.5)).astype(jnp.bfloat16)
    grad_q = jnp.einsum(
        "hqk,khd->qhd", grad_scores, k_heads, preferred_element_type=jnp.float32
    ).reshape(tokens, width)
    grad_k_all = jnp.einsum(
        "hqk,qhd->khd", grad_scores, q_heads, preferred_element_type=jnp.float32
    ).reshape(key_count, width)
    grad_v_all = jnp.einsum(
        "hqk,qhd->khd", probs_b, grad_att_heads, preferred_element_type=jnp.float32
    ).reshape(key_count, width)
    grad_k = own_half_sum(grad_k_all, place, tokens)
    grad_v = own_half_sum(grad_v_all, place, tokens)
    grad_proj_b = jnp.concatenate([grad_q, grad_k, grad_v], axis=1).astype(jnp.bfloat16)
    grad_norm1 = unspread(
        jnp.einsum("ne,de->nd", grad_proj_b, w_qkv, preferred_element_type=jnp.float32), height
    )
    grad_in_n, grad_g1, grad_b1 = norm_back(grad_norm1, x_hat1, inv_std1, norms[0])
    grad_input = grad_resid + grad_in_n
    norm_terms = jnp.concatenate([grad_g1, grad_b1, grad_g2, grad_b2])
    bias_terms = jnp.concatenate(
        [jnp.sum(grad_q, axis=0), jnp.sum(grad_v, axis=0), grad_bo, grad_bp]
    )
    small_terms = jnp.concatenate(
        [term.reshape(-1, 1, small) for term in (norm_terms, bias_terms, grad_up_bias)], axis=1
    )
    grad_attn = outer_sum(act_rows1, grad_proj_b)
    grad_wo = outer_sum(attended_rows, grad_resid_b)
    if height:
        joined = jnp.concatenate(
            [grad_attn.astype(jnp.bfloat16), grad_wo.astype(jnp.bfloat16)], axis=1
        )
        if packed:
            blocks = joined.reshape(-1, padded(height), 4 * width)
            row = small_terms.astype(jnp.bfloat16).reshape(-1, 1, 3 * small)
            row = jnp.pad(row, ((0, 0), (height, padded(height) - height - 1), (0, width * 4 - 3 * small)))
            joined = (blocks + row).reshape(joined.shape)
        sums = scatter_rows(joined, height)
        qkv_sums = sums[:height, : 3 * width].reshape(-1)
        out_sums = sums[:height, 3 * width :].reshape(-1)
    else:
        qkv_sums = scatter_flat(grad_attn, w_attn.shape[0])
        out_sums = scatter_flat(grad_wo, w_out.shape[0])
    if packed:
        small_sums = sums[height, : 3 * small].reshape(3, small)
    else:
        small_sums = lax.psum_scatter(small_terms, AXES, scatter_dimension=0, tiled=True)[0]
    norm_sums, bias_sums, fcb_sums = small_sums[0], small_sums[1], small_sums[2]
    return (
        result[None],
        grad_input[None],
        qkv_sums,
        out_sums,
        fc_sums,
        proj_sums,
        norm_sums,
        bias_sums,
        fcb_sums,
    )


MESH = pl.DeviceIdType.MESH


class Place:
    def __init__(self, nz):
        self.nz = nz
        self.dp = lax.axis_index("dp")
        self.core = lax.axis_index("seq")
        self.x = lax.rem(self.dp, 2)
        self.y = lax.rem(self.dp // 2, 2)
        self.z = self.dp // 4
        fx, fy = 1 - 2 * self.x, 2 - 4 * self.y
        self.flip = (0, fx, fy, fx + fy)

    def chip(self, dz, p):
        return self.dp + 4 * dz + self.flip[p]

    def has(self, dz):
        return jnp.logical_and(self.z + dz >= 0, self.z + dz < self.nz)

    def meet(self, other=False):
        barrier = pltpu.get_barrier_semaphore()
        for dz, p in ((0, 1), (0, 2)):
            pl.semaphore_signal(
                barrier, inc=1, device_id=(self.chip(dz, p), self.core), device_id_type=MESH
            )
        for dz in (1, -1):
            @pl.when(self.has(dz))
            def _():
                pl.semaphore_signal(
                    barrier, inc=1, device_id=(self.chip(dz, 0), self.core), device_id_type=MESH
                )
        if other:
            pl.semaphore_signal(
                barrier, inc=1, device_id=(self.dp, 1 - self.core), device_id_type=MESH
            )
        near = 3 if other else 2
        pl.semaphore_wait(barrier, near + self.has(1).astype(jnp.int32) + self.has(-1).astype(jnp.int32))


def slots(nz):
    return [0] + [s * k for k in range(1, nz) for s in (1, -1)]


def strips(width, fn):
    size = next(n for n in (384, 256, 128) if width % n == 0)

    def body(i, carry):
        fn(pl.multiple_of(i * size, 128), size)
        return carry

    lax.fori_loop(0, width // size, body, 0)


def far_first(nz):
    return [sorted(range(nz), key=lambda t: -abs(t - z)) for z in range(nz)]


def choose(scalar, values):
    picked = jnp.int32(values[0])
    for i, v in enumerate(values[1:], 1):
        picked = jnp.where(scalar == i, jnp.int32(v), picked)
    return picked


class Links:
    def __init__(self, at, send_sem, recv_sem):
        self.at, self.send_sem, self.recv_sem = at, send_sem, recv_sem
        self.used, self.events, self.ends = 0, [], []

    def numbers(self, size):
        self.used += size
        return self.used - size

    def add(self, when, fn):
        self.events.append((when, len(self.events), fn))

    def make(self, src, dst, n, chip, other=False):
        core = 1 - self.at.core if other else self.at.core
        return pltpu.make_async_remote_copy(
            src_ref=src,
            dst_ref=dst,
            send_sem=self.send_sem.at[n],
            recv_sem=self.recv_sem.at[n],
            device_id=(chip, core),
            device_id_type=MESH,
        )

    def go(self, src, dst, n, chip, other=False):
        self.make(src, dst, n, chip, other).start()
        self.ends.append(lambda: self.make(src, dst, n, chip, other).wait_send())

    def came(self, dst, n):
        self.make(dst, dst, n, self.at.dp).wait_recv()

    def run(self):
        for _, _, fn in sorted(self.events, key=lambda e: e[:2]):
            fn()
        for fn in self.ends:
            fn()


def line_cases(at, nz, dst):
    for step in (1, -1):
        ahead = dst > at.z if step > 0 else dst < at.z
        first = at.z == (0 if step > 0 else nz - 1)
        slot = dst if step > 0 else jnp.where(dst == at.z - 1, nz, dst)
        yield step, ahead, first, slot


def scatter_item(links, nz, dest, item, src, out, bufs, times):
    f32 = jnp.float32
    at = links.at
    _, lo, mid, hi, kind = item
    width, na = hi - lo, mid - lo
    part_d, part_x, part_y, line = bufs
    landing = {1: part_x, 2: part_y}
    halves = {"a": (0, na), "b": (na, width - na)}

    def mod4(chip):
        return lax.rem(chip, 4)

    def lanes(start, i, n):
        return pl.ds(pl.multiple_of(start + i, 128), n)

    def plane(k, value, finish):
        base = links.numbers(6)

        def cut(ref, half, first=0):
            start, size = halves[half]
            return ref.at[:, pl.ds(first + start, size)]

        def first():
            for p, half, n in ((2, "a", 0), (1, "b", 1)):
                ref, start = value(3)
                links.go(cut(ref, half, start), cut(part_d.at[k], half), base + n, at.chip(0, p))
            for p, half, n in ((1, "b", 2), (2, "a", 3)):
                ref, start = value(p)
                links.go(cut(ref, half, start), cut(landing[p].at[k], half), base + n, at.chip(0, p))

        def second():
            for p, half, n, m in ((1, "a", 0, 4), (2, "b", 1, 5)):
                here = cut(part_d.at[k], half)
                links.came(here, base + n)
                ref, start = value(p)
                l, size = halves[half]

                def one(i, n, ref=ref, start=start, l=l):
                    part_d[k, :, lanes(l, i, n)] = (
                        part_d[k, :, lanes(l, i, n)].astype(f32) + ref[:, lanes(start + l, i, n)].astype(f32)
                    ).astype(part_d.dtype)

                strips(size, one)
                links.go(here, cut(landing[p].at[k], half), base + m, at.chip(0, p))

        def third():
            for p, half, n in ((1, "b", 2), (2, "a", 3), (1, "a", 4), (2, "b", 5)):
                links.came(cut(landing[p].at[k], half), base + n)
            finish()

        links.add(times("first", k), first)
        links.add(times("second", k), second)
        links.add(times("third", k), third)

    if kind == "zp":
        line_n = links.numbers(nz + 1)
        for k in range(nz):
            dst = dest[k]

            def value(p, dst=dst):
                return src.at[dst * 4 + mod4(at.chip(0, p))], lo

            def total(i, n, k=k, dst=dst):
                return (
                    src[dst * 4 + mod4(at.dp), :, lanes(lo, i, n)].astype(f32)
                    + part_x[k, :, pl.ds(i, n)].astype(f32)
                    + part_y[k, :, pl.ds(i, n)].astype(f32)
                )

            if k < nz - 1:

                def finish(k=k, dst=dst, total=total):
                    for step, ahead, first, slot in line_cases(at, nz, dst):
                        def send(ref, step=step, slot=slot):
                            links.make(ref, line.at[slot], line_n + slot, at.chip(step, 0)).start()

                        @pl.when(jnp.logical_and(ahead, first))
                        def _():
                            def one(i, n):
                                part_x[k, :, pl.ds(i, n)] = total(i, n).astype(part_x.dtype)
                            strips(width, one)
                            send(part_x.at[k])

                        @pl.when(jnp.logical_and(ahead, jnp.logical_not(first)))
                        def _():
                            links.came(line.at[dst], line_n + dst)
                            def one(i, n):
                                line[dst, :, pl.ds(i, n)] = (
                                    total(i, n) + line[dst, :, pl.ds(i, n)].astype(f32)
                                ).astype(line.dtype)
                            strips(width, one)
                            send(line.at[dst])

                    def done():
                        for step, ahead, _, slot in line_cases(at, nz, dst):
                            @pl.when(ahead)
                            def _():
                                links.make(line.at[slot], line.at[slot], line_n + slot, at.chip(step, 0)).wait_send()
                    links.ends.append(done)

            else:

                def finish(total=total):
                    def one(i, n):
                        out[:, lanes(lo, i, n)] = total(i, n)
                    strips(width, one)
                    for step, slot in ((-1, at.z), (1, nz)):
                        @pl.when(at.has(step))
                        def _():
                            links.came(line.at[slot], line_n + slot)
                            def two(i, n):
                                out[:, lanes(lo, i, n)] += line[slot, :, pl.ds(i, n)].astype(f32)
                            strips(width, two)

            plane(k, value, finish)
        return
    line_n = links.numbers(4 * (nz + 1))
    mine = (nz + 1) * 4
    for k in range(nz - 1):
        dst = dest[k]
        for p in (3, 1, 2, 0):

            def chain(starts, p=p, dst=dst):
                piece = dst * 4 + mod4(at.chip(0, p))
                here = dst * 4 + p
                for step, ahead, first, plane_slot in line_cases(at, nz, dst):
                    slot = plane_slot * 4 + p

                    def send(ref, step=step, slot=slot):
                        links.make(ref, line.at[slot], line_n + slot, at.chip(step, 0)).start()

                    if starts:
                        @pl.when(jnp.logical_and(ahead, first))
                        def _():
                            send(src.at[piece, :, pl.ds(lo, width)])
                        continue

                    @pl.when(jnp.logical_and(ahead, jnp.logical_not(first)))
                    def _():
                        links.came(line.at[here], line_n + here)
                        def one(i, n):
                            line[here, :, pl.ds(i, n)] = (
                                src[piece, :, lanes(lo, i, n)].astype(f32)
                                + line[here, :, pl.ds(i, n)].astype(f32)
                            ).astype(line.dtype)
                        strips(width, one)
                        send(line.at[here])

                if starts:
                    return

                def done():
                    for step, ahead, _, plane_slot in line_cases(at, nz, dst):
                        slot = plane_slot * 4 + p
                        @pl.when(ahead)
                        def _():
                            links.make(line.at[slot], line.at[slot], line_n + slot, at.chip(step, 0)).wait_send()
                links.ends.append(done)

            links.add(times("start", k), functools.partial(chain, True))
            links.add(times("chain", k), functools.partial(chain, False))

    def gathered():
        for p in (3, 1, 2, 0):
            piece = at.z * 4 + mod4(at.chip(0, p))
            low, high = at.z * 4 + p, nz * 4 + p
            for step, slot in ((-1, low), (1, high)):
                @pl.when(at.has(step))
                def _():
                    links.came(line.at[slot], line_n + slot)

            def one(i, n):
                own = src[piece, :, lanes(lo, i, n)].astype(f32)
                below = jnp.where(at.has(-1), line[low, :, pl.ds(i, n)].astype(f32), 0.0)
                above = jnp.where(at.has(1), line[high, :, pl.ds(i, n)].astype(f32), 0.0)
                line[mine + p, :, pl.ds(i, n)] = (own + below + above).astype(line.dtype)
            strips(width, one)

    def value(p):
        return line.at[mine + p], 0

    def finish():
        def one(i, n):
            out[:, lanes(lo, i, n)] = (
                line[mine, :, pl.ds(i, n)].astype(f32)
                + part_x[0, :, pl.ds(i, n)].astype(f32)
                + part_y[0, :, pl.ds(i, n)].astype(f32)
            )
        strips(width, one)

    links.add(times("gathered", 0), gathered)
    plane(0, value, finish)


def item_bufs(nz, arrays, items):
    scratch, sems = [], 0
    for array, lo, mid, hi, kind in items:
        rows, width = arrays[array][1], hi - lo
        planes = nz if kind == "zp" else 1
        lines = nz + 1 if kind == "zp" else 4 * (nz + 1) + 4
        scratch += [pltpu.VMEM((n, rows, width), jnp.bfloat16) for n in (planes, planes, planes, lines)]
        sems += 7 * nz + 1 if kind == "zp" else 4 * (nz + 1) + 6
    return scratch, sems


NT = (((1,), (1,)), ((), ()))


def dot_nt(a, b):
    return lax.dot_general(a, b, NT, preferred_element_type=jnp.float32)


def dot_nn(a, b):
    return jnp.dot(a, b, preferred_element_type=jnp.float32)


def fill_spread(st_ref, rows, rp):
    wide, width = st_ref.shape
    step = 128

    def body(t, carry):
        at = pl.multiple_of(t * step, step)
        i = at + lax.broadcasted_iota(jnp.int32, (step, 1), 0)
        block = i // rp
        inner = i - block * rp
        column = jnp.where(inner < rows, block * rows + inner, -1)
        n = lax.broadcasted_iota(jnp.int32, (step, width), 1)
        st_ref[pl.ds(at, step), :] = jnp.where(n == column, 1.0, 0.0).astype(st_ref.dtype)
        return carry

    lax.fori_loop(0, wide // step, body, 0)


def stream(hbm, buf, sem, fn):
    size = buf.shape[1]
    count = hbm.shape[0] // size

    def copy(i, slot):
        rows = pl.ds(pl.multiple_of(i * size, 16), size)
        return pltpu.make_async_copy(hbm.at[rows, :], buf.at[slot], sem.at[slot])

    copy(0, 0).start()

    def body(i, carry):
        slot = lax.rem(i, 2)

        @pl.when(i + 1 < count)
        def _():
            copy(i + 1, 1 - slot).start()

        copy(i, slot).wait()
        fn(i, buf.at[slot])
        return carry

    lax.fori_loop(0, count, body, 0)


LOADED = ("slope", "a2t", "q", "k", "v", "lse", "xh1", "xh2", "rstd", "gains")


def back_kernel(nz, items, sizes, names, *refs):
    f32, bf16 = jnp.float32, jnp.bfloat16
    r = dict(zip(names, refs))
    bufs = refs[len(names) :]
    own_heads, rows, rp, fh, fp, half, over = sizes
    hw = own_heads * HD
    at = Place(nz)
    links = Links(at, r["send_sem"], r["recv_sem"])
    table = far_first(nz)
    dest = [choose(at.z, [table[z][k] for z in range(nz)]) for k in range(nz)]
    at.meet(True)
    cot, st, small, small_d = r["cot"], r["st"], r["small"], r["small_d"]
    dub, dp, drc = r["dub"], r["dp"], r["drc"]
    length, wide = cot.shape
    hidden = dub.shape[1]
    width = st.shape[1]
    joined = dp.shape[1]
    shift = joined - drc.shape[1]

    def tall(name):
        rows_in = r[name].shape[0]
        return pltpu.make_async_copy(r[name], r["tall"].at[pl.ds(0, rows_in), :], r["sem_tall"].at[0])

    def fetch(n, name):
        return pltpu.make_async_copy(r["far_" + name], r[name], r["in_sem"].at[n])

    def fetched(names_):
        for name in names_:
            fetch(LOADED.index(name), name).wait()

    def setup():
        tall("gt").start()
        for n, name in enumerate(LOADED):
            fetch(n, name).start()
        small[...] = jnp.zeros_like(small)
        small_d[...] = jnp.zeros_like(small_d)
        small_d[0:1, :] = jnp.sum(cot[...].astype(f32), axis=0, keepdims=True)
        tall("gt").wait()

    def grad_down(k):
        top = pl.multiple_of(dest[k] * 4 * fp, 16)
        step = wide // 3

        def body(i, carry):
            n = pl.ds(pl.multiple_of(i * step, 128), step)
            val = dot_nn(r["tall"][pl.ds(top, 4 * fp), :], cot[:, n]).reshape(4, fp, step)
            val = jnp.concatenate([val[:, : fp - 8], val[:, fp - 8 :] + small_d[:, n][None]], axis=1)
            r["g2"][pl.ds(dest[k] * 4, 4), :, n] = val.astype(bf16)
            return carry

        lax.fori_loop(0, 3, body, 0)

    def grad_hidden():
        def fn(i, w):
            n = pl.ds(pl.multiple_of(i * w.shape[0], 128), w.shape[0])
            val = dot_nt(cot[...], w[...]) * r["slope"][:, n].astype(f32)
            dub[:, n] = val.astype(bf16)
            small[6:7, n] = jnp.sum(val, axis=0, keepdims=True)

        stream(r["w_down"], r["buf_down"], r["sem_down"], fn)

    def grad_up(k):
        top = pl.multiple_of(dest[k] * 4 * rp, 16)
        step = 256

        def body(i, carry):
            n = pl.ds(pl.multiple_of(i * step, 128), step)
            val = dot_nn(r["a2t"][pl.ds(top, 4 * rp), :], dub[:, n])
            r["g1"][pl.ds(dest[k] * 4, 4), :, n] = val.reshape(4, rp, step).astype(bf16)
            return carry

        lax.fori_loop(0, hidden // step, body, 0)

    def swap(n, fn, weights):
        step = r["buf_up"].shape[1]
        slot = n % 2

        def part(i):
            cut = pl.ds(pl.multiple_of(i * step, 128), step)
            return links.make(
                r["send"].at[:, cut], r["came"].at[slot, :, cut], swap_n[n] + i, at.dp, True
            )

        def body(i, w):
            r["send"][:, pl.ds(pl.multiple_of(i * step, 128), step)] = fn(w)
            part(i).start()

        stream(weights, r["buf_up"], r["sem_up"], body)

        def finish(i, carry):
            part(i).wait()
            return carry

        lax.fori_loop(0, weights.shape[0] // step, finish, 0)

    swap_n = [links.numbers(wide // r["buf_up"].shape[1]) for _ in range(3)]

    def norm_grad(n, xh, rstd, gain, base, row, out_rows, store):
        step = out_rows

        def body(i, carry):
            at_i = pl.ds(pl.multiple_of(i * step, step), step)
            val = r["send"][at_i, :] + r["came"][n % 2, at_i, :]
            high = val.astype(bf16)
            low = (val - high.astype(f32)).astype(bf16)
            dh = dot_nn(high, st[...]) + dot_nn(low, st[...])
            x = xh[at_i, :]
            small[row : row + 1, 0:width] += jnp.sum(dh * x, axis=0, keepdims=True)
            small[row : row + 1, wide : wide + width] += jnp.sum(dh, axis=0, keepdims=True)
            dxh = dh * r["gains"][gain : gain + 1, 0:width]
            inner = (
                dxh
                - jnp.mean(dxh, axis=-1, keepdims=True)
                - x * jnp.mean(dxh * x, axis=-1, keepdims=True)
            )
            store(i, at_i, base[at_i, :].astype(f32)[:, :width] + r["rstd"][at_i, rstd : rstd + 1] * inner)
            return carry

        lax.fori_loop(0, length // step, body, 0)

    def mid():
        fill_spread(st, rows, rp)
        swap(0, lambda w: dot_nt(dub[...], w[...]), r["w_up"])
        drc[...] = jnp.zeros_like(drc)

        def store(i, at_i, val):
            r["dres"][at_i, :] = val
            small[7:8, wide : wide + width] += jnp.sum(val, axis=0, keepdims=True)
            own = jnp.where(at.core == 0, val[:, :half], val[:, half:])
            drc[at_i, 3 * hw - shift : 3 * hw - shift + half] = own.astype(bf16)

        norm_grad(0, r["xh2"], 1, 2, cot, 5, 128, store)
        swap(1, lambda w: dot_nt(drc[...], w[:, shift:]), r["w_joined"])
        summed = (r["send"][...] + r["came"][1]).astype(bf16)

        for c in range(2):
            @pl.when(at.core == c)
            def _():
                first = 0 if c == 0 else width - hw
                val = dot_nn(summed, st[:, first : first + hw])
                if c == 1 and over:
                    lane = lax.broadcasted_iota(jnp.int32, val.shape, 1)
                    val = jnp.where(lane < over, 0.0, val)
                r["do"][...] = val.astype(bf16)

    def attention():
        allowed = may_see(r["seg_rows"][...], r["seg_cols"][...])
        dp[:, shift:] = jnp.zeros((length, joined - shift), bf16)
        rows_dim = (((0,), (0,)), ((), ()))
        for h in range(own_heads):
            here = [slice(i * hw + h * HD, i * hw + (h + 1) * HD) for i in range(3)]
            q, k, v, do = (r[n][:, here[0]] for n in ("q", "k", "v", "do"))
            probs = jnp.exp(head_scores(q, k, allowed) - r["lse"][:, h : h + 1])
            grad_probs = dot_nt(do, v)
            delta = jnp.sum(probs * grad_probs, axis=-1, keepdims=True)
            grad_scores = (probs * (grad_probs - delta) * HD ** (-0.5)).astype(bf16)
            dq = dot_nn(grad_scores, k)
            dk = lax.dot_general(grad_scores, q, rows_dim, preferred_element_type=f32)
            dv = lax.dot_general(probs.astype(bf16), do, rows_dim, preferred_element_type=f32)
            small[7:8, here[0]] = jnp.sum(dq, axis=0, keepdims=True)
            small[7:8, here[1]] = jnp.sum(dv, axis=0, keepdims=True)
            for at_h, val in zip(here, (dq, dk, dv)):
                dp[:, at_h] = val.astype(bf16)

    def last_norm():
        cut = up_to(3 * hw, 128)
        swap(2, lambda w: dot_nt(dp[:, :cut], w[:, :cut]), r["w_joined"])

        def store(i, at_i, val):
            @pl.when(i == at.core)
            def _():
                r["grad_input"][...] = val

        norm_grad(2, r["xh1"], 0, 0, r["dres"], 4, length // 2, store)

    def grad_joined(k):
        top = pl.multiple_of(dest[k] * 4 * rp, 16)

        def put(n, val):
            val = val.reshape(4, rp, val.shape[-1])
            val = jnp.concatenate([val[:, : rp - 8], val[:, rp - 8 :] + small[:, n][None]], axis=1)
            r["g0"][pl.ds(dest[k] * 4, 4), :, n] = val.astype(bf16)

        step = 256

        def body(i, carry):
            n = pl.ds(pl.multiple_of(i * step, 128), step)
            put(n, dot_nn(r["tall"][pl.ds(top, 4 * rp), :], dp[:, n]))
            return carry

        lax.fori_loop(0, shift // step, body, 0)

        def both(i, carry):
            n = pl.ds(pl.multiple_of(shift + i * step, 128), step)
            m = pl.ds(pl.multiple_of(i * step, 128), step)
            put(
                n,
                dot_nn(r["tall"][pl.ds(top, 4 * rp), :], dp[:, n])
                + dot_nn(r["tall"][pl.ds(wide + top, 4 * rp), :], drc[:, m]),
            )
            return carry

        lax.fori_loop(0, (joined - shift) // step, both, 0)

    h = rows // 2
    part_n = links.numbers(4)

    def trade(sums, base, n):
        high = up_to(h, 8)
        for c in range(2):
            @pl.when(at.core == c)
            def _():
                for e in range(2):
                    r["send"][base + e * high : base + e * high + h, :] = sums[
                        (1 - c) * h : (2 - c) * h, e * wide : (e + 1) * wide
                    ]
        cut = pl.ds(base, 2 * high)
        return links.make(r["send"].at[cut, :], r["came"].at[1, cut, :], part_n + n, at.dp, True)

    def halves(sums, base):
        high = up_to(h, 8)
        for c in range(2):
            def rows_by(s, lo, hi, c=c):
                if s == c:
                    return sums[c * h : (c + 1) * h, lo:hi]
                if hi <= wide or lo >= wide:
                    e = 0 if hi <= wide else 1
                    top = base + e * high
                    return r["came"][1, top : top + h, lo - e * wide : hi - e * wide]
                return jnp.concatenate([rows_by(s, lo, wide), rows_by(s, wide, hi)], axis=1)
            yield c, rows_by

    def fc_out():
        sums = r["sums1"]
        copy = trade(sums, 0, 0)
        copy.start()
        copy.wait()
        for c, rows_by in halves(sums, 0):
            @pl.when(at.core == c)
            def _():
                for j in range(hidden // fp):
                    for s in range(2):
                        lo, to = j * fp, (2 * j + s) * fh
                        cuts = [lo, lo + fh] if not lo < wide < lo + fh else [lo, wide, lo + fh]
                        for u, v in zip(cuts, cuts[1:]):
                            r["fc_grad"][:, to + u - lo : to + v - lo] = rows_by(s, u, v)

    def attn_out():
        sums = r["sums0"]
        base = 2 * up_to(h, 8)
        copy = trade(sums, base, 1)
        copy.start()
        r["row"][...] = sums[rp - 8 :, :]
        row_copy = links.make(r["row"], r["row_came"], part_n + 2, at.dp, True)
        row_copy.start()
        copy.wait()
        row_copy.wait()
        for c, rows_by in halves(sums, base):
            @pl.when(at.core == c)
            def _():
                for i in range(4):
                    size, skip = (hw, over) if i < 3 else (half, 0)
                    to, out = (i * width, r["attn_grad"]) if i < 3 else (0, r["out_grad"])
                    for s, lo in ((0, i * hw), (1, i * hw + skip)):
                        hi = i * hw + size
                        cuts = [lo, hi] if not lo < wide < hi else [lo, wide, hi]
                        for u, v in zip(cuts, cuts[1:]):
                            out[:, to + u - lo : to + v - lo] = rows_by(s, u, v)
                        to += hi - lo
                kinds = r["kinds"]
                kinds[...] = jnp.zeros_like(kinds)
                own = r["row"]
                low, high = (r["row"], r["row_came"]) if c == 0 else (r["row_came"], r["row"])
                for i, (line, first) in enumerate(((4, 0), (4, wide), (5, 0), (5, wide))):
                    kinds[i : i + 1, 0:width] = own[line : line + 1, first : first + width]
                for i in range(2):
                    kinds[4 + i : 5 + i, 0:hw] = low[7:8, i * hw : (i + 1) * hw]
                    kinds[4 + i : 5 + i, hw:width] = high[7:8, i * hw + over : (i + 1) * hw]
                kinds[6:7, 0:width] = own[7:8, wide : wide + width]
                kinds[7:8, 0:width] = r["sums2"][fp - 8 : fp - 7, 0:width]
        size = width // (2 * nz)
        device = at.dp * 2 + at.core
        kind, block = device // (2 * nz), lax.rem(device, 2 * nz)
        for i, place in enumerate((kind, 4 + kind)):
            line = jnp.broadcast_to(r["kinds"][pl.ds(place, 1), :], (8, wide))
            r["small_out"][8 * i : 8 * i + 8, :] = pltpu.roll(line, lax.rem(wide - block * size, wide), 1)
        line = jnp.broadcast_to(r["row"][6:7, :], (8, hidden))
        line = pltpu.roll(line, lax.rem(hidden - at.dp * fp, hidden), 1)
        r["small_out"][16:24, :] = line[:, :wide]

    links.add(-1.0, setup)
    for k in range(nz):
        links.add(1.0 * k, functools.partial(grad_down, k))
    links.add(4.95, lambda: fetched(LOADED[:1]))
    links.add(9.95, lambda: fetched(LOADED[1:2]))
    links.add(19.95, lambda: fetched(LOADED[2:]))
    links.add(4.9, lambda: tall("a1t_ot").start())
    links.add(49.9, lambda: tall("a1t_ot").wait())
    links.add(5.0, grad_hidden)
    for k in range(nz):
        links.add(10.0 + k, functools.partial(grad_up, k))
    links.add(20.0, mid)
    links.add(31.0, attention)
    links.add(33.0, last_norm)
    for k in range(nz):
        links.add(50.0 + k, functools.partial(grad_joined, k))
    grads, sums = ("g0", "g1", "g2"), ("sums0", "sums1", "sums2")
    for n, item in enumerate(items):
        scatter_item(
            links, nz, dest, item, r[grads[item[0]]], r[sums[item[0]]],
            bufs[4 * n : 4 * n + 4], functools.partial(step_time, nz, item),
        )
    links.add(55.1, fc_out)
    links.add(99.0, attn_out)
    links.run()


def step_time(nz, item, stage, k):
    array, _, _, _, kind = item
    k = min(k, 3)
    if kind == "pz":
        return {
            "start": (0.6, 10.6, 20.5),
            "chain": (20.6, 31.7, 33.9),
            "gathered": (51.95,),
            "first": (51.96,),
            "second": (54.45,),
            "third": (55.5,),
        }[stage][k]
    return {
        2: {
            "first": (0.5, 1.5, 9.2, 18.2),
            "second": (9.0, 18.0, 30.0, 32.0),
            "third": (18.1, 30.1, 32.1, 41.0),
        },
        1: {
            "first": (18.3, 18.4, 30.2, 32.3),
            "second": (32.2, 41.1, 51.6, 54.0),
            "third": (41.2, 51.7, 54.3, 54.6),
        },
        0: {
            "first": (50.5, 51.5, 54.2, 54.8),
            "second": (54.1, 54.5, 54.9, 56.0),
            "third": (54.7, 55.0, 56.1, 56.2),
        },
    }[array][stage][k]


def back_call(nz, items, pieces, sizes, inputs, hbm, outs, collective_id):
    bf16, f32 = jnp.bfloat16, jnp.float32
    own_heads, rows, rp, fh, fp, half, over = sizes
    length, wide = inputs["cot"].shape
    width = hbm["xh1"].shape[1]
    hidden = hbm["slope"].shape[1]
    joined = hbm["w_joined"].shape[1]
    shift = 3 * own_heads * HD // 256 * 256
    bufs, sems = item_bufs(nz, pieces, items)
    sems += 3 * (wide // 384) + 4
    scratch = {
        "g0": pltpu.VMEM(pieces[0], bf16),
        "g1": pltpu.VMEM(pieces[1], bf16),
        "g2": pltpu.VMEM(pieces[2], bf16),
        "st": pltpu.VMEM((wide, width), bf16),
        "small": pltpu.VMEM((8, joined), f32),
        "small_d": pltpu.VMEM((8, wide), f32),
        "dub": pltpu.VMEM((length, hidden), bf16),
        "dp": pltpu.VMEM((length, joined), bf16),
        "drc": pltpu.VMEM((length, joined - shift), bf16),
        "do": pltpu.VMEM((length, own_heads * HD), bf16),
        "dres": pltpu.VMEM((length, width), f32),
        "send": pltpu.VMEM((length, wide), f32),
        "came": pltpu.VMEM((2, length, wide), f32),
        "sums0": pltpu.VMEM(pieces[0][1:], f32),
        "sums1": pltpu.VMEM(pieces[1][1:], f32),
        "tall": pltpu.VMEM((max(hidden, 2 * wide), length), bf16),
        "sem_tall": pltpu.SemaphoreType.DMA((1,)),
        "row": pltpu.VMEM((8, joined), f32),
        "row_came": pltpu.VMEM((8, joined), f32),
        "kinds": pltpu.VMEM((8, wide), f32),
        "buf_down": pltpu.VMEM((2, 256, wide), bf16),
        "buf_up": pltpu.VMEM((2, 384, joined), bf16),
        "sem_down": pltpu.SemaphoreType.DMA((2,)),
        "sem_up": pltpu.SemaphoreType.DMA((2,)),
        "send_sem": pltpu.SemaphoreType.DMA((sems,)),
        "recv_sem": pltpu.SemaphoreType.DMA((sems,)),
    }
    for n in LOADED:
        scratch[n] = pltpu.VMEM(hbm[n].shape, hbm[n].dtype)
    scratch["in_sem"] = pltpu.SemaphoreType.DMA((len(LOADED),))
    far_names = ["far_" + n if n in LOADED else n for n in hbm]
    names = (*inputs, *far_names, *outs, *scratch)
    vmem, far = pl.BlockSpec(memory_space=pltpu.VMEM), pl.BlockSpec(memory_space=pl.ANY)
    return pl.pallas_call(
        functools.partial(back_kernel, nz, items, sizes, names),
        out_shape=list(outs.values()),
        in_specs=[vmem] * len(inputs) + [far] * len(hbm),
        out_specs=[vmem] * len(outs),
        scratch_shapes=[*scratch.values(), *bufs],
        compiler_params=pltpu.CompilerParams(
            collective_id=collective_id, has_side_effects=True, vmem_limit_bytes=63 * 2**20
        ),
    )(*inputs.values(), *hbm.values())


def gather_item(links, nz, item, src, out, times):
    at = links.at
    _, lo, mid, hi, kind = item
    part = {"all": pl.ds(lo, hi - lo), "a": pl.ds(lo, mid - lo), "b": pl.ds(mid, hi - mid)}
    base = links.numbers((2 * nz - 1) * 8)

    def number(stage, q, p):
        return base + (q + nz - 1) * 8 + stage * 4 + p

    def send(n, piece, to, cut="all", own=False):
        q, p = piece

        def make(ref=None):
            dst = out.at[at.chip(q, p), :, part[cut]]
            return links.make(dst if ref is None else ref, dst, n, at.chip(*to))

        make(src.at[:, part[cut]] if own else None).start()

        def done():
            flag = jnp.logical_and(at.has(q), at.has(to[0]))
            pl.when(flag)(lambda: make().wait_send())

        links.ends.append(done)

    def came(n, chip, cut="all"):
        links.came(out.at[chip, :, part[cut]], n)

    def along(q, p, own=False):
        for go in (1, -1) if q == 0 else ((-1,) if q > 0 else (1,)):
            if abs(q - go) < nz:
                @pl.when(at.has(go))
                def _():
                    send(number(0, q - go, p), (q, p), (go, 0), "all", own)

    def across(q, own=False):
        for p in (1, 2):
            send(number(1, q, p - 1), (q, 0), (0, p), "all", own)

    def relay(q, p):
        came(number(1, q, p - 1), at.chip(q, p))
        send(number(1, q, p + 1), (q, p), (0, 3 - p), "ab"[p - 1])

    def corner(q):
        for p in (1, 2):
            came(number(1, q, p + 1), at.chip(q, 3), "ab"[p - 1])

    def put(when, q, fn):
        links.add(when, fn if q == 0 else lambda: pl.when(at.has(q))(fn))

    def arrive(q, p=0):
        came(number(0, q, p), at.chip(q, p))
        along(q, p)

    if kind == "zp":
        for q in slots(nz):
            if q == 0:
                put(times("z", 0), 0, lambda: along(0, 0, True))
                put(times("plane", 0), 0, lambda: across(0, True))
            else:
                put(times("z", q), q, lambda q=q: arrive(q))
                put(times("plane", q), q, lambda q=q: across(q))
            put(times("relay", q), q, lambda q=q: [relay(q, p) for p in (1, 2)] and None)
            put(times("last", q), q, lambda q=q: corner(q))
        return
    put(times("plane", 0), 0, lambda: across(0, True))
    put(times("own", 0), 0, lambda: along(0, 0, True))
    for p in (1, 2):
        put(times("relay", 0), 0, lambda p=p: relay(0, p))
        put(times("own", 0), 0, lambda p=p: along(0, p))

    def diagonal():
        corner(0)
        along(0, 3)

    put(times("own", 0) + 0.01, 0, diagonal)
    for q in slots(nz)[1:]:
        for p in range(4):
            put(times("z", q) + 0.01 * p, q, lambda q=q, p=p: arrive(q, p))


def gather_time(item, stage, q):
    array, _, _, _, kind = item
    d = abs(q)
    if kind == "pz":
        return {"plane": 3.2, "relay": 4.8, "own": 5.6, "z": (0, 9.9, 11.9, 13.9)[d]}[stage]
    if array == 0:
        return {"z": 1.0 * d, "plane": 1.0 * d + 0.01, "relay": 1.6 + 1.4 * d, "last": 6.2}[stage]
    if array == 1:
        return {
            "z": (3.0, 4.2, 5.4, 6.6)[d], "plane": (5.0, 5.5, 6.7, 7.4)[d],
            "relay": (7.4, 8.4, 10.0, 11.0)[d], "last": 12.0,
        }[stage]
    return {
        "z": (6.8, 7.45, 8.45, 9.95)[d], "plane": (10.1, 10.2, 10.3, 10.4)[d],
        "relay": (12.3, 12.4, 12.5, 12.6)[d], "last": 14.5,
    }[stage]


EARLY = ("a1t_ot", "a2t", "q", "k", "v", "lse", "xh1", "xh2", "rstd", "gains")
LATER = ("gt", "slope")


def forward_kernel(nz, items, sizes, names, *refs):
    f32, bf16 = jnp.float32, jnp.bfloat16
    r = dict(zip(names, refs))
    own_heads, rows, rp, fh, fp, half, over, small = sizes
    hw = own_heads * HD
    at = Place(nz)
    links = Links(at, r["send_sem"], r["recv_sem"])
    acts, st, par = r["acts"], r["st"], r["par"]
    length, width = acts.shape
    wide = st.shape[0]
    hidden = r["gt"].shape[0]
    joined = r["w2d"].shape[1]
    shift = 3 * hw // 128 * 128
    skip = 3 * hw - shift
    chips = 4 * nz
    outs = ("attn_all", "fc_all", "proj_all")
    ins = ("attn_piece", "fc_piece", "proj_piece")
    own = [
        pltpu.make_async_copy(r[i], r[o].at[at.dp], r["sem"].at[n])
        for n, (i, o) in enumerate(zip(ins, outs))
    ]
    for copy in own:
        copy.start()
    at.meet(True)
    trade_n = links.numbers(3)

    def trade(n, mine, theirs):
        copy = links.make(mine, theirs, trade_n + n, at.dp, True)
        copy.start()
        copy.wait()

    def normalise(value, xh_ref, column):
        mu = jnp.mean(value, axis=-1, keepdims=True)
        centred = value - mu
        inv = lax.rsqrt(jnp.mean(centred * centred, axis=-1, keepdims=True) + NORM_EPS)
        return centred * inv, inv

    step = 64

    def by_rows(fn):
        def body(i, carry):
            fn(pl.ds(pl.multiple_of(i * step, step), step))
            return carry
        lax.fori_loop(0, length // step, body, 0)

    def prepare():
        fill_spread(st, rows, rp)

        def one(cut):
            xh, inv = normalise(acts[cut, :].astype(f32), None, 0)
            r["xh1"][cut, :] = xh
            r["rstd"][cut, 0:1] = inv

        by_rows(one)

    def load(name, n):
        own[n].wait()
        copy = pltpu.make_async_copy(r[name], r["w3d"], r["sem"].at[3])
        copy.start()
        copy.wait()

    def flatten():
        def body(i, carry):
            r["w2d"][pl.ds(pl.multiple_of(i * 2 * rp, 16), 2 * rp), :] = jnp.concatenate(
                [r["w3d"][2 * i], r["w3d"][2 * i + 1]], axis=0
            )
            return carry
        lax.fori_loop(0, chips // 2, body, 0)

    def parameters():
        par[...] = jnp.zeros_like(par)
        r["up_bias"][...] = jnp.zeros_like(r["up_bias"])
        for j in range(chips):
            block = r["w3d"][j, rp - 8 :, 0 : 3 * small].astype(f32)
            for c in range(2):
                line = block[rows - rp + 8 + c : rows - rp + 9 + c, :]
                device = 2 * j + c
                kind, lane = device // (2 * nz), device % (2 * nz) * small
                par[kind : kind + 1, lane : lane + small] = line[:, 0:small]
                par[4 + kind : 5 + kind, lane : lane + small] = line[:, small : 2 * small]

                @pl.when(at.core == c)
                def _():
                    r["up_bias"][0:1, j * fp : j * fp + fh] = line[:, 2 * small :]

    def spread_both(value, t_ref, first_row):
        t_ref[first_row : first_row + wide, :] = dot_nt(st[...], value).astype(bf16)
        r["spread"][...] = dot_nt(value, st[...]).astype(bf16)

    def query_step():
        load("attn_all", 0)
        parameters()
        flatten()

        def one(cut):
            a = r["xh1"][cut, :] * par[0:1, 0:width] + par[1:2, 0:width]
            r["act"][cut, :] = a.astype(bf16)

        by_rows(one)
        spread_both(r["act"][...], r["a1t_ot"], 0)
        size = 256

        def body(i, carry):
            n = pl.ds(pl.multiple_of(i * size, 128), size)
            r["p"][:, n] = dot_nn(r["spread"][...], r["w2d"][:, n])
            return carry

        lax.fori_loop(0, r["p"].shape[1] // size, body, 0)
        low = at.core == 0
        for i, (name, line) in enumerate((("q", 4), ("k", None), ("v", 5))):
            val = r["p"][:, i * hw : (i + 1) * hw]
            if line is not None:
                val = val + jnp.where(
                    low, par[line : line + 1, 0:hw], par[line : line + 1, width - hw : width]
                )
            r[name][...] = val.astype(bf16)

    def attention():
        allowed = may_see(r["seg_rows"][...], r["seg_cols"][...])
        attend(head_scores, own_heads, r["lse"], r["q"], r["k"], r["v"], r["o"], allowed)

    def mix():
        low = at.core == 0
        trade(0, r["o"], r["o_came"])
        first = jnp.where(low, r["o"][...], r["o_came"][...])
        second = jnp.where(low, r["o_came"][...], r["o"][...])
        if over:
            lane = lax.broadcasted_iota(jnp.int32, second.shape, 1)
            second = jnp.where(lane < over, jnp.zeros((), bf16), second)
        st_low, st_high = st[:, 0:hw], st[:, width - hw : width]
        r["a1t_ot"][wide : 2 * wide, :] = (dot_nt(st_low, first) + dot_nt(st_high, second)).astype(bf16)
        r["spread"][...] = (dot_nt(first, st_low) + dot_nt(second, st_high)).astype(bf16)
        r["mixed"][...] = dot_nn(r["spread"][...], r["w2d"][:, shift:])
        trade(1, r["mixed"], r["mixed_came"])
        r["resid"][:, 0:half] = jnp.where(
            low, r["mixed"][:, skip : skip + half], r["mixed_came"][:, skip : skip + half]
        )
        r["resid"][:, half : 2 * half] = jnp.where(
            low, r["mixed_came"][:, skip : skip + half], r["mixed"][:, skip : skip + half]
        )

        def one(cut):
            val = acts[cut, :].astype(f32) + r["resid"][cut, :] + par[6:7, 0:width]
            r["resid"][cut, :] = val
            xh, inv = normalise(val, None, 1)
            r["xh2"][cut, :] = xh
            r["rstd"][cut, 1:2] = inv
            r["act"][cut, :] = (xh * par[2:3, 0:width] + par[3:4, 0:width]).astype(bf16)

        by_rows(one)
        spread_both(r["act"][...], r["a2t"], 0)
        r["gains"][...] = par[...]

    def hidden_step():
        load("fc_all", 1)
        flatten()
        size = 256

        def body(i, carry):
            n = pl.ds(pl.multiple_of(i * size, 128), size)
            u = dot_nn(r["spread"][...], r["w2d"][:, n]) + r["up_bias"][0:1, n]
            value, slope = gelu_parts(u)
            r["g"][:, n] = value.astype(bf16)
            r["gt"][n, :] = value.T.astype(bf16)
            r["slope"][:, n] = (slope * r["real"][0:1, n]).astype(bf16)
            return carry

        lax.fori_loop(0, hidden // size, body, 0)

    def result_step():
        own[2].wait()
        copy = pltpu.make_async_copy(r["proj_all"], r["wd3"], r["sem"].at[3])
        copy.start()
        copy.wait()
        size, some = 384, chips // 2
        tokens = length // 2

        def body(i, carry):
            n = pl.ds(pl.multiple_of(i * size, 128), size)
            total = 0.0
            for e in range(2):
                w = r["wd3"][e * some : (e + 1) * some, :, n].reshape(some * fp, size)
                total = total + dot_nn(r["g"][:, e * some * fp : (e + 1) * some * fp], w)
            r["down"][:, n] = total
            return carry

        lax.fori_loop(0, wide // size, body, 0)
        theirs = pl.ds(pl.multiple_of((1 - at.core) * tokens, tokens), tokens)
        mine = pl.ds(pl.multiple_of(at.core * tokens, tokens), tokens)
        trade(2, r["down"].at[theirs, :], r["down_came"])
        r["result"][...] = (
            r["resid"][mine, :]
            + (r["down"][mine, 0:width] + r["down_came"][:, 0:width])
            + par[7:8, 0:width]
        ).astype(bf16)

    def leave(names_, first):
        for n, name in enumerate(names_):
            pltpu.make_async_copy(r[name], r["far_" + name], r["out_sem"].at[first + n]).start()

    def left():
        for n, name in enumerate((*EARLY, *LATER)):
            pltpu.make_async_copy(r[name], r["far_" + name], r["out_sem"].at[n]).wait()

    links.add(12.1, lambda: leave(EARLY, 0))
    links.add(12.21, lambda: leave(LATER, len(EARLY)))
    links.add(99.0, left)
    links.add(0.5, prepare)
    links.add(6.3, query_step)
    links.add(7.42, attention)
    links.add(8.42, mix)
    links.add(12.2, hidden_step)
    links.add(15.0, result_step)
    for item in items:
        gather_item(links, nz, item, r[ins[item[0]]], r[outs[item[0]]], functools.partial(gather_time, item))
    links.run()


def forward_call(nz, items, sizes, inputs, pieces, collective_id):
    bf16, f32 = jnp.bfloat16, jnp.float32
    own_heads, rows, rp, fh, fp, half, over, small = sizes
    hw = own_heads * HD
    length, width = inputs["acts"].shape
    attn, fc, proj = pieces.values()
    chips, joined, hidden, wide = 4 * nz, attn.shape[1], fc.shape[1], proj.shape[1]
    shape = jax.ShapeDtypeStruct
    landing = {
        n: shape((chips, *p.shape), bf16)
        for n, p in zip(("attn_all", "fc_all", "proj_all"), (attn, fc, proj))
    }
    outs = {
        "a1t_ot": shape((2 * wide, length), bf16),
        "a2t": shape((wide, length), bf16),
        "gt": shape((hidden, length), bf16),
        "slope": shape((length, hidden), bf16),
        "q": shape((length, hw), bf16),
        "k": shape((length, hw), bf16),
        "v": shape((length, hw), bf16),
        "lse": shape((length, 128), f32),
        "xh1": shape((length, width), f32),
        "xh2": shape((length, width), f32),
        "rstd": shape((length, 2), f32),
        "gains": shape((8, wide), f32),
        "result": shape((length // 2, width), bf16),
    }
    mixed = joined - 3 * hw // 128 * 128
    sems = len(items) * (2 * nz - 1) * 8 + 3
    scratch = {
        "w3d": pltpu.VMEM((chips, *attn.shape), bf16),
        "w2d": pltpu.VMEM((chips * rp, joined), bf16),
        "wd3": pltpu.VMEM((chips, *proj.shape), bf16),
        "st": pltpu.VMEM((wide, width), bf16),
        "par": pltpu.VMEM((8, wide), f32),
        "up_bias": pltpu.VMEM((8, hidden), f32),
        "act": pltpu.VMEM((length, width), bf16),
        "spread": pltpu.VMEM((length, wide), bf16),
        "p": pltpu.VMEM((length, up_to(3 * hw, 256)), f32),
        "o": pltpu.VMEM((length, hw), bf16),
        "o_came": pltpu.VMEM((length, hw), bf16),
        "mixed": pltpu.VMEM((length, mixed), f32),
        "mixed_came": pltpu.VMEM((length, mixed), f32),
        "resid": pltpu.VMEM((length, width), f32),
        "g": pltpu.VMEM((length, hidden), bf16),
        "down": pltpu.VMEM((length, wide), f32),
        "down_came": pltpu.VMEM((length // 2, wide), f32),
        "sem": pltpu.SemaphoreType.DMA((4,)),
        "send_sem": pltpu.SemaphoreType.DMA((sems,)),
        "recv_sem": pltpu.SemaphoreType.DMA((sems,)),
    }
    far_names = [n if n == "result" else "far_" + n for n in outs]
    for n in (*EARLY, *LATER):
        scratch[n] = pltpu.VMEM(outs[n].shape, outs[n].dtype)
    scratch["out_sem"] = pltpu.SemaphoreType.DMA((len(EARLY) + len(LATER),))
    names = (*inputs, *pieces, *landing, *far_names, *scratch)
    vmem, far = pl.BlockSpec(memory_space=pltpu.VMEM), pl.BlockSpec(memory_space=pl.ANY)
    got = pl.pallas_call(
        functools.partial(forward_kernel, nz, items, sizes, names),
        out_shape=[*landing.values(), *outs.values()],
        in_specs=[vmem] * len(inputs) + [far] * len(pieces),
        out_specs=[far] * len(landing) + [vmem if n == "result" else far for n in outs],
        scratch_shapes=list(scratch.values()),
        compiler_params=pltpu.CompilerParams(
            collective_id=collective_id, has_side_effects=True, vmem_limit_bytes=60 * 2**20
        ),
    )(*inputs.values(), *pieces.values())
    return dict(zip((*landing, *outs), got))


def attend(scores_of, heads, lse_ref, q_ref, k_ref, v_ref, o_ref, allowed):
    for h in range(heads):
        at = slice(h * HD, (h + 1) * HD)
        scores = scores_of(q_ref[:, at], k_ref[:, at], allowed)
        top = jnp.max(scores, axis=-1, keepdims=True)
        total = top + jnp.log(jnp.sum(jnp.exp(scores - top), axis=-1, keepdims=True))
        probs = jnp.exp(scores - total).astype(jnp.bfloat16)
        lse_ref[:, h : h + 1] = total
        o_ref[:, at] = jnp.dot(
            probs, v_ref[:, at], preferred_element_type=jnp.float32
        ).astype(o_ref.dtype)


def head_scores(queries, key_rows, allowed):
    scores = lax.dot_general(
        queries, key_rows, (((1,), (1,)), ((), ())), preferred_element_type=jnp.float32
    ) * HD ** (-0.5)
    return jnp.where(allowed, scores, -1e30)


def may_see(seg_rows, seg_cols):
    length = seg_cols.shape[1]
    i = lax.broadcasted_iota(jnp.int32, (length, length), 0)
    j = lax.broadcasted_iota(jnp.int32, (length, length), 1)
    return (j <= i) & (seg_rows == seg_cols)


def up_to(value, step):
    return -(-value // step) * step


def per_device_grid(
    nz,
    layer_input,
    segments,
    w_attn,
    w_out,
    w_fc,
    w_proj,
    norm_params,
    lin_bias,
    fc_bias,
    out_cotangent,
):
    f32, bf16 = jnp.float32, jnp.bfloat16
    core = lax.axis_index("seq")
    low = core == 0
    chips = lax.axis_size("dp")
    tokens, width = layer_input.shape[1:]
    heads = width // HD
    own_heads = -(-heads // 2)
    hw = own_heads * HD
    over = 2 * hw - width
    half = width // 2
    small = norm_params.shape[0]
    h = w_out.shape[0] // width
    rows, rp = 2 * h, up_to(2 * h, 8)
    fh = w_proj.shape[0] // width
    fp = up_to(fh + 2, 16)
    hidden = chips * fp
    wide = up_to(width, 128)
    owide = up_to(3 * hw + half, 128) - 3 * hw

    def swap(value):
        return lax.ppermute(value, "seq", [(0, 1), (1, 0)])

    def pair(own, came):
        return jnp.where(low, own, came), jnp.where(low, came, own)

    def lanes_of(value, size):
        first, second = value[..., :size], value[..., value.shape[-1] - size :]
        return jnp.where(low, first, second), jnp.where(low, second, first)

    own_small = jnp.concatenate([norm_params, lin_bias, fc_bias])
    wa = w_attn.reshape(h, 3 * width)
    wo = w_out.reshape(h, width)
    wf = w_fc.reshape(h, chips, 2, fh)
    parts = [lanes_of(wa[:, i * width : (i + 1) * width], hw) for i in range(3)]
    parts.append(lanes_of(wo, half))
    gap = jnp.zeros((h, owide - half), bf16)
    attn_own, attn_other = (
        jnp.concatenate([p[i] for p in parts] + [gap], axis=1) for i in range(2)
    )
    fc_pads = ((0, 0), (0, 0), (0, fp - fh))
    fc_own, fc_other = (
        jnp.pad(jnp.where(low == first, wf[:, :, 0], wf[:, :, 1]), fc_pads).reshape(h, hidden)
        for first in (True, False)
    )
    attn_came, fc_came = swap(attn_other), swap(fc_other)
    acts_came = swap(jnp.stack([layer_input[0], out_cotangent[0]]))
    small_came = swap(own_small)
    row_pads = ((0, rp - rows), (0, 0))
    small_rows = jnp.pad(
        jnp.stack(pair(own_small, small_came)), ((0, rp - rows - 2), (0, 3 * hw + owide - 3 * small))
    )
    attn_piece = jnp.concatenate([*pair(attn_own, attn_came), small_rows])
    fc_piece = jnp.pad(jnp.concatenate(pair(fc_own, fc_came)), row_pads)
    proj_piece = jnp.pad(w_proj.reshape(fh, width), ((0, fp - fh), (0, wide - width)))
    acts = jnp.concatenate(pair(layer_input[0], acts_came[0]))
    cotangent = jnp.concatenate(pair(out_cotangent[0], acts_came[1]))
    cot_wide = jnp.pad(cotangent, ((0, 0), (0, wide - width)))
    seg_rows, seg_cols = segments.reshape(-1, 1), segments.reshape(1, -1)
    real = jnp.pad(jnp.ones((1, chips, fh), f32), ((0, 0), (0, 0), (0, fp - fh))).reshape(1, hidden)
    shape = jax.ShapeDtypeStruct
    third, joined = up_to(wide // 3, 128), attn_piece.shape[1]
    cuts = (
        (0, 0, up_to(joined // 2, 128), joined, "zp"),
        (1, 0, up_to(hidden // 2, 128), hidden, "zp"),
        (2, 2 * third, 2 * third + up_to((wide - 2 * third) // 2, 128), wide, "zp"),
        (2, 0, third, 2 * third, "pz"),
    )
    back_cuts = (
        (2, 0, up_to(third // 2, 128), third, "pz"),
        (2, third, 2 * third, wide, "zp"),
        (1, 0, up_to(hidden // 2, 128), hidden, "zp"),
        (0, 0, up_to(joined // 2, 128), joined, "zp"),
    )
    sizes = (own_heads, rows, rp, fh, fp, half, over)
    done = forward_call(
        nz,
        cuts,
        (*sizes, small),
        {"acts": acts, "seg_rows": seg_rows, "seg_cols": seg_cols, "real": real},
        {"attn_piece": attn_piece, "fc_piece": fc_piece, "proj_piece": proj_piece},
        0,
    )
    attn_grad, out_grad, fc_grad, sums2, grad_input, small_out = back_call(
        nz,
        back_cuts,
        tuple(done[n].shape for n in ("attn_all", "fc_all", "proj_all")),
        sizes,
        {
            "cot": cot_wide,
            "seg_rows": seg_rows,
            "seg_cols": seg_cols,
        },
        {
            **{n: done[n] for n in LOADED},
            "gt": done["gt"],
            "a1t_ot": done["a1t_ot"],
            "w_down": done["proj_all"].reshape(hidden, wide),
            "w_up": done["fc_all"].reshape(-1, hidden),
            "w_joined": done["attn_all"].reshape(-1, joined),
        },
        {
            "attn_grad": shape((h, 3 * width), f32),
            "out_grad": shape((h, width), f32),
            "fc_grad": shape((h, 2 * chips * fh), f32),
            "sums2": shape(proj_piece.shape, f32),
            "grad_input": shape((tokens, width), f32),
            "small_out": shape((24, wide), f32),
        },
        1,
    )

    return (
        done["result"][None],
        grad_input[None],
        attn_grad.reshape(-1),
        out_grad.reshape(-1),
        fc_grad.reshape(-1),
        sums2[:fh, :width].reshape(-1),
        small_out[0, :small],
        small_out[8, :small],
        small_out[16, :small],
    )


def grid_height(mesh):
    shape = dict(mesh.shape)
    devices = mesh.devices.reshape(-1)
    if tuple(mesh.axis_names) != AXES or shape["seq"] != 2 or shape["dp"] % 4:
        return 0
    nz = shape["dp"] // 4
    base = getattr(devices[0], "coords", None)
    if base is None:
        return 0
    for n, device in enumerate(devices):
        chip = n // 2
        place = (chip % 2, chip // 2 % 2, chip // 4)
        if tuple(a - b for a, b in zip(device.coords, base)) != place:
            return 0
    return nz if 1 < nz <= 4 else 0


def solution(mesh):
    nz = grid_height(mesh)
    return jax.shard_map(
        functools.partial(per_device_grid, nz) if nz else per_device,
        mesh=mesh,
        in_specs=(
            P("dp", "seq", None),
            P("dp", None),
            P(("dp", "seq")),
            P(("dp", "seq")),
            P(("dp", "seq")),
            P(("dp", "seq")),
            P(("dp", "seq")),
            P(("dp", "seq")),
            P(("dp", "seq")),
            P("dp", "seq", None),
        ),
        out_specs=(
            P("dp", "seq", None),
            P("dp", "seq", None),
            P(("dp", "seq")),
            P(("dp", "seq")),
            P(("dp", "seq")),
            P(("dp", "seq")),
            P(("dp", "seq")),
            P(("dp", "seq")),
            P(("dp", "seq")),
        ),
        check_vma=False,
    )
```

```python
import functools

import jax
import jax.numpy as jnp
from jax import lax
from jax.experimental import pallas as pl
from jax.experimental.pallas import tpu as pltpu
from jax.sharding import PartitionSpec as P

HD = 64
FF = 4352


GELU_C = 0.7978845608028654
NORM_EPS = 1e-05


def gelu_parts(inputs):
    tanh_value = jnp.tanh(GELU_C * (inputs + 0.044715 * inputs * inputs * inputs))
    value = 0.5 * inputs * (1.0 + tanh_value)
    slope = 0.5 * (1.0 + tanh_value) + 0.5 * inputs * (1.0 - tanh_value * tanh_value) * GELU_C * (
        1.0 + 3.0 * 0.044715 * inputs * inputs
    )
    return (value, slope)


def layer_norm(inputs, gains, offsets):
    average = jnp.mean(inputs, axis=-1, keepdims=True)
    centred = inputs - average
    inv_std = lax.rsqrt(jnp.mean(centred * centred, axis=-1, keepdims=True) + NORM_EPS)
    x_hat = centred * inv_std
    return (x_hat * gains + offsets, x_hat, inv_std)


def norm_back(grad_out, x_hat, inv_std, gains):
    grad_hat = grad_out * gains
    grad_in = inv_std * (
        grad_hat
        - jnp.mean(grad_hat, axis=-1, keepdims=True)
        - x_hat * jnp.mean(grad_hat * x_hat, axis=-1, keepdims=True)
    )
    return (grad_in, jnp.sum(grad_out * x_hat, axis=0), jnp.sum(grad_out, axis=0))


def score_block(queries, key_rows, allowed):
    scores = jnp.einsum(
        "qhd,khd->hqk", queries, key_rows, preferred_element_type=jnp.float32
    ) * HD ** (-0.5)
    return jnp.where(allowed[None], scores, -1e30)


def outer_sum(left, right):
    return jnp.einsum("na,nb->ab", left, right, preferred_element_type=jnp.float32)


AXES = ("dp", "seq")


def shard_height(shard, columns):
    size = shard.shape[0]
    return size // columns if size % columns == 0 else 0


def tile_height(shard, columns):
    height = shard_height(shard, columns)
    return 0 if height % 8 else height


def padded(height):
    return -(-height // 8) * 8


def gather_rows(shard, columns, height, extra=None):
    if not height:
        return lax.all_gather(shard, AXES, axis=0, tiled=True).reshape(-1, columns)
    block = shard.reshape(height, columns)
    room = padded(height) - height
    if extra is not None:
        row = jnp.pad(extra, (0, columns - extra.shape[0]))[None]
        block = jnp.concatenate([block, row], axis=0)
        room -= 1
    if room:
        block = jnp.pad(block, ((0, room), (0, 0)))
    return lax.all_gather(block, AXES, axis=0, tiled=True)


def spread(acts, height):
    room = padded(height) - height
    if not room:
        return acts
    tokens = acts.shape[0]
    parts = acts.reshape(tokens, -1, height)
    return jnp.pad(parts, ((0, 0), (0, 0), (0, room))).reshape(tokens, -1)


def unspread(acts, height):
    if padded(height) == height:
        return acts
    tokens = acts.shape[0]
    return acts.reshape(tokens, -1, padded(height))[:, :, :height].reshape(tokens, -1)


def scatter_rows(blocks, height):
    count = lax.axis_size(AXES)
    sums = lax.psum_scatter(
        blocks.astype(jnp.bfloat16).reshape(count, -1, blocks.shape[-1]),
        AXES,
        scatter_dimension=0,
        tiled=True,
    )[0]
    return sums.astype(jnp.float32)


def scatter_flat(block, shard):
    count = lax.axis_size(AXES)
    return lax.psum_scatter(
        block.reshape(count, shard), AXES, scatter_dimension=0, tiled=True
    )[0]


def own_half_sum(terms, place, tokens):
    if lax.axis_size("seq") != 2:
        return lax.psum_scatter(
            terms.astype(jnp.bfloat16), "seq", scatter_dimension=0, tiled=True
        ).astype(jnp.float32)
    own = lax.dynamic_slice_in_dim(terms, place * tokens, tokens)
    other = lax.dynamic_slice_in_dim(terms, (1 - place) * tokens, tokens)
    came = lax.ppermute(other.astype(jnp.bfloat16), "seq", [(0, 1), (1, 0)])
    return own + came.astype(jnp.float32)


def per_device(
    layer_input,
    segments,
    w_attn,
    w_out,
    w_fc,
    w_proj,
    norm_params,
    lin_bias,
    fc_bias,
    out_cotangent,
):
    tokens = layer_input.shape[1]
    width = layer_input.shape[2]
    heads = width // HD
    place = lax.axis_index("seq")
    first = place * tokens
    small = norm_params.shape[0]
    height = shard_height(w_attn, 3 * width)
    height = height if shard_height(w_out, width) == height == shard_height(w_fc, FF) else 0
    down_height = tile_height(w_proj, width)
    own_small = jnp.concatenate([norm_params, lin_bias, fc_bias])
    packed = height and padded(height) > height and own_small.shape[0] <= width
    if height:
        lanes = -(-width // 128) * 128
        joined_shard = jnp.concatenate(
            [
                jnp.pad(w_out.reshape(height, width), ((0, 0), (0, lanes - width))),
                w_attn.reshape(height, 3 * width),
            ],
            axis=1,
        ).reshape(-1)
        joined_w = gather_rows(
            joined_shard, lanes + 3 * width, height, own_small if packed else None
        )
        w_o = joined_w[:, :width]
        w_qkv = joined_w[:, lanes:]
    else:
        w_qkv = gather_rows(w_attn, 3 * width, 0)
        w_o = gather_rows(w_out, width, 0)
    w_up = gather_rows(w_fc, FF, height)
    w_down = gather_rows(w_proj, width, down_height)
    if packed:
        smalls = w_o.reshape(-1, padded(height), width)[:, height, : 3 * small]
    else:
        smalls = lax.all_gather(own_small, AXES, axis=0)
    smalls = smalls.astype(jnp.float32).reshape(-1, 3, small)
    norms = smalls[:, 0].reshape(4, width)
    biases = smalls[:, 1].reshape(4, width)
    up_bias = smalls[:, 2].reshape(FF)
    inputs_f = layer_input[0].astype(jnp.float32)
    normed1, x_hat1, inv_std1 = layer_norm(inputs_f, norms[0], norms[1])
    act_in1 = normed1.astype(jnp.bfloat16)
    act_rows1 = spread(act_in1, height)
    projected = jnp.dot(act_rows1, w_qkv, preferred_element_type=jnp.float32)
    queries = (projected[:, :width] + biases[0]).astype(jnp.bfloat16)
    own_keys = projected[:, width : 2 * width].astype(jnp.bfloat16)
    own_values = (projected[:, 2 * width :] + biases[1]).astype(jnp.bfloat16)
    key_rows, value_rows = (
        lax.all_gather(own_keys, "seq", axis=0, tiled=True),
        lax.all_gather(own_values, "seq", axis=0, tiled=True),
    )
    key_count = key_rows.shape[0]
    key_pos = jnp.arange(key_count)
    query_pos = first + jnp.arange(tokens)
    padded_seg = jnp.concatenate([jnp.full((tokens,), -1, jnp.int32), segments[0]])
    key_seg = lax.dynamic_slice_in_dim(padded_seg, tokens, key_count)
    query_seg = lax.dynamic_slice_in_dim(segments[0], first, tokens)
    allowed = (key_pos[None, :] <= query_pos[:, None]) & (key_seg[None, :] == query_seg[:, None])
    q_heads = queries.reshape(tokens, heads, HD)
    k_heads = key_rows.reshape(key_count, heads, HD)
    v_heads = value_rows.reshape(key_count, heads, HD)
    scores = score_block(q_heads, k_heads, allowed)
    top_score = jnp.max(scores, axis=-1, keepdims=True)
    log_total = top_score + jnp.log(jnp.sum(jnp.exp(scores - top_score), axis=-1, keepdims=True))
    attn_probs = jnp.exp(scores - log_total).astype(jnp.bfloat16)
    attended = jnp.einsum("hqk,khd->qhd", attn_probs, v_heads, preferred_element_type=jnp.float32)
    attended = attended.reshape(tokens, width).astype(jnp.bfloat16)
    attended_rows = spread(attended, height)
    resid = inputs_f + jnp.dot(attended_rows, w_o, preferred_element_type=jnp.float32) + biases[2]
    normed2, x_hat2, inv_std2 = layer_norm(resid, norms[2], norms[3])
    act_in2 = normed2.astype(jnp.bfloat16)
    act_rows2 = spread(act_in2, height)
    hidden_pre = jnp.dot(act_rows2, w_up, preferred_element_type=jnp.float32) + up_bias
    hidden_act, hidden_slope = gelu_parts(hidden_pre)
    hidden_b = hidden_act.astype(jnp.bfloat16)
    hidden_rows = spread(hidden_b, down_height)
    result = (
        resid + jnp.dot(hidden_rows, w_down, preferred_element_type=jnp.float32) + biases[3]
    ).astype(jnp.bfloat16)
    cotangent = out_cotangent[0]
    grad_out = cotangent.astype(jnp.float32)
    grad_bp = jnp.sum(grad_out, axis=0)
    grad_hidden = (
        unspread(
            jnp.einsum("nd,fd->nf", cotangent, w_down, preferred_element_type=jnp.float32),
            down_height,
        )
        * hidden_slope
    )
    grad_hidden_b = grad_hidden.astype(jnp.bfloat16)
    grad_down = outer_sum(hidden_rows, cotangent)
    if down_height:
        grad_hidden_b, grad_down = lax.optimization_barrier(
            (grad_hidden_b, grad_down.astype(jnp.bfloat16))
        )
    grad_up_bias = jnp.sum(grad_hidden, axis=0)
    if down_height:
        proj_sums = scatter_rows(grad_down, down_height)[:down_height].reshape(-1)
    else:
        proj_sums = scatter_flat(grad_down, w_proj.shape[0])
    grad_up = outer_sum(act_rows2, grad_hidden_b)
    if height:
        fc_sums = scatter_rows(grad_up, height)[:height].reshape(-1)
    else:
        fc_sums = scatter_flat(grad_up, w_fc.shape[0])
    grad_norm2 = unspread(
        jnp.einsum("nf,df->nd", grad_hidden_b, w_up, preferred_element_type=jnp.float32), height
    )
    grad_resid_n, grad_g2, grad_b2 = norm_back(grad_norm2, x_hat2, inv_std2, norms[2])
    grad_resid = grad_out + grad_resid_n
    grad_resid_b = grad_resid.astype(jnp.bfloat16)
    grad_bo = jnp.sum(grad_resid, axis=0)
    grad_att = unspread(
        jnp.einsum(
            "ne,de->nd", grad_resid_b, w_o, preferred_element_type=jnp.float32
        ).astype(jnp.bfloat16),
        height,
    )
    grad_att_heads = grad_att.reshape(tokens, heads, HD)
    probs_full = jnp.exp(score_block(q_heads, k_heads, allowed) - log_total)
    probs_b = probs_full.astype(jnp.bfloat16)
    grad_probs = jnp.einsum(
        "qhd,khd->hqk", grad_att_heads, v_heads, preferred_element_type=jnp.float32
    )
    delta = jnp.sum(probs_full * grad_probs, axis=-1, keepdims=True)
    grad_scores = (probs_full * (grad_probs - delta) * HD ** (-0.5)).astype(jnp.bfloat16)
    grad_q = jnp.einsum(
        "hqk,khd->qhd", grad_scores, k_heads, preferred_element_type=jnp.float32
    ).reshape(tokens, width)
    grad_k_all = jnp.einsum(
        "hqk,qhd->khd", grad_scores, q_heads, preferred_element_type=jnp.float32
    ).reshape(key_count, width)
    grad_v_all = jnp.einsum(
        "hqk,qhd->khd", probs_b, grad_att_heads, preferred_element_type=jnp.float32
    ).reshape(key_count, width)
    grad_k = own_half_sum(grad_k_all, place, tokens)
    grad_v = own_half_sum(grad_v_all, place, tokens)
    grad_proj_b = jnp.concatenate([grad_q, grad_k, grad_v], axis=1).astype(jnp.bfloat16)
    grad_norm1 = unspread(
        jnp.einsum("ne,de->nd", grad_proj_b, w_qkv, preferred_element_type=jnp.float32), height
    )
    grad_in_n, grad_g1, grad_b1 = norm_back(grad_norm1, x_hat1, inv_std1, norms[0])
    grad_input = grad_resid + grad_in_n
    norm_terms = jnp.concatenate([grad_g1, grad_b1, grad_g2, grad_b2])
    bias_terms = jnp.concatenate(
        [jnp.sum(grad_q, axis=0), jnp.sum(grad_v, axis=0), grad_bo, grad_bp]
    )
    small_terms = jnp.concatenate(
        [term.reshape(-1, 1, small) for term in (norm_terms, bias_terms, grad_up_bias)], axis=1
    )
    grad_attn = outer_sum(act_rows1, grad_proj_b)
    grad_wo = outer_sum(attended_rows, grad_resid_b)
    if height:
        joined = jnp.concatenate(
            [grad_attn.astype(jnp.bfloat16), grad_wo.astype(jnp.bfloat16)], axis=1
        )
        if packed:
            blocks = joined.reshape(-1, padded(height), 4 * width)
            row = small_terms.astype(jnp.bfloat16).reshape(-1, 1, 3 * small)
            row = jnp.pad(row, ((0, 0), (height, padded(height) - height - 1), (0, width * 4 - 3 * small)))
            joined = (blocks + row).reshape(joined.shape)
        sums = scatter_rows(joined, height)
        qkv_sums = sums[:height, : 3 * width].reshape(-1)
        out_sums = sums[:height, 3 * width :].reshape(-1)
    else:
        qkv_sums = scatter_flat(grad_attn, w_attn.shape[0])
        out_sums = scatter_flat(grad_wo, w_out.shape[0])
    if packed:
        small_sums = sums[height, : 3 * small].reshape(3, small)
    else:
        small_sums = lax.psum_scatter(small_terms, AXES, scatter_dimension=0, tiled=True)[0]
    norm_sums, bias_sums, fcb_sums = small_sums[0], small_sums[1], small_sums[2]
    return (
        result[None],
        grad_input[None],
        qkv_sums,
        out_sums,
        fc_sums,
        proj_sums,
        norm_sums,
        bias_sums,
        fcb_sums,
    )


MESH = pl.DeviceIdType.MESH


class Place:
    def __init__(self, nz):
        self.nz = nz
        self.dp = lax.axis_index("dp")
        self.core = lax.axis_index("seq")
        self.x = lax.rem(self.dp, 2)
        self.y = lax.rem(self.dp // 2, 2)
        self.z = self.dp // 4
        fx, fy = 1 - 2 * self.x, 2 - 4 * self.y
        self.flip = (0, fx, fy, fx + fy)

    def chip(self, dz, p):
        return self.dp + 4 * dz + self.flip[p]

    def has(self, dz):
        return jnp.logical_and(self.z + dz >= 0, self.z + dz < self.nz)

    def meet(self, other=False):
        barrier = pltpu.get_barrier_semaphore()
        for dz, p in ((0, 1), (0, 2)):
            pl.semaphore_signal(
                barrier, inc=1, device_id=(self.chip(dz, p), self.core), device_id_type=MESH
            )
        for dz in (1, -1):
            @pl.when(self.has(dz))
            def _():
                pl.semaphore_signal(
                    barrier, inc=1, device_id=(self.chip(dz, 0), self.core), device_id_type=MESH
                )
        if other:
            pl.semaphore_signal(
                barrier, inc=1, device_id=(self.dp, 1 - self.core), device_id_type=MESH
            )
        near = 3 if other else 2
        pl.semaphore_wait(barrier, near + self.has(1).astype(jnp.int32) + self.has(-1).astype(jnp.int32))


def slots(nz):
    return [0] + [s * k for k in range(1, nz) for s in (1, -1)]


def strips(width, fn):
    size = next(n for n in (384, 256, 128) if width % n == 0)

    def body(i, carry):
        fn(pl.multiple_of(i * size, 128), size)
        return carry

    lax.fori_loop(0, width // size, body, 0)


def far_first(nz):
    return [sorted(range(nz), key=lambda t: -abs(t - z)) for z in range(nz)]


def choose(scalar, values):
    picked = jnp.int32(values[0])
    for i, v in enumerate(values[1:], 1):
        picked = jnp.where(scalar == i, jnp.int32(v), picked)
    return picked


class Links:
    def __init__(self, at, send_sem, recv_sem):
        self.at, self.send_sem, self.recv_sem = at, send_sem, recv_sem
        self.used, self.events, self.ends = 0, [], []

    def numbers(self, size):
        self.used += size
        return self.used - size

    def add(self, when, fn):
        self.events.append((when, len(self.events), fn))

    def make(self, src, dst, n, chip, other=False):
        core = 1 - self.at.core if other else self.at.core
        return pltpu.make_async_remote_copy(
            src_ref=src,
            dst_ref=dst,
            send_sem=self.send_sem.at[n],
            recv_sem=self.recv_sem.at[n],
            device_id=(chip, core),
            device_id_type=MESH,
        )

    def go(self, src, dst, n, chip, other=False):
        self.make(src, dst, n, chip, other).start()
        self.ends.append(lambda: self.make(src, dst, n, chip, other).wait_send())

    def came(self, dst, n):
        self.make(dst, dst, n, self.at.dp).wait_recv()

    def run(self):
        for _, _, fn in sorted(self.events, key=lambda e: e[:2]):
            fn()
        for fn in self.ends:
            fn()


def line_cases(at, nz, dst):
    for step in (1, -1):
        ahead = dst > at.z if step > 0 else dst < at.z
        first = at.z == (0 if step > 0 else nz - 1)
        slot = dst if step > 0 else jnp.where(dst == at.z - 1, nz, dst)
        yield step, ahead, first, slot


def scatter_item(links, nz, dest, item, src, out, bufs, times):
    f32 = jnp.float32
    at = links.at
    _, lo, mid, hi, kind = item
    width, na = hi - lo, mid - lo
    part_d, part_x, part_y, line = bufs
    landing = {1: part_x, 2: part_y}
    halves = {"a": (0, na), "b": (na, width - na)}

    def mod4(chip):
        return lax.rem(chip, 4)

    def lanes(start, i, n):
        return pl.ds(pl.multiple_of(start + i, 128), n)

    def plane(k, value, finish):
        base = links.numbers(6)

        def cut(ref, half, first=0):
            start, size = halves[half]
            return ref.at[:, pl.ds(first + start, size)]

        def first():
            for p, half, n in ((2, "a", 0), (1, "b", 1)):
                ref, start = value(3)
                links.go(cut(ref, half, start), cut(part_d.at[k], half), base + n, at.chip(0, p))
            for p, half, n in ((1, "b", 2), (2, "a", 3)):
                ref, start = value(p)
                links.go(cut(ref, half, start), cut(landing[p].at[k], half), base + n, at.chip(0, p))

        def second():
            for p, half, n, m in ((1, "a", 0, 4), (2, "b", 1, 5)):
                here = cut(part_d.at[k], half)
                links.came(here, base + n)
                ref, start = value(p)
                l, size = halves[half]

                def one(i, n, ref=ref, start=start, l=l):
                    part_d[k, :, lanes(l, i, n)] = (
                        part_d[k, :, lanes(l, i, n)].astype(f32) + ref[:, lanes(start + l, i, n)].astype(f32)
                    ).astype(part_d.dtype)

                strips(size, one)
                links.go(here, cut(landing[p].at[k], half), base + m, at.chip(0, p))

        def third():
            for p, half, n in ((1, "b", 2), (2, "a", 3), (1, "a", 4), (2, "b", 5)):
                links.came(cut(landing[p].at[k], half), base + n)
            finish()

        links.add(times("first", k), first)
        links.add(times("second", k), second)
        links.add(times("third", k), third)

    if kind == "zp":
        line_n = links.numbers(nz + 1)
        for k in range(nz):
            dst = dest[k]

            def value(p, dst=dst):
                return src.at[dst * 4 + mod4(at.chip(0, p))], lo

            def total(i, n, k=k, dst=dst):
                return (
                    src[dst * 4 + mod4(at.dp), :, lanes(lo, i, n)].astype(f32)
                    + part_x[k, :, pl.ds(i, n)].astype(f32)
                    + part_y[k, :, pl.ds(i, n)].astype(f32)
                )

            if k < nz - 1:

                def finish(k=k, dst=dst, total=total):
                    for step, ahead, first, slot in line_cases(at, nz, dst):
                        def send(ref, step=step, slot=slot):
                            links.make(ref, line.at[slot], line_n + slot, at.chip(step, 0)).start()

                        @pl.when(jnp.logical_and(ahead, first))
                        def _():
                            def one(i, n):
                                part_x[k, :, pl.ds(i, n)] = total(i, n).astype(part_x.dtype)
                            strips(width, one)
                            send(part_x.at[k])

                        @pl.when(jnp.logical_and(ahead, jnp.logical_not(first)))
                        def _():
                            links.came(line.at[dst], line_n + dst)
                            def one(i, n):
                                line[dst, :, pl.ds(i, n)] = (
                                    total(i, n) + line[dst, :, pl.ds(i, n)].astype(f32)
                                ).astype(line.dtype)
                            strips(width, one)
                            send(line.at[dst])

                    def done():
                        for step, ahead, _, slot in line_cases(at, nz, dst):
                            @pl.when(ahead)
                            def _():
                                links.make(line.at[slot], line.at[slot], line_n + slot, at.chip(step, 0)).wait_send()
                    links.ends.append(done)

            else:

                def finish(total=total):
                    def one(i, n):
                        out[:, lanes(lo, i, n)] = total(i, n)
                    strips(width, one)
                    for step, slot in ((-1, at.z), (1, nz)):
                        @pl.when(at.has(step))
                        def _():
                            links.came(line.at[slot], line_n + slot)
                            def two(i, n):
                                out[:, lanes(lo, i, n)] += line[slot, :, pl.ds(i, n)].astype(f32)
                            strips(width, two)

            plane(k, value, finish)
        return
    line_n = links.numbers(4 * (nz + 1))
    mine = (nz + 1) * 4
    for k in range(nz - 1):
        dst = dest[k]
        for p in (3, 1, 2, 0):

            def chain(starts, p=p, dst=dst):
                piece = dst * 4 + mod4(at.chip(0, p))
                here = dst * 4 + p
                for step, ahead, first, plane_slot in line_cases(at, nz, dst):
                    slot = plane_slot * 4 + p

                    def send(ref, step=step, slot=slot):
                        links.make(ref, line.at[slot], line_n + slot, at.chip(step, 0)).start()

                    if starts:
                        @pl.when(jnp.logical_and(ahead, first))
                        def _():
                            send(src.at[piece, :, pl.ds(lo, width)])
                        continue

                    @pl.when(jnp.logical_and(ahead, jnp.logical_not(first)))
                    def _():
                        links.came(line.at[here], line_n + here)
                        def one(i, n):
                            line[here, :, pl.ds(i, n)] = (
                                src[piece, :, lanes(lo, i, n)].astype(f32)
                                + line[here, :, pl.ds(i, n)].astype(f32)
                            ).astype(line.dtype)
                        strips(width, one)
                        send(line.at[here])

                if starts:
                    return

                def done():
                    for step, ahead, _, plane_slot in line_cases(at, nz, dst):
                        slot = plane_slot * 4 + p
                        @pl.when(ahead)
                        def _():
                            links.make(line.at[slot], line.at[slot], line_n + slot, at.chip(step, 0)).wait_send()
                links.ends.append(done)

            links.add(times("start", k), functools.partial(chain, True))
            links.add(times("chain", k), functools.partial(chain, False))

    def gathered():
        for p in (3, 1, 2, 0):
            piece = at.z * 4 + mod4(at.chip(0, p))
            low, high = at.z * 4 + p, nz * 4 + p
            for step, slot in ((-1, low), (1, high)):
                @pl.when(at.has(step))
                def _():
                    links.came(line.at[slot], line_n + slot)

            def one(i, n):
                own = src[piece, :, lanes(lo, i, n)].astype(f32)
                below = jnp.where(at.has(-1), line[low, :, pl.ds(i, n)].astype(f32), 0.0)
                above = jnp.where(at.has(1), line[high, :, pl.ds(i, n)].astype(f32), 0.0)
                line[mine + p, :, pl.ds(i, n)] = (own + below + above).astype(line.dtype)
            strips(width, one)

    def value(p):
        return line.at[mine + p], 0

    def finish():
        def one(i, n):
            out[:, lanes(lo, i, n)] = (
                line[mine, :, pl.ds(i, n)].astype(f32)
                + part_x[0, :, pl.ds(i, n)].astype(f32)
                + part_y[0, :, pl.ds(i, n)].astype(f32)
            )
        strips(width, one)

    links.add(times("gathered", 0), gathered)
    plane(0, value, finish)


def item_bufs(nz, arrays, items):
    scratch, sems = [], 0
    for array, lo, mid, hi, kind in items:
        rows, width = arrays[array][1], hi - lo
        planes = nz if kind == "zp" else 1
        lines = nz + 1 if kind == "zp" else 4 * (nz + 1) + 4
        scratch += [pltpu.VMEM((n, rows, width), jnp.bfloat16) for n in (planes, planes, planes, lines)]
        sems += 7 * nz + 1 if kind == "zp" else 4 * (nz + 1) + 6
    return scratch, sems


NT = (((1,), (1,)), ((), ()))


def dot_nt(a, b):
    return lax.dot_general(a, b, NT, preferred_element_type=jnp.float32)


def dot_nn(a, b):
    return jnp.dot(a, b, preferred_element_type=jnp.float32)


def fill_spread(st_ref, rows, rp):
    wide, width = st_ref.shape
    step = 128

    def body(t, carry):
        at = pl.multiple_of(t * step, step)
        i = at + lax.broadcasted_iota(jnp.int32, (step, 1), 0)
        block = i // rp
        inner = i - block * rp
        column = jnp.where(inner < rows, block * rows + inner, -1)
        n = lax.broadcasted_iota(jnp.int32, (step, width), 1)
        st_ref[pl.ds(at, step), :] = jnp.where(n == column, 1.0, 0.0).astype(st_ref.dtype)
        return carry

    lax.fori_loop(0, wide // step, body, 0)


def stream(hbm, buf, sem, fn):
    size = buf.shape[1]
    count = hbm.shape[0] // size

    def copy(i, slot):
        rows = pl.ds(pl.multiple_of(i * size, 16), size)
        return pltpu.make_async_copy(hbm.at[rows, :], buf.at[slot], sem.at[slot])

    copy(0, 0).start()

    def body(i, carry):
        slot = lax.rem(i, 2)

        @pl.when(i + 1 < count)
        def _():
            copy(i + 1, 1 - slot).start()

        copy(i, slot).wait()
        fn(i, buf.at[slot])
        return carry

    lax.fori_loop(0, count, body, 0)


LOADED = ("slope", "a2t", "q", "k", "v", "lse", "xh1", "xh2", "rstd", "gains")


def back_kernel(nz, items, sizes, names, *refs):
    f32, bf16 = jnp.float32, jnp.bfloat16
    r = dict(zip(names, refs))
    bufs = refs[len(names) :]
    own_heads, rows, rp, fh, fp, half, over = sizes
    hw = own_heads * HD
    at = Place(nz)
    links = Links(at, r["send_sem"], r["recv_sem"])
    table = far_first(nz)
    dest = [choose(at.z, [table[z][k] for z in range(nz)]) for k in range(nz)]
    at.meet(True)
    cot, st, small, small_d = r["cot"], r["st"], r["small"], r["small_d"]
    dub, dp, drc = r["dub"], r["dp"], r["drc"]
    length, wide = cot.shape
    hidden = dub.shape[1]
    width = st.shape[1]
    joined = dp.shape[1]
    shift = joined - drc.shape[1]

    def tall(name):
        rows_in = r[name].shape[0]
        return pltpu.make_async_copy(r[name], r["tall"].at[pl.ds(0, rows_in), :], r["sem_tall"].at[0])

    def fetch(n, name):
        return pltpu.make_async_copy(r["far_" + name], r[name], r["in_sem"].at[n])

    def fetched(names_):
        for name in names_:
            fetch(LOADED.index(name), name).wait()

    def setup():
        tall("gt").start()
        for n, name in enumerate(LOADED):
            fetch(n, name).start()
        small[...] = jnp.zeros_like(small)
        small_d[...] = jnp.zeros_like(small_d)
        small_d[0:1, :] = jnp.sum(cot[...].astype(f32), axis=0, keepdims=True)
        tall("gt").wait()

    def grad_down(k):
        top = pl.multiple_of(dest[k] * 4 * fp, 16)
        step = wide // 3

        def body(i, carry):
            n = pl.ds(pl.multiple_of(i * step, 128), step)
            val = dot_nn(r["tall"][pl.ds(top, 4 * fp), :], cot[:, n]).reshape(4, fp, step)
            val = jnp.concatenate([val[:, : fp - 8], val[:, fp - 8 :] + small_d[:, n][None]], axis=1)
            r["g2"][pl.ds(dest[k] * 4, 4), :, n] = val.astype(bf16)
            return carry

        lax.fori_loop(0, 3, body, 0)

    def grad_hidden():
        def fn(i, w):
            n = pl.ds(pl.multiple_of(i * w.shape[0], 128), w.shape[0])
            val = dot_nt(cot[...], w[...]) * r["slope"][:, n].astype(f32)
            dub[:, n] = val.astype(bf16)
            small[6:7, n] = jnp.sum(val, axis=0, keepdims=True)

        stream(r["w_down"], r["buf_down"], r["sem_down"], fn)

    def grad_up(k):
        top = pl.multiple_of(dest[k] * 4 * rp, 16)
        step = 256

        def body(i, carry):
            n = pl.ds(pl.multiple_of(i * step, 128), step)
            val = dot_nn(r["a2t"][pl.ds(top, 4 * rp), :], dub[:, n])
            r["g1"][pl.ds(dest[k] * 4, 4), :, n] = val.reshape(4, rp, step).astype(bf16)
            return carry

        lax.fori_loop(0, hidden // step, body, 0)

    def swap(n, fn, weights):
        step = r["buf_up"].shape[1]
        slot = n % 2

        def part(i):
            cut = pl.ds(pl.multiple_of(i * step, 128), step)
            return links.make(
                r["send"].at[:, cut], r["came"].at[slot, :, cut], swap_n[n] + i, at.dp, True
            )

        def body(i, w):
            r["send"][:, pl.ds(pl.multiple_of(i * step, 128), step)] = fn(w)
            part(i).start()

        stream(weights, r["buf_up"], r["sem_up"], body)

        def finish(i, carry):
            part(i).wait()
            return carry

        lax.fori_loop(0, weights.shape[0] // step, finish, 0)

    swap_n = [links.numbers(wide // r["buf_up"].shape[1]) for _ in range(3)]

    def norm_grad(n, xh, rstd, gain, base, row, out_rows, store):
        step = out_rows

        def body(i, carry):
            at_i = pl.ds(pl.multiple_of(i * step, step), step)
            val = r["send"][at_i, :] + r["came"][n % 2, at_i, :]
            high = val.astype(bf16)
            low = (val - high.astype(f32)).astype(bf16)
            dh = dot_nn(high, st[...]) + dot_nn(low, st[...])
            x = xh[at_i, :]
            small[row : row + 1, 0:width] += jnp.sum(dh * x, axis=0, keepdims=True)
            small[row : row + 1, wide : wide + width] += jnp.sum(dh, axis=0, keepdims=True)
            dxh = dh * r["gains"][gain : gain + 1, 0:width]
            inner = (
                dxh
                - jnp.mean(dxh, axis=-1, keepdims=True)
                - x * jnp.mean(dxh * x, axis=-1, keepdims=True)
            )
            store(i, at_i, base[at_i, :].astype(f32)[:, :width] + r["rstd"][at_i, rstd : rstd + 1] * inner)
            return carry

        lax.fori_loop(0, length // step, body, 0)

    def mid():
        fill_spread(st, rows, rp)
        swap(0, lambda w: dot_nt(dub[...], w[...]), r["w_up"])
        drc[...] = jnp.zeros_like(drc)

        def store(i, at_i, val):
            r["dres"][at_i, :] = val
            small[7:8, wide : wide + width] += jnp.sum(val, axis=0, keepdims=True)
            own = jnp.where(at.core == 0, val[:, :half], val[:, half:])
            drc[at_i, 3 * hw - shift : 3 * hw - shift + half] = own.astype(bf16)

        norm_grad(0, r["xh2"], 1, 2, cot, 5, 128, store)
        swap(1, lambda w: dot_nt(drc[...], w[:, shift:]), r["w_joined"])
        summed = (r["send"][...] + r["came"][1]).astype(bf16)

        for c in range(2):
            @pl.when(at.core == c)
            def _():
                first = 0 if c == 0 else width - hw
                val = dot_nn(summed, st[:, first : first + hw])
                if c == 1 and over:
                    lane = lax.broadcasted_iota(jnp.int32, val.shape, 1)
                    val = jnp.where(lane < over, 0.0, val)
                r["do"][...] = val.astype(bf16)

    def attention():
        allowed = may_see(r["seg_rows"][...], r["seg_cols"][...])
        dp[:, shift:] = jnp.zeros((length, joined - shift), bf16)
        rows_dim = (((0,), (0,)), ((), ()))
        for h in range(own_heads):
            here = [slice(i * hw + h * HD, i * hw + (h + 1) * HD) for i in range(3)]
            q, k, v, do = (r[n][:, here[0]] for n in ("q", "k", "v", "do"))
            probs = jnp.exp(head_scores(q, k, allowed) - r["lse"][:, h : h + 1])
            grad_probs = dot_nt(do, v)
            delta = jnp.sum(probs * grad_probs, axis=-1, keepdims=True)
            grad_scores = (probs * (grad_probs - delta) * HD ** (-0.5)).astype(bf16)
            dq = dot_nn(grad_scores, k)
            dk = lax.dot_general(grad_scores, q, rows_dim, preferred_element_type=f32)
            dv = lax.dot_general(probs.astype(bf16), do, rows_dim, preferred_element_type=f32)
            small[7:8, here[0]] = jnp.sum(dq, axis=0, keepdims=True)
            small[7:8, here[1]] = jnp.sum(dv, axis=0, keepdims=True)
            for at_h, val in zip(here, (dq, dk, dv)):
                dp[:, at_h] = val.astype(bf16)

    def last_norm():
        cut = up_to(3 * hw, 128)
        swap(2, lambda w: dot_nt(dp[:, :cut], w[:, :cut]), r["w_joined"])

        def store(i, at_i, val):
            @pl.when(i == at.core)
            def _():
                r["grad_input"][...] = val.T

        norm_grad(2, r["xh1"], 0, 0, r["dres"], 4, length // 2, store)

    def grad_joined(k):
        top = pl.multiple_of(dest[k] * 4 * rp, 16)

        def put(n, val):
            val = val.reshape(4, rp, val.shape[-1])
            val = jnp.concatenate([val[:, : rp - 8], val[:, rp - 8 :] + small[:, n][None]], axis=1)
            r["g0"][pl.ds(dest[k] * 4, 4), :, n] = val.astype(bf16)

        step = 256

        def body(i, carry):
            n = pl.ds(pl.multiple_of(i * step, 128), step)
            put(n, dot_nn(r["tall"][pl.ds(top, 4 * rp), :], dp[:, n]))
            return carry

        lax.fori_loop(0, shift // step, body, 0)

        def both(i, carry):
            n = pl.ds(pl.multiple_of(shift + i * step, 128), step)
            m = pl.ds(pl.multiple_of(i * step, 128), step)
            put(
                n,
                dot_nn(r["tall"][pl.ds(top, 4 * rp), :], dp[:, n])
                + dot_nn(r["tall"][pl.ds(wide + top, 4 * rp), :], drc[:, m]),
            )
            return carry

        lax.fori_loop(0, (joined - shift) // step, both, 0)

    h = rows // 2
    part_n = links.numbers(4)

    def trade(sums, base, n):
        high = up_to(h, 8)
        for c in range(2):
            @pl.when(at.core == c)
            def _():
                for e in range(2):
                    r["send"][base + e * high : base + e * high + h, :] = sums[
                        (1 - c) * h : (2 - c) * h, e * wide : (e + 1) * wide
                    ]
        cut = pl.ds(base, 2 * high)
        return links.make(r["send"].at[cut, :], r["came"].at[1, cut, :], part_n + n, at.dp, True)

    def halves(sums, base):
        high = up_to(h, 8)
        for c in range(2):
            def rows_by(s, lo, hi, c=c):
                if s == c:
                    return sums[c * h : (c + 1) * h, lo:hi]
                if hi <= wide or lo >= wide:
                    e = 0 if hi <= wide else 1
                    top = base + e * high
                    return r["came"][1, top : top + h, lo - e * wide : hi - e * wide]
                return jnp.concatenate([rows_by(s, lo, wide), rows_by(s, wide, hi)], axis=1)
            yield c, rows_by

    def fc_out():
        sums = r["sums1"]
        copy = trade(sums, 0, 0)
        copy.start()
        copy.wait()
        for c, rows_by in halves(sums, 0):
            @pl.when(at.core == c)
            def _():
                for j in range(hidden // fp):
                    for s in range(2):
                        lo, to = j * fp, (2 * j + s) * fh
                        cuts = [lo, lo + fh] if not lo < wide < lo + fh else [lo, wide, lo + fh]
                        for u, v in zip(cuts, cuts[1:]):
                            r["fc_grad"][:, to + u - lo : to + v - lo] = rows_by(s, u, v)

    def attn_out():
        sums = r["sums0"]
        base = 2 * up_to(h, 8)
        copy = trade(sums, base, 1)
        copy.start()
        r["row"][...] = sums[rp - 8 :, :]
        row_copy = links.make(r["row"], r["row_came"], part_n + 2, at.dp, True)
        row_copy.start()
        copy.wait()
        row_copy.wait()
        for c, rows_by in halves(sums, base):
            @pl.when(at.core == c)
            def _():
                for i in range(4):
                    size, skip = (hw, over) if i < 3 else (half, 0)
                    to, out = (i * width, r["attn_grad"]) if i < 3 else (0, r["out_grad"])
                    for s, lo in ((0, i * hw), (1, i * hw + skip)):
                        hi = i * hw + size
                        cuts = [lo, hi] if not lo < wide < hi else [lo, wide, hi]
                        for u, v in zip(cuts, cuts[1:]):
                            out[:, to + u - lo : to + v - lo] = rows_by(s, u, v)
                        to += hi - lo
                kinds = r["kinds"]
                kinds[...] = jnp.zeros_like(kinds)
                own = r["row"]
                low, high = (r["row"], r["row_came"]) if c == 0 else (r["row_came"], r["row"])
                for i, (line, first) in enumerate(((4, 0), (4, wide), (5, 0), (5, wide))):
                    kinds[i : i + 1, 0:width] = own[line : line + 1, first : first + width]
                for i in range(2):
                    kinds[4 + i : 5 + i, 0:hw] = low[7:8, i * hw : (i + 1) * hw]
                    kinds[4 + i : 5 + i, hw:width] = high[7:8, i * hw + over : (i + 1) * hw]
                kinds[6:7, 0:width] = own[7:8, wide : wide + width]
                kinds[7:8, 0:width] = r["sums2"][fp - 8 : fp - 7, 0:width]
        size = width // (2 * nz)
        device = at.dp * 2 + at.core
        kind, block = device // (2 * nz), lax.rem(device, 2 * nz)
        for i, place in enumerate((kind, 4 + kind)):
            line = jnp.broadcast_to(r["kinds"][pl.ds(place, 1), :], (8, wide))
            r["small_out"][8 * i : 8 * i + 8, :] = pltpu.roll(line, lax.rem(wide - block * size, wide), 1)
        line = jnp.broadcast_to(r["row"][6:7, :], (8, hidden))
        line = pltpu.roll(line, lax.rem(hidden - at.dp * fp, hidden), 1)
        r["small_out"][16:24, :] = line[:, :wide]

    links.add(-1.0, setup)
    for k in range(nz):
        links.add(1.0 * k, functools.partial(grad_down, k))
    links.add(4.95, lambda: fetched(LOADED[:1]))
    links.add(9.95, lambda: fetched(LOADED[1:2]))
    links.add(19.95, lambda: fetched(LOADED[2:]))
    links.add(4.9, lambda: tall("a1t_ot").start())
    links.add(49.9, lambda: tall("a1t_ot").wait())
    links.add(5.0, grad_hidden)
    for k in range(nz):
        links.add(10.0 + k, functools.partial(grad_up, k))
    links.add(20.0, mid)
    links.add(31.0, attention)
    links.add(33.0, last_norm)
    for k in range(nz):
        links.add(50.0 + k, functools.partial(grad_joined, k))
    grads, sums = ("g0", "g1", "g2"), ("sums0", "sums1", "sums2")
    for n, item in enumerate(items):
        scatter_item(
            links, nz, dest, item, r[grads[item[0]]], r[sums[item[0]]],
            bufs[4 * n : 4 * n + 4], functools.partial(step_time, nz, item),
        )
    links.add(55.1, fc_out)
    links.add(99.0, attn_out)
    links.run()


def step_time(nz, item, stage, k):
    array, _, _, _, kind = item
    k = min(k, 3)
    if kind == "pz":
        return {
            "start": (0.6, 10.6, 20.5),
            "chain": (20.6, 31.7, 33.9),
            "gathered": (51.95,),
            "first": (51.96,),
            "second": (54.45,),
            "third": (55.5,),
        }[stage][k]
    return {
        2: {
            "first": (0.5, 1.5, 9.2, 18.2),
            "second": (9.0, 18.0, 30.0, 32.0),
            "third": (18.1, 30.1, 32.1, 41.0),
        },
        1: {
            "first": (18.3, 18.4, 30.2, 32.3),
            "second": (32.2, 41.1, 51.6, 54.0),
            "third": (41.2, 51.7, 54.3, 54.6),
        },
        0: {
            "first": (50.5, 51.5, 54.2, 54.8),
            "second": (54.1, 54.5, 54.9, 56.0),
            "third": (54.7, 55.0, 56.1, 56.2),
        },
    }[array][stage][k]


def back_call(nz, items, pieces, sizes, inputs, hbm, outs, collective_id):
    bf16, f32 = jnp.bfloat16, jnp.float32
    own_heads, rows, rp, fh, fp, half, over = sizes
    length, wide = inputs["cot"].shape
    width = hbm["xh1"].shape[1]
    hidden = hbm["slope"].shape[1]
    joined = hbm["w_joined"].shape[1]
    shift = 3 * own_heads * HD // 256 * 256
    bufs, sems = item_bufs(nz, pieces, items)
    sems += 3 * (wide // 384) + 4
    scratch = {
        "g0": pltpu.VMEM(pieces[0], bf16),
        "g1": pltpu.VMEM(pieces[1], bf16),
        "g2": pltpu.VMEM(pieces[2], bf16),
        "st": pltpu.VMEM((wide, width), bf16),
        "small": pltpu.VMEM((8, joined), f32),
        "small_d": pltpu.VMEM((8, wide), f32),
        "dub": pltpu.VMEM((length, hidden), bf16),
        "dp": pltpu.VMEM((length, joined), bf16),
        "drc": pltpu.VMEM((length, joined - shift), bf16),
        "do": pltpu.VMEM((length, own_heads * HD), bf16),
        "dres": pltpu.VMEM((length, width), f32),
        "send": pltpu.VMEM((length, wide), f32),
        "came": pltpu.VMEM((2, length, wide), f32),
        "sums0": pltpu.VMEM(pieces[0][1:], f32),
        "sums1": pltpu.VMEM(pieces[1][1:], f32),
        "tall": pltpu.VMEM((max(hidden, 2 * wide), length), bf16),
        "sem_tall": pltpu.SemaphoreType.DMA((1,)),
        "row": pltpu.VMEM((8, joined), f32),
        "row_came": pltpu.VMEM((8, joined), f32),
        "kinds": pltpu.VMEM((8, wide), f32),
        "buf_down": pltpu.VMEM((2, 256, wide), bf16),
        "buf_up": pltpu.VMEM((2, 384, joined), bf16),
        "sem_down": pltpu.SemaphoreType.DMA((2,)),
        "sem_up": pltpu.SemaphoreType.DMA((2,)),
        "send_sem": pltpu.SemaphoreType.DMA((sems,)),
        "recv_sem": pltpu.SemaphoreType.DMA((sems,)),
    }
    for n in LOADED:
        scratch[n] = pltpu.VMEM(hbm[n].shape, hbm[n].dtype)
    scratch["in_sem"] = pltpu.SemaphoreType.DMA((len(LOADED),))
    far_names = ["far_" + n if n in LOADED else n for n in hbm]
    names = (*inputs, *far_names, *outs, *scratch)
    vmem, far = pl.BlockSpec(memory_space=pltpu.VMEM), pl.BlockSpec(memory_space=pl.ANY)
    return pl.pallas_call(
        functools.partial(back_kernel, nz, items, sizes, names),
        out_shape=list(outs.values()),
        in_specs=[vmem] * len(inputs) + [far] * len(hbm),
        out_specs=[vmem] * len(outs),
        scratch_shapes=[*scratch.values(), *bufs],
        compiler_params=pltpu.CompilerParams(
            collective_id=collective_id, has_side_effects=True, vmem_limit_bytes=63 * 2**20
        ),
    )(*inputs.values(), *hbm.values())


def gather_item(links, nz, item, src, out, times):
    at = links.at
    _, lo, mid, hi, kind = item
    part = {"all": pl.ds(lo, hi - lo), "a": pl.ds(lo, mid - lo), "b": pl.ds(mid, hi - mid)}
    base = links.numbers((2 * nz - 1) * 8)

    def number(stage, q, p):
        return base + (q + nz - 1) * 8 + stage * 4 + p

    def send(n, piece, to, cut="all", own=False):
        q, p = piece

        def make(ref=None):
            dst = out.at[at.chip(q, p), :, part[cut]]
            return links.make(dst if ref is None else ref, dst, n, at.chip(*to))

        make(src.at[:, part[cut]] if own else None).start()

        def done():
            flag = jnp.logical_and(at.has(q), at.has(to[0]))
            pl.when(flag)(lambda: make().wait_send())

        links.ends.append(done)

    def came(n, chip, cut="all"):
        links.came(out.at[chip, :, part[cut]], n)

    def along(q, p, own=False):
        for go in (1, -1) if q == 0 else ((-1,) if q > 0 else (1,)):
            if abs(q - go) < nz:
                @pl.when(at.has(go))
                def _():
                    send(number(0, q - go, p), (q, p), (go, 0), "all", own)

    def across(q, own=False):
        for p in (1, 2):
            send(number(1, q, p - 1), (q, 0), (0, p), "all", own)

    def relay(q, p):
        came(number(1, q, p - 1), at.chip(q, p))
        send(number(1, q, p + 1), (q, p), (0, 3 - p), "ab"[p - 1])

    def corner(q):
        for p in (1, 2):
            came(number(1, q, p + 1), at.chip(q, 3), "ab"[p - 1])

    def put(when, q, fn):
        links.add(when, fn if q == 0 else lambda: pl.when(at.has(q))(fn))

    def arrive(q, p=0):
        came(number(0, q, p), at.chip(q, p))
        along(q, p)

    if kind == "zp":
        for q in slots(nz):
            if q == 0:
                put(times("z", 0), 0, lambda: along(0, 0, True))
                put(times("plane", 0), 0, lambda: across(0, True))
            else:
                put(times("z", q), q, lambda q=q: arrive(q))
                put(times("plane", q), q, lambda q=q: across(q))
            put(times("relay", q), q, lambda q=q: [relay(q, p) for p in (1, 2)] and None)
            put(times("last", q), q, lambda q=q: corner(q))
        return
    put(times("plane", 0), 0, lambda: across(0, True))
    put(times("own", 0), 0, lambda: along(0, 0, True))
    for p in (1, 2):
        put(times("relay", 0), 0, lambda p=p: relay(0, p))
        put(times("own", 0), 0, lambda p=p: along(0, p))

    def diagonal():
        corner(0)
        along(0, 3)

    put(times("own", 0) + 0.01, 0, diagonal)
    for q in slots(nz)[1:]:
        for p in range(4):
            put(times("z", q) + 0.01 * p, q, lambda q=q, p=p: arrive(q, p))


def gather_time(item, stage, q):
    array, _, _, _, kind = item
    d = abs(q)
    if kind == "pz":
        return {"plane": 3.2, "relay": 4.8, "own": 5.6, "z": (0, 9.9, 11.9, 13.9)[d]}[stage]
    if array == 0:
        return {"z": 1.0 * d, "plane": 1.0 * d + 0.01, "relay": 1.6 + 1.4 * d, "last": 6.2}[stage]
    if array == 1:
        return {
            "z": (3.0, 4.2, 5.4, 6.6)[d], "plane": (5.0, 5.5, 6.7, 7.4)[d],
            "relay": (7.4, 8.4, 10.0, 11.0)[d], "last": 12.0,
        }[stage]
    return {
        "z": (6.8, 7.45, 8.45, 9.95)[d], "plane": (10.1, 10.2, 10.3, 10.4)[d],
        "relay": (12.01, 12.02, 12.03, 12.04)[d], "last": 14.5,
    }[stage]


EARLY = ("a1t_ot", "a2t", "q", "k", "v", "lse", "xh1", "xh2", "rstd", "gains")
LATER = ("gt", "slope")


def forward_kernel(nz, items, sizes, names, *refs):
    f32, bf16 = jnp.float32, jnp.bfloat16
    r = dict(zip(names, refs))
    own_heads, rows, rp, fh, fp, half, over, small = sizes
    hw = own_heads * HD
    at = Place(nz)
    links = Links(at, r["send_sem"], r["recv_sem"])
    acts, st, par = r["acts"], r["st"], r["par"]
    length, width = acts.shape
    wide = st.shape[0]
    hidden = r["gt"].shape[0]
    joined = r["w2d"].shape[1]
    shift = 3 * hw // 128 * 128
    skip = 3 * hw - shift
    chips = 4 * nz
    outs = ("attn_all", "fc_all", "proj_all")
    ins = ("attn_piece", "fc_piece", "proj_piece")
    own = [
        pltpu.make_async_copy(r[i], r[o].at[at.dp], r["sem"].at[n])
        for n, (i, o) in enumerate(zip(ins, outs))
    ]
    for copy in own:
        copy.start()
    at.meet(True)
    trade_n = links.numbers(3)

    def trade(n, mine, theirs):
        copy = links.make(mine, theirs, trade_n + n, at.dp, True)
        copy.start()
        copy.wait()

    def normalise(value, xh_ref, column):
        mu = jnp.mean(value, axis=-1, keepdims=True)
        centred = value - mu
        inv = lax.rsqrt(jnp.mean(centred * centred, axis=-1, keepdims=True) + NORM_EPS)
        return centred * inv, inv

    step = 64

    def by_rows(fn):
        def body(i, carry):
            fn(pl.ds(pl.multiple_of(i * step, step), step))
            return carry
        lax.fori_loop(0, length // step, body, 0)

    def prepare():
        fill_spread(st, rows, rp)

        def one(cut):
            xh, inv = normalise(acts[cut, :].astype(f32), None, 0)
            r["xh1"][cut, :] = xh
            r["rstd"][cut, 0:1] = inv

        by_rows(one)

    def load(name, n):
        own[n].wait()
        copy = pltpu.make_async_copy(r[name], r["w3d"], r["sem"].at[3])
        copy.start()
        copy.wait()

    def flatten():
        def body(i, carry):
            r["w2d"][pl.ds(pl.multiple_of(i * 2 * rp, 16), 2 * rp), :] = jnp.concatenate(
                [r["w3d"][2 * i], r["w3d"][2 * i + 1]], axis=0
            )
            return carry
        lax.fori_loop(0, chips // 2, body, 0)

    def parameters():
        par[...] = jnp.zeros_like(par)
        r["up_bias"][...] = jnp.zeros_like(r["up_bias"])
        for j in range(chips):
            block = r["w3d"][j, rp - 8 :, 0 : 3 * small].astype(f32)
            for c in range(2):
                line = block[rows - rp + 8 + c : rows - rp + 9 + c, :]
                device = 2 * j + c
                kind, lane = device // (2 * nz), device % (2 * nz) * small
                par[kind : kind + 1, lane : lane + small] = line[:, 0:small]
                par[4 + kind : 5 + kind, lane : lane + small] = line[:, small : 2 * small]

                @pl.when(at.core == c)
                def _():
                    r["up_bias"][0:1, j * fp : j * fp + fh] = line[:, 2 * small :]

    def spread_both(value, t_ref, first_row):
        t_ref[first_row : first_row + wide, :] = dot_nt(st[...], value).astype(bf16)
        r["spread"][...] = dot_nt(value, st[...]).astype(bf16)

    def unpack_step():
        load("attn_all", 0)
        parameters()
        flatten()

    def query_step():
        def one(cut):
            a = r["xh1"][cut, :] * par[0:1, 0:width] + par[1:2, 0:width]
            r["act"][cut, :] = a.astype(bf16)

        by_rows(one)
        spread_both(r["act"][...], r["a1t_ot"], 0)
        size = 256

        def body(i, carry):
            n = pl.ds(pl.multiple_of(i * size, 128), size)
            r["p"][:, n] = dot_nn(r["spread"][...], r["w2d"][:, n])
            return carry

        lax.fori_loop(0, r["p"].shape[1] // size, body, 0)
        low = at.core == 0
        for i, (name, line) in enumerate((("q", 4), ("k", None), ("v", 5))):
            val = r["p"][:, i * hw : (i + 1) * hw]
            if line is not None:
                val = val + jnp.where(
                    low, par[line : line + 1, 0:hw], par[line : line + 1, width - hw : width]
                )
            r[name][...] = val.astype(bf16)

    def attention():
        allowed = may_see(r["seg_rows"][...], r["seg_cols"][...])
        attend(head_scores, own_heads, r["lse"], r["q"], r["k"], r["v"], r["o"], allowed)

    def mix():
        low = at.core == 0
        trade(0, r["o"], r["o_came"])
        first = jnp.where(low, r["o"][...], r["o_came"][...])
        second = jnp.where(low, r["o_came"][...], r["o"][...])
        if over:
            lane = lax.broadcasted_iota(jnp.int32, second.shape, 1)
            second = jnp.where(lane < over, jnp.zeros((), bf16), second)
        st_low, st_high = st[:, 0:hw], st[:, width - hw : width]
        r["a1t_ot"][wide : 2 * wide, :] = (dot_nt(st_low, first) + dot_nt(st_high, second)).astype(bf16)
        r["spread"][...] = (dot_nt(first, st_low) + dot_nt(second, st_high)).astype(bf16)
        r["mixed"][...] = dot_nn(r["spread"][...], r["w2d"][:, shift:])
        trade(1, r["mixed"], r["mixed_came"])
        r["resid"][:, 0:half] = jnp.where(
            low, r["mixed"][:, skip : skip + half], r["mixed_came"][:, skip : skip + half]
        )
        r["resid"][:, half : 2 * half] = jnp.where(
            low, r["mixed_came"][:, skip : skip + half], r["mixed"][:, skip : skip + half]
        )

        def one(cut):
            val = acts[cut, :].astype(f32) + r["resid"][cut, :] + par[6:7, 0:width]
            r["resid"][cut, :] = val
            xh, inv = normalise(val, None, 1)
            r["xh2"][cut, :] = xh
            r["rstd"][cut, 1:2] = inv
            r["act"][cut, :] = (xh * par[2:3, 0:width] + par[3:4, 0:width]).astype(bf16)

        by_rows(one)
        spread_both(r["act"][...], r["a2t"], 0)
        r["gains"][...] = par[...]

    def hidden_step():
        load("fc_all", 1)
        flatten()
        size = 256

        def body(i, carry):
            n = pl.ds(pl.multiple_of(i * size, 128), size)
            u = dot_nn(r["spread"][...], r["w2d"][:, n]) + r["up_bias"][0:1, n]
            value, slope = gelu_parts(u)
            r["g"][:, n] = value.astype(bf16)
            r["gt"][n, :] = value.T.astype(bf16)
            r["slope"][:, n] = (slope * r["real"][0:1, n]).astype(bf16)
            return carry

        lax.fori_loop(0, hidden // size, body, 0)

    def result_step():
        own[2].wait()
        copy = pltpu.make_async_copy(r["proj_all"], r["wd3"], r["sem"].at[3])
        copy.start()
        copy.wait()
        size, some = 384, chips // 2
        tokens = length // 2

        def body(i, carry):
            n = pl.ds(pl.multiple_of(i * size, 128), size)
            total = 0.0
            for e in range(2):
                w = r["wd3"][e * some : (e + 1) * some, :, n].reshape(some * fp, size)
                total = total + dot_nn(r["g"][:, e * some * fp : (e + 1) * some * fp], w)
            r["down"][:, n] = total
            return carry

        lax.fori_loop(0, wide // size, body, 0)
        theirs = pl.ds(pl.multiple_of((1 - at.core) * tokens, tokens), tokens)
        mine = pl.ds(pl.multiple_of(at.core * tokens, tokens), tokens)
        trade(2, r["down"].at[theirs, :], r["down_came"])
        total = (
            r["resid"][mine, :]
            + (r["down"][mine, 0:width] + r["down_came"][:, 0:width])
            + par[7:8, 0:width]
        )
        r["result"][...] = total.T.astype(bf16)

    def leave(names_, first):
        for n, name in enumerate(names_):
            pltpu.make_async_copy(r[name], r["far_" + name], r["out_sem"].at[first + n]).start()

    def left():
        for n, name in enumerate((*EARLY, *LATER)):
            pltpu.make_async_copy(r[name], r["far_" + name], r["out_sem"].at[n]).wait()

    links.add(12.1, lambda: leave(EARLY, 0))
    links.add(12.21, lambda: leave(LATER, len(EARLY)))
    links.add(99.0, left)
    links.add(0.5, prepare)
    links.add(6.3, unpack_step)
    links.add(6.9, query_step)
    links.add(7.42, attention)
    links.add(8.42, mix)
    links.add(12.2, hidden_step)
    links.add(15.0, result_step)
    for item in items:
        gather_item(links, nz, item, r[ins[item[0]]], r[outs[item[0]]], functools.partial(gather_time, item))
    links.run()


def forward_call(nz, items, sizes, inputs, pieces, collective_id):
    bf16, f32 = jnp.bfloat16, jnp.float32
    own_heads, rows, rp, fh, fp, half, over, small = sizes
    hw = own_heads * HD
    length, width = inputs["acts"].shape
    attn, fc, proj = pieces.values()
    chips, joined, hidden, wide = 4 * nz, attn.shape[1], fc.shape[1], proj.shape[1]
    shape = jax.ShapeDtypeStruct
    landing = {
        n: shape((chips, *p.shape), bf16)
        for n, p in zip(("attn_all", "fc_all", "proj_all"), (attn, fc, proj))
    }
    outs = {
        "a1t_ot": shape((2 * wide, length), bf16),
        "a2t": shape((wide, length), bf16),
        "gt": shape((hidden, length), bf16),
        "slope": shape((length, hidden), bf16),
        "q": shape((length, hw), bf16),
        "k": shape((length, hw), bf16),
        "v": shape((length, hw), bf16),
        "lse": shape((length, 128), f32),
        "xh1": shape((length, width), f32),
        "xh2": shape((length, width), f32),
        "rstd": shape((length, 2), f32),
        "gains": shape((8, wide), f32),
        "result": shape((width, length // 2), bf16),
    }
    mixed = joined - 3 * hw // 128 * 128
    sems = len(items) * (2 * nz - 1) * 8 + 3
    scratch = {
        "w3d": pltpu.VMEM((chips, *attn.shape), bf16),
        "w2d": pltpu.VMEM((chips * rp, joined), bf16),
        "wd3": pltpu.VMEM((chips, *proj.shape), bf16),
        "st": pltpu.VMEM((wide, width), bf16),
        "par": pltpu.VMEM((8, wide), f32),
        "up_bias": pltpu.VMEM((8, hidden), f32),
        "act": pltpu.VMEM((length, width), bf16),
        "spread": pltpu.VMEM((length, wide), bf16),
        "p": pltpu.VMEM((length, up_to(3 * hw, 256)), f32),
        "o": pltpu.VMEM((length, hw), bf16),
        "o_came": pltpu.VMEM((length, hw), bf16),
        "mixed": pltpu.VMEM((length, mixed), f32),
        "mixed_came": pltpu.VMEM((length, mixed), f32),
        "resid": pltpu.VMEM((length, width), f32),
        "g": pltpu.VMEM((length, hidden), bf16),
        "down": pltpu.VMEM((length, wide), f32),
        "down_came": pltpu.VMEM((length // 2, wide), f32),
        "sem": pltpu.SemaphoreType.DMA((4,)),
        "send_sem": pltpu.SemaphoreType.DMA((sems,)),
        "recv_sem": pltpu.SemaphoreType.DMA((sems,)),
    }
    far_names = [n if n == "result" else "far_" + n for n in outs]
    for n in (*EARLY, *LATER):
        scratch[n] = pltpu.VMEM(outs[n].shape, outs[n].dtype)
    scratch["out_sem"] = pltpu.SemaphoreType.DMA((len(EARLY) + len(LATER),))
    names = (*inputs, *pieces, *landing, *far_names, *scratch)
    vmem, far = pl.BlockSpec(memory_space=pltpu.VMEM), pl.BlockSpec(memory_space=pl.ANY)
    got = pl.pallas_call(
        functools.partial(forward_kernel, nz, items, sizes, names),
        out_shape=[*landing.values(), *outs.values()],
        in_specs=[vmem] * len(inputs) + [far] * len(pieces),
        out_specs=[far] * len(landing) + [vmem if n == "result" else far for n in outs],
        scratch_shapes=list(scratch.values()),
        compiler_params=pltpu.CompilerParams(
            collective_id=collective_id, has_side_effects=True, vmem_limit_bytes=60 * 2**20
        ),
    )(*inputs.values(), *pieces.values())
    return dict(zip((*landing, *outs), got))


def attend(scores_of, heads, lse_ref, q_ref, k_ref, v_ref, o_ref, allowed):
    for h in range(heads):
        at = slice(h * HD, (h + 1) * HD)
        scores = scores_of(q_ref[:, at], k_ref[:, at], allowed)
        top = jnp.max(scores, axis=-1, keepdims=True)
        total = top + jnp.log(jnp.sum(jnp.exp(scores - top), axis=-1, keepdims=True))
        probs = jnp.exp(scores - total).astype(jnp.bfloat16)
        lse_ref[:, h : h + 1] = total
        o_ref[:, at] = jnp.dot(
            probs, v_ref[:, at], preferred_element_type=jnp.float32
        ).astype(o_ref.dtype)


def head_scores(queries, key_rows, allowed):
    scores = lax.dot_general(
        queries, key_rows, (((1,), (1,)), ((), ())), preferred_element_type=jnp.float32
    ) * HD ** (-0.5)
    return jnp.where(allowed, scores, -1e30)


def may_see(seg_rows, seg_cols):
    length = seg_cols.shape[1]
    i = lax.broadcasted_iota(jnp.int32, (length, length), 0)
    j = lax.broadcasted_iota(jnp.int32, (length, length), 1)
    return (j <= i) & (seg_rows == seg_cols)


def up_to(value, step):
    return -(-value // step) * step


def per_device_grid(
    nz,
    layer_input,
    segments,
    w_attn,
    w_out,
    w_fc,
    w_proj,
    norm_params,
    lin_bias,
    fc_bias,
    out_cotangent,
):
    f32, bf16 = jnp.float32, jnp.bfloat16
    core = lax.axis_index("seq")
    low = core == 0
    chips = lax.axis_size("dp")
    tokens, width = layer_input.shape[1:]
    heads = width // HD
    own_heads = -(-heads // 2)
    hw = own_heads * HD
    over = 2 * hw - width
    half = width // 2
    small = norm_params.shape[0]
    h = w_out.shape[0] // width
    rows, rp = 2 * h, up_to(2 * h, 8)
    fh = w_proj.shape[0] // width
    fp = up_to(fh + 2, 16)
    hidden = chips * fp
    wide = up_to(width, 128)
    owide = up_to(3 * hw + half, 128) - 3 * hw

    def swap(value):
        return lax.ppermute(value, "seq", [(0, 1), (1, 0)])

    def pair(own, came):
        return jnp.where(low, own, came), jnp.where(low, came, own)

    def lanes_of(value, size):
        first, second = value[..., :size], value[..., value.shape[-1] - size :]
        return jnp.where(low, first, second), jnp.where(low, second, first)

    own_small = jnp.concatenate([norm_params, lin_bias, fc_bias])
    wa = w_attn.reshape(h, 3 * width)
    wo = w_out.reshape(h, width)
    wf = w_fc.reshape(h, chips, 2, fh)
    parts = [lanes_of(wa[:, i * width : (i + 1) * width], hw) for i in range(3)]
    parts.append(lanes_of(wo, half))
    gap = jnp.zeros((h, owide - half), bf16)
    attn_own, attn_other = (
        jnp.concatenate([p[i] for p in parts] + [gap], axis=1) for i in range(2)
    )
    fc_pads = ((0, 0), (0, 0), (0, fp - fh))
    fc_own, fc_other = (
        jnp.pad(jnp.where(low == first, wf[:, :, 0], wf[:, :, 1]), fc_pads).reshape(h, hidden)
        for first in (True, False)
    )
    attn_came, fc_came = swap(attn_other), swap(fc_other)
    acts_came = swap(jnp.stack([layer_input[0], out_cotangent[0]]))
    small_came = swap(own_small)
    row_pads = ((0, rp - rows), (0, 0))
    small_rows = jnp.pad(
        jnp.stack(pair(own_small, small_came)), ((0, rp - rows - 2), (0, 3 * hw + owide - 3 * small))
    )
    attn_piece = jnp.concatenate([*pair(attn_own, attn_came), small_rows])
    fc_piece = jnp.pad(jnp.concatenate(pair(fc_own, fc_came)), row_pads)
    proj_piece = jnp.pad(w_proj.reshape(fh, width), ((0, fp - fh), (0, wide - width)))
    acts = jnp.concatenate(pair(layer_input[0], acts_came[0]))
    cotangent = jnp.concatenate(pair(out_cotangent[0], acts_came[1]))
    cot_wide = jnp.pad(cotangent, ((0, 0), (0, wide - width)))
    seg_rows, seg_cols = segments.reshape(-1, 1), segments.reshape(1, -1)
    real = jnp.pad(jnp.ones((1, chips, fh), f32), ((0, 0), (0, 0), (0, fp - fh))).reshape(1, hidden)
    shape = jax.ShapeDtypeStruct
    third, joined = up_to(wide // 3, 128), attn_piece.shape[1]
    cuts = (
        (0, 0, up_to(joined // 2, 128), joined, "zp"),
        (1, 0, up_to(hidden // 2, 128), hidden, "zp"),
        (2, 2 * third, 2 * third + up_to((wide - 2 * third) // 2, 128), wide, "zp"),
        (2, 0, third, 2 * third, "pz"),
    )
    back_cuts = (
        (2, 0, up_to(third // 2, 128), third, "pz"),
        (2, third, 2 * third, wide, "zp"),
        (1, 0, up_to(hidden // 2, 128), hidden, "zp"),
        (0, 0, up_to(joined // 2, 128), joined, "zp"),
    )
    sizes = (own_heads, rows, rp, fh, fp, half, over)
    done = forward_call(
        nz,
        cuts,
        (*sizes, small),
        {"acts": acts, "seg_rows": seg_rows, "seg_cols": seg_cols, "real": real},
        {"attn_piece": attn_piece, "fc_piece": fc_piece, "proj_piece": proj_piece},
        0,
    )
    attn_grad, out_grad, fc_grad, sums2, grad_input, small_out = back_call(
        nz,
        back_cuts,
        tuple(done[n].shape for n in ("attn_all", "fc_all", "proj_all")),
        sizes,
        {
            "cot": cot_wide,
            "seg_rows": seg_rows,
            "seg_cols": seg_cols,
        },
        {
            **{n: done[n] for n in LOADED},
            "gt": done["gt"],
            "a1t_ot": done["a1t_ot"],
            "w_down": done["proj_all"].reshape(hidden, wide),
            "w_up": done["fc_all"].reshape(-1, hidden),
            "w_joined": done["attn_all"].reshape(-1, joined),
        },
        {
            "attn_grad": shape((h, 3 * width), f32),
            "out_grad": shape((h, width), f32),
            "fc_grad": shape((h, 2 * chips * fh), f32),
            "sums2": shape(proj_piece.shape, f32),
            "grad_input": shape((width, tokens), f32),
            "small_out": shape((24, wide), f32),
        },
        1,
    )

    return (
        done["result"].T[None],
        grad_input.T[None],
        attn_grad.reshape(-1),
        out_grad.reshape(-1),
        fc_grad.reshape(-1),
        sums2[:fh, :width].reshape(-1),
        small_out[0, :small],
        small_out[8, :small],
        small_out[16, :small],
    )


def grid_height(mesh):
    shape = dict(mesh.shape)
    devices = mesh.devices.reshape(-1)
    if tuple(mesh.axis_names) != AXES or shape["seq"] != 2 or shape["dp"] % 4:
        return 0
    nz = shape["dp"] // 4
    base = getattr(devices[0], "coords", None)
    if base is None:
        return 0
    for n, device in enumerate(devices):
        chip = n // 2
        place = (chip % 2, chip // 2 % 2, chip // 4)
        if tuple(a - b for a, b in zip(device.coords, base)) != place:
            return 0
    return nz if 1 < nz <= 4 else 0


def solution(mesh):
    nz = grid_height(mesh)
    return jax.shard_map(
        functools.partial(per_device_grid, nz) if nz else per_device,
        mesh=mesh,
        in_specs=(
            P("dp", "seq", None),
            P("dp", None),
            P(("dp", "seq")),
            P(("dp", "seq")),
            P(("dp", "seq")),
            P(("dp", "seq")),
            P(("dp", "seq")),
            P(("dp", "seq")),
            P(("dp", "seq")),
            P("dp", "seq", None),
        ),
        out_specs=(
            P("dp", "seq", None),
            P("dp", "seq", None),
            P(("dp", "seq")),
            P(("dp", "seq")),
            P(("dp", "seq")),
            P(("dp", "seq")),
            P(("dp", "seq")),
            P(("dp", "seq")),
            P(("dp", "seq")),
        ),
        check_vma=False,
    )
```

```python
import functools

import jax
import jax.numpy as jnp
from jax import lax
from jax.experimental import pallas as pl
from jax.experimental.pallas import tpu as pltpu
from jax.sharding import PartitionSpec as P

HD = 64
FF = 4352


GELU_C = 0.7978845608028654
NORM_EPS = 1e-05


def gelu_parts(inputs):
    tanh_value = jnp.tanh(GELU_C * (inputs + 0.044715 * inputs * inputs * inputs))
    value = 0.5 * inputs * (1.0 + tanh_value)
    slope = 0.5 * (1.0 + tanh_value) + 0.5 * inputs * (1.0 - tanh_value * tanh_value) * GELU_C * (
        1.0 + 3.0 * 0.044715 * inputs * inputs
    )
    return (value, slope)


def layer_norm(inputs, gains, offsets):
    average = jnp.mean(inputs, axis=-1, keepdims=True)
    centred = inputs - average
    inv_std = lax.rsqrt(jnp.mean(centred * centred, axis=-1, keepdims=True) + NORM_EPS)
    x_hat = centred * inv_std
    return (x_hat * gains + offsets, x_hat, inv_std)


def norm_back(grad_out, x_hat, inv_std, gains):
    grad_hat = grad_out * gains
    grad_in = inv_std * (
        grad_hat
        - jnp.mean(grad_hat, axis=-1, keepdims=True)
        - x_hat * jnp.mean(grad_hat * x_hat, axis=-1, keepdims=True)
    )
    return (grad_in, jnp.sum(grad_out * x_hat, axis=0), jnp.sum(grad_out, axis=0))


def score_block(queries, key_rows, allowed):
    scores = jnp.einsum(
        "qhd,khd->hqk", queries, key_rows, preferred_element_type=jnp.float32
    ) * HD ** (-0.5)
    return jnp.where(allowed[None], scores, -1e30)


def outer_sum(left, right):
    return jnp.einsum("na,nb->ab", left, right, preferred_element_type=jnp.float32)


AXES = ("dp", "seq")


def shard_height(shard, columns):
    size = shard.shape[0]
    return size // columns if size % columns == 0 else 0


def tile_height(shard, columns):
    height = shard_height(shard, columns)
    return 0 if height % 8 else height


def padded(height):
    return -(-height // 8) * 8


def gather_rows(shard, columns, height, extra=None):
    if not height:
        return lax.all_gather(shard, AXES, axis=0, tiled=True).reshape(-1, columns)
    block = shard.reshape(height, columns)
    room = padded(height) - height
    if extra is not None:
        row = jnp.pad(extra, (0, columns - extra.shape[0]))[None]
        block = jnp.concatenate([block, row], axis=0)
        room -= 1
    if room:
        block = jnp.pad(block, ((0, room), (0, 0)))
    return lax.all_gather(block, AXES, axis=0, tiled=True)


def spread(acts, height):
    room = padded(height) - height
    if not room:
        return acts
    tokens = acts.shape[0]
    parts = acts.reshape(tokens, -1, height)
    return jnp.pad(parts, ((0, 0), (0, 0), (0, room))).reshape(tokens, -1)


def unspread(acts, height):
    if padded(height) == height:
        return acts
    tokens = acts.shape[0]
    return acts.reshape(tokens, -1, padded(height))[:, :, :height].reshape(tokens, -1)


def scatter_rows(blocks, height):
    count = lax.axis_size(AXES)
    sums = lax.psum_scatter(
        blocks.astype(jnp.bfloat16).reshape(count, -1, blocks.shape[-1]),
        AXES,
        scatter_dimension=0,
        tiled=True,
    )[0]
    return sums.astype(jnp.float32)


def scatter_flat(block, shard):
    count = lax.axis_size(AXES)
    return lax.psum_scatter(
        block.reshape(count, shard), AXES, scatter_dimension=0, tiled=True
    )[0]


def own_half_sum(terms, place, tokens):
    if lax.axis_size("seq") != 2:
        return lax.psum_scatter(
            terms.astype(jnp.bfloat16), "seq", scatter_dimension=0, tiled=True
        ).astype(jnp.float32)
    own = lax.dynamic_slice_in_dim(terms, place * tokens, tokens)
    other = lax.dynamic_slice_in_dim(terms, (1 - place) * tokens, tokens)
    came = lax.ppermute(other.astype(jnp.bfloat16), "seq", [(0, 1), (1, 0)])
    return own + came.astype(jnp.float32)


def per_device(
    layer_input,
    segments,
    w_attn,
    w_out,
    w_fc,
    w_proj,
    norm_params,
    lin_bias,
    fc_bias,
    out_cotangent,
):
    tokens = layer_input.shape[1]
    width = layer_input.shape[2]
    heads = width // HD
    place = lax.axis_index("seq")
    first = place * tokens
    small = norm_params.shape[0]
    height = shard_height(w_attn, 3 * width)
    height = height if shard_height(w_out, width) == height == shard_height(w_fc, FF) else 0
    down_height = tile_height(w_proj, width)
    own_small = jnp.concatenate([norm_params, lin_bias, fc_bias])
    packed = height and padded(height) > height and own_small.shape[0] <= width
    if height:
        lanes = -(-width // 128) * 128
        joined_shard = jnp.concatenate(
            [
                jnp.pad(w_out.reshape(height, width), ((0, 0), (0, lanes - width))),
                w_attn.reshape(height, 3 * width),
            ],
            axis=1,
        ).reshape(-1)
        joined_w = gather_rows(
            joined_shard, lanes + 3 * width, height, own_small if packed else None
        )
        w_o = joined_w[:, :width]
        w_qkv = joined_w[:, lanes:]
    else:
        w_qkv = gather_rows(w_attn, 3 * width, 0)
        w_o = gather_rows(w_out, width, 0)
    w_up = gather_rows(w_fc, FF, height)
    w_down = gather_rows(w_proj, width, down_height)
    if packed:
        smalls = w_o.reshape(-1, padded(height), width)[:, height, : 3 * small]
    else:
        smalls = lax.all_gather(own_small, AXES, axis=0)
    smalls = smalls.astype(jnp.float32).reshape(-1, 3, small)
    norms = smalls[:, 0].reshape(4, width)
    biases = smalls[:, 1].reshape(4, width)
    up_bias = smalls[:, 2].reshape(FF)
    inputs_f = layer_input[0].astype(jnp.float32)
    normed1, x_hat1, inv_std1 = layer_norm(inputs_f, norms[0], norms[1])
    act_in1 = normed1.astype(jnp.bfloat16)
    act_rows1 = spread(act_in1, height)
    projected = jnp.dot(act_rows1, w_qkv, preferred_element_type=jnp.float32)
    queries = (projected[:, :width] + biases[0]).astype(jnp.bfloat16)
    own_keys = projected[:, width : 2 * width].astype(jnp.bfloat16)
    own_values = (projected[:, 2 * width :] + biases[1]).astype(jnp.bfloat16)
    key_rows, value_rows = (
        lax.all_gather(own_keys, "seq", axis=0, tiled=True),
        lax.all_gather(own_values, "seq", axis=0, tiled=True),
    )
    key_count = key_rows.shape[0]
    key_pos = jnp.arange(key_count)
    query_pos = first + jnp.arange(tokens)
    padded_seg = jnp.concatenate([jnp.full((tokens,), -1, jnp.int32), segments[0]])
    key_seg = lax.dynamic_slice_in_dim(padded_seg, tokens, key_count)
    query_seg = lax.dynamic_slice_in_dim(segments[0], first, tokens)
    allowed = (key_pos[None, :] <= query_pos[:, None]) & (key_seg[None, :] == query_seg[:, None])
    q_heads = queries.reshape(tokens, heads, HD)
    k_heads = key_rows.reshape(key_count, heads, HD)
    v_heads = value_rows.reshape(key_count, heads, HD)
    scores = score_block(q_heads, k_heads, allowed)
    top_score = jnp.max(scores, axis=-1, keepdims=True)
    log_total = top_score + jnp.log(jnp.sum(jnp.exp(scores - top_score), axis=-1, keepdims=True))
    attn_probs = jnp.exp(scores - log_total).astype(jnp.bfloat16)
    attended = jnp.einsum("hqk,khd->qhd", attn_probs, v_heads, preferred_element_type=jnp.float32)
    attended = attended.reshape(tokens, width).astype(jnp.bfloat16)
    attended_rows = spread(attended, height)
    resid = inputs_f + jnp.dot(attended_rows, w_o, preferred_element_type=jnp.float32) + biases[2]
    normed2, x_hat2, inv_std2 = layer_norm(resid, norms[2], norms[3])
    act_in2 = normed2.astype(jnp.bfloat16)
    act_rows2 = spread(act_in2, height)
    hidden_pre = jnp.dot(act_rows2, w_up, preferred_element_type=jnp.float32) + up_bias
    hidden_act, hidden_slope = gelu_parts(hidden_pre)
    hidden_b = hidden_act.astype(jnp.bfloat16)
    hidden_rows = spread(hidden_b, down_height)
    result = (
        resid + jnp.dot(hidden_rows, w_down, preferred_element_type=jnp.float32) + biases[3]
    ).astype(jnp.bfloat16)
    cotangent = out_cotangent[0]
    grad_out = cotangent.astype(jnp.float32)
    grad_bp = jnp.sum(grad_out, axis=0)
    grad_hidden = (
        unspread(
            jnp.einsum("nd,fd->nf", cotangent, w_down, preferred_element_type=jnp.float32),
            down_height,
        )
        * hidden_slope
    )
    grad_hidden_b = grad_hidden.astype(jnp.bfloat16)
    grad_down = outer_sum(hidden_rows, cotangent)
    if down_height:
        grad_hidden_b, grad_down = lax.optimization_barrier(
            (grad_hidden_b, grad_down.astype(jnp.bfloat16))
        )
    grad_up_bias = jnp.sum(grad_hidden, axis=0)
    if down_height:
        proj_sums = scatter_rows(grad_down, down_height)[:down_height].reshape(-1)
    else:
        proj_sums = scatter_flat(grad_down, w_proj.shape[0])
    grad_up = outer_sum(act_rows2, grad_hidden_b)
    if height:
        fc_sums = scatter_rows(grad_up, height)[:height].reshape(-1)
    else:
        fc_sums = scatter_flat(grad_up, w_fc.shape[0])
    grad_norm2 = unspread(
        jnp.einsum("nf,df->nd", grad_hidden_b, w_up, preferred_element_type=jnp.float32), height
    )
    grad_resid_n, grad_g2, grad_b2 = norm_back(grad_norm2, x_hat2, inv_std2, norms[2])
    grad_resid = grad_out + grad_resid_n
    grad_resid_b = grad_resid.astype(jnp.bfloat16)
    grad_bo = jnp.sum(grad_resid, axis=0)
    grad_att = unspread(
        jnp.einsum(
            "ne,de->nd", grad_resid_b, w_o, preferred_element_type=jnp.float32
        ).astype(jnp.bfloat16),
        height,
    )
    grad_att_heads = grad_att.reshape(tokens, heads, HD)
    probs_full = jnp.exp(score_block(q_heads, k_heads, allowed) - log_total)
    probs_b = probs_full.astype(jnp.bfloat16)
    grad_probs = jnp.einsum(
        "qhd,khd->hqk", grad_att_heads, v_heads, preferred_element_type=jnp.float32
    )
    delta = jnp.sum(probs_full * grad_probs, axis=-1, keepdims=True)
    grad_scores = (probs_full * (grad_probs - delta) * HD ** (-0.5)).astype(jnp.bfloat16)
    grad_q = jnp.einsum(
        "hqk,khd->qhd", grad_scores, k_heads, preferred_element_type=jnp.float32
    ).reshape(tokens, width)
    grad_k_all = jnp.einsum(
        "hqk,qhd->khd", grad_scores, q_heads, preferred_element_type=jnp.float32
    ).reshape(key_count, width)
    grad_v_all = jnp.einsum(
        "hqk,qhd->khd", probs_b, grad_att_heads, preferred_element_type=jnp.float32
    ).reshape(key_count, width)
    grad_k = own_half_sum(grad_k_all, place, tokens)
    grad_v = own_half_sum(grad_v_all, place, tokens)
    grad_proj_b = jnp.concatenate([grad_q, grad_k, grad_v], axis=1).astype(jnp.bfloat16)
    grad_norm1 = unspread(
        jnp.einsum("ne,de->nd", grad_proj_b, w_qkv, preferred_element_type=jnp.float32), height
    )
    grad_in_n, grad_g1, grad_b1 = norm_back(grad_norm1, x_hat1, inv_std1, norms[0])
    grad_input = grad_resid + grad_in_n
    norm_terms = jnp.concatenate([grad_g1, grad_b1, grad_g2, grad_b2])
    bias_terms = jnp.concatenate(
        [jnp.sum(grad_q, axis=0), jnp.sum(grad_v, axis=0), grad_bo, grad_bp]
    )
    small_terms = jnp.concatenate(
        [term.reshape(-1, 1, small) for term in (norm_terms, bias_terms, grad_up_bias)], axis=1
    )
    grad_attn = outer_sum(act_rows1, grad_proj_b)
    grad_wo = outer_sum(attended_rows, grad_resid_b)
    if height:
        joined = jnp.concatenate(
            [grad_attn.astype(jnp.bfloat16), grad_wo.astype(jnp.bfloat16)], axis=1
        )
        if packed:
            blocks = joined.reshape(-1, padded(height), 4 * width)
            row = small_terms.astype(jnp.bfloat16).reshape(-1, 1, 3 * small)
            row = jnp.pad(row, ((0, 0), (height, padded(height) - height - 1), (0, width * 4 - 3 * small)))
            joined = (blocks + row).reshape(joined.shape)
        sums = scatter_rows(joined, height)
        qkv_sums = sums[:height, : 3 * width].reshape(-1)
        out_sums = sums[:height, 3 * width :].reshape(-1)
    else:
        qkv_sums = scatter_flat(grad_attn, w_attn.shape[0])
        out_sums = scatter_flat(grad_wo, w_out.shape[0])
    if packed:
        small_sums = sums[height, : 3 * small].reshape(3, small)
    else:
        small_sums = lax.psum_scatter(small_terms, AXES, scatter_dimension=0, tiled=True)[0]
    norm_sums, bias_sums, fcb_sums = small_sums[0], small_sums[1], small_sums[2]
    return (
        result[None],
        grad_input[None],
        qkv_sums,
        out_sums,
        fc_sums,
        proj_sums,
        norm_sums,
        bias_sums,
        fcb_sums,
    )


MESH = pl.DeviceIdType.MESH


class Place:
    def __init__(self, nz):
        self.nz = nz
        self.dp = lax.axis_index("dp")
        self.core = lax.axis_index("seq")
        self.x = lax.rem(self.dp, 2)
        self.y = lax.rem(self.dp // 2, 2)
        self.z = self.dp // 4
        fx, fy = 1 - 2 * self.x, 2 - 4 * self.y
        self.flip = (0, fx, fy, fx + fy)

    def chip(self, dz, p):
        return self.dp + 4 * dz + self.flip[p]

    def has(self, dz):
        return jnp.logical_and(self.z + dz >= 0, self.z + dz < self.nz)

    def meet(self, other=False):
        barrier = pltpu.get_barrier_semaphore()
        for dz, p in ((0, 1), (0, 2)):
            pl.semaphore_signal(
                barrier, inc=1, device_id=(self.chip(dz, p), self.core), device_id_type=MESH
            )
        for dz in (1, -1):
            @pl.when(self.has(dz))
            def _():
                pl.semaphore_signal(
                    barrier, inc=1, device_id=(self.chip(dz, 0), self.core), device_id_type=MESH
                )
        if other:
            pl.semaphore_signal(
                barrier, inc=1, device_id=(self.dp, 1 - self.core), device_id_type=MESH
            )
        near = 3 if other else 2
        pl.semaphore_wait(barrier, near + self.has(1).astype(jnp.int32) + self.has(-1).astype(jnp.int32))


def slots(nz):
    return [0] + [s * k for k in range(1, nz) for s in (1, -1)]


def strips(width, fn):
    size = next(n for n in (384, 256, 128) if width % n == 0)

    def body(i, carry):
        fn(pl.multiple_of(i * size, 128), size)
        return carry

    lax.fori_loop(0, width // size, body, 0)


def far_first(nz):
    return [sorted(range(nz), key=lambda t: -abs(t - z)) for z in range(nz)]


def choose(scalar, values):
    picked = jnp.int32(values[0])
    for i, v in enumerate(values[1:], 1):
        picked = jnp.where(scalar == i, jnp.int32(v), picked)
    return picked


class Links:
    def __init__(self, at, send_sem, recv_sem):
        self.at, self.send_sem, self.recv_sem = at, send_sem, recv_sem
        self.used, self.events, self.ends = 0, [], []

    def numbers(self, size):
        self.used += size
        return self.used - size

    def add(self, when, fn):
        self.events.append((when, len(self.events), fn))

    def make(self, src, dst, n, chip, other=False):
        core = 1 - self.at.core if other else self.at.core
        return pltpu.make_async_remote_copy(
            src_ref=src,
            dst_ref=dst,
            send_sem=self.send_sem.at[n],
            recv_sem=self.recv_sem.at[n],
            device_id=(chip, core),
            device_id_type=MESH,
        )

    def go(self, src, dst, n, chip, other=False):
        self.make(src, dst, n, chip, other).start()
        self.ends.append(lambda: self.make(src, dst, n, chip, other).wait_send())

    def came(self, dst, n):
        self.make(dst, dst, n, self.at.dp).wait_recv()

    def run(self):
        for _, _, fn in sorted(self.events, key=lambda e: e[:2]):
            fn()
        for fn in self.ends:
            fn()


def line_cases(at, nz, dst):
    for step in (1, -1):
        ahead = dst > at.z if step > 0 else dst < at.z
        first = at.z == (0 if step > 0 else nz - 1)
        slot = dst if step > 0 else jnp.where(dst == at.z - 1, nz, dst)
        yield step, ahead, first, slot


def scatter_item(links, nz, dest, item, src, out, bufs, times):
    f32 = jnp.float32
    at = links.at
    _, lo, mid, hi, kind = item
    width, na = hi - lo, mid - lo
    part_d, part_x, part_y, line = bufs
    landing = {1: part_x, 2: part_y}
    halves = {"a": (0, na), "b": (na, width - na)}

    def mod4(chip):
        return lax.rem(chip, 4)

    def lanes(start, i, n):
        return pl.ds(pl.multiple_of(start + i, 128), n)

    def plane(k, value, finish):
        base = links.numbers(6)

        def cut(ref, half, first=0):
            start, size = halves[half]
            return ref.at[:, pl.ds(first + start, size)]

        def first():
            for p, half, n in ((2, "a", 0), (1, "b", 1)):
                ref, start = value(3)
                links.go(cut(ref, half, start), cut(part_d.at[k], half), base + n, at.chip(0, p))
            for p, half, n in ((1, "b", 2), (2, "a", 3)):
                ref, start = value(p)
                links.go(cut(ref, half, start), cut(landing[p].at[k], half), base + n, at.chip(0, p))

        def second():
            for p, half, n, m in ((1, "a", 0, 4), (2, "b", 1, 5)):
                here = cut(part_d.at[k], half)
                links.came(here, base + n)
                ref, start = value(p)
                l, size = halves[half]

                def one(i, n, ref=ref, start=start, l=l):
                    part_d[k, :, lanes(l, i, n)] = (
                        part_d[k, :, lanes(l, i, n)].astype(f32) + ref[:, lanes(start + l, i, n)].astype(f32)
                    ).astype(part_d.dtype)

                strips(size, one)
                links.go(here, cut(landing[p].at[k], half), base + m, at.chip(0, p))

        def third():
            for p, half, n in ((1, "b", 2), (2, "a", 3), (1, "a", 4), (2, "b", 5)):
                links.came(cut(landing[p].at[k], half), base + n)
            finish()

        links.add(times("first", k), first)
        links.add(times("second", k), second)
        links.add(times("third", k), third)

    if kind == "zp":
        line_n = links.numbers(nz + 1)
        for k in range(nz):
            dst = dest[k]

            def value(p, dst=dst):
                return src.at[dst * 4 + mod4(at.chip(0, p))], lo

            def total(i, n, k=k, dst=dst):
                return (
                    src[dst * 4 + mod4(at.dp), :, lanes(lo, i, n)].astype(f32)
                    + part_x[k, :, pl.ds(i, n)].astype(f32)
                    + part_y[k, :, pl.ds(i, n)].astype(f32)
                )

            if k < nz - 1:

                def finish(k=k, dst=dst, total=total):
                    for step, ahead, first, slot in line_cases(at, nz, dst):
                        def send(ref, step=step, slot=slot):
                            links.make(ref, line.at[slot], line_n + slot, at.chip(step, 0)).start()

                        @pl.when(jnp.logical_and(ahead, first))
                        def _():
                            def one(i, n):
                                part_x[k, :, pl.ds(i, n)] = total(i, n).astype(part_x.dtype)
                            strips(width, one)
                            send(part_x.at[k])

                        @pl.when(jnp.logical_and(ahead, jnp.logical_not(first)))
                        def _():
                            links.came(line.at[dst], line_n + dst)
                            def one(i, n):
                                line[dst, :, pl.ds(i, n)] = (
                                    total(i, n) + line[dst, :, pl.ds(i, n)].astype(f32)
                                ).astype(line.dtype)
                            strips(width, one)
                            send(line.at[dst])

                    def done():
                        for step, ahead, _, slot in line_cases(at, nz, dst):
                            @pl.when(ahead)
                            def _():
                                links.make(line.at[slot], line.at[slot], line_n + slot, at.chip(step, 0)).wait_send()
                    links.ends.append(done)

            else:

                def finish(total=total):
                    def one(i, n):
                        out[:, lanes(lo, i, n)] = total(i, n)
                    strips(width, one)
                    for step, slot in ((-1, at.z), (1, nz)):
                        @pl.when(at.has(step))
                        def _():
                            links.came(line.at[slot], line_n + slot)
                            def two(i, n):
                                out[:, lanes(lo, i, n)] += line[slot, :, pl.ds(i, n)].astype(f32)
                            strips(width, two)

            plane(k, value, finish)
        return
    line_n = links.numbers(4 * (nz + 1))
    mine = (nz + 1) * 4
    for k in range(nz - 1):
        dst = dest[k]
        for p in (3, 1, 2, 0):

            def chain(starts, p=p, dst=dst):
                piece = dst * 4 + mod4(at.chip(0, p))
                here = dst * 4 + p
                for step, ahead, first, plane_slot in line_cases(at, nz, dst):
                    slot = plane_slot * 4 + p

                    def send(ref, step=step, slot=slot):
                        links.make(ref, line.at[slot], line_n + slot, at.chip(step, 0)).start()

                    if starts:
                        @pl.when(jnp.logical_and(ahead, first))
                        def _():
                            send(src.at[piece, :, pl.ds(lo, width)])
                        continue

                    @pl.when(jnp.logical_and(ahead, jnp.logical_not(first)))
                    def _():
                        links.came(line.at[here], line_n + here)
                        def one(i, n):
                            line[here, :, pl.ds(i, n)] = (
                                src[piece, :, lanes(lo, i, n)].astype(f32)
                                + line[here, :, pl.ds(i, n)].astype(f32)
                            ).astype(line.dtype)
                        strips(width, one)
                        send(line.at[here])

                if starts:
                    return

                def done():
                    for step, ahead, _, plane_slot in line_cases(at, nz, dst):
                        slot = plane_slot * 4 + p
                        @pl.when(ahead)
                        def _():
                            links.make(line.at[slot], line.at[slot], line_n + slot, at.chip(step, 0)).wait_send()
                links.ends.append(done)

            links.add(times("start", k), functools.partial(chain, True))
            links.add(times("chain", k), functools.partial(chain, False))

    def gathered():
        for p in (3, 1, 2, 0):
            piece = at.z * 4 + mod4(at.chip(0, p))
            low, high = at.z * 4 + p, nz * 4 + p
            for step, slot in ((-1, low), (1, high)):
                @pl.when(at.has(step))
                def _():
                    links.came(line.at[slot], line_n + slot)

            def one(i, n):
                own = src[piece, :, lanes(lo, i, n)].astype(f32)
                below = jnp.where(at.has(-1), line[low, :, pl.ds(i, n)].astype(f32), 0.0)
                above = jnp.where(at.has(1), line[high, :, pl.ds(i, n)].astype(f32), 0.0)
                line[mine + p, :, pl.ds(i, n)] = (own + below + above).astype(line.dtype)
            strips(width, one)

    def value(p):
        return line.at[mine + p], 0

    def finish():
        def one(i, n):
            out[:, lanes(lo, i, n)] = (
                line[mine, :, pl.ds(i, n)].astype(f32)
                + part_x[0, :, pl.ds(i, n)].astype(f32)
                + part_y[0, :, pl.ds(i, n)].astype(f32)
            )
        strips(width, one)

    links.add(times("gathered", 0), gathered)
    plane(0, value, finish)


def item_bufs(nz, arrays, items):
    scratch, sems = [], 0
    for array, lo, mid, hi, kind in items:
        rows, width = arrays[array][1], hi - lo
        planes = nz if kind == "zp" else 1
        lines = nz + 1 if kind == "zp" else 4 * (nz + 1) + 4
        scratch += [pltpu.VMEM((n, rows, width), jnp.bfloat16) for n in (planes, planes, planes, lines)]
        sems += 7 * nz + 1 if kind == "zp" else 4 * (nz + 1) + 6
    return scratch, sems


NT = (((1,), (1,)), ((), ()))


def dot_nt(a, b):
    return lax.dot_general(a, b, NT, preferred_element_type=jnp.float32)


def dot_nn(a, b):
    return jnp.dot(a, b, preferred_element_type=jnp.float32)


def fill_spread(st_ref, rows, rp):
    wide, width = st_ref.shape
    step = 128

    def body(t, carry):
        at = pl.multiple_of(t * step, step)
        i = at + lax.broadcasted_iota(jnp.int32, (step, 1), 0)
        block = i // rp
        inner = i - block * rp
        column = jnp.where(inner < rows, block * rows + inner, -1)
        n = lax.broadcasted_iota(jnp.int32, (step, width), 1)
        st_ref[pl.ds(at, step), :] = jnp.where(n == column, 1.0, 0.0).astype(st_ref.dtype)
        return carry

    lax.fori_loop(0, wide // step, body, 0)


def stream(hbm, buf, sem, fn):
    size = buf.shape[1]
    count = hbm.shape[0] // size

    def copy(i, slot):
        rows = pl.ds(pl.multiple_of(i * size, 16), size)
        return pltpu.make_async_copy(hbm.at[rows, :], buf.at[slot], sem.at[slot])

    copy(0, 0).start()

    def body(i, carry):
        slot = lax.rem(i, 2)

        @pl.when(i + 1 < count)
        def _():
            copy(i + 1, 1 - slot).start()

        copy(i, slot).wait()
        fn(i, buf.at[slot])
        return carry

    lax.fori_loop(0, count, body, 0)


LOADED = ("slope", "a2t", "q", "k", "v", "lse", "xh1", "xh2", "rstd", "gains")


def back_kernel(nz, items, sizes, names, *refs):
    f32, bf16 = jnp.float32, jnp.bfloat16
    r = dict(zip(names, refs))
    bufs = refs[len(names) :]
    own_heads, rows, rp, fh, fp, half, over = sizes
    hw = own_heads * HD
    at = Place(nz)
    links = Links(at, r["send_sem"], r["recv_sem"])
    table = far_first(nz)
    dest = [choose(at.z, [table[z][k] for z in range(nz)]) for k in range(nz)]
    at.meet(True)
    cot, st, small, small_d = r["cot"], r["st"], r["small"], r["small_d"]
    dub, dp, drc = r["dub"], r["dp"], r["drc"]
    length, wide = cot.shape
    hidden = dub.shape[1]
    width = st.shape[1]
    joined = dp.shape[1]
    shift = joined - drc.shape[1]

    def tall(name):
        rows_in = r[name].shape[0]
        return pltpu.make_async_copy(r[name], r["tall"].at[pl.ds(0, rows_in), :], r["sem_tall"].at[0])

    def fetch(n, name):
        return pltpu.make_async_copy(r["far_" + name], r[name], r["in_sem"].at[n])

    def fetched(names_):
        for name in names_:
            fetch(LOADED.index(name), name).wait()

    def setup():
        tall("gt").start()
        for n, name in enumerate(LOADED):
            fetch(n, name).start()
        small[...] = jnp.zeros_like(small)
        small_d[...] = jnp.zeros_like(small_d)
        small_d[0:1, :] = jnp.sum(cot[...].astype(f32), axis=0, keepdims=True)
        tall("gt").wait()

    def grad_down(k):
        top = pl.multiple_of(dest[k] * 4 * fp, 16)
        step = wide // 3

        def body(i, carry):
            n = pl.ds(pl.multiple_of(i * step, 128), step)
            val = dot_nn(r["tall"][pl.ds(top, 4 * fp), :], cot[:, n]).reshape(4, fp, step)
            val = jnp.concatenate([val[:, : fp - 8], val[:, fp - 8 :] + small_d[:, n][None]], axis=1)
            r["g2"][pl.ds(dest[k] * 4, 4), :, n] = val.astype(bf16)
            return carry

        lax.fori_loop(0, 3, body, 0)

    def grad_hidden():
        def fn(i, w):
            n = pl.ds(pl.multiple_of(i * w.shape[0], 128), w.shape[0])
            val = dot_nt(cot[...], w[...]) * r["slope"][:, n].astype(f32)
            dub[:, n] = val.astype(bf16)
            small[6:7, n] = jnp.sum(val, axis=0, keepdims=True)

        stream(r["w_down"], r["buf_down"], r["sem_down"], fn)

    def grad_up(k):
        top = pl.multiple_of(dest[k] * 4 * rp, 16)
        step = 256

        def body(i, carry):
            n = pl.ds(pl.multiple_of(i * step, 128), step)
            val = dot_nn(r["a2t"][pl.ds(top, 4 * rp), :], dub[:, n])
            r["g1"][pl.ds(dest[k] * 4, 4), :, n] = val.reshape(4, rp, step).astype(bf16)
            return carry

        lax.fori_loop(0, hidden // step, body, 0)

    def swap(n, fn, weights):
        step = r["buf_up"].shape[1]
        slot = n % 2

        def part(i):
            cut = pl.ds(pl.multiple_of(i * step, 128), step)
            return links.make(
                r["send"].at[:, cut], r["came"].at[slot, :, cut], swap_n[n] + i, at.dp, True
            )

        def body(i, w):
            r["send"][:, pl.ds(pl.multiple_of(i * step, 128), step)] = fn(w)
            part(i).start()

        stream(weights, r["buf_up"], r["sem_up"], body)

        def finish(i, carry):
            part(i).wait()
            return carry

        lax.fori_loop(0, weights.shape[0] // step, finish, 0)

    swap_n = [links.numbers(wide // r["buf_up"].shape[1]) for _ in range(3)]

    def norm_grad(n, xh, rstd, gain, base, row, out_rows, store):
        step = out_rows

        def body(i, carry):
            at_i = pl.ds(pl.multiple_of(i * step, step), step)
            val = r["send"][at_i, :] + r["came"][n % 2, at_i, :]
            high = val.astype(bf16)
            low = (val - high.astype(f32)).astype(bf16)
            dh = dot_nn(high, st[...]) + dot_nn(low, st[...])
            x = xh[at_i, :]
            small[row : row + 1, 0:width] += jnp.sum(dh * x, axis=0, keepdims=True)
            small[row : row + 1, wide : wide + width] += jnp.sum(dh, axis=0, keepdims=True)
            dxh = dh * r["gains"][gain : gain + 1, 0:width]
            inner = (
                dxh
                - jnp.mean(dxh, axis=-1, keepdims=True)
                - x * jnp.mean(dxh * x, axis=-1, keepdims=True)
            )
            store(i, at_i, base[at_i, :].astype(f32)[:, :width] + r["rstd"][at_i, rstd : rstd + 1] * inner)
            return carry

        lax.fori_loop(0, length // step, body, 0)

    def mid():
        fill_spread(st, rows, rp)
        swap(0, lambda w: dot_nt(dub[...], w[...]), r["w_up"])
        drc[...] = jnp.zeros_like(drc)

        def store(i, at_i, val):
            r["dres"][at_i, :] = val
            small[7:8, wide : wide + width] += jnp.sum(val, axis=0, keepdims=True)
            own = jnp.where(at.core == 0, val[:, :half], val[:, half:])
            drc[at_i, 3 * hw - shift : 3 * hw - shift + half] = own.astype(bf16)

        norm_grad(0, r["xh2"], 1, 2, cot, 5, 128, store)
        swap(1, lambda w: dot_nt(drc[...], w[:, shift:]), r["w_joined"])
        summed = (r["send"][...] + r["came"][1]).astype(bf16)

        for c in range(2):
            @pl.when(at.core == c)
            def _():
                first = 0 if c == 0 else width - hw
                val = dot_nn(summed, st[:, first : first + hw])
                if c == 1 and over:
                    lane = lax.broadcasted_iota(jnp.int32, val.shape, 1)
                    val = jnp.where(lane < over, 0.0, val)
                r["do"][...] = val.astype(bf16)

    def attention():
        allowed = may_see(r["seg_rows"][...], r["seg_cols"][...])
        dp[:, shift:] = jnp.zeros((length, joined - shift), bf16)
        rows_dim = (((0,), (0,)), ((), ()))
        for h in range(own_heads):
            here = [slice(i * hw + h * HD, i * hw + (h + 1) * HD) for i in range(3)]
            q, k, v, do = (r[n][:, here[0]] for n in ("q", "k", "v", "do"))
            probs = jnp.exp(head_scores(q, k, allowed) - r["lse"][:, h : h + 1])
            grad_probs = dot_nt(do, v)
            delta = jnp.sum(probs * grad_probs, axis=-1, keepdims=True)
            grad_scores = (probs * (grad_probs - delta) * HD ** (-0.5)).astype(bf16)
            dq = dot_nn(grad_scores, k)
            dk = lax.dot_general(grad_scores, q, rows_dim, preferred_element_type=f32)
            dv = lax.dot_general(probs.astype(bf16), do, rows_dim, preferred_element_type=f32)
            small[7:8, here[0]] = jnp.sum(dq, axis=0, keepdims=True)
            small[7:8, here[1]] = jnp.sum(dv, axis=0, keepdims=True)
            for at_h, val in zip(here, (dq, dk, dv)):
                dp[:, at_h] = val.astype(bf16)

    def last_norm():
        cut = up_to(3 * hw, 128)
        swap(2, lambda w: dot_nt(dp[:, :cut], w[:, :cut]), r["w_joined"])

        def store(i, at_i, val):
            @pl.when(i == at.core)
            def _():
                r["grad_input"][...] = val.T

        norm_grad(2, r["xh1"], 0, 0, r["dres"], 4, length // 2, store)

    def grad_joined(k):
        top = pl.multiple_of(dest[k] * 4 * rp, 16)

        def put(n, val):
            val = val.reshape(4, rp, val.shape[-1])
            val = jnp.concatenate([val[:, : rp - 8], val[:, rp - 8 :] + small[:, n][None]], axis=1)
            r["g0"][pl.ds(dest[k] * 4, 4), :, n] = val.astype(bf16)

        step = 256

        def body(i, carry):
            n = pl.ds(pl.multiple_of(i * step, 128), step)
            put(n, dot_nn(r["tall"][pl.ds(top, 4 * rp), :], dp[:, n]))
            return carry

        lax.fori_loop(0, shift // step, body, 0)

        def both(i, carry):
            n = pl.ds(pl.multiple_of(shift + i * step, 128), step)
            m = pl.ds(pl.multiple_of(i * step, 128), step)
            put(
                n,
                dot_nn(r["tall"][pl.ds(top, 4 * rp), :], dp[:, n])
                + dot_nn(r["tall"][pl.ds(wide + top, 4 * rp), :], drc[:, m]),
            )
            return carry

        lax.fori_loop(0, (joined - shift) // step, both, 0)

    h = rows // 2
    part_n = links.numbers(4)

    def trade(sums, base, n):
        high = up_to(h, 8)
        for c in range(2):
            @pl.when(at.core == c)
            def _():
                for e in range(2):
                    r["send"][base + e * high : base + e * high + h, :] = sums[
                        (1 - c) * h : (2 - c) * h, e * wide : (e + 1) * wide
                    ]
        cut = pl.ds(base, 2 * high)
        return links.make(r["send"].at[cut, :], r["came"].at[1, cut, :], part_n + n, at.dp, True)

    def halves(sums, base):
        high = up_to(h, 8)
        for c in range(2):
            def rows_by(s, lo, hi, c=c):
                if s == c:
                    return sums[c * h : (c + 1) * h, lo:hi]
                if hi <= wide or lo >= wide:
                    e = 0 if hi <= wide else 1
                    top = base + e * high
                    return r["came"][1, top : top + h, lo - e * wide : hi - e * wide]
                return jnp.concatenate([rows_by(s, lo, wide), rows_by(s, wide, hi)], axis=1)
            yield c, rows_by

    def fc_out():
        sums = r["sums1"]
        copy = trade(sums, 0, 0)
        copy.start()
        copy.wait()
        for c, rows_by in halves(sums, 0):
            @pl.when(at.core == c)
            def _():
                for j in range(hidden // fp):
                    for s in range(2):
                        lo, to = j * fp, (2 * j + s) * fh
                        cuts = [lo, lo + fh] if not lo < wide < lo + fh else [lo, wide, lo + fh]
                        for u, v in zip(cuts, cuts[1:]):
                            r["fc_grad"][:, to + u - lo : to + v - lo] = rows_by(s, u, v)

    def attn_out():
        sums = r["sums0"]
        base = 2 * up_to(h, 8)
        copy = trade(sums, base, 1)
        copy.start()
        r["row"][...] = sums[rp - 8 :, :]
        row_copy = links.make(r["row"], r["row_came"], part_n + 2, at.dp, True)
        row_copy.start()
        copy.wait()
        row_copy.wait()
        for c, rows_by in halves(sums, base):
            @pl.when(at.core == c)
            def _():
                for i in range(4):
                    size, skip = (hw, over) if i < 3 else (half, 0)
                    to, out = (i * width, r["attn_grad"]) if i < 3 else (0, r["out_grad"])
                    for s, lo in ((0, i * hw), (1, i * hw + skip)):
                        hi = i * hw + size
                        cuts = [lo, hi] if not lo < wide < hi else [lo, wide, hi]
                        for u, v in zip(cuts, cuts[1:]):
                            out[:, to + u - lo : to + v - lo] = rows_by(s, u, v)
                        to += hi - lo
                kinds = r["kinds"]
                kinds[...] = jnp.zeros_like(kinds)
                own = r["row"]
                low, high = (r["row"], r["row_came"]) if c == 0 else (r["row_came"], r["row"])
                for i, (line, first) in enumerate(((4, 0), (4, wide), (5, 0), (5, wide))):
                    kinds[i : i + 1, 0:width] = own[line : line + 1, first : first + width]
                for i in range(2):
                    kinds[4 + i : 5 + i, 0:hw] = low[7:8, i * hw : (i + 1) * hw]
                    kinds[4 + i : 5 + i, hw:width] = high[7:8, i * hw + over : (i + 1) * hw]
                kinds[6:7, 0:width] = own[7:8, wide : wide + width]
                kinds[7:8, 0:width] = r["sums2"][fp - 8 : fp - 7, 0:width]
        size = width // (2 * nz)
        device = at.dp * 2 + at.core
        kind, block = device // (2 * nz), lax.rem(device, 2 * nz)
        for i, place in enumerate((kind, 4 + kind)):
            line = jnp.broadcast_to(r["kinds"][pl.ds(place, 1), :], (8, wide))
            r["small_out"][8 * i : 8 * i + 8, :] = pltpu.roll(line, lax.rem(wide - block * size, wide), 1)
        line = jnp.broadcast_to(r["row"][6:7, :], (8, hidden))
        line = pltpu.roll(line, lax.rem(hidden - at.dp * fp, hidden), 1)
        r["small_out"][16:24, :] = line[:, :wide]

    links.add(-1.0, setup)
    for k in range(nz):
        links.add(1.0 * k, functools.partial(grad_down, k))
    links.add(4.95, lambda: fetched(LOADED[:1]))
    links.add(9.95, lambda: fetched(LOADED[1:2]))
    links.add(19.95, lambda: fetched(LOADED[2:]))
    links.add(4.9, lambda: tall("a1t_ot").start())
    links.add(49.9, lambda: tall("a1t_ot").wait())
    links.add(5.0, grad_hidden)
    for k in range(nz):
        links.add(10.0 + k, functools.partial(grad_up, k))
    links.add(20.0, mid)
    links.add(31.0, attention)
    links.add(33.0, last_norm)
    for k in range(nz):
        links.add(50.0 + k, functools.partial(grad_joined, k))
    grads, sums = ("g0", "g1", "g2"), ("sums0", "sums1", "sums2")
    for n, item in enumerate(items):
        scatter_item(
            links, nz, dest, item, r[grads[item[0]]], r[sums[item[0]]],
            bufs[4 * n : 4 * n + 4], functools.partial(step_time, nz, item),
        )
    links.add(55.1, fc_out)
    links.add(99.0, attn_out)
    links.run()


def step_time(nz, item, stage, k):
    array, _, _, _, kind = item
    k = min(k, 3)
    if kind == "pz":
        return {
            "start": (0.6, 10.6, 20.5),
            "chain": (20.6, 31.7, 33.9),
            "gathered": (51.95,),
            "first": (51.96,),
            "second": (54.45,),
            "third": (55.5,),
        }[stage][k]
    return {
        2: {
            "first": (0.5, 1.5, 9.2, 18.2),
            "second": (9.0, 18.0, 30.0, 32.0),
            "third": (18.1, 30.1, 32.1, 41.0),
        },
        1: {
            "first": (18.3, 18.4, 30.2, 32.3),
            "second": (32.2, 41.1, 51.6, 54.0),
            "third": (41.2, 51.7, 54.3, 54.6),
        },
        0: {
            "first": (50.5, 51.5, 54.2, 54.8),
            "second": (54.1, 54.5, 54.9, 56.0),
            "third": (54.7, 55.0, 56.1, 56.2),
        },
    }[array][stage][k]


def back_call(nz, items, pieces, sizes, inputs, hbm, outs, collective_id):
    bf16, f32 = jnp.bfloat16, jnp.float32
    own_heads, rows, rp, fh, fp, half, over = sizes
    length, wide = inputs["cot"].shape
    width = hbm["xh1"].shape[1]
    hidden = hbm["slope"].shape[1]
    joined = hbm["w_joined"].shape[1]
    shift = 3 * own_heads * HD // 256 * 256
    bufs, sems = item_bufs(nz, pieces, items)
    sems += 3 * (wide // 384) + 4
    scratch = {
        "g0": pltpu.VMEM(pieces[0], bf16),
        "g1": pltpu.VMEM(pieces[1], bf16),
        "g2": pltpu.VMEM(pieces[2], bf16),
        "st": pltpu.VMEM((wide, width), bf16),
        "small": pltpu.VMEM((8, joined), f32),
        "small_d": pltpu.VMEM((8, wide), f32),
        "dub": pltpu.VMEM((length, hidden), bf16),
        "dp": pltpu.VMEM((length, joined), bf16),
        "drc": pltpu.VMEM((length, joined - shift), bf16),
        "do": pltpu.VMEM((length, own_heads * HD), bf16),
        "dres": pltpu.VMEM((length, width), f32),
        "send": pltpu.VMEM((length, wide), f32),
        "came": pltpu.VMEM((2, length, wide), f32),
        "sums0": pltpu.VMEM(pieces[0][1:], f32),
        "sums1": pltpu.VMEM(pieces[1][1:], f32),
        "tall": pltpu.VMEM((max(hidden, 2 * wide), length), bf16),
        "sem_tall": pltpu.SemaphoreType.DMA((1,)),
        "row": pltpu.VMEM((8, joined), f32),
        "row_came": pltpu.VMEM((8, joined), f32),
        "kinds": pltpu.VMEM((8, wide), f32),
        "buf_down": pltpu.VMEM((2, 256, wide), bf16),
        "buf_up": pltpu.VMEM((2, 384, joined), bf16),
        "sem_down": pltpu.SemaphoreType.DMA((2,)),
        "sem_up": pltpu.SemaphoreType.DMA((2,)),
        "send_sem": pltpu.SemaphoreType.DMA((sems,)),
        "recv_sem": pltpu.SemaphoreType.DMA((sems,)),
    }
    for n in LOADED:
        scratch[n] = pltpu.VMEM(hbm[n].shape, hbm[n].dtype)
    scratch["in_sem"] = pltpu.SemaphoreType.DMA((len(LOADED),))
    far_names = ["far_" + n if n in LOADED else n for n in hbm]
    names = (*inputs, *far_names, *outs, *scratch)
    vmem, far = pl.BlockSpec(memory_space=pltpu.VMEM), pl.BlockSpec(memory_space=pl.ANY)
    return pl.pallas_call(
        functools.partial(back_kernel, nz, items, sizes, names),
        out_shape=list(outs.values()),
        in_specs=[vmem] * len(inputs) + [far] * len(hbm),
        out_specs=[vmem] * len(outs),
        scratch_shapes=[*scratch.values(), *bufs],
        compiler_params=pltpu.CompilerParams(
            collective_id=collective_id, has_side_effects=True, vmem_limit_bytes=63 * 2**20
        ),
    )(*inputs.values(), *hbm.values())


def gather_item(links, nz, item, src, out, times):
    at = links.at
    _, lo, mid, hi, kind = item
    part = {"all": pl.ds(lo, hi - lo), "a": pl.ds(lo, mid - lo), "b": pl.ds(mid, hi - mid)}
    base = links.numbers((2 * nz - 1) * 8)

    def number(stage, q, p):
        return base + (q + nz - 1) * 8 + stage * 4 + p

    def send(n, piece, to, cut="all", own=False):
        q, p = piece

        def make(ref=None):
            dst = out.at[at.chip(q, p), :, part[cut]]
            return links.make(dst if ref is None else ref, dst, n, at.chip(*to))

        make(src.at[:, part[cut]] if own else None).start()

        def done():
            flag = jnp.logical_and(at.has(q), at.has(to[0]))
            pl.when(flag)(lambda: make().wait_send())

        links.ends.append(done)

    def came(n, chip, cut="all"):
        links.came(out.at[chip, :, part[cut]], n)

    def along(q, p, own=False):
        for go in (1, -1) if q == 0 else ((-1,) if q > 0 else (1,)):
            if abs(q - go) < nz:
                @pl.when(at.has(go))
                def _():
                    send(number(0, q - go, p), (q, p), (go, 0), "all", own)

    def across(q, own=False):
        for p in (1, 2):
            send(number(1, q, p - 1), (q, 0), (0, p), "all", own)

    def relay(q, p):
        came(number(1, q, p - 1), at.chip(q, p))
        send(number(1, q, p + 1), (q, p), (0, 3 - p), "ab"[p - 1])

    def corner(q):
        for p in (1, 2):
            came(number(1, q, p + 1), at.chip(q, 3), "ab"[p - 1])

    def put(when, q, fn):
        links.add(when, fn if q == 0 else lambda: pl.when(at.has(q))(fn))

    def arrive(q, p=0):
        came(number(0, q, p), at.chip(q, p))
        along(q, p)

    if kind == "zp":
        for q in slots(nz):
            if q == 0:
                put(times("z", 0), 0, lambda: along(0, 0, True))
                put(times("plane", 0), 0, lambda: across(0, True))
            else:
                put(times("z", q), q, lambda q=q: arrive(q))
                put(times("plane", q), q, lambda q=q: across(q))
            put(times("relay", q), q, lambda q=q: [relay(q, p) for p in (1, 2)] and None)
            put(times("last", q), q, lambda q=q: corner(q))
        return
    put(times("plane", 0), 0, lambda: across(0, True))
    put(times("own", 0), 0, lambda: along(0, 0, True))
    for p in (1, 2):
        put(times("relay", 0), 0, lambda p=p: relay(0, p))
        put(times("own", 0), 0, lambda p=p: along(0, p))

    def diagonal():
        corner(0)
        along(0, 3)

    put(times("own", 0) + 0.01, 0, diagonal)
    for q in slots(nz)[1:]:
        for p in range(4):
            put(times("z", q) + 0.01 * p, q, lambda q=q, p=p: arrive(q, p))


def gather_time(item, stage, q):
    array, _, _, _, kind = item
    d = abs(q)
    if kind == "pz":
        return {"plane": 3.2, "relay": 4.8, "own": 5.6, "z": (0, 9.9, 12.3, 13.9)[d]}[stage]
    if array == 0:
        return {"z": 1.0 * d, "plane": 1.0 * d + 0.01, "relay": 1.6 + 1.4 * d, "last": 6.2}[stage]
    if array == 1:
        return {
            "z": (3.0, 4.2, 5.4, 6.6)[d], "plane": (5.0, 5.5, 6.7, 7.4)[d],
            "relay": (7.0, 8.4, 8.5, 11.0)[d], "last": 12.0,
        }[stage]
    return {
        "z": (6.8, 7.45, 8.45, 9.95)[d], "plane": (10.1, 10.2, 10.3, 10.4)[d],
        "relay": (12.5, 12.51, 12.52, 12.53)[d], "last": 14.5,
    }[stage]


EARLY = ("a1t_ot", "a2t", "q", "k", "v", "lse", "xh1", "xh2", "rstd", "gains")
LATER = ("gt", "slope")


def forward_kernel(nz, items, sizes, names, *refs):
    f32, bf16 = jnp.float32, jnp.bfloat16
    r = dict(zip(names, refs))
    own_heads, rows, rp, fh, fp, half, over, small = sizes
    hw = own_heads * HD
    at = Place(nz)
    links = Links(at, r["send_sem"], r["recv_sem"])
    acts, st, par = r["acts"], r["st"], r["par"]
    length, width = acts.shape
    wide = st.shape[0]
    hidden = r["gt"].shape[0]
    joined = r["w2d"].shape[1]
    shift = 3 * hw // 128 * 128
    skip = 3 * hw - shift
    chips = 4 * nz
    outs = ("attn_all", "fc_all", "proj_all")
    ins = ("attn_piece", "fc_piece", "proj_piece")
    own = [
        pltpu.make_async_copy(r[i], r[o].at[at.dp], r["sem"].at[n])
        for n, (i, o) in enumerate(zip(ins, outs))
    ]
    for copy in own:
        copy.start()
    at.meet(True)
    trade_n = links.numbers(3)

    def trade(n, mine, theirs):
        copy = links.make(mine, theirs, trade_n + n, at.dp, True)
        copy.start()
        copy.wait()

    def normalise(value, xh_ref, column):
        mu = jnp.mean(value, axis=-1, keepdims=True)
        centred = value - mu
        inv = lax.rsqrt(jnp.mean(centred * centred, axis=-1, keepdims=True) + NORM_EPS)
        return centred * inv, inv

    step = 64

    def by_rows(fn):
        def body(i, carry):
            fn(pl.ds(pl.multiple_of(i * step, step), step))
            return carry
        lax.fori_loop(0, length // step, body, 0)

    def prepare():
        fill_spread(st, rows, rp)

        def one(cut):
            xh, inv = normalise(acts[cut, :].astype(f32), None, 0)
            r["xh1"][cut, :] = xh
            r["rstd"][cut, 0:1] = inv

        by_rows(one)

    def load(name, n):
        own[n].wait()
        copy = pltpu.make_async_copy(r[name], r["w3d"], r["sem"].at[3])
        copy.start()
        copy.wait()

    def flatten():
        def body(i, carry):
            r["w2d"][pl.ds(pl.multiple_of(i * 2 * rp, 16), 2 * rp), :] = jnp.concatenate(
                [r["w3d"][2 * i], r["w3d"][2 * i + 1]], axis=0
            )
            return carry
        lax.fori_loop(0, chips // 2, body, 0)

    def parameters():
        par[...] = jnp.zeros_like(par)
        r["up_bias"][...] = jnp.zeros_like(r["up_bias"])
        for j in range(chips):
            block = r["w3d"][j, rp - 8 :, 0 : 3 * small].astype(f32)
            for c in range(2):
                line = block[rows - rp + 8 + c : rows - rp + 9 + c, :]
                device = 2 * j + c
                kind, lane = device // (2 * nz), device % (2 * nz) * small
                par[kind : kind + 1, lane : lane + small] = line[:, 0:small]
                par[4 + kind : 5 + kind, lane : lane + small] = line[:, small : 2 * small]

                @pl.when(at.core == c)
                def _():
                    r["up_bias"][0:1, j * fp : j * fp + fh] = line[:, 2 * small :]

    def spread_both(value, t_ref, first_row):
        t_ref[first_row : first_row + wide, :] = dot_nt(st[...], value).astype(bf16)
        r["spread"][...] = dot_nt(value, st[...]).astype(bf16)

    def unpack_step():
        load("attn_all", 0)
        parameters()
        flatten()

    def query_step():
        def one(cut):
            a = r["xh1"][cut, :] * par[0:1, 0:width] + par[1:2, 0:width]
            r["act"][cut, :] = a.astype(bf16)

        by_rows(one)
        spread_both(r["act"][...], r["a1t_ot"], 0)
        size = 256

        def body(i, carry):
            n = pl.ds(pl.multiple_of(i * size, 128), size)
            r["p"][:, n] = dot_nn(r["spread"][...], r["w2d"][:, n])
            return carry

        lax.fori_loop(0, r["p"].shape[1] // size, body, 0)
        low = at.core == 0
        for i, (name, line) in enumerate((("q", 4), ("k", None), ("v", 5))):
            val = r["p"][:, i * hw : (i + 1) * hw]
            if line is not None:
                val = val + jnp.where(
                    low, par[line : line + 1, 0:hw], par[line : line + 1, width - hw : width]
                )
            r[name][...] = val.astype(bf16)

    def attention():
        allowed = may_see(r["seg_rows"][...], r["seg_cols"][...])
        attend(head_scores, own_heads, r["lse"], r["q"], r["k"], r["v"], r["o"], allowed)

    def mix():
        low = at.core == 0
        trade(0, r["o"], r["o_came"])
        first = jnp.where(low, r["o"][...], r["o_came"][...])
        second = jnp.where(low, r["o_came"][...], r["o"][...])
        if over:
            lane = lax.broadcasted_iota(jnp.int32, second.shape, 1)
            second = jnp.where(lane < over, jnp.zeros((), bf16), second)
        st_low, st_high = st[:, 0:hw], st[:, width - hw : width]
        r["a1t_ot"][wide : 2 * wide, :] = (dot_nt(st_low, first) + dot_nt(st_high, second)).astype(bf16)
        r["spread"][...] = (dot_nt(first, st_low) + dot_nt(second, st_high)).astype(bf16)
        r["mixed"][...] = dot_nn(r["spread"][...], r["w2d"][:, shift:])

    def second_norm():
        low = at.core == 0
        trade(1, r["mixed"], r["mixed_came"])
        r["resid"][:, 0:half] = jnp.where(
            low, r["mixed"][:, skip : skip + half], r["mixed_came"][:, skip : skip + half]
        )
        r["resid"][:, half : 2 * half] = jnp.where(
            low, r["mixed_came"][:, skip : skip + half], r["mixed"][:, skip : skip + half]
        )

        def one(cut):
            val = acts[cut, :].astype(f32) + r["resid"][cut, :] + par[6:7, 0:width]
            r["resid"][cut, :] = val
            xh, inv = normalise(val, None, 1)
            r["xh2"][cut, :] = xh
            r["rstd"][cut, 1:2] = inv
            r["act"][cut, :] = (xh * par[2:3, 0:width] + par[3:4, 0:width]).astype(bf16)

        by_rows(one)
        spread_both(r["act"][...], r["a2t"], 0)
        r["gains"][...] = par[...]

    def hidden_step(part):
        if part == 0:
            load("fc_all", 1)
            flatten()
        size = 256

        def body(i, carry):
            n = pl.ds(pl.multiple_of(i * size, 128), size)
            u = dot_nn(r["spread"][...], r["w2d"][:, n]) + r["up_bias"][0:1, n]
            value, slope = gelu_parts(u)
            r["g"][:, n] = value.astype(bf16)
            r["gt"][n, :] = value.T.astype(bf16)
            r["slope"][:, n] = (slope * r["real"][0:1, n]).astype(bf16)
            return carry

        count = hidden // size
        lax.fori_loop(part * count // 3, (part + 1) * count // 3, body, 0)

    def result_step():
        own[2].wait()
        copy = pltpu.make_async_copy(r["proj_all"], r["wd3"], r["sem"].at[3])
        copy.start()
        copy.wait()
        size, some = 384, chips // 2
        tokens = length // 2

        def body(i, carry):
            n = pl.ds(pl.multiple_of(i * size, 128), size)
            total = 0.0
            for e in range(2):
                w = r["wd3"][e * some : (e + 1) * some, :, n].reshape(some * fp, size)
                total = total + dot_nn(r["g"][:, e * some * fp : (e + 1) * some * fp], w)
            r["down"][:, n] = total
            return carry

        lax.fori_loop(0, wide // size, body, 0)
        theirs = pl.ds(pl.multiple_of((1 - at.core) * tokens, tokens), tokens)
        mine = pl.ds(pl.multiple_of(at.core * tokens, tokens), tokens)
        trade(2, r["down"].at[theirs, :], r["down_came"])
        total = (
            r["resid"][mine, :]
            + (r["down"][mine, 0:width] + r["down_came"][:, 0:width])
            + par[7:8, 0:width]
        )
        r["result"][...] = total.T.astype(bf16)

    def leave(names_, first):
        for n, name in enumerate(names_):
            pltpu.make_async_copy(r[name], r["far_" + name], r["out_sem"].at[first + n]).start()

    def left():
        for n, name in enumerate((*EARLY, *LATER)):
            pltpu.make_async_copy(r[name], r["far_" + name], r["out_sem"].at[n]).wait()

    links.add(12.1, lambda: leave(EARLY, 0))
    links.add(12.66, lambda: leave(LATER, len(EARLY)))
    links.add(99.0, left)
    links.add(0.5, prepare)
    links.add(6.3, unpack_step)
    links.add(6.9, query_step)
    links.add(7.42, attention)
    links.add(8.42, mix)
    links.add(9.0, second_norm)
    for part, when in enumerate((12.2, 12.45, 12.65)):
        links.add(when, functools.partial(hidden_step, part))
    links.add(15.0, result_step)
    for item in items:
        gather_item(links, nz, item, r[ins[item[0]]], r[outs[item[0]]], functools.partial(gather_time, item))
    links.run()


def forward_call(nz, items, sizes, inputs, pieces, collective_id):
    bf16, f32 = jnp.bfloat16, jnp.float32
    own_heads, rows, rp, fh, fp, half, over, small = sizes
    hw = own_heads * HD
    length, width = inputs["acts"].shape
    attn, fc, proj = pieces.values()
    chips, joined, hidden, wide = 4 * nz, attn.shape[1], fc.shape[1], proj.shape[1]
    shape = jax.ShapeDtypeStruct
    landing = {
        n: shape((chips, *p.shape), bf16)
        for n, p in zip(("attn_all", "fc_all", "proj_all"), (attn, fc, proj))
    }
    outs = {
        "a1t_ot": shape((2 * wide, length), bf16),
        "a2t": shape((wide, length), bf16),
        "gt": shape((hidden, length), bf16),
        "slope": shape((length, hidden), bf16),
        "q": shape((length, hw), bf16),
        "k": shape((length, hw), bf16),
        "v": shape((length, hw), bf16),
        "lse": shape((length, 128), f32),
        "xh1": shape((length, width), f32),
        "xh2": shape((length, width), f32),
        "rstd": shape((length, 2), f32),
        "gains": shape((8, wide), f32),
        "result": shape((width, length // 2), bf16),
    }
    mixed = joined - 3 * hw // 128 * 128
    sems = len(items) * (2 * nz - 1) * 8 + 3
    scratch = {
        "w3d": pltpu.VMEM((chips, *attn.shape), bf16),
        "w2d": pltpu.VMEM((chips * rp, joined), bf16),
        "wd3": pltpu.VMEM((chips, *proj.shape), bf16),
        "st": pltpu.VMEM((wide, width), bf16),
        "par": pltpu.VMEM((8, wide), f32),
        "up_bias": pltpu.VMEM((8, hidden), f32),
        "act": pltpu.VMEM((length, width), bf16),
        "spread": pltpu.VMEM((length, wide), bf16),
        "p": pltpu.VMEM((length, up_to(3 * hw, 256)), f32),
        "o": pltpu.VMEM((length, hw), bf16),
        "o_came": pltpu.VMEM((length, hw), bf16),
        "mixed": pltpu.VMEM((length, mixed), f32),
        "mixed_came": pltpu.VMEM((length, mixed), f32),
        "resid": pltpu.VMEM((length, width), f32),
        "g": pltpu.VMEM((length, hidden), bf16),
        "down": pltpu.VMEM((length, wide), f32),
        "down_came": pltpu.VMEM((length // 2, wide), f32),
        "sem": pltpu.SemaphoreType.DMA((4,)),
        "send_sem": pltpu.SemaphoreType.DMA((sems,)),
        "recv_sem": pltpu.SemaphoreType.DMA((sems,)),
    }
    far_names = [n if n == "result" else "far_" + n for n in outs]
    for n in (*EARLY, *LATER):
        scratch[n] = pltpu.VMEM(outs[n].shape, outs[n].dtype)
    scratch["out_sem"] = pltpu.SemaphoreType.DMA((len(EARLY) + len(LATER),))
    names = (*inputs, *pieces, *landing, *far_names, *scratch)
    vmem, far = pl.BlockSpec(memory_space=pltpu.VMEM), pl.BlockSpec(memory_space=pl.ANY)
    got = pl.pallas_call(
        functools.partial(forward_kernel, nz, items, sizes, names),
        out_shape=[*landing.values(), *outs.values()],
        in_specs=[vmem] * len(inputs) + [far] * len(pieces),
        out_specs=[far] * len(landing) + [vmem if n == "result" else far for n in outs],
        scratch_shapes=list(scratch.values()),
        compiler_params=pltpu.CompilerParams(
            collective_id=collective_id, has_side_effects=True, vmem_limit_bytes=60 * 2**20
        ),
    )(*inputs.values(), *pieces.values())
    return dict(zip((*landing, *outs), got))


def attend(scores_of, heads, lse_ref, q_ref, k_ref, v_ref, o_ref, allowed):
    for h in range(heads):
        at = slice(h * HD, (h + 1) * HD)
        scores = scores_of(q_ref[:, at], k_ref[:, at], allowed)
        top = jnp.max(scores, axis=-1, keepdims=True)
        total = top + jnp.log(jnp.sum(jnp.exp(scores - top), axis=-1, keepdims=True))
        probs = jnp.exp(scores - total).astype(jnp.bfloat16)
        lse_ref[:, h : h + 1] = total
        o_ref[:, at] = jnp.dot(
            probs, v_ref[:, at], preferred_element_type=jnp.float32
        ).astype(o_ref.dtype)


def head_scores(queries, key_rows, allowed):
    scores = lax.dot_general(
        queries, key_rows, (((1,), (1,)), ((), ())), preferred_element_type=jnp.float32
    ) * HD ** (-0.5)
    return jnp.where(allowed, scores, -1e30)


def may_see(seg_rows, seg_cols):
    length = seg_cols.shape[1]
    i = lax.broadcasted_iota(jnp.int32, (length, length), 0)
    j = lax.broadcasted_iota(jnp.int32, (length, length), 1)
    return (j <= i) & (seg_rows == seg_cols)


def up_to(value, step):
    return -(-value // step) * step


def per_device_grid(
    nz,
    layer_input,
    segments,
    w_attn,
    w_out,
    w_fc,
    w_proj,
    norm_params,
    lin_bias,
    fc_bias,
    out_cotangent,
):
    f32, bf16 = jnp.float32, jnp.bfloat16
    core = lax.axis_index("seq")
    low = core == 0
    chips = lax.axis_size("dp")
    tokens, width = layer_input.shape[1:]
    heads = width // HD
    own_heads = -(-heads // 2)
    hw = own_heads * HD
    over = 2 * hw - width
    half = width // 2
    small = norm_params.shape[0]
    h = w_out.shape[0] // width
    rows, rp = 2 * h, up_to(2 * h, 8)
    fh = w_proj.shape[0] // width
    fp = up_to(fh + 2, 16)
    hidden = chips * fp
    wide = up_to(width, 128)
    owide = up_to(3 * hw + half, 128) - 3 * hw

    def swap(value):
        return lax.ppermute(value, "seq", [(0, 1), (1, 0)])

    def pair(own, came):
        return jnp.where(low, own, came), jnp.where(low, came, own)

    def lanes_of(value, size):
        first, second = value[..., :size], value[..., value.shape[-1] - size :]
        return jnp.where(low, first, second), jnp.where(low, second, first)

    own_small = jnp.concatenate([norm_params, lin_bias, fc_bias])
    wa = w_attn.reshape(h, 3 * width)
    wo = w_out.reshape(h, width)
    wf = w_fc.reshape(h, chips, 2, fh)
    parts = [lanes_of(wa[:, i * width : (i + 1) * width], hw) for i in range(3)]
    parts.append(lanes_of(wo, half))
    gap = jnp.zeros((h, owide - half), bf16)
    attn_own, attn_other = (
        jnp.concatenate([p[i] for p in parts] + [gap], axis=1) for i in range(2)
    )
    fc_pads = ((0, 0), (0, 0), (0, fp - fh))
    fc_own, fc_other = (
        jnp.pad(jnp.where(low == first, wf[:, :, 0], wf[:, :, 1]), fc_pads).reshape(h, hidden)
        for first in (True, False)
    )
    attn_came, fc_came = swap(attn_other), swap(fc_other)
    acts_came = swap(jnp.stack([layer_input[0], out_cotangent[0]]))
    small_came = swap(own_small)
    row_pads = ((0, rp - rows), (0, 0))
    small_rows = jnp.pad(
        jnp.stack(pair(own_small, small_came)), ((0, rp - rows - 2), (0, 3 * hw + owide - 3 * small))
    )
    attn_piece = jnp.concatenate([*pair(attn_own, attn_came), small_rows])
    fc_piece = jnp.pad(jnp.concatenate(pair(fc_own, fc_came)), row_pads)
    proj_piece = jnp.pad(w_proj.reshape(fh, width), ((0, fp - fh), (0, wide - width)))
    acts = jnp.concatenate(pair(layer_input[0], acts_came[0]))
    cotangent = jnp.concatenate(pair(out_cotangent[0], acts_came[1]))
    cot_wide = jnp.pad(cotangent, ((0, 0), (0, wide - width)))
    seg_rows, seg_cols = segments.reshape(-1, 1), segments.reshape(1, -1)
    real = jnp.pad(jnp.ones((1, chips, fh), f32), ((0, 0), (0, 0), (0, fp - fh))).reshape(1, hidden)
    shape = jax.ShapeDtypeStruct
    third, joined = up_to(wide // 3, 128), attn_piece.shape[1]
    cuts = (
        (0, 0, up_to(joined // 2, 128), joined, "zp"),
        (1, 0, up_to(hidden // 2, 128), hidden, "zp"),
        (2, 2 * third, 2 * third + up_to((wide - 2 * third) // 2, 128), wide, "zp"),
        (2, 0, third, 2 * third, "pz"),
    )
    back_cuts = (
        (2, 0, up_to(third // 2, 128), third, "pz"),
        (2, third, 2 * third, wide, "zp"),
        (1, 0, up_to(hidden // 2, 128), hidden, "zp"),
        (0, 0, up_to(joined // 2, 128), joined, "zp"),
    )
    sizes = (own_heads, rows, rp, fh, fp, half, over)
    done = forward_call(
        nz,
        cuts,
        (*sizes, small),
        {"acts": acts, "seg_rows": seg_rows, "seg_cols": seg_cols, "real": real},
        {"attn_piece": attn_piece, "fc_piece": fc_piece, "proj_piece": proj_piece},
        0,
    )
    attn_grad, out_grad, fc_grad, sums2, grad_input, small_out = back_call(
        nz,
        back_cuts,
        tuple(done[n].shape for n in ("attn_all", "fc_all", "proj_all")),
        sizes,
        {
            "cot": cot_wide,
            "seg_rows": seg_rows,
            "seg_cols": seg_cols,
        },
        {
            **{n: done[n] for n in LOADED},
            "gt": done["gt"],
            "a1t_ot": done["a1t_ot"],
            "w_down": done["proj_all"].reshape(hidden, wide),
            "w_up": done["fc_all"].reshape(-1, hidden),
            "w_joined": done["attn_all"].reshape(-1, joined),
        },
        {
            "attn_grad": shape((h, 3 * width), f32),
            "out_grad": shape((h, width), f32),
            "fc_grad": shape((h, 2 * chips * fh), f32),
            "sums2": shape(proj_piece.shape, f32),
            "grad_input": shape((width, tokens), f32),
            "small_out": shape((24, wide), f32),
        },
        1,
    )

    return (
        done["result"].T[None],
        grad_input.T[None],
        attn_grad.reshape(-1),
        out_grad.reshape(-1),
        fc_grad.reshape(-1),
        sums2[:fh, :width].reshape(-1),
        small_out[0, :small],
        small_out[8, :small],
        small_out[16, :small],
    )


def grid_height(mesh):
    shape = dict(mesh.shape)
    devices = mesh.devices.reshape(-1)
    if tuple(mesh.axis_names) != AXES or shape["seq"] != 2 or shape["dp"] % 4:
        return 0
    nz = shape["dp"] // 4
    base = getattr(devices[0], "coords", None)
    if base is None:
        return 0
    for n, device in enumerate(devices):
        chip = n // 2
        place = (chip % 2, chip // 2 % 2, chip // 4)
        if tuple(a - b for a, b in zip(device.coords, base)) != place:
            return 0
    return nz if 1 < nz <= 4 else 0


def solution(mesh):
    nz = grid_height(mesh)
    return jax.shard_map(
        functools.partial(per_device_grid, nz) if nz else per_device,
        mesh=mesh,
        in_specs=(
            P("dp", "seq", None),
            P("dp", None),
            P(("dp", "seq")),
            P(("dp", "seq")),
            P(("dp", "seq")),
            P(("dp", "seq")),
            P(("dp", "seq")),
            P(("dp", "seq")),
            P(("dp", "seq")),
            P("dp", "seq", None),
        ),
        out_specs=(
            P("dp", "seq", None),
            P("dp", "seq", None),
            P(("dp", "seq")),
            P(("dp", "seq")),
            P(("dp", "seq")),
            P(("dp", "seq")),
            P(("dp", "seq")),
            P(("dp", "seq")),
            P(("dp", "seq")),
        ),
        check_vma=False,
    )
```
